32 devices in a mesh: seq: 16 (over z, x, core), wshard: 2 (over y).
Axes of the slice: x: 2, y: 2, z: 4, core: 2. Of those that a mesh axis runs over, the one named last changes fastest.
Arguments:
- inputs: float32 [2, 4096, 768], P('wshard', 'seq'), may hold values from -6 to 6
- lengths: int32 [2], P('wshard'), may hold values from 1024 to 4096, as said below
- cotangent: float32 [2, 4096, 768], P('wshard', 'seq'), may hold values from -6 to 6
- query_weight: float32 [768, 768], P('wshard'), may hold values from -0.21875 to 0.21875
- query_bias: float32 [768], P('wshard'), may hold values from -2 to 2
- key_weight: float32 [768, 768], P('wshard'), may hold values from -0.21875 to 0.21875
- value_weight: float32 [768, 768], P('wshard'), may hold values from -0.21875 to 0.21875
- value_bias: float32 [768], P('wshard'), may hold values from -2 to 2
- output_weight: float32 [768, 768], P('wshard'), may hold values from -6 to 6
- output_bias: float32 [768], P('wshard'), may hold values from -2 to 2
- first_gain: float32 [768], P('wshard'), may hold values from 0.25 to 1.75
- first_shift: float32 [768], P('wshard'), may hold values from -2 to 2
- up_weight: float32 [768, 3072], P('wshard'), may hold values from -0.21875 to 0.21875
- up_bias: float32 [3072], P('wshard'), may hold values from -2 to 2
- down_weight: float32 [3072, 768], P('wshard'), may hold values from -0.109375 to 0.109375
- down_bias: float32 [768], P('wshard'), may hold values from -2 to 2
- second_gain: float32 [768], P('wshard'), may hold values from 0.25 to 1.75
- second_shift: float32 [768], P('wshard'), may hold values from -2 to 2
Outputs:
- outputs: float32 [2, 4096, 768], P('wshard', 'seq')
- input_grad: float32 [2, 4096, 768], P('wshard', 'seq')
- grad_query_weight: float32 [768, 768], P('wshard')
- grad_query_bias: float32 [768], P('wshard')
- grad_key_weight: float32 [768, 768], P('wshard')
- grad_value_weight: float32 [768, 768], P('wshard')
- grad_value_bias: float32 [768], P('wshard')
- grad_output_weight: float32 [768, 768], P('wshard')
- grad_output_bias: float32 [768], P('wshard')
- grad_first_gain: float32 [768], P('wshard')
- grad_first_shift: float32 [768], P('wshard')
- grad_up_weight: float32 [768, 3072], P('wshard')
- grad_up_bias: float32 [3072], P('wshard')
- grad_down_weight: float32 [3072, 768], P('wshard')
- grad_down_bias: float32 [768], P('wshard')
- grad_second_gain: float32 [768], P('wshard')
- grad_second_shift: float32 [768], P('wshard')
The draws below stay inside these ranges and needn't reach their ends.
Inputs may be any that keep to these rules, and one draw needn't show every extreme that they name: `lengths`: some sequence has all 4096 positions valid in every draw.
All inputs are finite; a program needn't handle non-finite values.
Results may differ from the reference program's by a relative error of at most 0.024.
Values may be sent and summed in bfloat16 or wider, within the bound.
No kernel may reach another device: no remote copies, remote signals or barrier semaphores. Data moves between devices by JAX's collectives and lax.ppermute only.
A program may use at most 256 MiB of HBM per device.

```python
import jax
import jax.numpy as jnp
from jax import lax

D = 768
HEADS = 12
HD = 64
FF = 3072
SEQ_LEN = 4096
SEQS = 2


def draw_lengths(key, part):
    low_end = SEQ_LEN // 4
    drawn = jax.random.randint(jax.random.fold_in(key, 11), (SEQS,), low_end, SEQ_LEN + 1)
    longest = jax.random.randint(jax.random.fold_in(key, 12), (), 0, SEQS)
    return jnp.where(jnp.arange(SEQS) == longest, SEQ_LEN, drawn).astype(jnp.int32)


def block_scale(key, shape, cuts, low, top_value):
    gain = 1.0
    for axis_at, parts in cuts:
        draws = jax.random.uniform(jax.random.fold_in(jax.random.fold_in(key, 6), axis_at), (parts,), jnp.float32, low / len(cuts), top_value / len(cuts))
        gain = gain * jnp.repeat(jnp.exp(draws), shape[axis_at] // parts).reshape((-1,) + (1,) * (len(shape) - 1 - axis_at))
    return gain


def noise(stream_key, extent, scale, limit, shards=(), kind=jnp.bfloat16):
    loudness = block_scale(stream_key, extent, shards, -0.22, 0.18) if shards else 1.0
    values = jax.random.normal(stream_key, extent, jnp.float32) * scale * loudness
    return jnp.minimum(jnp.maximum(values, -limit), limit).astype(kind)


def setup_inputs(seed: int = 0) -> dict:
    arg_keys = jax.random.split(jax.random.key(seed), 19)
    return {
        "inputs": noise(arg_keys[0], (SEQS, SEQ_LEN, D), 1.0, 6.0, ((0, 2), (1, 16)), jnp.float32),
        "lengths": draw_lengths(jax.random.fold_in(arg_keys[18], 71), 0),
        "cotangent": noise(arg_keys[2], (SEQS, SEQ_LEN, D), 1.0, 6.0, ((0, 2), (1, 16)), jnp.float32),
        "query_weight": noise(arg_keys[3], (D, D), D ** -0.5, 0.21875, ((0, 2),), jnp.float32),
        "query_bias": noise(arg_keys[4], (D,), 0.3, 2.0, ((0, 2),), jnp.float32),
        "key_weight": noise(arg_keys[5], (D, D), D ** -0.5, 0.21875, ((0, 2),), jnp.float32),
        "value_weight": noise(arg_keys[6], (D, D), D ** -0.5, 0.21875, ((0, 2),), jnp.float32),
        "value_bias": noise(arg_keys[7], (D,), 0.3, 2.0, ((0, 2),), jnp.float32),
        "output_weight": noise(arg_keys[8], (D, D), 1.5, 6.0, ((0, 2),), jnp.float32),
        "output_bias": noise(arg_keys[9], (D,), 0.3, 2.0, ((0, 2),), jnp.float32),
        "first_gain": jnp.clip(1.0 + 0.15 * jax.random.normal(arg_keys[10], (D,), jnp.float32), 0.25, 1.75),
        "first_shift": noise(arg_keys[11], (D,), 0.3, 2.0, ((0, 2),), jnp.float32),
        "up_weight": noise(arg_keys[12], (D, FF), D ** -0.5, 0.21875, ((0, 2),), jnp.float32),
        "up_bias": noise(arg_keys[13], (FF,), 0.3, 2.0, ((0, 2),), jnp.float32),
        "down_weight": noise(arg_keys[14], (FF, D), FF ** -0.5, 0.109375, ((0, 2),), jnp.float32),
        "down_bias": noise(arg_keys[15], (D,), 0.3, 2.0, ((0, 2),), jnp.float32),
        "second_gain": jnp.clip(1.0 + 0.15 * jax.random.normal(arg_keys[16], (D,), jnp.float32), 0.25, 1.75),
        "second_shift": noise(arg_keys[17], (D,), 0.3, 2.0, ((0, 2),), jnp.float32),
    }


@jax.custom_vjp
def low(v):
    return lax.optimization_barrier(v.astype(jnp.bfloat16)).astype(jnp.float32)

@jax.custom_vjp
def low_back(v):
    return v

def low_keep(v):
    return (low(v), None)

def low_pass(kept, grad):
    return (grad,)

def back_keep(v):
    return (v, None)

def back_low(kept, grad):
    return (low(grad),)
low.defvjp(low_keep, low_pass)
low_back.defvjp(back_keep, back_low)

def matmul(left_side, right_side):
    return jnp.dot(left_side, right_side, precision=lax.Precision.HIGHEST, preferred_element_type=jnp.float32)

def layer_norm(features, norm_gain, norm_shift):
    average = lax.optimization_barrier(jnp.mean(features, axis=-1, keepdims=True))
    centered = features - average
    variance = lax.optimization_barrier(jnp.mean(centered * centered, axis=-1, keepdims=True))
    return centered * lax.rsqrt(variance + 1e-12) * norm_gain + norm_shift

def attend(queries, key_rows, value_rows, length):
    total_rows = queries.shape[0]
    block_rows = min(512, total_rows)
    key_valid = jnp.arange(total_rows, dtype=jnp.int32) < length
    query_blocks = queries.reshape(total_rows // block_rows, block_rows, HEADS, HD)
    key_heads = key_rows.reshape(total_rows, HEADS, HD)
    value_heads = value_rows.reshape(total_rows, HEADS, HD)

    def one_block(query_block):
        scores = jnp.einsum('qhd,khd->hqk', query_block, key_heads, precision=lax.Precision.HIGHEST) * HD ** (-0.5)
        scores = low_back(scores)
        scores = jnp.where(key_valid[None, None, :], scores, -1e+30)
        row_max = lax.optimization_barrier(jnp.max(scores, axis=-1, keepdims=True))
        weights = jnp.exp(scores - row_max)
        probabilities = low(weights / lax.optimization_barrier(jnp.sum(weights, axis=-1, keepdims=True)))
        return jnp.einsum('hqk,khd->qhd', probabilities, value_heads, precision=lax.Precision.HIGHEST)
    attended = lax.map(jax.checkpoint(one_block), query_blocks)
    return attended.reshape(total_rows, HEADS * HD)

def layer(params, inputs, length):
    query_weight, query_bias, key_weight, value_weight, value_bias, output_weight, output_bias, first_gain, first_shift, up_weight, up_bias, down_weight, down_bias, second_gain, second_shift = params
    rounded = low(inputs)
    queries = low(low_back(matmul(rounded, query_weight) + query_bias))
    key_rows = low(low_back(matmul(rounded, key_weight)))
    value_rows = low(low_back(matmul(rounded, value_weight) + value_bias))
    mixed = low(low_back(attend(queries, key_rows, value_rows, length)))
    branch = low_back(matmul(mixed, output_weight) + output_bias)
    normed = layer_norm(inputs + branch, first_gain, first_shift)
    pre_act = low_back(matmul(low(normed), up_weight) + up_bias)
    activated = low(jax.nn.gelu(pre_act, approximate=False))
    ffn_out = low_back(matmul(activated, down_weight) + down_bias)
    return layer_norm(normed + ffn_out, second_gain, second_shift)

def reference(inputs, lengths, cotangent, query_weight, query_bias, key_weight, value_weight, value_bias, output_weight, output_bias, first_gain, first_shift, up_weight, up_bias, down_weight, down_bias, second_gain, second_shift):
    params = (query_weight, query_bias, key_weight, value_weight, value_bias, output_weight, output_bias, first_gain, first_shift, up_weight, up_bias, down_weight, down_bias, second_gain, second_shift)
    positions = jnp.arange(SEQ_LEN, dtype=jnp.int32)
    valid = (positions[None, :] < lengths[:, None]).astype(jnp.float32)
    seed_grad = cotangent * valid[:, :, None]

    def forward(params, inputs):
        sent_params = tuple((low(item_param) for item_param in params))

        def per_seq(loop_carry, sliced):
            return (loop_carry, layer(sent_params, sliced[0], sliced[1]))
        _, outputs = lax.scan(jax.checkpoint(per_seq), jnp.zeros((), jnp.float32), (inputs, lengths))
        return outputs
    outputs, pullback = jax.vjp(forward, params, inputs)
    param_grads, input_grad = pullback(seed_grad)
    return (outputs, input_grad) + tuple(param_grads)
```

```python
from functools import partial

import jax
import jax.numpy as jnp
from jax import lax
from jax.experimental import pallas as pl
from jax.experimental.pallas import tpu as pltpu
from jax.sharding import Mesh, PartitionSpec as P

HEADS = 12
ZS = 4
NEG_FILL = -1e30
SWAP = ((0, 1), (1, 0))
F32 = jnp.float32
BF16 = jnp.bfloat16


def layer_norm(features, norm_gain, norm_shift):
    average = jnp.mean(features, axis=-1, keepdims=True)
    centered = features - average
    variance = jnp.mean(centered * centered, axis=-1, keepdims=True)
    return centered * lax.rsqrt(variance + 1e-12) * norm_gain + norm_shift


def matmul(left_side, right_side):
    return jnp.dot(left_side, right_side, preferred_element_type=F32)


def left_trans(left_side, right_side):
    return lax.dot_general(
        left_side, right_side, (((0,), (0,)), ((), ())), preferred_element_type=F32
    )


def right_trans(left_side, right_side):
    return lax.dot_general(
        left_side, right_side, (((1,), (1,)), ((), ())), preferred_element_type=F32
    )


def swap(value, axis):
    return lax.ppermute(value, axis, SWAP)


def key_rows_at(length, blocks, rows, outer, per_outer):
    group = per_outer * rows
    left = length - outer * (ZS * group)
    whole = jnp.clip(left // group, 0, ZS)
    touched = jnp.clip((left + group - 1) // group, 0, ZS)
    return whole, touched


def forward_kernel(meta_ref, q_ref, *refs, blocks, rows):
    kv_refs = refs[:blocks]
    out_ref, log_ref = refs[blocks : blocks + 2]
    value_refs = refs[blocks + 2 :]
    head_dim, query_count = q_ref.shape
    length = meta_ref[0]
    for block in range(blocks):
        for part in range(ZS):
            cut = slice(part * rows, (part + 1) * rows)
            value_refs[block][:, cut] = kv_refs[block][cut, :].T[head_dim:, :]
    query = jnp.concatenate([q_ref[...], jnp.zeros((head_dim, query_count), BF16)], axis=0)

    def step(group, carry, members, masked):
        top, total, acc = carry
        start = pl.multiple_of(group * rows, rows)
        found = []
        for block in members:
            scores = matmul(kv_refs[block][pl.ds(start, rows), :], query)
            if masked:
                place = (meta_ref[1 + block] + group * 4) * rows
                place = place + lax.broadcasted_iota(jnp.int32, scores.shape, 0)
                scores = jnp.where(place < length, scores, NEG_FILL)
            found.append(scores)
        new_top = top
        for scores in found:
            new_top = jnp.maximum(new_top, jnp.max(scores, axis=0, keepdims=True))
        fade = jnp.exp(top - new_top)
        total = total * fade
        acc = acc * fade
        for block, scores in zip(members, found):
            weights = jnp.exp(scores - new_top)
            total = total + jnp.sum(weights, axis=0, keepdims=True)
            acc = acc + matmul(
                value_refs[block][:, pl.ds(start, rows)], weights.astype(BF16)
            )
        return new_top, total, acc

    carry = (
        jnp.full((1, query_count), NEG_FILL, F32),
        jnp.zeros((1, query_count), F32),
        jnp.zeros((head_dim, query_count), F32),
    )
    for first in range(0, blocks, 4):
        members = tuple(range(first, first + 4))
        whole, touched = key_rows_at(length, blocks, rows, meta_ref[1 + first] // 16, 4)
        carry = lax.fori_loop(
            0, whole, lambda g, c: step(g, c, members, False), carry
        )
        carry = lax.fori_loop(
            whole, touched, lambda g, c: step(g, c, members, True), carry
        )
    top, total, acc = carry
    out_ref[...] = acc * (1.0 / total)
    log_ref[0] = top + jnp.log(total)


def attend_forward(meta, queries, kv_blocks):
    blocks = len(kv_blocks)
    block_rows, width = kv_blocks[0].shape
    heads = width // 128
    head_dim = queries.shape[0] // heads
    query_count = queries.shape[1]
    head_rows = pl.BlockSpec((head_dim, query_count), lambda h, m: (h, 0))
    head_cols = pl.BlockSpec((block_rows, 128), lambda h, m: (0, h))
    head_stat = pl.BlockSpec((1, 1, query_count), lambda h, m: (h, 0, 0))
    keys = blocks * block_rows
    return pl.pallas_call(
        partial(forward_kernel, blocks=blocks, rows=block_rows // ZS),
        grid_spec=pltpu.PrefetchScalarGridSpec(
            num_scalar_prefetch=1,
            grid=(heads,),
            in_specs=[head_rows] + [head_cols] * blocks,
            out_specs=[head_rows, head_stat],
            scratch_shapes=[pltpu.VMEM((head_dim, block_rows), BF16)] * blocks,
        ),
        out_shape=[
            jax.ShapeDtypeStruct((heads * head_dim, query_count), F32),
            jax.ShapeDtypeStruct((heads, 1, query_count), F32),
        ],
        compiler_params=pltpu.CompilerParams(vmem_limit_bytes=56 << 20),
        cost_estimate=pl.CostEstimate(
            flops=4 * heads * query_count * keys * head_dim * 4,
            bytes_accessed=keys * width * 2,
            transcendentals=heads * query_count * keys,
        ),
        name="attend_forward",
    )(meta, queries, *kv_blocks)


def backward_kernel(meta_ref, q_ref, go_ref, out_ref, log_ref, *refs, blocks, rows):
    kv_refs = refs[:blocks]
    dq_ref = refs[blocks]
    dkv_refs = refs[blocks + 1 : 2 * blocks + 1]
    key_refs = refs[2 * blocks + 1 : 3 * blocks + 1]
    qn_ref, gn_ref, acc_ref = refs[3 * blocks + 1 :]
    head_dim, query_count = q_ref.shape
    length = meta_ref[0]
    blank = jnp.zeros((head_dim, query_count), BF16)
    for block in range(blocks):
        for part in range(ZS):
            cut = slice(part * rows, (part + 1) * rows)
            key_refs[block][:, cut] = kv_refs[block][cut, :].T[:head_dim, :]
    query = jnp.concatenate([q_ref[...], blank], axis=0)
    grad = jnp.concatenate([blank, go_ref[...]], axis=0)
    qn_ref[...] = query.T
    gn_ref[...] = grad.T
    delta = jnp.sum(go_ref[...].astype(F32) * out_ref[...], axis=0, keepdims=True)
    log_sum = log_ref[0]
    acc_ref[...] = jnp.zeros_like(acc_ref)

    def step(group, members, masked):
        start = pl.multiple_of(group * rows, rows)
        for block in members:
            kv = kv_refs[block][pl.ds(start, rows), :]
            scores = matmul(kv, query)
            prob_grad = matmul(kv, grad)
            prob = jnp.exp(scores - log_sum)
            if masked:
                place = (meta_ref[1 + block] + group * 4) * rows
                place = place + lax.broadcasted_iota(jnp.int32, scores.shape, 0)
                prob = jnp.where(place < length, prob, 0.0)
            score_grad = (prob * (prob_grad - delta)).astype(BF16)
            dkv_refs[block][pl.ds(start, rows), :] = (
                matmul(prob.astype(BF16), gn_ref[...]) + matmul(score_grad, qn_ref[...])
            ).astype(BF16)
            acc_ref[...] += matmul(key_refs[block][:, pl.ds(start, rows)], score_grad)

    def clear(group, members):
        start = pl.multiple_of(group * rows, rows)
        for block in members:
            dkv_refs[block][pl.ds(start, rows), :] = jnp.zeros((rows, 128), BF16)

    def loop(low, high, fn):
        def one(group, carry):
            fn(group)
            return carry

        lax.fori_loop(low, high, one, 0)

    for first in range(0, blocks, 4):
        members = tuple(range(first, first + 4))
        whole, touched = key_rows_at(length, blocks, rows, meta_ref[1 + first] // 16, 4)
        loop(0, whole, lambda g: step(g, members, False))
        loop(whole, touched, lambda g: step(g, members, True))
        loop(touched, ZS, lambda g: clear(g, members))
    dq_ref[...] = (acc_ref[...] * head_dim ** (-0.5)).astype(BF16)


def attend_backward(meta, queries, grads, outs, logs, kv_blocks):
    blocks = len(kv_blocks)
    block_rows, width = kv_blocks[0].shape
    heads = width // 128
    head_dim = queries.shape[0] // heads
    query_count = queries.shape[1]
    head_rows = pl.BlockSpec((head_dim, query_count), lambda h, m: (h, 0))
    head_cols = pl.BlockSpec((block_rows, 128), lambda h, m: (0, h))
    head_stat = pl.BlockSpec((1, 1, query_count), lambda h, m: (h, 0, 0))
    keys = blocks * block_rows
    return pl.pallas_call(
        partial(backward_kernel, blocks=blocks, rows=block_rows // ZS),
        grid_spec=pltpu.PrefetchScalarGridSpec(
            num_scalar_prefetch=1,
            grid=(heads,),
            in_specs=[head_rows, head_rows, head_rows, head_stat] + [head_cols] * blocks,
            out_specs=[head_rows] + [head_cols] * blocks,
            scratch_shapes=[pltpu.VMEM((head_dim, block_rows), BF16)] * blocks
            + [
                pltpu.VMEM((query_count, 128), BF16),
                pltpu.VMEM((query_count, 128), BF16),
                pltpu.VMEM((head_dim, query_count), F32),
            ],
        ),
        out_shape=[jax.ShapeDtypeStruct((heads * head_dim, query_count), BF16)]
        + [jax.ShapeDtypeStruct((block_rows, width), BF16)] * blocks,
        compiler_params=pltpu.CompilerParams(vmem_limit_bytes=56 << 20),
        cost_estimate=pl.CostEstimate(
            flops=10 * heads * query_count * keys * head_dim * 4,
            bytes_accessed=2 * keys * width * 2,
            transcendentals=heads * query_count * keys,
        ),
        name="attend_backward",
    )(meta, queries, grads, outs, logs, *kv_blocks)


def in_order(index, own, other, axis):
    return jnp.where(
        index == 0,
        jnp.concatenate([own, other], axis=axis),
        jnp.concatenate([other, own], axis=axis),
    )


def part_of(value, index, count, axis):
    size = value.shape[axis] // count
    return lax.dynamic_slice_in_dim(value, index * size, size, axis)


def body(
    inputs,
    lengths,
    cotangent,
    query_weight,
    query_bias,
    key_weight,
    value_weight,
    value_bias,
    output_weight,
    output_bias,
    first_gain,
    first_shift,
    up_weight,
    up_bias,
    down_weight,
    down_bias,
    second_gain,
    second_shift,
    *,
    sizes,
):
    count_o, count_w = sizes
    w_at = lax.axis_index("w")
    z_at = lax.axis_index("z")
    c_at = lax.axis_index("c")
    x_at = lax.axis_index("x")
    o_at = lax.axis_index("o")
    tokens = inputs[0]
    local_rows, width = tokens.shape
    head_dim = width // HEADS
    heads = HEADS // ZS
    part = heads * head_dim
    length = lengths[0]

    def gather_w(own):
        if count_w == 2:
            return in_order(w_at, own, swap(own, "w"), 0)
        return lax.all_gather(own, "w", axis=0, tiled=True)

    def gather_w_half(own):
        if count_w == 2:
            got = swap(part_of(own, c_at, 2, 0), "w")
            return in_order(w_at, own, in_order(c_at, got, swap(got, "c"), 0), 0)
        return lax.all_gather(own, "w", axis=0, tiled=True)

    def head_slice(weight):
        return lax.dynamic_slice_in_dim(weight, z_at * part, part, 1).astype(BF16)

    low_tokens = tokens.astype(BF16)
    token_all = lax.all_gather(low_tokens, "z", axis=0, tiled=True)
    own_rows = query_weight.shape[0]
    own_kv = jnp.concatenate(
        [
            head_slice(key_weight).reshape(own_rows, heads, 1, head_dim),
            head_slice(value_weight).reshape(own_rows, heads, 1, head_dim),
        ],
        axis=2,
    ).reshape(own_rows, 2 * part)
    attn_full = gather_w(jnp.concatenate([head_slice(query_weight), own_kv], axis=1))
    query_full = attn_full[:, :part]
    kv_full = attn_full[:, part:]
    small = jnp.concatenate(
        [
            item.astype(BF16).reshape(-1, own_rows)
            for item in (
                query_bias,
                value_bias,
                output_bias,
                first_gain,
                first_shift,
                down_bias,
                second_gain,
                second_shift,
                up_bias,
            )
        ],
        axis=0,
    )
    small_all = lax.all_gather(small, "w", axis=0, tiled=False).astype(F32)
    vectors = [small_all[:, at].reshape(width) for at in range(8)]
    query_offset, value_offset, out_offset, first_scale, first_offset = vectors[:5]
    down_offset, second_scale, second_offset = vectors[5:]
    up_offset = small_all[:, 8:].reshape(-1)
    out_full = gather_w_half(output_weight.astype(BF16))
    up_full = gather_w_half(up_weight.astype(BF16))
    down_full = gather_w_half(down_weight.astype(BF16))

    query_own = lax.dynamic_slice_in_dim(query_offset, z_at * part, part, 0)
    value_own = lax.dynamic_slice_in_dim(value_offset, z_at * part, part, 0)
    kv_own = jnp.concatenate(
        [jnp.zeros((heads, 1, head_dim), F32), value_own.reshape(heads, 1, head_dim)],
        axis=1,
    ).reshape(2 * part)
    queries = (
        lax.dot_general(
            query_full, token_all, (((0,), (1,)), ((), ())), preferred_element_type=F32
        )
        + query_own[:, None]
    ).astype(BF16)
    queries = queries * jnp.array(head_dim ** (-0.5), BF16)
    key_values = (matmul(token_all, kv_full) + kv_own).astype(BF16)
    kv_blocks = [key_values]
    kv_blocks = kv_blocks + [swap(item, "x") for item in kv_blocks]
    kv_blocks = kv_blocks + [swap(item, "c") for item in kv_blocks]
    if count_o == 2:
        kv_blocks = kv_blocks + [swap(item, "o") for item in kv_blocks]
    places = []
    for at in range(len(kv_blocks)):
        o_of = o_at ^ (at >> 2)
        places.append(o_of * 16 + (x_at ^ (at & 1)) * 2 + (c_at ^ ((at >> 1) & 1)))
    meta = jnp.stack([length] + places).astype(jnp.int32)
    attended, logs = attend_forward(meta, queries, kv_blocks)
    low_mixed = lax.all_to_all(attended.astype(BF16), "z", 1, 0, tiled=True)

    branch = left_trans(low_mixed, out_full) + out_offset
    normed, first_pull = jax.vjp(layer_norm, tokens + branch, first_scale, first_offset)
    low_normed = normed.astype(BF16)
    pre_act = matmul(low_normed, up_full) + up_offset
    activated, gelu_pull = jax.vjp(partial(jax.nn.gelu, approximate=False), pre_act)
    low_act = activated.astype(BF16)
    ffn_out = matmul(low_act, down_full) + down_offset
    outputs, second_pull = jax.vjp(
        layer_norm, normed + ffn_out, second_scale, second_offset
    )
    my_index = o_at * 16 + z_at * 4 + x_at * 2 + c_at
    positions = my_index * local_rows + jnp.arange(local_rows, dtype=jnp.int32)
    valid = (positions < length).astype(F32)
    seed_grad = cotangent[0] * valid[:, None]
    sum_grad, grad_second_gain, grad_second_shift = second_pull(seed_grad)
    ffn_grad = sum_grad.astype(BF16)
    grad_down_bias = jnp.sum(ffn_grad.astype(F32), axis=0)
    (act_grad,) = gelu_pull(right_trans(ffn_grad, down_full))
    pre_grad = act_grad.astype(BF16)
    grad_up_bias = jnp.sum(pre_grad.astype(F32), axis=0)
    normed_grad = right_trans(pre_grad, up_full) + sum_grad
    resid_grad, grad_first_gain, grad_first_shift = first_pull(normed_grad)
    branch_grad = resid_grad.astype(BF16)
    grad_output_bias = jnp.sum(branch_grad.astype(F32), axis=0)
    mixed_grad = right_trans(out_full, branch_grad).astype(BF16)
    head_grads = lax.all_to_all(mixed_grad, "z", 0, 1, tiled=True)

    def sum_w(slabs):
        if count_w == 2:
            kept = lax.dynamic_index_in_dim(slabs, w_at, 0, keepdims=False)
            sent = lax.dynamic_index_in_dim(slabs, 1 - w_at, 0, keepdims=False)
            return (kept.astype(F32) + swap(sent, "w").astype(F32)).astype(BF16)
        return lax.psum_scatter(slabs, "w", scatter_dimension=0, tiled=True)[0]

    hidden = low_act.shape[1]
    act_cut = low_act.reshape(local_rows, count_w, 2, hidden // count_w // 2)
    act_own = lax.dynamic_index_in_dim(act_cut, c_at, 2, keepdims=False)
    act_sent = lax.dynamic_index_in_dim(act_cut, 1 - c_at, 2, keepdims=False)
    act_rows = jnp.concatenate([act_own, swap(act_sent, "c")], axis=0)
    ffn_rows = jnp.concatenate([ffn_grad, swap(ffn_grad, "c")], axis=0)
    down_slabs = lax.dot_general(
        act_rows, ffn_rows, (((0,), (0,)), ((), ())), preferred_element_type=F32
    ).astype(BF16)
    pre_own = part_of(pre_grad, c_at, 2, 1)
    pre_rows = jnp.concatenate([pre_own, swap(part_of(pre_grad, 1 - c_at, 2, 1), "c")], axis=0)
    normed_rows = jnp.concatenate([low_normed, swap(low_normed, "c")], axis=0)
    up_slabs = left_trans(normed_rows, pre_rows).astype(BF16)
    up_slabs = up_slabs.reshape(count_w, own_rows, hidden // 2)
    branch_rows = jnp.concatenate(
        [part_of(branch_grad, c_at, 2, 1), swap(part_of(branch_grad, 1 - c_at, 2, 1), "c")],
        axis=0,
    )
    mixed_rows = jnp.concatenate([low_mixed, swap(low_mixed, "c")], axis=1)
    out_slabs = matmul(mixed_rows, branch_rows).astype(BF16)
    out_slabs = out_slabs.reshape(count_w, own_rows, width // 2)
    line = ("o", "z", "x")
    down_sum = lax.psum(sum_w(down_slabs), line)
    up_sum = lax.psum(sum_w(up_slabs), line)
    out_sum = lax.psum(sum_w(out_slabs), line)
    total_down = in_order(c_at, down_sum, swap(down_sum, "c"), 0).astype(F32)
    total_up = in_order(c_at, up_sum, swap(up_sum, "c"), 1).astype(F32)
    total_out = in_order(c_at, out_sum, swap(out_sum, "c"), 1).astype(F32)

    query_low, *kv_parts = attend_backward(
        meta, queries, head_grads, attended, logs, kv_blocks
    )

    def add_pair(kept, got):
        return (kept.astype(F32) + got.astype(F32)).astype(BF16)

    if count_o == 2:
        kv_parts = [add_pair(kv_parts[at], swap(kv_parts[at + 4], "o")) for at in range(4)]
    kv_parts = [add_pair(kv_parts[at], swap(kv_parts[at + 2], "c")) for at in range(2)]
    kv_low = add_pair(kv_parts[0], swap(kv_parts[1], "x"))
    token_part = (
        lax.dot_general(
            query_low, query_full, (((0,), (1,)), ((), ())), preferred_element_type=F32
        )
        + right_trans(kv_low, kv_full)
    ).astype(BF16)
    token_grad = lax.psum_scatter(token_part, "z", scatter_dimension=0, tiled=True)
    input_grad = resid_grad + token_grad.astype(F32)
    attn_part = jnp.concatenate(
        [
            lax.dot_general(
                token_all, query_low, (((0,), (1,)), ((), ())), preferred_element_type=F32
            ),
            left_trans(token_all, kv_low),
        ],
        axis=1,
    ).astype(BF16)
    attn_own = sum_w(attn_part.reshape(count_w, own_rows, 3 * part))
    attn_own = lax.psum(attn_own, ("o", "x", "c"))
    attn_all = lax.all_gather(attn_own, "z", axis=0, tiled=False).astype(F32)
    total_query = jnp.transpose(attn_all[:, :, :part], (1, 0, 2)).reshape(own_rows, width)
    pairs = attn_all[:, :, part:].reshape(ZS, own_rows, heads, 2, head_dim)
    pairs = jnp.transpose(pairs, (3, 1, 0, 2, 4)).reshape(2, own_rows, width)
    total_key, total_value = pairs[0], pairs[1]

    query_sum = jnp.sum(query_low.astype(F32), axis=1)
    value_sum = jnp.sum(kv_low.astype(F32), axis=0).reshape(heads, 2, head_dim)[:, 1]
    blank = jnp.zeros((width,), F32)
    grad_query_bias = lax.dynamic_update_slice_in_dim(blank, query_sum, z_at * part, 0)
    grad_value_bias = lax.dynamic_update_slice_in_dim(
        blank, value_sum.reshape(part), z_at * part, 0
    )
    packed = jnp.concatenate(
        [
            item.reshape(-1, 128)
            for item in (
                grad_query_bias,
                grad_value_bias,
                grad_output_bias,
                grad_first_gain,
                grad_first_shift,
                grad_down_bias,
                grad_second_gain,
                grad_second_shift,
                grad_up_bias,
            )
        ],
        axis=0,
    )
    packed = lax.psum(packed, ("o", "z", "x", "c", "w"))
    each = width // 128
    totals = [
        part_of(packed[at * each : (at + 1) * each].reshape(width), w_at, count_w, 0)
        for at in range(8)
    ]
    total_up_bias = part_of(packed[8 * each :].reshape(-1), w_at, count_w, 0)
    return (
        outputs[None],
        input_grad[None],
        total_query,
        totals[0],
        total_key,
        total_value,
        totals[1],
        total_out,
        totals[2],
        totals[3],
        totals[4],
        total_up,
        total_up_bias,
        total_down,
        totals[5],
        totals[6],
        totals[7],
    )


def solution(mesh):
    count_s = mesh.shape["seq"]
    count_w = mesh.shape["wshard"]
    count_o = count_s // 16
    fine = Mesh(
        mesh.devices.reshape(count_o, ZS, 2, 2, count_w), ("o", "z", "x", "c", "w")
    )
    seq = ("o", "z", "x", "c")
    rows = P("w", seq, None)
    matrix = P("w", None)
    vector = P("w")
    placed = (
        rows,
        vector,
        rows,
        matrix,
        vector,
        matrix,
        matrix,
        vector,
        matrix,
        vector,
        vector,
        vector,
        matrix,
        vector,
        matrix,
        vector,
        vector,
        vector,
    )
    return jax.shard_map(
        partial(body, sizes=(count_o, count_w)),
        mesh=fine,
        in_specs=placed,
        out_specs=(
            rows,
            rows,
            matrix,
            vector,
            matrix,
            matrix,
            vector,
            matrix,
            vector,
            vector,
            vector,
            matrix,
            vector,
            matrix,
            vector,
            vector,
            vector,
        ),
        check_vma=False,
    )
```

```python
from functools import partial

import jax
import jax.numpy as jnp
from jax import lax
from jax.experimental import pallas as pl
from jax.experimental.pallas import tpu as pltpu
from jax.sharding import Mesh, PartitionSpec as P

HEADS = 12
ZS = 4
NEG_FILL = -1e30
SWAP = ((0, 1), (1, 0))
F32 = jnp.float32
BF16 = jnp.bfloat16


def matmul(left_side, right_side):
    return jnp.dot(left_side, right_side, preferred_element_type=F32)


def right_trans(left_side, right_side):
    return lax.dot_general(
        left_side, right_side, (((1,), (1,)), ((), ())), preferred_element_type=F32
    )


def swap(value, axis):
    return lax.ppermute(value, axis, SWAP)


def key_rows_at(length, blocks, rows, outer, per_outer):
    group = per_outer * rows
    left = length - outer * (ZS * group)
    whole = jnp.clip(left // group, 0, ZS)
    touched = jnp.clip((left + group - 1) // group, 0, ZS)
    return whole, touched


def forward_kernel(meta_ref, q_ref, *refs, blocks, rows):
    kv_refs = refs[:blocks]
    out_ref, log_ref = refs[blocks : blocks + 2]
    value_refs = refs[blocks + 2 :]
    head_dim, query_count = q_ref.shape
    length = meta_ref[0]
    for block in range(blocks):
        for part in range(ZS):
            cut = slice(part * rows, (part + 1) * rows)
            value_refs[block][:, cut] = kv_refs[block][cut, :].T[head_dim:, :]
    query = jnp.concatenate([q_ref[...], jnp.zeros((head_dim, query_count), BF16)], axis=0)

    def step(group, carry, members, masked):
        top, total, acc = carry
        start = pl.multiple_of(group * rows, rows)
        found = []
        for block in members:
            scores = matmul(kv_refs[block][pl.ds(start, rows), :], query)
            if masked:
                place = (meta_ref[1 + block] + group * 4) * rows
                place = place + lax.broadcasted_iota(jnp.int32, scores.shape, 0)
                scores = jnp.where(place < length, scores, NEG_FILL)
            found.append(scores)
        new_top = top
        for scores in found:
            new_top = jnp.maximum(new_top, jnp.max(scores, axis=0, keepdims=True))
        fade = jnp.exp(top - new_top)
        total = total * fade
        acc = acc * fade
        for block, scores in zip(members, found):
            weights = jnp.exp(scores - new_top)
            total = total + jnp.sum(weights, axis=0, keepdims=True)
            acc = acc + matmul(
                value_refs[block][:, pl.ds(start, rows)], weights.astype(BF16)
            )
        return new_top, total, acc

    carry = (
        jnp.full((1, query_count), NEG_FILL, F32),
        jnp.zeros((1, query_count), F32),
        jnp.zeros((head_dim, query_count), F32),
    )
    for first in range(0, blocks, 4):
        members = tuple(range(first, first + 4))
        whole, touched = key_rows_at(length, blocks, rows, meta_ref[1 + first] // 16, 4)
        carry = lax.fori_loop(
            0, whole, lambda g, c: step(g, c, members, False), carry
        )
        carry = lax.fori_loop(
            whole, touched, lambda g, c: step(g, c, members, True), carry
        )
    top, total, acc = carry
    out_ref[...] = acc * (1.0 / total)
    log_ref[0] = top + jnp.log(total)


def attend_forward(meta, queries, kv_blocks):
    blocks = len(kv_blocks)
    block_rows, width = kv_blocks[0].shape
    heads = width // 128
    head_dim = queries.shape[0] // heads
    query_count = queries.shape[1]
    head_rows = pl.BlockSpec((head_dim, query_count), lambda h, m: (h, 0))
    head_cols = pl.BlockSpec((block_rows, 128), lambda h, m: (0, h))
    head_stat = pl.BlockSpec((1, 1, query_count), lambda h, m: (h, 0, 0))
    keys = blocks * block_rows
    return pl.pallas_call(
        partial(forward_kernel, blocks=blocks, rows=block_rows // ZS),
        grid_spec=pltpu.PrefetchScalarGridSpec(
            num_scalar_prefetch=1,
            grid=(heads,),
            in_specs=[head_rows] + [head_cols] * blocks,
            out_specs=[head_rows, head_stat],
            scratch_shapes=[pltpu.VMEM((head_dim, block_rows), BF16)] * blocks,
        ),
        out_shape=[
            jax.ShapeDtypeStruct((heads * head_dim, query_count), F32),
            jax.ShapeDtypeStruct((heads, 1, query_count), F32),
        ],
        compiler_params=pltpu.CompilerParams(vmem_limit_bytes=56 << 20),
        cost_estimate=pl.CostEstimate(
            flops=4 * heads * query_count * keys * head_dim * 4,
            bytes_accessed=keys * width * 2,
            transcendentals=heads * query_count * keys,
        ),
        name="attend_forward",
    )(meta, queries, *kv_blocks)


def backward_kernel(meta_ref, q_ref, go_ref, out_ref, log_ref, *refs, blocks, rows):
    kv_refs = refs[:blocks]
    dq_ref = refs[blocks]
    dkv_refs = refs[blocks + 1 : 2 * blocks + 1]
    key_refs = refs[2 * blocks + 1 : 3 * blocks + 1]
    qn_ref, gn_ref, acc_ref = refs[3 * blocks + 1 :]
    head_dim, query_count = q_ref.shape
    length = meta_ref[0]
    blank = jnp.zeros((head_dim, query_count), BF16)
    for block in range(blocks):
        for part in range(ZS):
            cut = slice(part * rows, (part + 1) * rows)
            key_refs[block][:, cut] = kv_refs[block][cut, :].T[:head_dim, :]
    query = jnp.concatenate([q_ref[...], blank], axis=0)
    grad = jnp.concatenate([blank, go_ref[...]], axis=0)
    qn_ref[...] = query.T
    gn_ref[...] = grad.T
    delta = jnp.sum(go_ref[...].astype(F32) * out_ref[...], axis=0, keepdims=True)
    log_sum = log_ref[0]
    acc_ref[...] = jnp.zeros_like(acc_ref)

    def step(group, members, masked):
        start = pl.multiple_of(group * rows, rows)
        for block in members:
            kv = kv_refs[block][pl.ds(start, rows), :]
            scores = matmul(kv, query)
            prob_grad = matmul(kv, grad)
            prob = jnp.exp(scores - log_sum)
            if masked:
                place = (meta_ref[1 + block] + group * 4) * rows
                place = place + lax.broadcasted_iota(jnp.int32, scores.shape, 0)
                prob = jnp.where(place < length, prob, 0.0)
            score_grad = (prob * (prob_grad - delta)).astype(BF16)
            dkv_refs[block][pl.ds(start, rows), :] = (
                matmul(prob.astype(BF16), gn_ref[...]) + matmul(score_grad, qn_ref[...])
            ).astype(BF16)
            acc_ref[...] += matmul(key_refs[block][:, pl.ds(start, rows)], score_grad)

    def clear(group, members):
        start = pl.multiple_of(group * rows, rows)
        for block in members:
            dkv_refs[block][pl.ds(start, rows), :] = jnp.zeros((rows, 128), BF16)

    def loop(low, high, fn):
        def one(group, carry):
            fn(group)
            return carry

        lax.fori_loop(low, high, one, 0)

    for first in range(0, blocks, 4):
        members = tuple(range(first, first + 4))
        whole, touched = key_rows_at(length, blocks, rows, meta_ref[1 + first] // 16, 4)
        loop(0, whole, lambda g: step(g, members, False))
        loop(whole, touched, lambda g: step(g, members, True))
        loop(touched, ZS, lambda g: clear(g, members))
    dq_ref[...] = (acc_ref[...] * head_dim ** (-0.5)).astype(BF16)


def attend_backward(meta, queries, grads, outs, logs, kv_blocks):
    blocks = len(kv_blocks)
    block_rows, width = kv_blocks[0].shape
    heads = width // 128
    head_dim = queries.shape[0] // heads
    query_count = queries.shape[1]
    head_rows = pl.BlockSpec((head_dim, query_count), lambda h, m: (h, 0))
    head_cols = pl.BlockSpec((block_rows, 128), lambda h, m: (0, h))
    head_stat = pl.BlockSpec((1, 1, query_count), lambda h, m: (h, 0, 0))
    keys = blocks * block_rows
    return pl.pallas_call(
        partial(backward_kernel, blocks=blocks, rows=block_rows // ZS),
        grid_spec=pltpu.PrefetchScalarGridSpec(
            num_scalar_prefetch=1,
            grid=(heads,),
            in_specs=[head_rows, head_rows, head_rows, head_stat] + [head_cols] * blocks,
            out_specs=[head_rows] + [head_cols] * blocks,
            scratch_shapes=[pltpu.VMEM((head_dim, block_rows), BF16)] * blocks
            + [
                pltpu.VMEM((query_count, 128), BF16),
                pltpu.VMEM((query_count, 128), BF16),
                pltpu.VMEM((head_dim, query_count), F32),
            ],
        ),
        out_shape=[jax.ShapeDtypeStruct((heads * head_dim, query_count), BF16)]
        + [jax.ShapeDtypeStruct((block_rows, width), BF16)] * blocks,
        compiler_params=pltpu.CompilerParams(vmem_limit_bytes=56 << 20),
        cost_estimate=pl.CostEstimate(
            flops=10 * heads * query_count * keys * head_dim * 4,
            bytes_accessed=2 * keys * width * 2,
            transcendentals=heads * query_count * keys,
        ),
        name="attend_backward",
    )(meta, queries, grads, outs, logs, *kv_blocks)


def project_kernel(tokens_ref, weight_ref, bias_ref, query_ref, kv_ref, turned_ref):
    part = query_ref.shape[0]
    tokens = tokens_ref[...]
    kv = matmul(tokens, weight_ref[:, : 2 * part]) + bias_ref[:, : 2 * part]
    kv_ref[...] = kv.astype(BF16)
    query = matmul(tokens, weight_ref[:, 2 * part :]) + bias_ref[:, 2 * part :]
    query = query.astype(BF16) * jnp.array((part // 3) ** (-0.5), BF16)
    query_ref[...] = query.T
    turned_ref[...] = tokens.T


def project(tokens, weight, bias):
    rows, width = tokens.shape
    part = weight.shape[1] // 3
    return pl.pallas_call(
        project_kernel,
        out_shape=[
            jax.ShapeDtypeStruct((part, rows), BF16),
            jax.ShapeDtypeStruct((rows, 2 * part), BF16),
            jax.ShapeDtypeStruct((width, rows), BF16),
        ],
        compiler_params=pltpu.CompilerParams(vmem_limit_bytes=40 << 20),
        name="project",
    )(tokens, weight, bias)


def middle_kernel(meta_ref, mixed_ref, tokens_ref, seed_ref, vec_ref, upoff_ref, *refs, counts, chunk):
    pieces = refs[: sum(counts)]
    (
        outputs_ref,
        resid_ref,
        mgrad_ref,
        act_ref,
        pre_ref,
        ffn_ref,
        normed_ref,
        branch_ref,
        small_ref,
        upsum_ref,
        out_w,
        up_w,
        down_w,
        slope_ref,
        sems,
    ) = refs[sum(counts) :]
    groups = []
    at = 0
    for count, target in zip(counts, (out_w, up_w, down_w)):
        group = []
        for piece in range(count):
            source = pieces[at]
            unit = source.shape[0] if piece else source.shape[0] // 2
            if count == 1:
                place = target
            else:
                start = pl.multiple_of(meta_ref[1 + piece] * unit, unit)
                place = target.at[pl.ds(start, source.shape[0]), :]
            copy = pltpu.make_async_copy(source, place, sems.at[at])
            copy.start()
            group.append(copy)
            at += 1
        groups.append(group)
    rows, width = tokens_ref.shape
    hidden = upoff_ref.shape[1]

    def mean(value):
        return jnp.mean(value, axis=-1, keepdims=True)

    def norm(value):
        centered = value - mean(value)
        scale = lax.rsqrt(mean(centered * centered) + 1e-12)
        return centered * scale, scale

    def norm_back(grad, normal, scale):
        return scale * (grad - mean(grad) - normal * mean(grad * normal))

    def column(value):
        return jnp.sum(value, axis=0, keepdims=True)

    mixed = mixed_ref[...].T
    for copy in groups[0]:
        copy.wait()
    first_n, first_r = norm(tokens_ref[...] + (matmul(mixed, out_w[...]) + vec_ref[2:3, :]))
    normed = first_n * vec_ref[3:4, :] + vec_ref[4:5, :]
    low = normed.astype(BF16)
    normed_ref[...] = low.T
    for copy in groups[1] + groups[2]:
        copy.wait()
    acc = None
    for at in range(0, hidden, chunk):
        cut = slice(at, at + chunk)
        pre_act = matmul(low, up_w[:, cut]) + upoff_ref[:, cut]
        phi = 0.5 + 0.5 * lax.erf(pre_act * (0.5**0.5))
        act = (pre_act * phi).astype(BF16)
        slope_ref[:, cut] = phi + pre_act * (
            jnp.exp(-0.5 * pre_act * pre_act) * 0.3989422804014327
        )
        act_ref[cut, :] = act.T
        term = matmul(act, down_w[cut, :])
        acc = term if acc is None else acc + term
    second_n, second_r = norm(normed + (acc + vec_ref[5:6, :]))
    outputs_ref[...] = second_n * vec_ref[6:7, :] + vec_ref[7:8, :]
    place = lax.broadcasted_iota(jnp.int32, (rows, 1), 0)
    seed = jnp.where(place < meta_ref[0], seed_ref[...], 0.0)
    sum_grad = norm_back(seed * vec_ref[6:7, :], second_n, second_r)
    ffn = sum_grad.astype(BF16)
    ffn_ref[...] = ffn
    small_ref[3:4, :] = column(ffn.astype(F32))
    small_ref[4:5, :] = column(seed * second_n)
    small_ref[5:6, :] = column(seed)
    acc = sum_grad
    for at in range(0, hidden, chunk):
        cut = slice(at, at + chunk)
        pre = (right_trans(ffn, down_w[cut, :]) * slope_ref[:, cut]).astype(BF16)
        pre_ref[:, cut] = pre
        upsum_ref[:, cut] = column(pre.astype(F32))
        acc = acc + right_trans(pre, up_w[:, cut])
    small_ref[1:2, :] = column(acc * first_n)
    small_ref[2:3, :] = column(acc)
    resid = norm_back(acc * vec_ref[3:4, :], first_n, first_r)
    resid_ref[...] = resid
    branch = resid.astype(BF16)
    branch_ref[...] = branch
    small_ref[0:1, :] = column(branch.astype(F32))
    small_ref[6:8, :] = jnp.zeros((2, width), F32)
    mgrad_ref[...] = right_trans(out_w[...], branch).astype(BF16)


def middle(meta, mixed, tokens, seed, vec, upoff, pieces, *, chunk=1024):
    rows, width = tokens.shape
    hidden = upoff.shape[1]
    in_vmem = pl.BlockSpec(memory_space=pltpu.VMEM)
    in_place = pl.BlockSpec(memory_space=pl.ANY)
    flat = [item for group in pieces for item in group]
    return pl.pallas_call(
        partial(middle_kernel, counts=tuple(len(group) for group in pieces), chunk=chunk),
        grid_spec=pltpu.PrefetchScalarGridSpec(
            num_scalar_prefetch=1,
            grid=(),
            in_specs=[in_vmem] * 5 + [in_place] * len(flat),
            out_specs=[in_vmem] * 10,
            scratch_shapes=[
                pltpu.VMEM((width, width), BF16),
                pltpu.VMEM((width, hidden), BF16),
                pltpu.VMEM((hidden, width), BF16),
                pltpu.VMEM((rows, hidden), F32),
                pltpu.SemaphoreType.DMA((len(flat),)),
            ],
        ),
        out_shape=[
            jax.ShapeDtypeStruct((rows, width), F32),
            jax.ShapeDtypeStruct((rows, width), F32),
            jax.ShapeDtypeStruct((width, rows), BF16),
            jax.ShapeDtypeStruct((hidden, rows), BF16),
            jax.ShapeDtypeStruct((rows, hidden), BF16),
            jax.ShapeDtypeStruct((rows, width), BF16),
            jax.ShapeDtypeStruct((width, rows), BF16),
            jax.ShapeDtypeStruct((rows, width), BF16),
            jax.ShapeDtypeStruct((8, width), F32),
            jax.ShapeDtypeStruct((1, hidden), F32),
        ],
        compiler_params=pltpu.CompilerParams(vmem_limit_bytes=56 << 20),
        name="middle",
    )(meta, mixed, tokens, seed, vec, upoff, *flat)


def down_kernel(meta_ref, act_ref, ffn_ref, *refs):
    value = matmul(act_ref[...], ffn_ref[...])
    if len(refs) == 2:
        value = value + refs[0][...].astype(F32)
    refs[-1][...] = value.astype(BF16)


def down_slab(meta, act, ffn, count, got=None):
    rows, width = ffn.shape
    block = act.shape[0] // count
    whole = pl.BlockSpec((block, width), lambda i, m: (0, 0))
    return pl.pallas_call(
        down_kernel,
        grid_spec=pltpu.PrefetchScalarGridSpec(
            num_scalar_prefetch=1,
            grid=(1,),
            in_specs=[
                pl.BlockSpec((block, rows), lambda i, m: (m[0] * 2 + m[1], 0)),
                pl.BlockSpec((rows, width), lambda i, m: (0, 0)),
            ]
            + ([] if got is None else [whole]),
            out_specs=whole,
        ),
        out_shape=jax.ShapeDtypeStruct((block, width), BF16),
        compiler_params=pltpu.CompilerParams(vmem_limit_bytes=24 << 20),
        name="down_slab",
    )(meta, act, ffn, *(() if got is None else (got,)))


def up_kernel(meta_ref, normed_ref, pre_ref, mixed_ref, branch_ref, *refs, small):
    out_ref = refs[-1]
    first = pre_ref.shape[1]
    second = first + branch_ref.shape[1]
    got = None
    if small:
        small_ref, upsum_ref = refs[:2]
        refs = refs[2:]
    if len(refs) == 2:
        got = refs[0]

    def put(value, rows, columns):
        if got is not None:
            value = value + got[rows, columns].astype(F32)
        out_ref[rows, columns] = value.astype(BF16)

    every = slice(0, out_ref.shape[0])
    put(matmul(normed_ref[...], pre_ref[...]), every, slice(0, first))
    put(matmul(mixed_ref[...], branch_ref[...]), every, slice(first, second))
    if small:
        lanes = slice(second, second + 128)
        groups = small_ref.shape[1] // 128
        lines = upsum_ref.shape[1] // 128
        values = [small_ref[:, at * 128 : (at + 1) * 128] for at in range(groups)]
        values += [upsum_ref[:, at * 128 : (at + 1) * 128] for at in range(lines)]
        used = 8 * groups + lines
        total = out_ref.shape[0]
        values += [jnp.zeros((total - used, 128), F32)]
        put(jnp.concatenate(values, axis=0), every, lanes)


def up_slab(meta, normed, pre, mixed, branch, small, count_w, got=None):
    width, rows = normed.shape
    hidden = pre.shape[1]
    block = width // count_w
    columns = hidden // 2 + width // 2 + (128 if small else 0)
    whole = pl.BlockSpec((block, columns), lambda i, m: (0, 0))
    specs = [
        pl.BlockSpec((block, rows), lambda i, m: (m[0], 0)),
        pl.BlockSpec((rows, hidden // 2), lambda i, m: (0, m[1])),
        pl.BlockSpec((block, rows), lambda i, m: (m[0], 0)),
        pl.BlockSpec((rows, width // 2), lambda i, m: (0, m[1])),
    ]
    extra = []
    if small:
        specs += [
            pl.BlockSpec((8, width // count_w), lambda i, m: (0, m[0])),
            pl.BlockSpec((1, hidden // count_w), lambda i, m: (0, m[0])),
        ]
        extra += list(small)
    if got is not None:
        specs.append(whole)
        extra.append(got)
    return pl.pallas_call(
        partial(up_kernel, small=bool(small)),
        grid_spec=pltpu.PrefetchScalarGridSpec(
            num_scalar_prefetch=1, grid=(1,), in_specs=specs, out_specs=whole
        ),
        out_shape=jax.ShapeDtypeStruct((block, columns), BF16),
        compiler_params=pltpu.CompilerParams(vmem_limit_bytes=24 << 20),
        name="up_slab",
    )(meta, normed, pre, mixed, branch, *extra)


def head_kernel(meta_ref, turned_ref, query_ref, kv_ref, *refs):
    block = turned_ref.shape[0]
    part = query_ref.shape[0]
    out_ref = refs[-1]

    def put(value, rows, columns):
        if len(refs) == 2:
            value = value + refs[0][rows, columns].astype(F32)
        out_ref[rows, columns] = value.astype(BF16)

    kv = kv_ref[...]
    query = query_ref[...]
    turned = turned_ref[...]
    rows = slice(0, block)
    put(matmul(turned, kv), rows, slice(0, 2 * part))
    put(right_trans(turned, query), rows, slice(2 * part, 3 * part))
    rest = slice(block, block + 16)
    ones = jnp.ones((16, kv.shape[0]), BF16)
    put(matmul(ones, kv), rest, slice(0, 2 * part))
    put(right_trans(ones, query), rest, slice(2 * part, 3 * part))


def head_slab(meta, turned, query, kv, count, got=None):
    width, rows = turned.shape
    part = query.shape[0]
    block = width // count
    whole = pl.BlockSpec((block + 16, 3 * part), lambda i, m: (0, 0))
    return pl.pallas_call(
        head_kernel,
        grid_spec=pltpu.PrefetchScalarGridSpec(
            num_scalar_prefetch=1,
            grid=(1,),
            in_specs=[
                pl.BlockSpec((block, rows), lambda i, m: (m[0] * 2 + m[1], 0)),
                pl.BlockSpec((part, rows), lambda i, m: (0, 0)),
                pl.BlockSpec((rows, 2 * part), lambda i, m: (0, 0)),
            ]
            + ([] if got is None else [whole]),
            out_specs=whole,
        ),
        out_shape=jax.ShapeDtypeStruct((block + 16, 3 * part), BF16),
        compiler_params=pltpu.CompilerParams(vmem_limit_bytes=24 << 20),
        name="head_slab",
    )(meta, turned, query, kv, *(() if got is None else (got,)))


def token_kernel(query_ref, kv_ref, weight_ref, out_ref):
    part = query_ref.shape[0]
    out_ref[...] = (
        right_trans(kv_ref[...], weight_ref[:, : 2 * part])
        + right_trans(query_ref[...].T, weight_ref[:, 2 * part :])
    ).astype(BF16)


def token_part(query, kv, weight):
    return pl.pallas_call(
        token_kernel,
        out_shape=jax.ShapeDtypeStruct((kv.shape[0], weight.shape[0]), BF16),
        compiler_params=pltpu.CompilerParams(vmem_limit_bytes=32 << 20),
        name="token_part",
    )(query, kv, weight)


def down_finish_kernel(meta_ref, *refs):
    block = refs[0].shape[0]
    c_at, x_at = meta_ref[0], meta_ref[1]
    for at in range(4):
        place = (c_at ^ (at >> 1)) * 2 + (x_at ^ (at & 1))
        start = pl.multiple_of(place * block, 8)
        refs[4][pl.ds(start, block), :] = refs[at][...].astype(F32)


def down_finish(meta, pieces):
    block, width = pieces[0].shape
    in_vmem = pl.BlockSpec(memory_space=pltpu.VMEM)
    return pl.pallas_call(
        down_finish_kernel,
        grid_spec=pltpu.PrefetchScalarGridSpec(
            num_scalar_prefetch=1, grid=(), in_specs=[in_vmem] * 4, out_specs=in_vmem
        ),
        out_shape=jax.ShapeDtypeStruct((4 * block, width), F32),
        compiler_params=pltpu.CompilerParams(vmem_limit_bytes=32 << 20),
        name="down_finish",
    )(meta, *pieces)


def up_finish_kernel(meta_ref, *refs, first):
    pieces = refs[:4]
    up_ref, out_ref, *rest = refs[4:]
    block = pieces[0].shape[0]
    c_at, x_at = meta_ref[0], meta_ref[1]
    second = first + out_ref.shape[1] // 2
    for at in range(4):
        start = pl.multiple_of((x_at ^ (at & 1)) * block, 8)
        core = c_at ^ (at >> 1)
        up_ref[pl.ds(start, block), pl.ds(pl.multiple_of(core * first, 128), first)] = (
            pieces[at][:, :first].astype(F32)
        )
        width = second - first
        out_ref[pl.ds(start, block), pl.ds(pl.multiple_of(core * width, 128), width)] = (
            pieces[at][:, first:second].astype(F32)
        )
        if rest and at < 2:
            rest[0][pl.ds(start, block), :] = pieces[at][:, second:].astype(F32)


def up_finish(meta, pieces, hidden, width):
    block, columns = pieces[0].shape
    in_vmem = pl.BlockSpec(memory_space=pltpu.VMEM)
    shapes = [(2 * block, hidden), (2 * block, width)]
    if columns > hidden // 2 + width // 2:
        shapes.append((2 * block, 128))
    return pl.pallas_call(
        partial(up_finish_kernel, first=hidden // 2),
        grid_spec=pltpu.PrefetchScalarGridSpec(
            num_scalar_prefetch=1,
            grid=(),
            in_specs=[in_vmem] * 4,
            out_specs=[in_vmem] * len(shapes),
        ),
        out_shape=[jax.ShapeDtypeStruct(shape, F32) for shape in shapes],
        compiler_params=pltpu.CompilerParams(vmem_limit_bytes=40 << 20),
        name="up_finish",
    )(meta, *pieces)


def head_finish_kernel(meta_ref, own_ref, got_ref, query_ref, key_ref, value_ref, bias_ref, *, part):
    block = own_ref.shape[1] - 16
    head_dim = part // 3
    for at, source in enumerate((own_ref, got_ref)):
        start = pl.multiple_of((meta_ref[0] ^ at) * block, 8)
        rows = pl.ds(start, block)
        keys, values, queries = [], [], []
        for z in range(ZS):
            item = source[z].astype(F32)
            for head in range(3):
                low = head * 2 * head_dim
                keys.append(item[:, low : low + head_dim])
                values.append(item[:, low + head_dim : low + 2 * head_dim])
            queries.append(item[:, 2 * part :])
        key = jnp.concatenate(keys, axis=1)
        value = jnp.concatenate(values, axis=1)
        query = jnp.concatenate(queries, axis=1)
        query_ref[rows, :] = query[:block]
        key_ref[rows, :] = key[:block]
        value_ref[rows, :] = value[:block]
        if at == 0:
            bias_ref[0:8, :] = query[block : block + 8]
            bias_ref[8:16, :] = value[block : block + 8]


def head_finish(meta, own, got):
    _, block, columns = own.shape
    rows = 2 * (block - 16)
    width = ZS * columns // 3
    in_vmem = pl.BlockSpec(memory_space=pltpu.VMEM)
    return pl.pallas_call(
        partial(head_finish_kernel, part=columns // 3),
        grid_spec=pltpu.PrefetchScalarGridSpec(
            num_scalar_prefetch=1, grid=(), in_specs=[in_vmem] * 2, out_specs=[in_vmem] * 4
        ),
        out_shape=[jax.ShapeDtypeStruct((rows, width), F32)] * 3
        + [jax.ShapeDtypeStruct((16, width), F32)],
        compiler_params=pltpu.CompilerParams(vmem_limit_bytes=40 << 20),
        name="head_finish",
    )(meta, own, got)


def in_order(index, own, other, axis):
    return jnp.where(
        index == 0,
        jnp.concatenate([own, other], axis=axis),
        jnp.concatenate([other, own], axis=axis),
    )


def part_of(value, index, count, axis):
    size = value.shape[axis] // count
    return lax.dynamic_slice_in_dim(value, index * size, size, axis)


def body(
    inputs,
    lengths,
    cotangent,
    query_weight,
    query_bias,
    key_weight,
    value_weight,
    value_bias,
    output_weight,
    output_bias,
    first_gain,
    first_shift,
    up_weight,
    up_bias,
    down_weight,
    down_bias,
    second_gain,
    second_shift,
    *,
    sizes,
):
    count_o, count_w = sizes
    w_at = lax.axis_index("w")
    z_at = lax.axis_index("z")
    c_at = lax.axis_index("c")
    x_at = lax.axis_index("x")
    o_at = lax.axis_index("o")
    tokens = inputs[0]
    local_rows, width = tokens.shape
    head_dim = width // HEADS
    heads = HEADS // ZS
    part = heads * head_dim
    length = lengths[0]

    hold = lax.optimization_barrier

    def head_slice(weight):
        return lax.dynamic_slice_in_dim(weight, z_at * part, part, 1).astype(BF16)

    low_tokens = tokens.astype(BF16)
    token_all = lax.all_gather(low_tokens, "z", axis=0, tiled=True)
    own_rows = query_weight.shape[0]
    key_own = head_slice(key_weight)
    value_own = head_slice(value_weight)
    own_kv = []
    for head in range(heads):
        cut = slice(head * head_dim, (head + 1) * head_dim)
        own_kv += [key_own[:, cut], value_own[:, cut]]
    attn_own = jnp.concatenate(own_kv + [head_slice(query_weight)], axis=1)
    small = jnp.concatenate(
        [
            item.astype(BF16)
            for item in (
                query_bias,
                value_bias,
                output_bias,
                first_gain,
                first_shift,
                down_bias,
                second_gain,
                second_shift,
                up_bias,
            )
        ]
    ).reshape(-1, 3 * part)
    attn_pack = jnp.concatenate([attn_own, small], axis=0)
    if count_w == 2:
        attn_got = swap(attn_pack, "w")
        attn_full = in_order(w_at, attn_own, attn_got[:own_rows], 0)
        small_all = in_order(w_at, small[None], attn_got[None, own_rows:], 0)
    else:
        attn_all = lax.all_gather(attn_pack, "w", axis=0, tiled=False)
        attn_full = attn_all[:, :own_rows].reshape(width, 3 * part)
        small_all = attn_all[:, own_rows:]
    small_all = small_all.astype(F32).reshape(count_w, -1, own_rows)
    vec = jnp.transpose(small_all[:, :8], (1, 0, 2)).reshape(8, width)
    up_offset = small_all[:, 8:].reshape(1, -1)
    attn_pack, output_weight, up_weight, down_weight = hold(
        (attn_pack, output_weight, up_weight, down_weight)
    )
    low_weights = [item.astype(BF16) for item in (output_weight, up_weight, down_weight)]
    if count_w == 2:
        got_weights = [swap(part_of(item, c_at, 2, 0), "w") for item in low_weights]
    else:
        got_weights = [lax.all_gather(item, "w", axis=0, tiled=True) for item in low_weights]

    own_bias = lax.dynamic_slice_in_dim(vec[:2], z_at * part, part, 1)
    value_bias_own = own_bias[1].reshape(heads, 1, head_dim)
    kv_bias = jnp.concatenate([jnp.zeros_like(value_bias_own), value_bias_own], axis=1)
    bias_row = jnp.concatenate([kv_bias.reshape(1, 2 * part), own_bias[:1]], axis=1)
    queries, key_values, turned = project(token_all, attn_full, bias_row)
    kv_blocks = [key_values]
    kv_blocks = kv_blocks + [swap(item, "x") for item in kv_blocks]
    kv_blocks = kv_blocks + [swap(item, "c") for item in kv_blocks]
    if count_o == 2:
        kv_blocks = kv_blocks + [swap(item, "o") for item in kv_blocks]
    places = []
    for at in range(len(kv_blocks)):
        o_of = o_at ^ (at >> 2)
        places.append(o_of * 16 + (x_at ^ (at & 1)) * 2 + (c_at ^ ((at >> 1) & 1)))
    meta = jnp.stack([length] + places).astype(jnp.int32)
    attended, logs = attend_forward(meta, queries, kv_blocks)
    attended, *got_weights = hold((attended, *got_weights))
    low_mixed = lax.all_to_all(attended.astype(BF16), "z", 1, 0, tiled=True)
    if count_w == 2:
        pieces = [
            (own, got, swap(got, "c")) for own, got in zip(low_weights, got_weights)
        ]
    else:
        pieces = [(item,) for item in got_weights]

    my_index = o_at * 16 + z_at * 4 + x_at * 2 + c_at
    rest = jnp.clip(length - my_index * local_rows, 0, local_rows)
    other = 2 * (1 - w_at)
    spots = jnp.stack([rest, 2 * w_at, other + c_at, other + 1 - c_at]).astype(jnp.int32)
    (
        outputs,
        resid_grad,
        mixed_grad,
        act_turned,
        pre_grad,
        ffn_grad,
        normed_turned,
        branch_grad,
        small_sum,
        upsum,
    ) = middle(spots, low_mixed, tokens, cotangent[0], vec, up_offset, pieces)
    head_grads = lax.all_to_all(mixed_grad, "z", 0, 1, tiled=True)
    hidden = pre_grad.shape[1]

    def add_pair(kept, got):
        return (kept.astype(F32) + got.astype(F32)).astype(BF16)

    def halve(value, axis, bit, perm, dim):
        got = lax.ppermute(part_of(value, 1 - bit, 2, dim), axis, perm)
        return add_pair(part_of(value, bit, 2, dim), got)

    def unite(value, axis, bit, perm, dim):
        return in_order(bit, value, lax.ppermute(value, axis, perm), dim)

    near = ((0, 1), (1, 0), (2, 3), (3, 2))
    far = ((0, 2), (2, 0), (1, 3), (3, 1))

    def sum_line(value):
        if count_o == 2:
            value = add_pair(value, swap(value, "o"))
        value = halve(value, "x", x_at, SWAP, 0)
        value = halve(value, "z", z_at & 1, near, 0)
        value = halve(value, "z", z_at >> 1, far, 0)
        value = unite(value, "z", z_at >> 1, far, 0)
        return unite(value, "z", z_at & 1, near, 0)

    def four_pieces(value):
        got = swap(value, "x")
        return [value, got, swap(value, "c"), swap(got, "c")]

    def pick(w, c):
        return jnp.stack([jnp.asarray(w), jnp.asarray(c)]).astype(jnp.int32)

    def core_sum(slab):
        if count_w == 2:
            got_far = swap(slab(pick(1 - w_at, 1 - c_at)), "c")
            got_near = swap(slab(pick(1 * w_at, 1 - c_at)), "c")
            return slab(pick(1 - w_at, c_at), got_far), slab(pick(1 * w_at, c_at), got_near)
        got = [swap(slab(pick(w, 1 - c_at)), "c") for w in range(count_w)]
        return (jnp.stack([slab(pick(w, c_at), got[w]) for w in range(count_w)]),)

    def y_sum(sums):
        if count_w == 2:
            return add_pair(sums[1], swap(sums[0], "w"))
        return lax.psum_scatter(sums[0], "w", scatter_dimension=0, tiled=True)[0]

    smalls = (small_sum, upsum) if count_w == 2 else ()
    down_sums = core_sum(
        lambda m, got=None: down_slab(m, act_turned, ffn_grad, 2 * count_w, got)
    )
    up_sums = core_sum(
        lambda m, got=None: up_slab(
            m, normed_turned, pre_grad, low_mixed, branch_grad, smalls, count_w, got
        )
    )
    down_sums, up_sums, head_grads = hold((down_sums, up_sums, head_grads))
    down_sum = sum_line(y_sum(down_sums))
    up_sum = sum_line(y_sum(up_sums))
    spot = jnp.stack([c_at, x_at]).astype(jnp.int32)
    total_down = down_finish(spot, four_pieces(down_sum))
    total_up, total_out, *small_total = up_finish(spot, four_pieces(up_sum), hidden, width)

    query_low, *kv_parts = attend_backward(
        meta, queries, head_grads, attended, logs, kv_blocks
    )
    if count_o == 2:
        kv_parts = [add_pair(kv_parts[at], swap(kv_parts[at + 4], "o")) for at in range(4)]
    kv_parts = [add_pair(kv_parts[at], swap(kv_parts[at + 2], "c")) for at in range(2)]
    kv_low = add_pair(kv_parts[0], swap(kv_parts[1], "x"))
    token_sum = token_part(query_low, kv_low, attn_full)
    token_grad = lax.psum_scatter(token_sum, "z", scatter_dimension=0, tiled=True)
    input_grad = resid_grad + token_grad.astype(F32)
    head_sum = y_sum(
        core_sum(lambda m, got=None: head_slab(m, turned, query_low, kv_low, 2 * count_w, got))
    )
    head_sum = add_pair(head_sum, swap(head_sum, "x"))
    if count_o == 2:
        head_sum = add_pair(head_sum, swap(head_sum, "o"))
    head_two = unite(head_sum[None], "z", z_at & 1, near, 0)
    head_four = unite(head_two, "z", z_at >> 1, far, 0)
    total_query, total_key, total_value, head_bias = head_finish(
        spot, head_four, swap(head_four, "c")
    )
    totals = [part_of(head_bias[at], w_at, count_w, 0) for at in (0, 8)]
    if count_w == 2:
        groups = own_rows // 128
        table = small_total[0][: 8 * groups].reshape(groups, 8, 128)
        totals += [table[:, at].reshape(own_rows) for at in range(6)]
        lines = hidden // count_w // 128
        total_up_bias = small_total[0][8 * groups : 8 * groups + lines].reshape(-1)
    else:
        every = ("o", "z", "x", "c", "w")
        small_sum, upsum = lax.psum((small_sum, upsum), every)
        totals += [part_of(small_sum[at], w_at, count_w, 0) for at in range(6)]
        total_up_bias = part_of(upsum[0], w_at, count_w, 0)
    return (
        outputs[None],
        input_grad[None],
        total_query,
        totals[0],
        total_key,
        total_value,
        totals[1],
        total_out,
        totals[2],
        totals[3],
        totals[4],
        total_up,
        total_up_bias,
        total_down,
        totals[5],
        totals[6],
        totals[7],
    )


def solution(mesh):
    count_s = mesh.shape["seq"]
    count_w = mesh.shape["wshard"]
    count_o = count_s // 16
    fine = Mesh(
        mesh.devices.reshape(count_o, ZS, 2, 2, count_w), ("o", "z", "x", "c", "w")
    )
    seq = ("o", "z", "x", "c")
    rows = P("w", seq, None)
    matrix = P("w", None)
    vector = P("w")
    placed = (
        rows,
        vector,
        rows,
        matrix,
        vector,
        matrix,
        matrix,
        vector,
        matrix,
        vector,
        vector,
        vector,
        matrix,
        vector,
        matrix,
        vector,
        vector,
        vector,
    )
    return jax.shard_map(
        partial(body, sizes=(count_o, count_w)),
        mesh=fine,
        in_specs=placed,
        out_specs=(
            rows,
            rows,
            matrix,
            vector,
            matrix,
            matrix,
            vector,
            matrix,
            vector,
            vector,
            vector,
            matrix,
            vector,
            matrix,
            vector,
            vector,
            vector,
        ),
        check_vma=False,
    )
```

```python
from functools import partial

import jax
import jax.numpy as jnp
from jax import lax
from jax.experimental import pallas as pl
from jax.experimental.pallas import tpu as pltpu
from jax.sharding import Mesh, PartitionSpec as P

HEADS = 12
ZS = 4
NEG_FILL = -1e30
SWAP = ((0, 1), (1, 0))
F32 = jnp.float32
BF16 = jnp.bfloat16


def matmul(left_side, right_side):
    return jnp.dot(left_side, right_side, preferred_element_type=F32)


def right_trans(left_side, right_side):
    return lax.dot_general(
        left_side, right_side, (((1,), (1,)), ((), ())), preferred_element_type=F32
    )


def work(units):
    return pl.CostEstimate(flops=int(units * 1e3), bytes_accessed=1, transcendentals=0)


def swap(value, axis):
    return lax.ppermute(value, axis, SWAP)


def touched_groups(length, rows, outer):
    group = 4 * rows
    left = length - outer * (ZS * group)
    return jnp.clip((left + group - 1) // group, 0, ZS)


def with_mask(kv, place, length):
    at = place + lax.broadcasted_iota(jnp.int32, kv.shape, 0)
    lane = lax.broadcasted_iota(jnp.int32, kv.shape, 1)
    fill = jnp.where(at < length, 0.0, jnp.where(lane == 0, NEG_FILL, 0.0))
    return jnp.concatenate([kv, fill.astype(BF16)], axis=1)


def forward_kernel(meta_ref, q_ref, *refs, blocks, rows):
    kv_refs = refs[:blocks]
    out_ref = refs[blocks]
    piece_refs = refs[blocks + 1 : blocks + 1 + ZS]
    log_ref = refs[blocks + 1 + ZS]
    value_refs = refs[blocks + 2 + ZS : 2 * blocks + 2 + ZS]
    low_ref = refs[-1]
    head_dim, query_count = q_ref.shape
    length, z_at = meta_ref[0], meta_ref[1]
    for block in range(blocks):
        for part in range(ZS):
            cut = slice(part * rows, (part + 1) * rows)
            value_refs[block][:, cut] = kv_refs[block][cut, :].T[head_dim:, :]
    query = jnp.concatenate(
        [
            q_ref[...],
            jnp.zeros((head_dim, query_count), BF16),
            jnp.ones((128, query_count), BF16),
        ],
        axis=0,
    )

    def step(group, carry, members):
        top, total, acc = carry
        start = pl.multiple_of(group * rows, rows)
        found = []
        for block in members:
            place = (meta_ref[2 + block] + group * 4) * rows
            kv = with_mask(kv_refs[block][pl.ds(start, rows), :], place, length)
            found.append(matmul(kv, query))
        new_top = top
        for scores in found:
            new_top = jnp.maximum(new_top, jnp.max(scores, axis=0, keepdims=True))
        fade = jnp.exp(top - new_top)
        total = total * fade
        acc = acc * fade
        for block, scores in zip(members, found):
            weights = jnp.exp(scores - new_top)
            total = total + jnp.sum(weights, axis=0, keepdims=True)
            acc = acc + matmul(
                value_refs[block][:, pl.ds(start, rows)], weights.astype(BF16)
            )
        return new_top, total, acc

    carry = (
        jnp.full((1, query_count), NEG_FILL, F32),
        jnp.zeros((1, query_count), F32),
        jnp.zeros((head_dim, query_count), F32),
    )
    for first in range(0, blocks, 4):
        members = tuple(range(first, first + 4))
        count = touched_groups(length, rows, meta_ref[2 + first] // 16)
        carry = lax.fori_loop(0, count, lambda g, c: step(g, c, members), carry)
    top, total, acc = carry
    out = acc * (1.0 / total)
    out_ref[...] = out
    low_ref[...] = out.astype(BF16)
    size = query_count // ZS
    for at in range(ZS):
        start = pl.multiple_of((z_at ^ at) * size, 128)
        piece_refs[at][...] = low_ref[:, pl.ds(start, size)]
    log_ref[0] = top + jnp.log(total)


def attend_forward(meta, queries, kv_blocks, first, head_dim):
    blocks = len(kv_blocks)
    block_rows, columns = kv_blocks[0].shape
    heads = columns // 128
    query_count = queries.shape[1]
    size = query_count // ZS
    head_rows = pl.BlockSpec((head_dim, query_count), lambda i, m: (i, 0))
    return pl.pallas_call(
        partial(forward_kernel, blocks=blocks, rows=block_rows // ZS),
        grid_spec=pltpu.PrefetchScalarGridSpec(
            num_scalar_prefetch=1,
            grid=(heads,),
            in_specs=[pl.BlockSpec((head_dim, query_count), lambda i, m: (i + first, 0))]
            + [pl.BlockSpec((block_rows, 128), lambda i, m: (0, i))] * blocks,
            out_specs=[head_rows]
            + [pl.BlockSpec((head_dim, size), lambda i, m: (i, 0))] * ZS
            + [pl.BlockSpec((1, 1, query_count), lambda i, m: (i, 0, 0))],
            scratch_shapes=[pltpu.VMEM((head_dim, block_rows), BF16)] * blocks
            + [pltpu.VMEM((head_dim, query_count), BF16)],
        ),
        out_shape=[jax.ShapeDtypeStruct((heads * head_dim, query_count), F32)]
        + [jax.ShapeDtypeStruct((heads * head_dim, size), BF16)] * ZS
        + [jax.ShapeDtypeStruct((heads, 1, query_count), F32)],
        compiler_params=pltpu.CompilerParams(vmem_limit_bytes=40 << 20),
        cost_estimate=work(8 * heads),
        name="attend_forward",
    )(meta, queries, *kv_blocks)


def backward_kernel(meta_ref, q_ref, out_ref, log_ref, *refs, blocks, rows):
    piece_refs = refs[:ZS]
    kv_refs = refs[ZS : ZS + blocks]
    refs = refs[ZS + blocks :]
    dq_ref = refs[0]
    pairs = refs[1 : 1 + blocks // 2]
    key_refs = refs[1 + blocks // 2 : 1 + blocks // 2 + blocks]
    go_ref, qn_ref, gn_ref, acc_ref = refs[1 + blocks // 2 + blocks :]
    head_dim, query_count = q_ref.shape
    length, z_at = meta_ref[0], meta_ref[1]
    block_rows = ZS * rows
    size = query_count // ZS
    for at in range(ZS):
        start = pl.multiple_of((z_at ^ at) * size, 128)
        go_ref[:, pl.ds(start, size)] = piece_refs[at][...]
    blank = jnp.zeros((head_dim, query_count), BF16)
    for block in range(blocks):
        for part in range(ZS):
            cut = slice(part * rows, (part + 1) * rows)
            key_refs[block][:, cut] = kv_refs[block][cut, :].T[:head_dim, :]
    grads = go_ref[...]
    query = jnp.concatenate([q_ref[...], blank], axis=0)
    grad = jnp.concatenate([blank, grads], axis=0)
    qn_ref[...] = query.T
    gn_ref[...] = grad.T
    query = jnp.concatenate([query, jnp.ones((128, query_count), BF16)], axis=0)
    delta = jnp.sum(grads.astype(F32) * out_ref[...], axis=0, keepdims=True)
    log_sum = log_ref[0]
    acc_ref[...] = jnp.zeros_like(acc_ref)

    def step(group, members):
        start = pl.multiple_of(group * rows, rows)
        for block in members:
            kv = kv_refs[block][pl.ds(start, rows), :]
            place = (meta_ref[2 + block] + group * 4) * rows
            scores = matmul(with_mask(kv, place, length), query)
            prob_grad = matmul(kv, grad)
            prob = jnp.exp(scores - log_sum)
            score_grad = (prob * (prob_grad - delta)).astype(BF16)
            pairs[block // 2][pl.ds(start + (block & 1) * block_rows, rows), :] = (
                matmul(prob.astype(BF16), gn_ref[...]) + matmul(score_grad, qn_ref[...])
            ).astype(BF16)
            acc_ref[...] += matmul(key_refs[block][:, pl.ds(start, rows)], score_grad)

    def clear(group, members):
        start = pl.multiple_of(group * rows, rows)
        for block in members:
            pairs[block // 2][pl.ds(start + (block & 1) * block_rows, rows), :] = jnp.zeros(
                (rows, 128), BF16
            )

    def loop(low, high, fn):
        def one(group, carry):
            fn(group)
            return carry

        lax.fori_loop(low, high, one, 0)

    for first in range(0, blocks, 4):
        members = tuple(range(first, first + 4))
        count = touched_groups(length, rows, meta_ref[2 + first] // 16)
        loop(0, count, lambda g: step(g, members))
        loop(count, ZS, lambda g: clear(g, members))
    dq_ref[...] = (acc_ref[...] * head_dim ** (-0.5)).astype(BF16)


def attend_backward(meta, queries, grads, out, log_sum, kv_blocks, first, head_dim):
    blocks = len(kv_blocks)
    block_rows, columns = kv_blocks[0].shape
    heads = columns // 128
    query_count = queries.shape[1]
    size = query_count // ZS
    head_rows = pl.BlockSpec((head_dim, query_count), lambda i, m: (i, 0))
    return pl.pallas_call(
        partial(backward_kernel, blocks=blocks, rows=block_rows // ZS),
        grid_spec=pltpu.PrefetchScalarGridSpec(
            num_scalar_prefetch=1,
            grid=(heads,),
            in_specs=[
                pl.BlockSpec((head_dim, query_count), lambda i, m: (i + first, 0)),
                head_rows,
                pl.BlockSpec((1, 1, query_count), lambda i, m: (i, 0, 0)),
            ]
            + [pl.BlockSpec((head_dim, size), lambda i, m: (i + first, 0))] * ZS
            + [pl.BlockSpec((block_rows, 128), lambda i, m: (0, i))] * blocks,
            out_specs=[head_rows]
            + [pl.BlockSpec((2 * block_rows, 128), lambda i, m: (0, i))] * (blocks // 2),
            scratch_shapes=[pltpu.VMEM((head_dim, block_rows), BF16)] * blocks
            + [
                pltpu.VMEM((head_dim, query_count), BF16),
                pltpu.VMEM((query_count, 128), BF16),
                pltpu.VMEM((query_count, 128), BF16),
                pltpu.VMEM((head_dim, query_count), F32),
            ],
        ),
        out_shape=[jax.ShapeDtypeStruct((heads * head_dim, query_count), BF16)]
        + [jax.ShapeDtypeStruct((2 * block_rows, columns), BF16)] * (blocks // 2),
        compiler_params=pltpu.CompilerParams(vmem_limit_bytes=48 << 20),
        cost_estimate=work(12 * heads),
        name="attend_backward",
    )(meta, queries, out, log_sum, *grads, *kv_blocks)


def project_kernel(tokens_ref, weight_ref, bias_ref, query_ref, *refs):
    kv_refs, turned_ref = refs[:-1], refs[-1]
    part = query_ref.shape[0]
    tokens = tokens_ref[...]
    split = 2 * part
    kv = matmul(tokens, weight_ref[:, :split]) + bias_ref[:, :split]
    kv = kv.astype(BF16)
    low = 0
    for ref in kv_refs:
        ref[...] = kv[:, low : low + ref.shape[1]]
        low += ref.shape[1]
    query = matmul(tokens, weight_ref[:, split:]) + bias_ref[:, split:]
    scale = (part * ZS // HEADS) ** (-0.5)
    query_ref[...] = (query.astype(BF16) * jnp.array(scale, BF16)).T
    turned_ref[...] = tokens.T


def project(tokens, weight, bias, counts):
    rows, width = tokens.shape
    part = weight.shape[1] // 3
    return pl.pallas_call(
        project_kernel,
        out_shape=[jax.ShapeDtypeStruct((part, rows), BF16)]
        + [jax.ShapeDtypeStruct((rows, 128 * count), BF16) for count in counts]
        + [jax.ShapeDtypeStruct((width, rows), BF16)],
        compiler_params=pltpu.CompilerParams(vmem_limit_bytes=40 << 20),
        cost_estimate=work(2),
        name="project",
    )(tokens, weight, bias)


def middle_kernel(meta_ref, tokens_ref, seed_ref, vec_ref, upoff_ref, *refs, groups, shared):
    mixed_refs = [refs[at * ZS : (at + 1) * ZS] for at in range(len(groups))]
    refs = refs[ZS * len(groups) :]
    weight_refs = refs[: 5 if shared else 3]
    refs = refs[len(weight_refs) :]
    outputs_ref, resid_ref = refs[:2]
    mgrad_refs = refs[2 : 2 + ZS]
    (
        send_ref,
        keep_ref,
        small_ref,
        out_w,
        up_w,
        down_w,
        slope_ref,
        wide_ref,
        tall_ref,
        sems,
    ) = refs[2 + ZS :]
    w_at, core, z_at = meta_ref[1], meta_ref[2], meta_ref[3]
    moves = [[], [], []]
    if shared:
        outs, ups, downs, got, pair = weight_refs
        count_o, count_u, count_d = outs.shape[0], ups.shape[0], downs.shape[0]
        for kind, (source, target) in enumerate(((outs, out_w), (ups, up_w), (downs, down_w))):
            start = pl.multiple_of(w_at * source.shape[0], source.shape[0])
            moves[kind].append((source, target.at[pl.ds(start, source.shape[0]), :]))
        lanes = got.shape[1]
        for source, which in ((got, core), (pair, 1 - core)):
            half = count_o // 2
            start = pl.multiple_of(((1 - w_at) * 2 + which) * half, half)
            moves[0].append((source.at[pl.ds(0, half), :], out_w.at[pl.ds(start, half), :]))
            low = half
            start = pl.multiple_of((1 - w_at) * count_u, count_u)
            for block in range(up_w.shape[1] // 2 // lanes):
                lane = pl.multiple_of(which * (up_w.shape[1] // 2) + block * lanes, 128)
                moves[1].append(
                    (
                        source.at[pl.ds(low, count_u), :],
                        up_w.at[pl.ds(start, count_u), pl.ds(lane, lanes)],
                    )
                )
                low += count_u
            half = count_d // 2
            start = pl.multiple_of(((1 - w_at) * 2 + which) * half, half)
            moves[2].append((source.at[pl.ds(low, half), :], down_w.at[pl.ds(start, half), :]))
    else:
        for kind, pair in enumerate(zip(weight_refs, (out_w, up_w, down_w))):
            moves[kind].append(pair)
    copies = []
    at = 0
    for kind in range(3):
        made = []
        for source, target in moves[kind]:
            made.append(pltpu.make_async_copy(source, target, sems.at[at]))
            made[-1].start()
            at += 1
        copies.append(made)
    rows, width = tokens_ref.shape
    hidden = upoff_ref.shape[1]
    part = width // ZS
    head_dim = width // HEADS
    quarter = hidden // 4

    def mean(value):
        return jnp.mean(value, axis=-1, keepdims=True)

    def norm(value):
        centered = value - mean(value)
        scale = lax.rsqrt(mean(centered * centered) + 1e-12)
        return centered * scale, scale

    def norm_back(grad, normal, scale):
        return scale * (grad - mean(grad) - normal * mean(grad * normal))

    def column(value):
        return jnp.sum(value, axis=0, keepdims=True)

    normed_at = 2 * quarter
    mixed_at = normed_at + width
    branch_at = mixed_at + width
    act_at = 5 * quarter
    for (first, count), pieces in zip(groups, mixed_refs):
        size = count * head_dim
        for at in range(ZS):
            low = mixed_at + (z_at ^ at) * part + first * head_dim
            send_ref[pl.ds(pl.multiple_of(low, head_dim), size), :] = pieces[at][...]
    mixed = send_ref[mixed_at:branch_at, :].T
    for copy in copies[0]:
        copy.wait()
    first_n, first_r = norm(tokens_ref[...] + (matmul(mixed, out_w[...]) + vec_ref[2:3, :]))
    normed = first_n * vec_ref[3:4, :] + vec_ref[4:5, :]
    low = normed.astype(BF16)
    send_ref[normed_at:mixed_at, :] = low.T
    for copy in copies[1] + copies[2]:
        copy.wait()
    quarters = []
    for half in range(2):
        for kept in (False, True):
            at = half * 2 * quarter + (core if kept else 1 - core) * quarter
            quarters.append((half, kept, pl.multiple_of(at, quarter)))
    acc = None
    for at, (half, kept, start) in enumerate(quarters):
        cut = pl.ds(start, quarter)
        pre_act = matmul(low, up_w[:, cut]) + upoff_ref[:, cut]
        phi = 0.5 + 0.5 * lax.erf(pre_act * (0.5**0.5))
        act = (pre_act * phi).astype(BF16)
        slope_ref[:, at * quarter : (at + 1) * quarter] = phi + pre_act * (
            jnp.exp(-0.5 * pre_act * pre_act) * 0.3989422804014327
        )
        target, base = (keep_ref, 0) if kept else (send_ref, act_at)
        target[base + half * quarter : base + (half + 1) * quarter, :] = act.T
        term = matmul(act, down_w[cut, :])
        acc = term if acc is None else acc + term
    second_n, second_r = norm(normed + (acc + vec_ref[5:6, :]))
    outputs_ref[...] = second_n * vec_ref[6:7, :] + vec_ref[7:8, :]
    place = lax.broadcasted_iota(jnp.int32, (rows, 1), 0)
    seed = jnp.where(place < meta_ref[0], seed_ref[...], 0.0)
    sum_grad = norm_back(seed * vec_ref[6:7, :], second_n, second_r)
    ffn = sum_grad.astype(BF16)
    for at in range(width // 256):
        low_row = act_at + 2 * quarter + at * rows
        send_ref[low_row : low_row + rows, :] = ffn[:, at * 256 : (at + 1) * 256]
    small_ref[3:4, :] = column(ffn.astype(F32))
    small_ref[4:5, :] = column(seed * second_n)
    small_ref[5:6, :] = column(seed)
    acc = sum_grad
    for at, (half, kept, start) in enumerate(quarters):
        cut = pl.ds(start, quarter)
        pre = right_trans(ffn, down_w[cut, :]) * slope_ref[:, at * quarter : (at + 1) * quarter]
        pre = pre.astype(BF16)
        target, base = (keep_ref, 2 * quarter) if kept else (send_ref, 0)
        for block in range(quarter // 256):
            row = base + (half * (quarter // 256) + block) * rows
            target[row : row + rows, :] = pre[:, block * 256 : (block + 1) * 256]
        sums = column(pre.astype(F32))
        line = 8 + half * (2 * quarter // width) + (core if kept else 1 - core)
        small_ref[pl.ds(line, 1), :] = sums
        acc = acc + right_trans(pre, up_w[:, cut])
    small_ref[1:2, :] = column(acc * first_n)
    small_ref[2:3, :] = column(acc)
    resid = norm_back(acc * vec_ref[3:4, :], first_n, first_r)
    resid_ref[...] = resid
    branch = resid.astype(BF16)
    wide_ref[...] = branch
    side = width // 2
    for target, base, which in (
        (send_ref, branch_at, 1 - core),
        (keep_ref, 4 * quarter, core),
    ):
        values = wide_ref[:, pl.ds(pl.multiple_of(which * side, 128), side)]
        target[base : base + rows, :] = values[:, :256]
        target[base + rows : base + 2 * rows, : side - 256] = values[:, 256:]
        target[base + rows : base + 2 * rows, side - 256 :] = jnp.zeros(
            (rows, 512 - side), BF16
        )
    small_ref[0:1, :] = column(branch.astype(F32))
    small_ref[6:8, :] = jnp.zeros((2, width), F32)
    small_ref[12:16, :] = jnp.zeros((4, width), F32)
    gap = branch_at + 2 * rows
    send_ref[gap:act_at, :] = jnp.zeros((act_at - gap, 256), BF16)
    tall_ref[...] = right_trans(out_w[...], branch).astype(BF16)
    for at in range(ZS):
        start = pl.multiple_of((z_at ^ at) * part, part)
        mgrad_refs[at][...] = tall_ref[pl.ds(start, part), :]


def middle(meta, mixed, groups, tokens, seed, vec, upoff, weights):
    rows, width = tokens.shape
    hidden = upoff.shape[1]
    in_vmem = pl.BlockSpec(memory_space=pltpu.VMEM)
    in_place = pl.BlockSpec(memory_space=pl.ANY)
    flat = [item for group in mixed for item in group]
    part = jax.ShapeDtypeStruct((width // ZS, rows), BF16)
    return pl.pallas_call(
        partial(middle_kernel, groups=groups, shared=len(weights) == 5),
        grid_spec=pltpu.PrefetchScalarGridSpec(
            num_scalar_prefetch=1,
            grid=(),
            in_specs=[in_vmem] * (4 + len(flat)) + [in_place] * len(weights),
            out_specs=[in_vmem] * (5 + ZS),
            scratch_shapes=[
                pltpu.VMEM((width, width), BF16),
                pltpu.VMEM((width, hidden), BF16),
                pltpu.VMEM((hidden, width), BF16),
                pltpu.VMEM((rows, hidden), F32),
                pltpu.VMEM((rows, width), BF16),
                pltpu.VMEM((width, rows), BF16),
                pltpu.SemaphoreType.DMA((11,)),
            ],
        ),
        out_shape=[jax.ShapeDtypeStruct((rows, width), F32)] * 2
        + [part] * ZS
        + [
            jax.ShapeDtypeStruct((2 * hidden, 256), BF16),
            jax.ShapeDtypeStruct((hidden + 2 * rows, 256), BF16),
            jax.ShapeDtypeStruct((16, width), F32),
        ],
        compiler_params=pltpu.CompilerParams(vmem_limit_bytes=56 << 20),
        cost_estimate=work(15),
        name="middle",
    )(meta, tokens, seed, vec, upoff, *flat, *weights)


def down_kernel(meta_ref, keep_ref, got_ref, own_ffn_ref, got_ffn_ref, out_ref):
    keep, got = keep_ref[...], got_ref[...]
    rows = keep.shape[1]
    for at in range(out_ref.shape[1] // 256):
        cut = slice(at * rows, (at + 1) * rows)
        value = matmul(keep, own_ffn_ref[cut, :]) + matmul(got, got_ffn_ref[cut, :])
        out_ref[:, at * 256 : (at + 1) * 256] = value.astype(BF16)


def down_slab(meta, keep, send, got):
    block = send.shape[0] // 8
    kept = pl.BlockSpec((block, send.shape[1]), lambda i, m: (m[0], 0))
    act = pl.BlockSpec((block, send.shape[1]), lambda i, m: (5 + m[0], 0))
    ffn = pl.BlockSpec((block, send.shape[1]), lambda i, m: (7, 0))
    return pl.pallas_call(
        down_kernel,
        grid_spec=pltpu.PrefetchScalarGridSpec(
            num_scalar_prefetch=1,
            grid=(1,),
            in_specs=[kept, act, ffn, ffn],
            out_specs=pl.BlockSpec((block, block), lambda i, m: (0, 0)),
        ),
        out_shape=jax.ShapeDtypeStruct((block, block), BF16),
        compiler_params=pltpu.CompilerParams(vmem_limit_bytes=24 << 20),
        cost_estimate=work(2),
        name="down_slab",
    )(meta, keep, got, send, got)


def up_kernel(meta_ref, keep_ref, send_ref, got_ref, own_small_ref, got_small_ref, *refs):
    out_refs, table_ref = refs[:2], refs[2]
    rows = send_ref.shape[1]
    width = own_small_ref.shape[1]
    block = width // 4
    side = width // 2
    normed_at = 2 * width
    branch_at = normed_at + 2 * width
    x_at = meta_ref[0]
    pre_keep = 2 * width
    for w in range(2):
        small = own_small_ref[...] + got_small_ref[...]
        table_ref[...] = jnp.zeros_like(table_ref)
        for at in range(side // 128):
            low = w * side + at * 128
            table_ref[at * 8 : (at + 1) * 8, :] = small[:8, low : low + 128]
        base = side // 128 * 8
        for at in range(2 * width // 128):
            line = 8 + 2 * w + at // (width // 128)
            low = at % (width // 128) * 128
            table_ref[base + at : base + at + 1, :] = small[line : line + 1, low : low + 128]
        for out_ref, which in zip(out_refs, (1 - x_at, x_at)):
            start = pl.multiple_of(which * block, block)
            target = slice(w * block, (w + 1) * block)
            own = send_ref[pl.ds(normed_at + w * side + start, block), :]
            got = got_ref[pl.ds(normed_at + w * side + start, block), :]
            for at in range(normed_at // rows):
                cut = slice(at * rows, (at + 1) * rows)
                value = matmul(own, keep_ref[pre_keep + at * rows : pre_keep + (at + 1) * rows, :])
                value = value + matmul(got, got_ref[cut, :])
                out_ref[target, at * 256 : (at + 1) * 256] = value.astype(BF16)
            own = send_ref[pl.ds(normed_at + width + w * side + start, block), :]
            got = got_ref[pl.ds(normed_at + width + w * side + start, block), :]
            lane = normed_at // rows * 256
            for at in range(2):
                mine = 4 * width + at * rows
                theirs = branch_at + at * rows
                value = matmul(own, keep_ref[mine : mine + rows, :])
                value = value + matmul(got, got_ref[theirs : theirs + rows, :])
                value = value[:, : min(256, side - at * 256)].astype(BF16)
                out_ref[target, lane : lane + value.shape[1]] = value
                lane += value.shape[1]
            out_ref[target, lane : lane + 128] = table_ref[pl.ds(start, block), :].astype(BF16)


def up_slabs(meta, keep, send, got, own_small, got_small):
    width = own_small.shape[1]
    columns = 2 * width + width // 2 + 128
    first = pl.BlockSpec((5 * width, send.shape[1]), lambda i, m: (0, 0))

    def whole(value):
        return pl.BlockSpec(value.shape, lambda i, m: (0, 0))

    return pl.pallas_call(
        up_kernel,
        grid_spec=pltpu.PrefetchScalarGridSpec(
            num_scalar_prefetch=1,
            grid=(1,),
            in_specs=[whole(keep), first, first, whole(own_small), whole(own_small)],
            out_specs=[pl.BlockSpec((width // 2, columns), lambda i, m: (0, 0))] * 2,
            scratch_shapes=[pltpu.VMEM((width // 2, 128), F32)],
        ),
        out_shape=[jax.ShapeDtypeStruct((width // 2, columns), BF16)] * 2,
        compiler_params=pltpu.CompilerParams(vmem_limit_bytes=40 << 20),
        cost_estimate=work(4),
        name="up_slabs",
    )(meta, keep, send, got, own_small, got_small)


def head_kernel(meta_ref, turned_ref, *refs, count):
    query_refs, kv_refs = refs[:count], refs[count : 2 * count]
    refs = refs[2 * count :]
    block = turned_ref.shape[0]
    out_ref = refs[-1]

    def put(value, rows, low):
        columns = slice(low, low + value.shape[1])
        if len(refs) == 2:
            value = value + refs[0][rows, columns].astype(F32)
        out_ref[rows, columns] = value.astype(BF16)
        return low + value.shape[1]

    query = jnp.concatenate([ref[...] for ref in query_refs], axis=0)
    turned = turned_ref[...]
    ones = jnp.ones((16, turned.shape[1]), BF16)
    for left, rows in ((turned, slice(0, block)), (ones, slice(block, block + 16))):
        low = 0
        for ref in kv_refs:
            low = put(matmul(left, ref[...]), rows, low)
        put(right_trans(left, query), rows, low)


def head_slab(meta, turned, query, kv, count, got=None):
    width, rows = turned.shape
    block = width // count
    columns = 3 * width // ZS
    whole = pl.BlockSpec((block + 16, columns), lambda i, m: (0, 0))
    return pl.pallas_call(
        partial(head_kernel, count=len(query)),
        grid_spec=pltpu.PrefetchScalarGridSpec(
            num_scalar_prefetch=1,
            grid=(1,),
            in_specs=[pl.BlockSpec((block, rows), lambda i, m: (m[0] * 2 + m[1], 0))]
            + [pl.BlockSpec(item.shape, lambda i, m: (0, 0)) for item in [*query, *kv]]
            + ([] if got is None else [whole]),
            out_specs=whole,
        ),
        out_shape=jax.ShapeDtypeStruct((block + 16, columns), BF16),
        compiler_params=pltpu.CompilerParams(vmem_limit_bytes=24 << 20),
        cost_estimate=work(2),
        name="head_slab",
    )(meta, turned, *query, *kv, *(() if got is None else (got,)))


def token_kernel(*refs, count):
    query_refs, kv_refs = refs[:count], refs[count : 2 * count]
    weight_ref, out_ref = refs[2 * count :]
    kv = jnp.concatenate([ref[...] for ref in kv_refs], axis=1)
    query = jnp.concatenate([ref[...] for ref in query_refs], axis=0).T
    split = kv.shape[1]
    out_ref[...] = (
        right_trans(kv, weight_ref[:, :split]) + right_trans(query, weight_ref[:, split:])
    ).astype(BF16)


def token_part(query, kv, weight):
    return pl.pallas_call(
        partial(token_kernel, count=len(query)),
        out_shape=jax.ShapeDtypeStruct((kv[0].shape[0], weight.shape[0]), BF16),
        compiler_params=pltpu.CompilerParams(vmem_limit_bytes=32 << 20),
        cost_estimate=work(2),
        name="token_part",
    )(*query, *kv, weight)


def down_finish_kernel(meta_ref, *refs):
    block = refs[0].shape[0]
    c_at, x_at = meta_ref[0], meta_ref[1]
    for at in range(4):
        place = (c_at ^ (at >> 1)) * 2 + (x_at ^ (at & 1))
        start = pl.multiple_of(place * block, 8)
        refs[4][pl.ds(start, block), :] = refs[at][...].astype(F32)


def down_finish(meta, pieces):
    block, width = pieces[0].shape
    in_vmem = pl.BlockSpec(memory_space=pltpu.VMEM)
    return pl.pallas_call(
        down_finish_kernel,
        grid_spec=pltpu.PrefetchScalarGridSpec(
            num_scalar_prefetch=1, grid=(), in_specs=[in_vmem] * 4, out_specs=in_vmem
        ),
        out_shape=jax.ShapeDtypeStruct((4 * block, width), F32),
        compiler_params=pltpu.CompilerParams(vmem_limit_bytes=32 << 20),
        cost_estimate=work(4),
        name="down_finish",
    )(meta, *pieces)


def up_finish_kernel(meta_ref, *refs):
    pieces = refs[:4]
    up_ref, out_ref, small_ref = refs[4:]
    block = pieces[0].shape[0]
    quarter = up_ref.shape[1] // 4
    side = out_ref.shape[1] // 2
    c_at, x_at = meta_ref[0], meta_ref[1]
    for at in range(4):
        start = pl.multiple_of((x_at ^ (at & 1)) * block, 8)
        rows = pl.ds(start, block)
        core = c_at ^ (at >> 1)
        for half in range(2):
            lanes = pl.ds(pl.multiple_of((2 * half + core) * quarter, 128), quarter)
            up_ref[rows, lanes] = pieces[at][:, half * quarter : (half + 1) * quarter].astype(F32)
        out_ref[rows, pl.ds(pl.multiple_of(core * side, 128), side)] = (
            pieces[at][:, 2 * quarter : 2 * quarter + side].astype(F32)
        )
        if at < 2:
            small_ref[rows, :] = pieces[at][:, 2 * quarter + side :].astype(F32)


def up_finish(meta, pieces, hidden, width):
    block = pieces[0].shape[0]
    in_vmem = pl.BlockSpec(memory_space=pltpu.VMEM)
    shapes = [(2 * block, hidden), (2 * block, width), (2 * block, 128)]
    return pl.pallas_call(
        up_finish_kernel,
        grid_spec=pltpu.PrefetchScalarGridSpec(
            num_scalar_prefetch=1,
            grid=(),
            in_specs=[in_vmem] * 4,
            out_specs=[in_vmem] * 3,
        ),
        out_shape=[jax.ShapeDtypeStruct(shape, F32) for shape in shapes],
        compiler_params=pltpu.CompilerParams(vmem_limit_bytes=40 << 20),
        cost_estimate=work(5),
        name="up_finish",
    )(meta, *pieces)


def head_finish_kernel(meta_ref, own_ref, got_ref, query_ref, key_ref, value_ref, bias_ref, *, part):
    block = own_ref.shape[1] - 16
    head_dim = part // 3
    for at, source in enumerate((own_ref, got_ref)):
        start = pl.multiple_of((meta_ref[0] ^ at) * block, 8)
        rows = pl.ds(start, block)
        keys, values, queries = [], [], []
        for z in range(ZS):
            item = source[(z & 1) * 2 + (z >> 1)].astype(F32)
            for head in range(3):
                low = head * 2 * head_dim
                keys.append(item[:, low : low + head_dim])
                values.append(item[:, low + head_dim : low + 2 * head_dim])
            queries.append(item[:, 2 * part :])
        key = jnp.concatenate(keys, axis=1)
        value = jnp.concatenate(values, axis=1)
        query = jnp.concatenate(queries, axis=1)
        query_ref[rows, :] = query[:block]
        key_ref[rows, :] = key[:block]
        value_ref[rows, :] = value[:block]
        if at == 0:
            bias_ref[0:8, :] = query[block : block + 8]
            bias_ref[8:16, :] = value[block : block + 8]


def head_finish(meta, own, got):
    _, block, columns = own.shape
    rows = 2 * (block - 16)
    width = ZS * columns // 3
    in_vmem = pl.BlockSpec(memory_space=pltpu.VMEM)
    return pl.pallas_call(
        partial(head_finish_kernel, part=columns // 3),
        grid_spec=pltpu.PrefetchScalarGridSpec(
            num_scalar_prefetch=1, grid=(), in_specs=[in_vmem] * 2, out_specs=[in_vmem] * 4
        ),
        out_shape=[jax.ShapeDtypeStruct((rows, width), F32)] * 3
        + [jax.ShapeDtypeStruct((16, width), F32)],
        compiler_params=pltpu.CompilerParams(vmem_limit_bytes=40 << 20),
        cost_estimate=work(4),
        name="head_finish",
    )(meta, own, got)


def in_order(index, own, other, axis):
    return jnp.where(
        index == 0,
        jnp.concatenate([own, other], axis=axis),
        jnp.concatenate([other, own], axis=axis),
    )


def part_of(value, index, count, axis):
    size = value.shape[axis] // count
    return lax.dynamic_slice_in_dim(value, index * size, size, axis)


def body(
    inputs,
    lengths,
    cotangent,
    query_weight,
    query_bias,
    key_weight,
    value_weight,
    value_bias,
    output_weight,
    output_bias,
    first_gain,
    first_shift,
    up_weight,
    up_bias,
    down_weight,
    down_bias,
    second_gain,
    second_shift,
    *,
    sizes,
):
    count_o, count_w = sizes
    w_at = lax.axis_index("w")
    z_at = lax.axis_index("z")
    c_at = lax.axis_index("c")
    x_at = lax.axis_index("x")
    o_at = lax.axis_index("o")
    tokens = inputs[0]
    local_rows, width = tokens.shape
    head_dim = width // HEADS
    heads = HEADS // ZS
    part = heads * head_dim
    length = lengths[0]

    hold = lax.optimization_barrier

    def head_slice(weight):
        return lax.dynamic_slice_in_dim(weight, z_at * part, part, 1).astype(BF16)

    low_tokens = tokens.astype(BF16)
    token_all = lax.all_gather(low_tokens, "z", axis=0, tiled=True)
    own_rows = query_weight.shape[0]
    key_own = head_slice(key_weight)
    value_own = head_slice(value_weight)
    own_kv = []
    for head in range(heads):
        cut = slice(head * head_dim, (head + 1) * head_dim)
        own_kv += [key_own[:, cut], value_own[:, cut]]
    attn_own = jnp.concatenate(own_kv + [head_slice(query_weight)], axis=1)
    small = jnp.concatenate(
        [
            item.astype(BF16)
            for item in (
                query_bias,
                value_bias,
                output_bias,
                first_gain,
                first_shift,
                down_bias,
                second_gain,
                second_shift,
                up_bias,
            )
        ]
    ).reshape(-1, 3 * part)
    attn_pack = jnp.concatenate([attn_own, small], axis=0)
    if count_w == 2:
        attn_got = swap(attn_pack, "w")
        attn_full = in_order(w_at, attn_own, attn_got[:own_rows], 0)
        small_all = in_order(w_at, small[None], attn_got[None, own_rows:], 0)
    else:
        attn_all = lax.all_gather(attn_pack, "w", axis=0, tiled=False)
        attn_full = attn_all[:, :own_rows].reshape(width, 3 * part)
        small_all = attn_all[:, own_rows:]
    small_all = small_all.astype(F32).reshape(count_w, -1, own_rows)
    vec = jnp.transpose(small_all[:, :8], (1, 0, 2)).reshape(8, width)
    up_offset = small_all[:, 8:].reshape(1, -1)
    attn_pack, output_weight, up_weight, down_weight = hold(
        (attn_pack, output_weight, up_weight, down_weight)
    )
    low_weights = [item.astype(BF16) for item in (output_weight, up_weight, down_weight)]
    low_out, low_up, low_down = low_weights
    if count_w == 2:
        up_half = part_of(low_up, c_at, 2, 1)
        weight_pack = jnp.concatenate(
            [part_of(low_out, c_at, 2, 0)]
            + [up_half[:, at : at + width] for at in range(0, up_half.shape[1], width)]
            + [part_of(low_down, c_at, 2, 0)],
            axis=0,
        )
        attn_got, weight_pack = hold((attn_got, weight_pack))
        weight_got = swap(weight_pack, "w")
    else:
        weight_got = [lax.all_gather(item, "w", axis=0, tiled=True) for item in low_weights]

    own_bias = lax.dynamic_slice_in_dim(vec[:2], z_at * part, part, 1)
    value_bias_own = own_bias[1].reshape(heads, 1, head_dim)
    kv_bias = jnp.concatenate([jnp.zeros_like(value_bias_own), value_bias_own], axis=1)
    bias_row = jnp.concatenate([kv_bias.reshape(1, 2 * part), own_bias[:1]], axis=1)
    groups = ((0, heads),)
    queries, *key_values, turned = project(
        token_all, attn_full, bias_row, [count for _, count in groups]
    )
    places = []
    for at in range(4 * count_o):
        o_of = o_at ^ (at >> 2)
        places.append(o_of * 16 + (x_at ^ (at & 1)) * 2 + (c_at ^ ((at >> 1) & 1)))
    meta = jnp.stack([length, z_at] + places).astype(jnp.int32)
    near = ((0, 1), (1, 0), (2, 3), (3, 2))
    far = ((0, 2), (2, 0), (1, 3), (3, 1))
    cross = ((0, 3), (3, 0), (1, 2), (2, 1))

    def exchange(pieces):
        return [pieces[0]] + [
            lax.ppermute(item, "z", perm) for item, perm in zip(pieces[1:], (near, far, cross))
        ]

    kv_groups = []
    for item in key_values:
        kv_blocks = [item]
        for axis in ("x", "c", "o")[: 3 if count_o == 2 else 2]:
            kv_blocks = kv_blocks + [swap(item, axis) for item in kv_blocks]
        kv_groups.append(kv_blocks)
    attended, mixed, logs = [], [], []
    for (first, _), kv_blocks in zip(groups, kv_groups):
        out, *made = attend_forward(meta, queries, kv_blocks, first, head_dim)
        attended.append(out)
        mixed.append(exchange(made[:ZS]))
        logs.append(made[ZS])
    if count_w == 2:
        attended[0], weight_got = hold((attended[0], weight_got))
        weights = [*low_weights, weight_got, swap(weight_got, "c")]
    else:
        weights = weight_got

    split = count_w == 2 and count_o == 1
    my_index = o_at * 16 + z_at * 4 + x_at * 2 + c_at
    rest = jnp.clip(length - my_index * local_rows, 0, local_rows)
    core = c_at if split else jnp.zeros_like(c_at)
    spots = jnp.stack([rest, w_at, core, z_at]).astype(jnp.int32)
    outputs, resid_grad, *made = middle(
        spots, mixed, groups, tokens, cotangent[0], vec, up_offset, weights
    )
    head_grads = exchange(made[:ZS])
    send, keep, small_own = made[ZS:]
    hidden = up_offset.shape[1]

    def add_pair(kept, got):
        return (kept.astype(F32) + got.astype(F32)).astype(BF16)

    def unite(value, got, bit):
        return in_order(bit, value, got, 0)

    near_bit, far_bit = z_at & 1, z_at >> 1
    spot = jnp.stack([c_at, x_at]).astype(jnp.int32)
    token = [spot]

    def arrive(*values):
        token[0], *values = hold((token[0], *values))
        return values[0] if len(values) == 1 else values

    def backward(at):
        return attend_backward(
            meta,
            queries,
            head_grads,
            attended[at],
            logs[at],
            kv_groups[at],
            groups[at][0],
            head_dim,
        )

    def to_near(value):
        return lax.ppermute(value, "z", near)

    def to_far(value):
        return lax.ppermute(value, "z", far)

    def head_part(at, got=None):
        return head_slab(at, turned, [query_low], [kv_low], 2 * count_w, got)

    def pick(w, c):
        return jnp.stack([jnp.asarray(w), jnp.asarray(c)]).astype(jnp.int32)

    if split:
        got, small_got = swap(send, "c"), swap(small_own, "c")
        down_far = down_slab(pick(1 - w_at, 0), keep, send, got)
        up_sent, up_kept = up_slabs(
            jnp.stack([x_at]).astype(jnp.int32), keep, send, got, small_own, small_got
        )
        down_near = down_slab(pick(1 * w_at, 0), keep, send, got)
        down_far, up_sent, down_near, *head_grads = hold(
            (down_far, up_sent, down_near, *head_grads)
        )
        query_low, *pairs = backward(0)
        down_got, up_got, query_low, *pairs = arrive(
            swap(down_far, "w"), swap(up_sent, "x"), query_low, *pairs
        )
        pair_got = swap(pairs[1], "c")
        down_sum = add_pair(down_near, down_got)
        down_got = swap(part_of(down_sum, 1 - x_at, 2, 0), "x")
        up_sum = add_pair(up_kept, up_got).reshape(2, own_rows // 2, -1)
        up_got = swap(lax.dynamic_index_in_dim(up_sum, 1 - w_at, 0, keepdims=False), "w")
        pair_got = arrive(pair_got)
        half_rows = pair_got.shape[0] // 2
        pair_sent = add_pair(pairs[0][half_rows:], pair_got[half_rows:])
        pair_kept = add_pair(pairs[0][:half_rows], pair_got[:half_rows])
        pair_sent, pair_kept = arrive(pair_sent, pair_kept)
        pair_got = swap(pair_sent, "x")
        down_got = arrive(down_got)
        down_sum = add_pair(part_of(down_sum, x_at, 2, 0), down_got)
        down_got = to_near(part_of(down_sum, 1 - near_bit, 2, 0))
        up_got = arrive(up_got)
        up_sum = add_pair(lax.dynamic_index_in_dim(up_sum, w_at, 0, keepdims=False), up_got)
        up_got = to_near(part_of(up_sum, 1 - near_bit, 2, 0))
        down_got = arrive(down_got)
        down_sum = add_pair(part_of(down_sum, near_bit, 2, 0), down_got)
        down_got = to_far(part_of(down_sum, 1 - far_bit, 2, 0))
        up_got = arrive(up_got)
        up_sum = add_pair(part_of(up_sum, near_bit, 2, 0), up_got)
        up_got = to_far(part_of(up_sum, 1 - far_bit, 2, 0))
        down_got = arrive(down_got)
        down_sum = add_pair(part_of(down_sum, far_bit, 2, 0), down_got)
        down_got = to_far(down_sum)
        pair_got = arrive(pair_got)
        kv_low = add_pair(pair_kept, pair_got)
        token_sum = token_part([query_low], [kv_low], attn_full)
        token_grad = lax.psum_scatter(token_sum, "z", scatter_dimension=0, tiled=True)
        head_far = swap(head_part(pick(1 - w_at, 1 - c_at)), "c")
        head_near = swap(head_part(pick(1 * w_at, 1 - c_at)), "c")
        head_far = arrive(head_far)
        head_sent = swap(head_part(pick(1 - w_at, c_at), head_far), "w")
        head_near = arrive(head_near)
        head_sum = head_part(pick(1 * w_at, c_at), head_near)
        up_got = arrive(up_got)
        up_sum = add_pair(part_of(up_sum, far_bit, 2, 0), up_got)
        up_got = to_far(up_sum)
        down_got = arrive(down_got)
        down_sum = unite(down_sum, down_got, far_bit)
        down_got = to_near(down_sum)
        head_sent = arrive(head_sent)
        head_sum = add_pair(head_sum, head_sent)
        head_got = swap(head_sum, "x")
        up_got = arrive(up_got)
        up_sum = unite(up_sum, up_got, far_bit)
        up_got = to_near(up_sum)
        down_got = arrive(down_got)
        down_sum = unite(down_sum, down_got, near_bit)
        down_x = swap(down_sum, "x")
        down_c = swap(down_sum, "c")
        head_got = arrive(head_got)
        head_sum = add_pair(head_sum, head_got)
        head_got = to_far(head_sum)
        up_got = arrive(up_got)
        up_sum = unite(up_sum, up_got, near_bit)
        up_x = swap(up_sum, "x")
        up_c = swap(up_sum, "c")
        down_x = arrive(down_x)
        down_pieces = [down_sum, down_x, down_c, swap(down_x, "c")]
        head_got = arrive(head_got)
        head_two = unite(head_sum[None], head_got[None], far_bit)
        head_got = to_near(head_two)
        total_down = down_finish(spot, down_pieces)
        up_x = arrive(up_x)
        up_pieces = [up_sum, up_x, up_c, swap(up_x, "c")]
        head_got = arrive(head_got)
        head_four = unite(head_two, head_got, near_bit)
        head_other = swap(head_four, "c")
        total_up, total_out, table = up_finish(token[0], up_pieces, hidden, width)
        groups = own_rows // 128
        small_total = table[: 8 * groups].reshape(groups, 8, 128)
        vectors = [small_total[:, at].reshape(own_rows) for at in range(6)]
        lines = hidden // count_w // 128
        total_up_bias = table[8 * groups : 8 * groups + lines].reshape(-1)
    else:
        query_low, *pairs = backward(0)
        if count_o == 2:
            pairs = [add_pair(pairs[at], swap(pairs[at + 2], "o")) for at in range(2)]
        pair = add_pair(pairs[0], swap(pairs[1], "c"))
        half_rows = pair.shape[0] // 2
        kv_low = add_pair(pair[:half_rows], swap(pair[half_rows:], "x"))
        token_sum = token_part([query_low], [kv_low], attn_full)
        token_grad = lax.psum_scatter(token_sum, "z", scatter_dimension=0, tiled=True)
        got = [swap(head_part(pick(w, 1 - c_at)), "c") for w in range(count_w)]
        slabs = [head_part(pick(w, c_at), got[w]) for w in range(count_w)]
        slabs = jnp.stack(slabs)
        head_sum = lax.psum_scatter(slabs, "w", scatter_dimension=0, tiled=True)[0]
        head_sum = add_pair(head_sum, swap(head_sum, "x"))
        if count_o == 2:
            head_sum = add_pair(head_sum, swap(head_sum, "o"))
        head_two = unite(head_sum[None], to_far(head_sum)[None], far_bit)
        head_four = unite(head_two, to_near(head_two), near_bit)
        head_other = swap(head_four, "c")
        quarter = hidden // 4
        count = quarter // 256
        act_at = 5 * quarter
        act = [keep[:quarter], send[act_at : act_at + quarter], keep[quarter : 2 * quarter]]
        act += [send[act_at + quarter : act_at + 2 * quarter]]
        act = jnp.concatenate(act, axis=0)

        def rows_of(value, low, at):
            return value[low + at * local_rows : low + (at + 1) * local_rows]

        ffn_at = act_at + 2 * quarter
        ffn = jnp.concatenate([rows_of(send, ffn_at, at) for at in range(width // 256)], axis=1)
        pre = []
        for half in range(2):
            pre += [rows_of(keep, 2 * quarter, half * count + at) for at in range(count)]
            pre += [rows_of(send, 0, half * count + at) for at in range(count)]
        pre = jnp.concatenate(pre, axis=1)
        normed_turned = send[2 * quarter : 2 * quarter + width]
        mixed_turned = send[2 * quarter + width : 2 * quarter + 2 * width]
        side = width // 2
        branch = jnp.concatenate(
            [
                rows_of(keep, 4 * quarter, 0),
                rows_of(keep, 4 * quarter, 1)[:, : side - 256],
                rows_of(send, 2 * quarter + 2 * width, 0),
                rows_of(send, 2 * quarter + 2 * width, 1)[:, : side - 256],
            ],
            axis=1,
        )

        def sum_all(value):
            value = value.astype(BF16)
            value = lax.psum_scatter(value, "w", scatter_dimension=0, tiled=True)
            return lax.psum(value, ("o", "z", "x", "c")).astype(F32)

        total_down = sum_all(matmul(act, ffn))
        total_up = sum_all(matmul(normed_turned, pre))
        total_out = sum_all(matmul(mixed_turned, branch))
        small_own = lax.psum(small_own, ("o", "z", "x", "c", "w"))
        vectors = [part_of(small_own[at], w_at, count_w, 0) for at in range(6)]
        total_up_bias = part_of(small_own[8:12].reshape(-1), w_at, count_w, 0)

    input_grad = resid_grad + token_grad.astype(F32)
    total_query, total_key, total_value, head_bias = head_finish(
        spot, head_four, head_other
    )
    totals = [part_of(head_bias[at], w_at, count_w, 0) for at in (0, 8)] + vectors
    return (
        outputs[None],
        input_grad[None],
        total_query,
        totals[0],
        total_key,
        total_value,
        totals[1],
        total_out,
        totals[2],
        totals[3],
        totals[4],
        total_up,
        total_up_bias,
        total_down,
        totals[5],
        totals[6],
        totals[7],
    )


def solution(mesh):
    count_s = mesh.shape["seq"]
    count_w = mesh.shape["wshard"]
    count_o = count_s // 16
    fine = Mesh(
        mesh.devices.reshape(count_o, ZS, 2, 2, count_w), ("o", "z", "x", "c", "w")
    )
    seq = ("o", "z", "x", "c")
    rows = P("w", seq, None)
    matrix = P("w", None)
    vector = P("w")
    placed = (
        rows,
        vector,
        rows,
        matrix,
        vector,
        matrix,
        matrix,
        vector,
        matrix,
        vector,
        vector,
        vector,
        matrix,
        vector,
        matrix,
        vector,
        vector,
        vector,
    )
    return jax.shard_map(
        partial(body, sizes=(count_o, count_w)),
        mesh=fine,
        in_specs=placed,
        out_specs=(
            rows,
            rows,
            matrix,
            vector,
            matrix,
            matrix,
            vector,
            matrix,
            vector,
            vector,
            vector,
            matrix,
            vector,
            matrix,
            vector,
            vector,
            vector,
        ),
        check_vma=False,
    )
```

```python
from functools import partial

import jax
import jax.numpy as jnp
from jax import lax
from jax.experimental import pallas as pl
from jax.experimental.pallas import tpu as pltpu
from jax.sharding import Mesh, PartitionSpec as P

HEADS = 12
ZS = 4
NEG_FILL = -1e30
SWAP = ((0, 1), (1, 0))
F32 = jnp.float32
BF16 = jnp.bfloat16


def matmul(left_side, right_side):
    return jnp.dot(left_side, right_side, preferred_element_type=F32)


def right_trans(left_side, right_side):
    return lax.dot_general(
        left_side, right_side, (((1,), (1,)), ((), ())), preferred_element_type=F32
    )


def work(units):
    return pl.CostEstimate(flops=int(units * 1e3), bytes_accessed=1, transcendentals=0)


def swap(value, axis):
    return lax.ppermute(value, axis, SWAP)


def touched_groups(length, rows, outer):
    group = 4 * rows
    left = length - outer * (ZS * group)
    return jnp.clip((left + group - 1) // group, 0, ZS)


def with_mask(kv, place, length):
    at = place + lax.broadcasted_iota(jnp.int32, kv.shape, 0)
    lane = lax.broadcasted_iota(jnp.int32, kv.shape, 1)
    fill = jnp.where(at < length, 0.0, jnp.where(lane == 0, NEG_FILL, 0.0))
    return jnp.concatenate([kv, fill.astype(BF16)], axis=1)


def load_head(kv_refs, rows_ref, turned_ref, low):
    head_dim = turned_ref.shape[1]
    for at, ref in enumerate(kv_refs):
        block, half = at // 2, at % 2
        size = ref.shape[0]
        for start in range(0, size, 256):
            value = ref[start : start + 256, :]
            place = slice(half * size + start, half * size + start + 256)
            rows_ref[block, place, :] = value
            turned_ref[block, :, place] = value.T[low : low + head_dim, :]


def forward_kernel(meta_ref, *refs, blocks, rows):
    query_refs, kv_refs = refs[:2], refs[2 : 2 + 2 * blocks]
    out_ref, *refs = refs[2 + 2 * blocks :]
    piece_refs, (log_ref, rows_ref, turned_ref) = refs[:ZS], refs[ZS:]
    head_dim, query_count = out_ref.shape
    length, z_at = meta_ref[0], meta_ref[1]
    load_head(kv_refs, rows_ref, turned_ref, head_dim)
    query = jnp.concatenate([ref[...] for ref in query_refs], axis=1)
    query = jnp.concatenate(
        [
            query,
            jnp.zeros((head_dim, query_count), BF16),
            jnp.ones((128, query_count), BF16),
        ],
        axis=0,
    )

    def step(group, carry, members):
        top, total, acc = carry
        start = pl.multiple_of((group ^ z_at) * rows, rows)
        found = []
        for block in members:
            place = (meta_ref[2 + block] + group * 4) * rows
            kv = with_mask(rows_ref[block, pl.ds(start, rows), :], place, length)
            found.append(matmul(kv, query))
        new_top = top
        for scores in found:
            new_top = jnp.maximum(new_top, jnp.max(scores, axis=0, keepdims=True))
        fade = jnp.exp(top - new_top)
        total = total * fade
        acc = acc * fade
        for block, scores in zip(members, found):
            weights = jnp.exp(scores - new_top)
            total = total + jnp.sum(weights, axis=0, keepdims=True)
            acc = acc + matmul(
                turned_ref[block, :, pl.ds(start, rows)], weights.astype(BF16)
            )
        return new_top, total, acc

    carry = (
        jnp.full((1, query_count), NEG_FILL, F32),
        jnp.zeros((1, query_count), F32),
        jnp.zeros((head_dim, query_count), F32),
    )
    for first in range(0, blocks, 4):
        members = tuple(range(first, first + 4))
        count = touched_groups(length, rows, meta_ref[2 + first] // 16)
        carry = lax.fori_loop(0, count, lambda g, c: step(g, c, members), carry)
    top, total, acc = carry
    out = acc * (1.0 / total)
    out_ref[...] = out
    size = query_count // ZS
    for at in range(ZS):
        piece_refs[at][...] = out[:, at * size : (at + 1) * size].astype(BF16)
    log_ref[0] = top + jnp.log(total)


def attend_forward(meta, queries, kv_blocks, heads):
    blocks = len(kv_blocks)
    half_rows = kv_blocks[0][0].shape[0]
    part, half_count = queries[0].shape
    head_dim, query_count = part // heads, 2 * half_count
    size = query_count // ZS
    return pl.pallas_call(
        partial(forward_kernel, blocks=blocks, rows=2 * half_rows // ZS),
        grid_spec=pltpu.PrefetchScalarGridSpec(
            num_scalar_prefetch=1,
            grid=(heads,),
            in_specs=[pl.BlockSpec((head_dim, half_count), lambda i, m: (i, 0))] * 2
            + [pl.BlockSpec((half_rows, 128), lambda i, m: (0, i))] * (2 * blocks),
            out_specs=[pl.BlockSpec((head_dim, query_count), lambda i, m: (i, 0))]
            + [pl.BlockSpec((head_dim, size), lambda i, m: (i, 0))] * ZS
            + [pl.BlockSpec((1, 1, query_count), lambda i, m: (i, 0, 0))],
            scratch_shapes=[
                pltpu.VMEM((blocks, 2 * half_rows, 128), BF16),
                pltpu.VMEM((blocks, head_dim, 2 * half_rows), BF16),
            ],
        ),
        out_shape=[jax.ShapeDtypeStruct((part, query_count), F32)]
        + [jax.ShapeDtypeStruct((part, size), BF16)] * ZS
        + [jax.ShapeDtypeStruct((heads, 1, query_count), F32)],
        compiler_params=pltpu.CompilerParams(vmem_limit_bytes=40 << 20),
        cost_estimate=work(8 * heads),
        name="attend_forward",
    )(meta, *queries, *[item for pair in kv_blocks for item in pair])


def backward_kernel(meta_ref, *refs, blocks, rows, extra):
    query_refs, (out_ref, log_ref), refs = refs[:2], refs[2:4], refs[4:]
    grad_refs, kv_refs = refs[:ZS], refs[ZS : ZS + 2 * blocks]
    refs = refs[ZS + 2 * blocks + extra :]
    dq_refs, pairs = refs[:ZS], refs[ZS : ZS + blocks // 2]
    rows_ref, turned_ref, qn_ref, gn_ref, acc_ref = refs[ZS + blocks // 2 :]
    head_dim, query_count = out_ref.shape
    length, z_at = meta_ref[0], meta_ref[1]
    block_rows = ZS * rows
    load_head(kv_refs, rows_ref, turned_ref, 0)
    query = jnp.concatenate([ref[...] for ref in query_refs], axis=1)
    grads = jnp.concatenate([ref[...] for ref in grad_refs], axis=1)
    blank = jnp.zeros((head_dim, query_count), BF16)
    query = jnp.concatenate([query, blank], axis=0)
    grad = jnp.concatenate([blank, grads], axis=0)
    qn_ref[...] = query.T
    gn_ref[...] = grad.T
    query = jnp.concatenate([query, jnp.ones((128, query_count), BF16)], axis=0)
    delta = jnp.sum(grads.astype(F32) * out_ref[...], axis=0, keepdims=True)
    log_sum = log_ref[0]
    acc_ref[...] = jnp.zeros_like(acc_ref)

    def put(block, start, value):
        pairs[block // 2][pl.ds(start + (block & 1) * block_rows, rows), :] = value

    def step(group, members):
        start = pl.multiple_of((group ^ z_at) * rows, rows)
        for block in members:
            kv = rows_ref[block, pl.ds(start, rows), :]
            place = (meta_ref[2 + block] + group * 4) * rows
            scores = matmul(with_mask(kv, place, length), query)
            prob_grad = matmul(kv, grad)
            prob = jnp.exp(scores - log_sum)
            score_grad = (prob * (prob_grad - delta)).astype(BF16)
            value = matmul(prob.astype(BF16), gn_ref[...]) + matmul(score_grad, qn_ref[...])
            put(block, start, value.astype(BF16))
            acc_ref[...] += matmul(turned_ref[block, :, pl.ds(start, rows)], score_grad)

    def clear(group, members):
        start = pl.multiple_of((group ^ z_at) * rows, rows)
        for block in members:
            put(block, start, jnp.zeros((rows, 128), BF16))

    def loop(low, high, fn):
        def one(group, carry):
            fn(group)
            return carry

        lax.fori_loop(low, high, one, 0)

    for first in range(0, blocks, 4):
        members = tuple(range(first, first + 4))
        count = touched_groups(length, rows, meta_ref[2 + first] // 16)
        loop(0, count, lambda g: step(g, members))
        loop(count, ZS, lambda g: clear(g, members))
    dq = (acc_ref[...] * head_dim ** (-0.5)).astype(BF16)
    size = query_count // ZS
    for at in range(ZS):
        dq_refs[at][...] = dq[:, at * size : (at + 1) * size]


def attend_backward(meta, queries, grads, out, log_sum, kv_blocks, first, count, made=()):
    blocks = len(kv_blocks)
    half_rows, columns = kv_blocks[0][0].shape
    heads = columns // 128
    part, half_count = queries[0].shape
    head_dim, query_count = part // heads, 2 * half_count
    size = query_count // ZS
    piece = pl.BlockSpec((head_dim, size), lambda i, m: (i + first, 0))
    ins = [
        *queries,
        out,
        log_sum,
        *grads,
        *[item for pair in kv_blocks for item in pair],
        *made,
    ]
    return pl.pallas_call(
        partial(backward_kernel, blocks=blocks, rows=2 * half_rows // ZS, extra=len(made)),
        grid_spec=pltpu.PrefetchScalarGridSpec(
            num_scalar_prefetch=1,
            grid=(count,),
            in_specs=[pl.BlockSpec((head_dim, half_count), lambda i, m: (i + first, 0))] * 2
            + [
                pl.BlockSpec((head_dim, query_count), lambda i, m: (i + first, 0)),
                pl.BlockSpec((1, 1, query_count), lambda i, m: (i + first, 0, 0)),
            ]
            + [piece] * ZS
            + [pl.BlockSpec((half_rows, 128), lambda i, m: (0, i + first))] * (2 * blocks)
            + [pl.BlockSpec(memory_space=pl.ANY)] * len(made),
            out_specs=[piece] * ZS
            + [pl.BlockSpec((4 * half_rows, 128), lambda i, m: (0, i + first))] * (blocks // 2),
            scratch_shapes=[
                pltpu.VMEM((blocks, 2 * half_rows, 128), BF16),
                pltpu.VMEM((blocks, head_dim, 2 * half_rows), BF16),
                pltpu.VMEM((query_count, 128), BF16),
                pltpu.VMEM((query_count, 128), BF16),
                pltpu.VMEM((head_dim, query_count), F32),
            ],
        ),
        out_shape=[jax.ShapeDtypeStruct((part, size), BF16)] * ZS
        + [jax.ShapeDtypeStruct((4 * half_rows, columns), BF16)] * (blocks // 2),
        input_output_aliases={
            1 + len(ins) - len(made) + at: at for at in range(len(made))
        },
        compiler_params=pltpu.CompilerParams(vmem_limit_bytes=48 << 20),
        cost_estimate=work(12 * count),
        name="attend_backward",
    )(meta, *ins)


IN_VMEM = pl.BlockSpec(memory_space=pltpu.VMEM)


def small_call(kernel, meta, values, shapes, scratch=(), limit=32, name=None):
    return pl.pallas_call(
        kernel,
        grid_spec=pltpu.PrefetchScalarGridSpec(
            num_scalar_prefetch=1,
            grid=(),
            in_specs=[IN_VMEM] * len(values),
            out_specs=[IN_VMEM] * len(shapes),
            scratch_shapes=list(scratch),
        ),
        out_shape=[jax.ShapeDtypeStruct(shape, kind) for shape, kind in shapes],
        compiler_params=pltpu.CompilerParams(vmem_limit_bytes=limit << 20),
        cost_estimate=work(1),
        name=name,
    )(meta, *values)


def fold_kernel(meta_ref, kept_ref, got_ref, keep_ref, sent_ref, sum_ref):
    sum_ref[...] = (kept_ref[...].astype(F32) + got_ref[...].astype(F32)).astype(BF16)
    rows = keep_ref.shape[0]
    for at, ref in enumerate((keep_ref, sent_ref)):
        start = pl.multiple_of((meta_ref[0] ^ at) * rows, 16)
        ref[...] = sum_ref[pl.ds(start, rows), :]


def fold(bit, kept, got):
    rows, columns = kept.shape
    half = ((rows // 2, columns), BF16)
    return small_call(
        fold_kernel,
        bit,
        (kept, got),
        [half, half],
        [pltpu.VMEM((rows, columns), BF16)],
        name="fold",
    )


def unite_kernel(meta_ref, own_ref, got_ref, out_ref):
    rows = own_ref.shape[0]
    for at, ref in enumerate((own_ref, got_ref)):
        start = pl.multiple_of((meta_ref[0] ^ at) * rows, 16)
        out_ref[pl.ds(start, rows), :] = ref[...]


def unite(bit, own, got):
    rows, columns = own.shape
    return small_call(
        unite_kernel, bit, (own, got), [((2 * rows, columns), BF16)], name="unite"
    )[0]


def plus_kernel(meta_ref, one_ref, two_ref, out_ref, *, low):
    cut = slice(low, low + out_ref.shape[0])
    out_ref[...] = (one_ref[cut, :].astype(F32) + two_ref[cut, :].astype(F32)).astype(BF16)


def plus(meta, one, two, low=0):
    rows, columns = one.shape
    return small_call(
        partial(plus_kernel, low=low),
        meta,
        (one, two),
        [((rows - low, columns), BF16)],
        name="plus",
    )[0]


def prepare_kernel(meta_ref, *refs):
    sources, refs = refs[:4], refs[4:]
    low_ref, pack_ref, low_refs, head_ref = refs[0], refs[1], refs[2:5], refs[5]
    places, sems = refs[6:10], refs[10]
    copies = []
    for at in range(4):
        copies.append(pltpu.make_async_copy(sources[at], places[at], sems.at[at]))
        copies[-1].start()
    z_at, c_at = meta_ref[0], meta_ref[1]
    width = places[0].shape[1]
    part = width // ZS
    head_dim = width // HEADS
    copies[0].wait()
    low_ref[...] = places[0][...].astype(BF16)
    parts = []
    for kind in range(3):
        ref = places[kind + 1]
        copies[kind + 1].wait()
        value = ref[...]
        low_refs[kind][...] = value.astype(BF16)
        half = ref.shape[0] // 2
        rows = ref[pl.ds(pl.multiple_of(c_at * half, half), half), :]
        head_ref[kind * half : (kind + 1) * half, :] = rows.astype(BF16)
        turn = lax.rem(width - z_at * part, width)
        parts.append(pltpu.roll(value, turn, 1)[:, :part])
    columns = []
    for head in range(part // head_dim):
        cut = slice(head * head_dim, (head + 1) * head_dim)
        columns += [parts[1][:, cut], parts[2][:, cut]]
    pack_ref[...] = jnp.concatenate(columns + [parts[0]], axis=1).astype(BF16)


def prepare(meta, tokens, weights):
    rows, width = tokens.shape
    count = weights[0].shape[0]
    shapes = [(rows, width), (count, 3 * width // ZS)] + [(count, width)] * 3
    shapes.append((3 * count // 2, width))
    return pl.pallas_call(
        prepare_kernel,
        grid_spec=pltpu.PrefetchScalarGridSpec(
            num_scalar_prefetch=1,
            grid=(),
            in_specs=[pl.BlockSpec(memory_space=pltpu.MemorySpace.HBM)] * 4,
            out_specs=[IN_VMEM] * len(shapes),
            scratch_shapes=[pltpu.VMEM((rows, width), F32)]
            + [pltpu.VMEM((count, width), F32)] * 3
            + [pltpu.SemaphoreType.DMA((4,))],
        ),
        out_shape=[jax.ShapeDtypeStruct(shape, BF16) for shape in shapes],
        compiler_params=pltpu.CompilerParams(vmem_limit_bytes=40 << 20),
        cost_estimate=work(1),
        name="prepare",
    )(meta, tokens, *weights)


def round_kernel(meta_ref, out_w, up_w, down_w, low_out, low_up, low_down, pack_ref):
    core = meta_ref[1]
    for source, target in ((out_w, low_out), (up_w, low_up), (down_w, low_down)):
        target[...] = source[...].astype(BF16)
    width = pack_ref.shape[1]
    low = 0
    half = out_w.shape[0] // 2
    rows = pl.ds(pl.multiple_of(core * half, half), half)
    pack_ref[low : low + half, :] = out_w[rows, :].astype(BF16)
    low += half
    count = up_w.shape[1] // 2
    for block in range(count // width):
        lanes = pl.ds(pl.multiple_of(core * count + block * width, 128), width)
        pack_ref[low : low + up_w.shape[0], :] = up_w[:, lanes].astype(BF16)
        low += up_w.shape[0]
    half = down_w.shape[0] // 2
    rows = pl.ds(pl.multiple_of(core * half, half), half)
    pack_ref[low : low + half, :] = down_w[rows, :].astype(BF16)


def round_weights(meta, weights):
    out_w, up_w, down_w = weights
    width = out_w.shape[1]
    total = out_w.shape[0] // 2 + up_w.shape[0] * (up_w.shape[1] // 2 // width)
    total += down_w.shape[0] // 2
    return small_call(
        round_kernel,
        meta,
        weights,
        [(item.shape, BF16) for item in weights] + [((total, width), BF16)],
        limit=48,
        name="round_weights",
    )


def project_kernel(meta_ref, first_ref, second_ref, *refs, shared):
    query_ref, kv_ref, turned_ref, token_ref, bias_ref = refs[-5:]
    part = query_ref.shape[0]
    rows, width = first_ref.shape
    split = 2 * part
    token_ref[:rows, :] = first_ref[...]
    token_ref[rows:, :] = second_ref[...]
    if shared:
        w_at, z_at = meta_ref[0], meta_ref[1]
        both = None
        bias_ref[...] = jnp.zeros_like(bias_ref)
        for at in range(2):
            count = refs[at].shape[0]
            cut = pl.ds(pl.multiple_of((w_at ^ at) * count, 128), count)
            term = matmul(token_ref[:, cut], refs[at][...])
            both = term if both is None else both + term
            bias_ref[0:2, cut] = refs[2 + at][0:2, :].astype(F32)
        turn = lax.rem(width - z_at * part, width)
        bias = pltpu.roll(bias_ref[...], turn, 1)[:, :part]
        head_dim = width // HEADS
        pieces = []
        for head in range(part // head_dim):
            pieces.append(jnp.zeros((1, head_dim), F32))
            pieces.append(bias[1:2, head * head_dim : (head + 1) * head_dim])
        both = both + jnp.concatenate(pieces + [bias[0:1, :]], axis=1)
    else:
        both = matmul(token_ref[...], refs[0][...]) + refs[1][...]
    kv_ref[...] = both[:, :split].astype(BF16)
    scale = (part * ZS // HEADS) ** (-0.5)
    query_ref[...] = (both[:, split:].astype(BF16) * jnp.array(scale, BF16)).T
    turned_ref[...] = token_ref[...].T


def project(meta, first, second, sources):
    rows, width = first.shape
    part = sources[0].shape[1] // 3
    return small_call(
        partial(project_kernel, shared=len(sources) == 4),
        meta,
        (first, second, *sources),
        [((part, 2 * rows), BF16), ((2 * rows, 2 * part), BF16), ((width, 2 * rows), BF16)],
        [pltpu.VMEM((2 * rows, width), BF16), pltpu.VMEM((8, width), F32)],
        limit=40,
        name="project",
    )


def middle_kernel(meta_ref, tokens_ref, seed_ref, vec_ref, upoff_ref, *refs, groups, shared):
    mixed_refs = [refs[at * ZS : (at + 1) * ZS] for at in range(len(groups))]
    refs = refs[ZS * len(groups) :]
    weight_refs = refs[: 5 if shared else 3]
    refs = refs[len(weight_refs) :]
    outputs_ref, resid_ref = refs[:2]
    mgrad_refs = refs[2 : 2 + ZS]
    (
        send_ref,
        keep_ref,
        small_ref,
        out_w,
        up_w,
        down_w,
        slope_ref,
        wide_ref,
        tall_ref,
        sems,
    ) = refs[2 + ZS :]
    w_at, core, z_at = meta_ref[1], meta_ref[2], meta_ref[3]
    moves = [[], [], []]
    if shared:
        outs, ups, downs, got, pair = weight_refs
        count_o, count_u, count_d = outs.shape[0], ups.shape[0], downs.shape[0]
        for kind, (source, target) in enumerate(((outs, out_w), (ups, up_w), (downs, down_w))):
            start = pl.multiple_of(w_at * source.shape[0], source.shape[0])
            moves[kind].append((source, target.at[pl.ds(start, source.shape[0]), :]))
        lanes = got.shape[1]
        for source, which in ((got, core), (pair, 1 - core)):
            half = count_o // 2
            start = pl.multiple_of(((1 - w_at) * 2 + which) * half, half)
            moves[0].append((source.at[pl.ds(0, half), :], out_w.at[pl.ds(start, half), :]))
            low = half
            start = pl.multiple_of((1 - w_at) * count_u, count_u)
            for block in range(up_w.shape[1] // 2 // lanes):
                lane = pl.multiple_of(which * (up_w.shape[1] // 2) + block * lanes, 128)
                moves[1].append(
                    (
                        source.at[pl.ds(low, count_u), :],
                        up_w.at[pl.ds(start, count_u), pl.ds(lane, lanes)],
                    )
                )
                low += count_u
            half = count_d // 2
            start = pl.multiple_of(((1 - w_at) * 2 + which) * half, half)
            moves[2].append((source.at[pl.ds(low, half), :], down_w.at[pl.ds(start, half), :]))
    else:
        for kind, pair in enumerate(zip(weight_refs, (out_w, up_w, down_w))):
            moves[kind].append(pair)
    copies = []
    at = 0
    for kind in range(3):
        made = []
        for source, target in moves[kind]:
            made.append(pltpu.make_async_copy(source, target, sems.at[at]))
            made[-1].start()
            at += 1
        copies.append(made)
    rows, width = tokens_ref.shape
    hidden = upoff_ref.shape[1]
    part = width // ZS
    head_dim = width // HEADS
    quarter = hidden // 4

    def mean(value):
        return jnp.mean(value, axis=-1, keepdims=True)

    def norm(value):
        centered = value - mean(value)
        scale = lax.rsqrt(mean(centered * centered) + 1e-12)
        return centered * scale, scale

    def norm_back(grad, normal, scale):
        return scale * (grad - mean(grad) - normal * mean(grad * normal))

    def column(value):
        return jnp.sum(value, axis=0, keepdims=True)

    normed_at = 2 * quarter
    mixed_at = normed_at + width
    branch_at = mixed_at + width
    act_at = 5 * quarter
    for (first, count), pieces in zip(groups, mixed_refs):
        size = count * head_dim
        for at in range(ZS):
            low = mixed_at + (z_at ^ at) * part + first * head_dim
            send_ref[pl.ds(pl.multiple_of(low, head_dim), size), :] = pieces[at][...]
    mixed = send_ref[mixed_at:branch_at, :].T
    for copy in copies[0]:
        copy.wait()
    first_n, first_r = norm(tokens_ref[...] + (matmul(mixed, out_w[...]) + vec_ref[2:3, :]))
    normed = first_n * vec_ref[3:4, :] + vec_ref[4:5, :]
    low = normed.astype(BF16)
    send_ref[normed_at:mixed_at, :] = low.T
    for copy in copies[1] + copies[2]:
        copy.wait()
    quarters = []
    for half in range(2):
        for kept in (False, True):
            at = half * 2 * quarter + (core if kept else 1 - core) * quarter
            quarters.append((half, kept, pl.multiple_of(at, quarter)))
    acc = None
    for at, (half, kept, start) in enumerate(quarters):
        cut = pl.ds(start, quarter)
        pre_act = matmul(low, up_w[:, cut]) + upoff_ref[:, cut]
        phi = 0.5 + 0.5 * lax.erf(pre_act * (0.5**0.5))
        act = (pre_act * phi).astype(BF16)
        slope_ref[:, at * quarter : (at + 1) * quarter] = phi + pre_act * (
            jnp.exp(-0.5 * pre_act * pre_act) * 0.3989422804014327
        )
        target, base = (keep_ref, 0) if kept else (send_ref, act_at)
        target[base + half * quarter : base + (half + 1) * quarter, :] = act.T
        term = matmul(act, down_w[cut, :])
        acc = term if acc is None else acc + term
    second_n, second_r = norm(normed + (acc + vec_ref[5:6, :]))
    outputs_ref[...] = second_n * vec_ref[6:7, :] + vec_ref[7:8, :]
    place = lax.broadcasted_iota(jnp.int32, (rows, 1), 0)
    seed = jnp.where(place < meta_ref[0], seed_ref[...], 0.0)
    sum_grad = norm_back(seed * vec_ref[6:7, :], second_n, second_r)
    ffn = sum_grad.astype(BF16)
    for at in range(width // 256):
        low_row = act_at + 2 * quarter + at * rows
        send_ref[low_row : low_row + rows, :] = ffn[:, at * 256 : (at + 1) * 256]
    small_ref[3:4, :] = column(ffn.astype(F32))
    small_ref[4:5, :] = column(seed * second_n)
    small_ref[5:6, :] = column(seed)
    acc = sum_grad
    for at, (half, kept, start) in enumerate(quarters):
        cut = pl.ds(start, quarter)
        pre = right_trans(ffn, down_w[cut, :]) * slope_ref[:, at * quarter : (at + 1) * quarter]
        pre = pre.astype(BF16)
        target, base = (keep_ref, 2 * quarter) if kept else (send_ref, 0)
        for block in range(quarter // 256):
            row = base + (half * (quarter // 256) + block) * rows
            target[row : row + rows, :] = pre[:, block * 256 : (block + 1) * 256]
        sums = column(pre.astype(F32))
        line = 8 + half * (2 * quarter // width) + (core if kept else 1 - core)
        small_ref[pl.ds(line, 1), :] = sums
        acc = acc + right_trans(pre, up_w[:, cut])
    small_ref[1:2, :] = column(acc * first_n)
    small_ref[2:3, :] = column(acc)
    resid = norm_back(acc * vec_ref[3:4, :], first_n, first_r)
    resid_ref[...] = resid
    branch = resid.astype(BF16)
    wide_ref[...] = branch
    side = width // 2
    for target, base, which in (
        (send_ref, branch_at, 1 - core),
        (keep_ref, 4 * quarter, core),
    ):
        values = wide_ref[:, pl.ds(pl.multiple_of(which * side, 128), side)]
        target[base : base + rows, :] = values[:, :256]
        target[base + rows : base + 2 * rows, : side - 256] = values[:, 256:]
        target[base + rows : base + 2 * rows, side - 256 :] = jnp.zeros(
            (rows, 512 - side), BF16
        )
    small_ref[0:1, :] = column(branch.astype(F32))
    small_ref[6:8, :] = jnp.zeros((2, width), F32)
    small_ref[12:16, :] = jnp.zeros((4, width), F32)
    gap = branch_at + 2 * rows
    send_ref[gap:act_at, :] = jnp.zeros((act_at - gap, 256), BF16)
    tall_ref[...] = right_trans(out_w[...], branch).astype(BF16)
    for at in range(ZS):
        start = pl.multiple_of((z_at ^ at) * part, part)
        mgrad_refs[at][...] = tall_ref[pl.ds(start, part), :]


def middle(meta, mixed, groups, tokens, seed, vec, upoff, weights):
    rows, width = tokens.shape
    hidden = upoff.shape[1]
    in_vmem = pl.BlockSpec(memory_space=pltpu.VMEM)
    in_place = pl.BlockSpec(memory_space=pl.ANY)
    flat = [item for group in mixed for item in group]
    part = jax.ShapeDtypeStruct((width // ZS, rows), BF16)
    return pl.pallas_call(
        partial(middle_kernel, groups=groups, shared=len(weights) == 5),
        grid_spec=pltpu.PrefetchScalarGridSpec(
            num_scalar_prefetch=1,
            grid=(),
            in_specs=[in_vmem] * (4 + len(flat)) + [in_place] * len(weights),
            out_specs=[in_vmem] * (5 + ZS),
            scratch_shapes=[
                pltpu.VMEM((width, width), BF16),
                pltpu.VMEM((width, hidden), BF16),
                pltpu.VMEM((hidden, width), BF16),
                pltpu.VMEM((rows, hidden), F32),
                pltpu.VMEM((rows, width), BF16),
                pltpu.VMEM((width, rows), BF16),
                pltpu.SemaphoreType.DMA((11,)),
            ],
        ),
        out_shape=[jax.ShapeDtypeStruct((rows, width), F32)] * 2
        + [part] * ZS
        + [
            jax.ShapeDtypeStruct((2 * hidden, 256), BF16),
            jax.ShapeDtypeStruct((hidden + 2 * rows, 256), BF16),
            jax.ShapeDtypeStruct((16, width), F32),
        ],
        compiler_params=pltpu.CompilerParams(vmem_limit_bytes=56 << 20),
        cost_estimate=work(15),
        name="middle",
    )(meta, tokens, seed, vec, upoff, *flat, *weights)


def down_kernel(meta_ref, keep_ref, got_ref, own_ffn_ref, got_ffn_ref, out_ref):
    keep, got = keep_ref[...], got_ref[...]
    rows = keep.shape[1]
    for at in range(out_ref.shape[1] // 256):
        cut = slice(at * rows, (at + 1) * rows)
        value = matmul(keep, own_ffn_ref[cut, :]) + matmul(got, got_ffn_ref[cut, :])
        out_ref[:, at * 256 : (at + 1) * 256] = value.astype(BF16)


def down_slab(meta, keep, send, got):
    block = send.shape[0] // 8
    kept = pl.BlockSpec((block, send.shape[1]), lambda i, m: (m[0], 0))
    act = pl.BlockSpec((block, send.shape[1]), lambda i, m: (5 + m[0], 0))
    ffn = pl.BlockSpec((block, send.shape[1]), lambda i, m: (7, 0))
    return pl.pallas_call(
        down_kernel,
        grid_spec=pltpu.PrefetchScalarGridSpec(
            num_scalar_prefetch=1,
            grid=(1,),
            in_specs=[kept, act, ffn, ffn],
            out_specs=pl.BlockSpec((block, block), lambda i, m: (0, 0)),
        ),
        out_shape=jax.ShapeDtypeStruct((block, block), BF16),
        compiler_params=pltpu.CompilerParams(vmem_limit_bytes=24 << 20),
        cost_estimate=work(2),
        name="down_slab",
    )(meta, keep, got, send, got)


def up_kernel(meta_ref, keep_ref, send_ref, got_ref, own_small_ref, got_small_ref, *refs):
    out_refs, table_ref = refs[:2], refs[2]
    rows = send_ref.shape[1]
    width = own_small_ref.shape[1]
    block = width // 4
    side = width // 2
    normed_at = 2 * width
    branch_at = normed_at + 2 * width
    x_at = meta_ref[0]
    pre_keep = 2 * width
    for w in range(2):
        small = own_small_ref[...] + got_small_ref[...]
        table_ref[...] = jnp.zeros_like(table_ref)
        for at in range(side // 128):
            low = w * side + at * 128
            table_ref[at * 8 : (at + 1) * 8, :] = small[:8, low : low + 128]
        base = side // 128 * 8
        for at in range(2 * width // 128):
            line = 8 + 2 * w + at // (width // 128)
            low = at % (width // 128) * 128
            table_ref[base + at : base + at + 1, :] = small[line : line + 1, low : low + 128]
        for out_ref, which in zip(out_refs, (1 - x_at, x_at)):
            start = pl.multiple_of(which * block, block)
            target = slice(w * block, (w + 1) * block)
            own = send_ref[pl.ds(normed_at + w * side + start, block), :]
            got = got_ref[pl.ds(normed_at + w * side + start, block), :]
            for at in range(normed_at // rows):
                cut = slice(at * rows, (at + 1) * rows)
                value = matmul(own, keep_ref[pre_keep + at * rows : pre_keep + (at + 1) * rows, :])
                value = value + matmul(got, got_ref[cut, :])
                out_ref[target, at * 256 : (at + 1) * 256] = value.astype(BF16)
            own = send_ref[pl.ds(normed_at + width + w * side + start, block), :]
            got = got_ref[pl.ds(normed_at + width + w * side + start, block), :]
            lane = normed_at // rows * 256
            for at in range(2):
                mine = 4 * width + at * rows
                theirs = branch_at + at * rows
                value = matmul(own, keep_ref[mine : mine + rows, :])
                value = value + matmul(got, got_ref[theirs : theirs + rows, :])
                value = value[:, : min(256, side - at * 256)].astype(BF16)
                out_ref[target, lane : lane + value.shape[1]] = value
                lane += value.shape[1]
            out_ref[target, lane : lane + 128] = table_ref[pl.ds(start, block), :].astype(BF16)


def up_slabs(meta, keep, send, got, own_small, got_small):
    width = own_small.shape[1]
    columns = 2 * width + width // 2 + 128
    first = pl.BlockSpec((5 * width, send.shape[1]), lambda i, m: (0, 0))

    def whole(value):
        return pl.BlockSpec(value.shape, lambda i, m: (0, 0))

    return pl.pallas_call(
        up_kernel,
        grid_spec=pltpu.PrefetchScalarGridSpec(
            num_scalar_prefetch=1,
            grid=(1,),
            in_specs=[whole(keep), first, first, whole(own_small), whole(own_small)],
            out_specs=[pl.BlockSpec((width // 2, columns), lambda i, m: (0, 0))] * 2,
            scratch_shapes=[pltpu.VMEM((width // 2, 128), F32)],
        ),
        out_shape=[jax.ShapeDtypeStruct((width // 2, columns), BF16)] * 2,
        compiler_params=pltpu.CompilerParams(vmem_limit_bytes=40 << 20),
        cost_estimate=work(4),
        name="up_slabs",
    )(meta, keep, send, got, own_small, got_small)


def key_sum_kernel(own_ref, core_ref, got_ref, *out_refs):
    size = out_refs[0].shape[1]
    for at, ref in enumerate(out_refs):
        cut = slice(at * size, (at + 1) * size)
        kept = (own_ref[cut, :].astype(F32) + core_ref[cut, :].astype(F32)).astype(BF16)
        ref[...] = (kept.astype(F32) + got_ref[cut, :].astype(F32)).astype(BF16).T


def key_sum(own, core, got):
    rows, columns = got.shape
    half = pl.BlockSpec((rows, columns), lambda i: (0, 0))
    return pl.pallas_call(
        key_sum_kernel,
        grid=(1,),
        in_specs=[half] * 3,
        out_specs=[pl.BlockSpec((columns, rows // ZS), lambda i: (0, 0))] * ZS,
        out_shape=[jax.ShapeDtypeStruct((columns, rows // ZS), BF16)] * ZS,
        compiler_params=pltpu.CompilerParams(vmem_limit_bytes=24 << 20),
        cost_estimate=work(2),
        name="key_sum",
    )(own, core, got)


def head_kernel(meta_ref, *refs):
    turned_refs, query_refs, kv_refs = refs[:2], refs[2 : 2 + ZS], refs[2 + ZS : 2 + 2 * ZS]
    refs = refs[2 + 2 * ZS :]
    out_ref = refs[-1]
    block = turned_refs[0].shape[0]

    def put(value, rows):
        if len(refs) == 2:
            value = value + refs[0][rows, :].astype(F32)
        out_ref[rows, :] = value.astype(BF16)

    grads = [jnp.concatenate([ref[...] for ref in items], axis=1) for items in (query_refs, kv_refs)]
    grads = jnp.concatenate(grads, axis=0)
    turned = jnp.concatenate([ref[...] for ref in turned_refs], axis=1)
    put(right_trans(turned, grads), slice(0, block))
    ones = jnp.ones((16, turned.shape[1]), BF16)
    put(right_trans(ones, grads), slice(block, block + 16))


def head_slab(meta, turned, query, kv, count, slabs, got=None, first=0):
    width, rows = turned[0].shape
    block = width // count
    columns = query[0].shape[0] + kv[0].shape[0]
    return pl.pallas_call(
        head_kernel,
        grid_spec=pltpu.PrefetchScalarGridSpec(
            num_scalar_prefetch=1,
            grid=(slabs,),
            in_specs=[pl.BlockSpec((block, rows), lambda i, m: (m[i] * 2 + m[slabs], 0))] * 2
            + [pl.BlockSpec(item.shape, lambda i, m: (0, 0)) for item in [*query, *kv]]
            + (
                []
                if got is None
                else [pl.BlockSpec((block + 16, columns), lambda i, m: (first + i, 0))]
            ),
            out_specs=pl.BlockSpec((block + 16, columns), lambda i, m: (i, 0)),
        ),
        out_shape=jax.ShapeDtypeStruct((slabs * (block + 16), columns), BF16),
        compiler_params=pltpu.CompilerParams(vmem_limit_bytes=24 << 20),
        cost_estimate=work(2),
        name="head_slab",
    )(meta, *turned, *query, *kv, *(() if got is None else (got,)))


def token_kernel(meta_ref, resid_ref, *refs, shared):
    query_refs, kv_refs, refs = refs[:ZS], refs[ZS : 2 * ZS], refs[2 * ZS :]
    weight_refs, refs = refs[: 5 if shared else 3], refs[5 if shared else 3 :]
    out_ref, full_ref, turned_ref, sems = refs
    w_at, c_at, z_at = meta_ref[1], meta_ref[2], meta_ref[3]
    width = full_ref.shape[1]
    moves = []
    if shared:
        count = weight_refs[0].shape[0]
        half = count // 2
        for kind in range(3):
            start = pl.multiple_of(w_at * count, count)
            moves.append((weight_refs[kind], full_ref.at[kind, pl.ds(start, count), :]))
            for ref, core in ((weight_refs[3], c_at), (weight_refs[4], 1 - c_at)):
                start = pl.multiple_of(((1 - w_at) * 2 + core) * half, half)
                moves.append(
                    (
                        ref.at[pl.ds(kind * half, half), :],
                        full_ref.at[kind, pl.ds(start, half), :],
                    )
                )
    else:
        for kind in range(3):
            moves.append((weight_refs[kind], full_ref.at[kind]))
    copies = []
    for at, (source, target) in enumerate(moves):
        copies.append(pltpu.make_async_copy(source, target, sems.at[at]))
        copies[-1].start()
    part = width // ZS
    head_dim = width // HEADS
    for at in range(ZS):
        low = (z_at ^ at) * part
        turned_ref[0, pl.ds(pl.multiple_of(low, part), part), :] = query_refs[at][...]
        for head in range(part // head_dim):
            start = pl.ds(pl.multiple_of(low + head * head_dim, head_dim), head_dim)
            for kind in (1, 2):
                row = (2 * head + kind - 1) * head_dim
                turned_ref[kind, start, :] = kv_refs[at][row : row + head_dim, :]
    parts = [turned_ref[kind].T for kind in range(3)]
    for copy in copies:
        copy.wait()
    out = resid_ref[...]
    for kind in range(3):
        out = out + right_trans(parts[kind], full_ref[kind])
    out_ref[...] = out


def token_gradient(meta, resid, query, kv, weights):
    rows, width = resid.shape
    in_vmem = pl.BlockSpec(memory_space=pltpu.VMEM)
    in_place = pl.BlockSpec(memory_space=pl.ANY)
    return pl.pallas_call(
        partial(token_kernel, shared=len(weights) == 5),
        grid_spec=pltpu.PrefetchScalarGridSpec(
            num_scalar_prefetch=1,
            grid=(),
            in_specs=[in_vmem] * (1 + 2 * ZS) + [in_place] * len(weights),
            out_specs=in_vmem,
            scratch_shapes=[
                pltpu.VMEM((3, width, width), BF16),
                pltpu.VMEM((3, width, rows), BF16),
                pltpu.SemaphoreType.DMA((9,)),
            ],
        ),
        out_shape=jax.ShapeDtypeStruct((rows, width), F32),
        compiler_params=pltpu.CompilerParams(vmem_limit_bytes=32 << 20),
        cost_estimate=work(4),
        name="token_gradient",
    )(meta, resid, *query, *kv, *weights)


def down_finish_kernel(meta_ref, *refs):
    block = refs[0].shape[0] // 4
    c_at, x_at = meta_ref[0], meta_ref[1]
    for at in range(4):
        for z in range(4):
            place = (c_at ^ (at >> 1)) * 8 + z * 2 + (x_at ^ (at & 1))
            start = pl.multiple_of(place * block, 8)
            refs[4][pl.ds(start, block), :] = refs[at][z * block : (z + 1) * block, :].astype(F32)


def down_finish(meta, pieces):
    block, width = pieces[0].shape
    in_vmem = pl.BlockSpec(memory_space=pltpu.VMEM)
    return pl.pallas_call(
        down_finish_kernel,
        grid_spec=pltpu.PrefetchScalarGridSpec(
            num_scalar_prefetch=1, grid=(), in_specs=[in_vmem] * 4, out_specs=in_vmem
        ),
        out_shape=jax.ShapeDtypeStruct((4 * block, width), F32),
        compiler_params=pltpu.CompilerParams(vmem_limit_bytes=32 << 20),
        cost_estimate=work(4),
        name="down_finish",
    )(meta, *pieces)


def up_finish_kernel(meta_ref, *refs):
    pieces = refs[:4]
    up_ref, out_ref, small_ref = refs[4:]
    block = pieces[0].shape[0]
    quarter = up_ref.shape[1] // 4
    side = out_ref.shape[1] // 2
    c_at, x_at = meta_ref[0], meta_ref[1]
    for at in range(4):
        start = pl.multiple_of((x_at ^ (at & 1)) * block, 8)
        rows = pl.ds(start, block)
        core = c_at ^ (at >> 1)
        for half in range(2):
            lanes = pl.ds(pl.multiple_of((2 * half + core) * quarter, 128), quarter)
            up_ref[rows, lanes] = pieces[at][:, half * quarter : (half + 1) * quarter].astype(F32)
        out_ref[rows, pl.ds(pl.multiple_of(core * side, 128), side)] = (
            pieces[at][:, 2 * quarter : 2 * quarter + side].astype(F32)
        )
        if at < 2:
            small_ref[rows, :] = pieces[at][:, 2 * quarter + side :].astype(F32)


def up_finish(meta, pieces, hidden, width):
    block = pieces[0].shape[0]
    in_vmem = pl.BlockSpec(memory_space=pltpu.VMEM)
    shapes = [(2 * block, hidden), (2 * block, width), (2 * block, 128)]
    return pl.pallas_call(
        up_finish_kernel,
        grid_spec=pltpu.PrefetchScalarGridSpec(
            num_scalar_prefetch=1,
            grid=(),
            in_specs=[in_vmem] * 4,
            out_specs=[in_vmem] * 3,
        ),
        out_shape=[jax.ShapeDtypeStruct(shape, F32) for shape in shapes],
        compiler_params=pltpu.CompilerParams(vmem_limit_bytes=40 << 20),
        cost_estimate=work(5),
        name="up_finish",
    )(meta, *pieces)


def head_finish_kernel(meta_ref, own_ref, got_ref, query_ref, key_ref, value_ref, bias_ref, *, part):
    size = own_ref.shape[0] // ZS
    block = size - 16
    head_dim = part // 3
    for at, source in enumerate((own_ref, got_ref)):
        start = pl.multiple_of((meta_ref[0] ^ at) * block, 8)
        rows = pl.ds(start, block)
        keys, values, queries = [], [], []
        for z in range(ZS):
            item = source[((z & 1) * 2 + (z >> 1)) * size :][:size].astype(F32)
            for head in range(3):
                low = part + head * 2 * head_dim
                keys.append(item[:, low : low + head_dim])
                values.append(item[:, low + head_dim : low + 2 * head_dim])
            queries.append(item[:, :part])
        key = jnp.concatenate(keys, axis=1)
        value = jnp.concatenate(values, axis=1)
        query = jnp.concatenate(queries, axis=1)
        query_ref[rows, :] = query[:block]
        key_ref[rows, :] = key[:block]
        value_ref[rows, :] = value[:block]
        if at == 0:
            bias_ref[0:8, :] = query[block : block + 8]
            bias_ref[8:16, :] = value[block : block + 8]


def head_finish(meta, own, got):
    rows, columns = own.shape
    rows = 2 * (rows // ZS - 16)
    width = ZS * columns // 3
    return small_call(
        partial(head_finish_kernel, part=columns // 3),
        meta,
        (own, got),
        [((rows, width), F32)] * 3 + [((16, width), F32)],
        limit=40,
        name="head_finish",
    )


def in_order(index, own, other, axis):
    return jnp.where(
        index == 0,
        jnp.concatenate([own, other], axis=axis),
        jnp.concatenate([other, own], axis=axis),
    )


def part_of(value, index, count, axis):
    size = value.shape[axis] // count
    return lax.dynamic_slice_in_dim(value, index * size, size, axis)


def body(
    inputs,
    lengths,
    cotangent,
    query_weight,
    query_bias,
    key_weight,
    value_weight,
    value_bias,
    output_weight,
    output_bias,
    first_gain,
    first_shift,
    up_weight,
    up_bias,
    down_weight,
    down_bias,
    second_gain,
    second_shift,
    *,
    sizes,
):
    count_o, count_w = sizes
    w_at = lax.axis_index("w")
    z_at = lax.axis_index("z")
    c_at = lax.axis_index("c")
    x_at = lax.axis_index("x")
    o_at = lax.axis_index("o")
    tokens = inputs[0]
    local_rows, width = tokens.shape
    head_dim = width // HEADS
    heads = HEADS // ZS
    part = heads * head_dim
    length = lengths[0]

    hold = lax.optimization_barrier

    near = ((0, 1), (1, 0), (2, 3), (3, 2))
    far = ((0, 2), (2, 0), (1, 3), (3, 1))
    cross = ((0, 3), (3, 0), (1, 2), (2, 1))

    def exchange(pieces):
        return [pieces[0]] + [
            lax.ppermute(item, "z", perm) for item, perm in zip(pieces[1:], (near, far, cross))
        ]

    own_rows = query_weight.shape[0]
    big_weights = (output_weight, up_weight, down_weight)
    sides = jnp.stack([z_at, c_at]).astype(jnp.int32)
    low_tokens, attn_own, *low_heads, head_pack = prepare(
        sides, tokens, (query_weight, key_weight, value_weight)
    )
    line_tokens = [low_tokens, lax.ppermute(low_tokens, "z", near)]
    line_tokens.append(lax.ppermute(low_tokens, "z", far))
    small = jnp.stack(
        [
            item.reshape(-1, own_rows)[row]
            for item in (
                query_bias,
                value_bias,
                output_bias,
                first_gain,
                first_shift,
                down_bias,
                second_gain,
                second_shift,
                up_bias,
            )
            for row in range(item.shape[0] // own_rows)
        ]
    ).astype(BF16)
    if count_w == 2:
        attn_got, small_got = swap(attn_own, "w"), swap(small, "w")
        *low_weights, weight_pack = round_weights(sides, big_weights)
        attn_got, small_got, weight_pack, *line_tokens[1:3] = hold(
            (attn_got, small_got, weight_pack, *line_tokens[1:3])
        )
        weight_got = swap(weight_pack, "w")
        sources = (attn_own, attn_got, small, small_got)
    else:
        attn_full = lax.all_gather(attn_own, "w", axis=0, tiled=True)
        small_all = lax.all_gather(small, "w", axis=0, tiled=False)
        low_weights = [item.astype(BF16) for item in big_weights]
        weight_got = [lax.all_gather(item, "w", axis=0, tiled=True) for item in low_weights]
        head_weights = [lax.all_gather(item, "w", axis=0, tiled=True) for item in low_heads]
        pair = jnp.transpose(small_all[:, :2], (1, 0, 2)).reshape(2, width).astype(F32)
        own_bias = lax.dynamic_slice_in_dim(pair, z_at * part, part, 1)
        value_bias_own = own_bias[1].reshape(heads, 1, head_dim)
        kv_bias = jnp.concatenate([jnp.zeros_like(value_bias_own), value_bias_own], axis=1)
        bias_row = jnp.concatenate([kv_bias.reshape(1, 2 * part), own_bias[:1]], axis=1)
        sources = (attn_full, bias_row)

    line_tokens.append(lax.ppermute(line_tokens[2], "z", near))
    corner = jnp.stack([w_at, z_at]).astype(jnp.int32)
    made = [project(corner, *line_tokens[:2], sources)]
    made[0], *line_tokens[2:] = hold((made[0], *line_tokens[2:]))
    made.append(project(corner, *line_tokens[2:], sources))
    queries = [item[0] for item in made]
    turned = [item[2] for item in made]
    kv_blocks = [[item[1] for item in made]]
    for axis in ("x", "c", "o")[: 3 if count_o == 2 else 2]:
        kv_blocks = kv_blocks + [[swap(item, axis) for item in pair] for pair in kv_blocks]
    places = []
    for at in range(4 * count_o):
        o_of = o_at ^ (at >> 2)
        places.append(o_of * 16 + (x_at ^ (at & 1)) * 2 + (c_at ^ ((at >> 1) & 1)))
    meta = jnp.stack([length, z_at] + places).astype(jnp.int32)
    kv_blocks = [
        [pltpu.with_memory_space_constraint(item, pltpu.MemorySpace.HBM) for item in pair]
        for pair in kv_blocks
    ]
    attended, *made = attend_forward(meta, queries, kv_blocks, heads)
    logs = made[ZS]
    if count_w == 2:
        attended, weight_got, head_pack, small_own, small_got = hold(
            (attended, weight_got, head_pack, small, small_got)
        )
        small_all = in_order(w_at, small_own[None], small_got[None], 0)
        weights = [*low_weights, weight_got, swap(weight_got, "c")]
        head_got = swap(head_pack, "w")
    else:
        weights = weight_got
    mixed = exchange(made[:ZS])
    small_all = small_all.astype(F32)
    vec = jnp.transpose(small_all[:, :8], (1, 0, 2)).reshape(8, width)
    up_offset = small_all[:, 8:].reshape(1, -1)

    split = count_w == 2 and count_o == 1
    my_index = o_at * 16 + z_at * 4 + x_at * 2 + c_at
    rest = jnp.clip(length - my_index * local_rows, 0, local_rows)
    core = c_at if split else jnp.zeros_like(c_at)
    spots = jnp.stack([rest, w_at, core, z_at]).astype(jnp.int32)
    outputs, resid_grad, *made = middle(
        spots, [mixed], ((0, heads),), tokens, cotangent[0], vec, up_offset, weights
    )
    head_grads = exchange(made[:ZS])
    send, keep, small_own = made[ZS:]
    hidden = up_offset.shape[1]

    near_bit, far_bit = z_at & 1, z_at >> 1

    def add_pair(kept, got):
        return (kept.astype(F32) + got.astype(F32)).astype(BF16)

    def join(value, got, bit):
        return in_order(bit, value, got, 0)

    spot = jnp.stack([c_at, x_at]).astype(jnp.int32)
    token = [spot]

    def arrive(*values):
        token[0], *values = hold((token[0], *values))
        return values[0] if len(values) == 1 else values

    def backward(first, count, made=()):
        return attend_backward(
            meta, queries, head_grads, attended, logs, kv_blocks, first, count, made
        )

    def to_near(value):
        return lax.ppermute(value, "z", near)

    def to_far(value):
        return lax.ppermute(value, "z", far)

    def head_part(ws, core, got=None, first=0):
        at = jnp.stack([jnp.asarray(item) for item in (*ws, core)]).astype(jnp.int32)
        return head_slab(at, turned, query_low, kv_low, 2 * count_w, len(ws), got, first)

    def pick(w, c):
        return jnp.stack([jnp.asarray(w), jnp.asarray(c)]).astype(jnp.int32)

    if split:
        got, small_got = swap(send, "c"), swap(small_own, "c")
        down_far = down_slab(pick(1 - w_at, 0), keep, send, got)
        up_sent, up_kept = up_slabs(
            jnp.stack([x_at]).astype(jnp.int32), keep, send, got, small_own, small_got
        )
        down_near = down_slab(pick(1 * w_at, 0), keep, send, got)
        down_far, up_sent, down_near, *head_grads = hold(
            (down_far, up_sent, down_near, *head_grads)
        )
        made = backward(0, heads - 1)
        down_got, *made = arrive(swap(down_far, "w"), *made)
        down_sum = add_pair(down_near, down_got)
        down_got = to_near(part_of(down_sum, 1 - near_bit, 2, 0))
        down_sum, *head_grads = arrive(down_sum, *head_grads)
        made = backward(heads - 1, 1, made)
        down_got, up_got, head_got, *made = arrive(
            down_got, swap(up_sent, "x"), head_got, *made
        )
        query_low, pairs = made[:ZS], made[ZS:]
        head_weights = [*low_heads, head_got, swap(head_got, "c")]
        pair_got = swap(pairs[1], "c")
        query_got = exchange(query_low)
        down_sum = add_pair(part_of(down_sum, near_bit, 2, 0), down_got)
        down_got = to_far(part_of(down_sum, 1 - far_bit, 2, 0))
        up_sum = add_pair(up_kept, up_got).reshape(2, own_rows // 2, -1)
        up_got = swap(lax.dynamic_index_in_dim(up_sum, 1 - w_at, 0, keepdims=False), "w")
        pair_got = arrive(pair_got)
        half_rows = pair_got.shape[0] // 2
        pair_sent = add_pair(pairs[0][half_rows:], pair_got[half_rows:])
        pair_sent = arrive(pair_sent)
        key_got = swap(pair_sent, "x")
        down_got = arrive(down_got)
        down_sum = add_pair(part_of(down_sum, far_bit, 2, 0), down_got)
        down_got = swap(part_of(down_sum, 1 - x_at, 2, 0), "x")
        up_got = arrive(up_got)
        up_sum = add_pair(lax.dynamic_index_in_dim(up_sum, w_at, 0, keepdims=False), up_got)
        up_got = to_near(part_of(up_sum, 1 - near_bit, 2, 0))
        key_got, *query_got = arrive(key_got, *query_got)
        kv_low = key_sum(pairs[0], pair_got, key_got)
        head_far = swap(head_part((1 - w_at,), 1 - c_at), "c")
        kv_got = exchange(kv_low)
        head_near = swap(head_part((1 * w_at,), 1 - c_at), "c")
        down_got = arrive(down_got)
        down_sum = add_pair(part_of(down_sum, x_at, 2, 0), down_got)
        down_got = to_far(down_sum)
        head_far = arrive(head_far)
        head_sent = swap(head_part((1 - w_at,), c_at, head_far), "w")
        head_near = arrive(head_near)
        head_sum = head_part((1 * w_at,), c_at, head_near)
        up_got = arrive(up_got)
        up_sum = add_pair(part_of(up_sum, near_bit, 2, 0), up_got)
        up_got = to_far(part_of(up_sum, 1 - far_bit, 2, 0))
        head_sent = arrive(head_sent)
        head_sum = add_pair(head_sum, head_sent)
        head_got = swap(head_sum, "x")
        kv_got = arrive(*kv_got)
        input_grad = token_gradient(
            spots, resid_grad, query_got, kv_got, head_weights
        )
        up_got = arrive(up_got)
        up_sum = add_pair(part_of(up_sum, far_bit, 2, 0), up_got)
        up_got = to_far(up_sum)
        down_got = arrive(down_got)
        down_sum = join(down_sum[None], down_got[None], far_bit)
        down_got = to_near(down_sum)
        head_got = arrive(head_got)
        head_sum = add_pair(head_sum, head_got)
        head_got = to_far(head_sum)
        up_got = arrive(up_got)
        up_sum = join(up_sum, up_got, far_bit)
        up_got = to_near(up_sum)
        down_got = arrive(down_got)
        down_sum = join(down_sum[None], down_got[None], near_bit)
        down_sum = down_sum.reshape(-1, width)
        down_x = swap(down_sum, "x")
        down_c = swap(down_sum, "c")
        head_got = arrive(head_got)
        head_two = join(head_sum, head_got, far_bit)
        head_got = to_near(head_two)
        up_got = arrive(up_got)
        up_sum = join(up_sum, up_got, near_bit)
        up_x = swap(up_sum, "x")
        up_c = swap(up_sum, "c")
        down_x, input_grad = arrive(down_x, input_grad)
        down_pieces = [down_sum, down_x, down_c, swap(down_x, "c")]
        head_got = arrive(head_got)
        head_four = join(head_two, head_got, near_bit)
        head_other = swap(head_four, "c")
        total_down = down_finish(spot, down_pieces)
        up_x, total_down = arrive(up_x, total_down)
        up_pieces = [up_sum, up_x, up_c, swap(up_x, "c")]
        total_query, total_key, total_value, head_bias = head_finish(
            spot, head_four, head_other
        )
        total_query, total_key, total_value = arrive(total_query, total_key, total_value)
        total_up, total_out, table = up_finish(token[0], up_pieces, hidden, width)
        groups = own_rows // 128
        small_total = table[: 8 * groups].reshape(groups, 8, 128)
        vectors = [small_total[:, at].reshape(own_rows) for at in range(6)]
        lines = hidden // count_w // 128
        total_up_bias = table[8 * groups : 8 * groups + lines].reshape(-1)
    else:
        made = backward(0, heads)
        query_low, pairs = made[:ZS], made[ZS:]
        if count_o == 2:
            pairs = [plus(spot, pairs[at], swap(pairs[at + 2], "o")) for at in range(2)]
        pair_got = swap(pairs[1], "c")
        half_rows = pair_got.shape[0] // 2
        key_got = swap(plus(spot, pairs[0], pair_got, half_rows), "x")
        kv_low = key_sum(pairs[0], pair_got, key_got)
        if count_w == 2:
            head_weights = [*low_heads, head_got, swap(head_got, "c")]
        input_grad = token_gradient(
            spots.at[2].set(c_at.astype(jnp.int32)),
            resid_grad,
            exchange(query_low),
            exchange(kv_low),
            head_weights,
        )
        every_w = tuple(range(count_w))
        slabs = head_part(every_w, c_at, swap(head_part(every_w, 1 - c_at), "c"))
        head_sum = lax.psum_scatter(slabs, "w", scatter_dimension=0, tiled=True)
        head_sum = plus(spot, head_sum, swap(head_sum, "x"))
        if count_o == 2:
            head_sum = plus(spot, head_sum, swap(head_sum, "o"))
        n_bit, f_bit = [
            jnp.stack([bit, bit]).astype(jnp.int32) for bit in (near_bit, far_bit)
        ]
        head_sum = unite(f_bit, head_sum, to_far(head_sum))
        head_sum = unite(n_bit, head_sum, to_near(head_sum))
        total_query, total_key, total_value, head_bias = head_finish(
            spot, head_sum, swap(head_sum, "c")
        )
        quarter = hidden // 4
        count = quarter // 256
        act_at = 5 * quarter
        act = [keep[:quarter], send[act_at : act_at + quarter], keep[quarter : 2 * quarter]]
        act += [send[act_at + quarter : act_at + 2 * quarter]]
        act = jnp.concatenate(act, axis=0)

        def rows_of(value, low, at):
            return value[low + at * local_rows : low + (at + 1) * local_rows]

        ffn_at = act_at + 2 * quarter
        ffn = jnp.concatenate([rows_of(send, ffn_at, at) for at in range(width // 256)], axis=1)
        pre = []
        for half in range(2):
            pre += [rows_of(keep, 2 * quarter, half * count + at) for at in range(count)]
            pre += [rows_of(send, 0, half * count + at) for at in range(count)]
        pre = jnp.concatenate(pre, axis=1)
        normed_turned = send[2 * quarter : 2 * quarter + width]
        mixed_turned = send[2 * quarter + width : 2 * quarter + 2 * width]
        side = width // 2
        branch = jnp.concatenate(
            [
                rows_of(keep, 4 * quarter, 0),
                rows_of(keep, 4 * quarter, 1)[:, : side - 256],
                rows_of(send, 2 * quarter + 2 * width, 0),
                rows_of(send, 2 * quarter + 2 * width, 1)[:, : side - 256],
            ],
            axis=1,
        )

        def sum_all(value):
            value = value.astype(BF16)
            value = lax.psum_scatter(value, "w", scatter_dimension=0, tiled=True)
            return lax.psum(value, ("o", "z", "x", "c")).astype(F32)

        total_down = sum_all(matmul(act, ffn))
        total_up = sum_all(matmul(normed_turned, pre))
        total_out = sum_all(matmul(mixed_turned, branch))
        small_own = lax.psum(small_own, ("o", "z", "x", "c", "w"))
        vectors = [part_of(small_own[at], w_at, count_w, 0) for at in range(6)]
        total_up_bias = part_of(small_own[8:12].reshape(-1), w_at, count_w, 0)

    totals = [part_of(head_bias[at], w_at, count_w, 0) for at in (0, 8)] + vectors
    return (
        outputs[None],
        input_grad[None],
        total_query,
        totals[0],
        total_key,
        total_value,
        totals[1],
        total_out,
        totals[2],
        totals[3],
        totals[4],
        total_up,
        total_up_bias,
        total_down,
        totals[5],
        totals[6],
        totals[7],
    )


def solution(mesh):
    count_s = mesh.shape["seq"]
    count_w = mesh.shape["wshard"]
    count_o = count_s // 16
    fine = Mesh(
        mesh.devices.reshape(count_o, ZS, 2, 2, count_w), ("o", "z", "x", "c", "w")
    )
    seq = ("o", "z", "x", "c")
    rows = P("w", seq, None)
    matrix = P("w", None)
    vector = P("w")
    placed = (
        rows,
        vector,
        rows,
        matrix,
        vector,
        matrix,
        matrix,
        vector,
        matrix,
        vector,
        vector,
        vector,
        matrix,
        vector,
        matrix,
        vector,
        vector,
        vector,
    )
    return jax.shard_map(
        partial(body, sizes=(count_o, count_w)),
        mesh=fine,
        in_specs=placed,
        out_specs=(
            rows,
            rows,
            matrix,
            vector,
            matrix,
            matrix,
            vector,
            matrix,
            vector,
            vector,
            vector,
            matrix,
            vector,
            matrix,
            vector,
            vector,
            vector,
        ),
        check_vma=False,
    )
```

```python
from functools import partial

import jax
import jax.numpy as jnp
from jax import lax
from jax.experimental import pallas as pl
from jax.experimental.pallas import tpu as pltpu
from jax.sharding import Mesh, PartitionSpec as P

HEADS = 12
ZS = 4
NEG_FILL = -1e30
VMEM_LIMIT = 60 << 20
SWAP = ((0, 1), (1, 0))
F32 = jnp.float32
BF16 = jnp.bfloat16


def matmul(left_side, right_side):
    return jnp.dot(left_side, right_side, preferred_element_type=F32)


def right_trans(left_side, right_side):
    return lax.dot_general(
        left_side, right_side, (((1,), (1,)), ((), ())), preferred_element_type=F32
    )


def work(units):
    return pl.CostEstimate(flops=int(units * 1e3), bytes_accessed=1, transcendentals=0)


def swap(value, axis):
    return lax.ppermute(value, axis, SWAP)


def touched_groups(length, rows, outer):
    group = 4 * rows
    left = length - outer * (ZS * group)
    return jnp.clip((left + group - 1) // group, 0, ZS)


def with_mask(kv, place, length):
    at = place + lax.broadcasted_iota(jnp.int32, kv.shape, 0)
    lane = lax.broadcasted_iota(jnp.int32, kv.shape, 1)
    fill = jnp.where(at < length, 0.0, jnp.where(lane == 0, NEG_FILL, 0.0))
    return jnp.concatenate([kv, fill.astype(BF16)], axis=1)


def load_head(kv_refs, rows_ref, turned_ref, low):
    head_dim = turned_ref.shape[1]
    for at, ref in enumerate(kv_refs):
        block, half = at // 2, at % 2
        size = ref.shape[0]
        for start in range(0, size, 256):
            value = ref[start : start + 256, :]
            place = slice(half * size + start, half * size + start + 256)
            rows_ref[block, place, :] = value
            turned_ref[block, :, place] = value.T[low : low + head_dim, :]


def forward_kernel(meta_ref, *refs, blocks, rows):
    query_refs, kv_refs = refs[:2], refs[2 : 2 + 2 * blocks]
    out_ref, *refs = refs[2 + 2 * blocks :]
    piece_refs, (log_ref, rows_ref, turned_ref) = refs[:ZS], refs[ZS:]
    head_dim, query_count = out_ref.shape
    length, z_at = meta_ref[0], meta_ref[1]
    load_head(kv_refs, rows_ref, turned_ref, head_dim)
    query = jnp.concatenate([ref[...] for ref in query_refs], axis=1)
    query = jnp.concatenate(
        [
            query,
            jnp.zeros((head_dim, query_count), BF16),
            jnp.ones((128, query_count), BF16),
        ],
        axis=0,
    )

    def step(group, carry, members):
        top, total, acc = carry
        start = pl.multiple_of((group ^ z_at) * rows, rows)
        found = []
        for block in members:
            place = (meta_ref[2 + block] + group * 4) * rows
            kv = with_mask(rows_ref[block, pl.ds(start, rows), :], place, length)
            found.append(matmul(kv, query))
        new_top = top
        for scores in found:
            new_top = jnp.maximum(new_top, jnp.max(scores, axis=0, keepdims=True))
        fade = jnp.exp(top - new_top)
        total = total * fade
        acc = acc * fade
        for block, scores in zip(members, found):
            weights = jnp.exp(scores - new_top)
            total = total + jnp.sum(weights, axis=0, keepdims=True)
            acc = acc + matmul(
                turned_ref[block, :, pl.ds(start, rows)], weights.astype(BF16)
            )
        return new_top, total, acc

    carry = (
        jnp.full((1, query_count), NEG_FILL, F32),
        jnp.zeros((1, query_count), F32),
        jnp.zeros((head_dim, query_count), F32),
    )
    for first in range(0, blocks, 4):
        members = tuple(range(first, first + 4))
        count = touched_groups(length, rows, meta_ref[2 + first] // 16)
        carry = lax.fori_loop(0, count, lambda g, c: step(g, c, members), carry)
    top, total, acc = carry
    out = acc * (1.0 / total)
    out_ref[...] = out
    size = query_count // ZS
    for at in range(ZS):
        piece_refs[at][...] = out[:, at * size : (at + 1) * size].astype(BF16)
    log_ref[0] = top + jnp.log(total)


def attend_forward(meta, queries, kv_blocks, heads):
    blocks = len(kv_blocks)
    half_rows = kv_blocks[0][0].shape[0]
    part, half_count = queries[0].shape
    head_dim, query_count = part // heads, 2 * half_count
    size = query_count // ZS
    return pl.pallas_call(
        partial(forward_kernel, blocks=blocks, rows=2 * half_rows // ZS),
        grid_spec=pltpu.PrefetchScalarGridSpec(
            num_scalar_prefetch=1,
            grid=(heads,),
            in_specs=[pl.BlockSpec((head_dim, half_count), lambda i, m: (i, 0))] * 2
            + [pl.BlockSpec((half_rows, 128), lambda i, m: (0, i))] * (2 * blocks),
            out_specs=[pl.BlockSpec((head_dim, query_count), lambda i, m: (i, 0))]
            + [pl.BlockSpec((head_dim, size), lambda i, m: (i, 0))] * ZS
            + [pl.BlockSpec((1, 1, query_count), lambda i, m: (i, 0, 0))],
            scratch_shapes=[
                pltpu.VMEM((blocks, 2 * half_rows, 128), BF16),
                pltpu.VMEM((blocks, head_dim, 2 * half_rows), BF16),
            ],
        ),
        out_shape=[jax.ShapeDtypeStruct((part, query_count), F32)]
        + [jax.ShapeDtypeStruct((part, size), BF16)] * ZS
        + [jax.ShapeDtypeStruct((heads, 1, query_count), F32)],
        compiler_params=pltpu.CompilerParams(vmem_limit_bytes=VMEM_LIMIT),
        cost_estimate=work(8 * heads),
        name="attend_forward",
    )(meta, *queries, *[item for pair in kv_blocks for item in pair])


def backward_kernel(meta_ref, *refs, blocks, rows, extra):
    query_refs, (out_ref, log_ref), refs = refs[:2], refs[2:4], refs[4:]
    grad_refs, kv_refs = refs[:ZS], refs[ZS : ZS + 2 * blocks]
    refs = refs[ZS + 2 * blocks + extra :]
    dq_refs, pairs = refs[:ZS], refs[ZS : ZS + blocks // 2]
    rows_ref, turned_ref, qn_ref, gn_ref, acc_ref = refs[ZS + blocks // 2 :]
    head_dim, query_count = out_ref.shape
    length, z_at = meta_ref[0], meta_ref[1]
    block_rows = ZS * rows
    load_head(kv_refs, rows_ref, turned_ref, 0)
    query = jnp.concatenate([ref[...] for ref in query_refs], axis=1)
    grads = jnp.concatenate([ref[...] for ref in grad_refs], axis=1)
    blank = jnp.zeros((head_dim, query_count), BF16)
    query = jnp.concatenate([query, blank], axis=0)
    grad = jnp.concatenate([blank, grads], axis=0)
    qn_ref[...] = query.T
    gn_ref[...] = grad.T
    query = jnp.concatenate([query, jnp.ones((128, query_count), BF16)], axis=0)
    delta = jnp.sum(grads.astype(F32) * out_ref[...], axis=0, keepdims=True)
    log_sum = log_ref[0]
    acc_ref[...] = jnp.zeros_like(acc_ref)

    def put(block, start, value):
        pairs[block // 2][pl.ds(start + (block & 1) * block_rows, rows), :] = value

    def step(group, members):
        start = pl.multiple_of((group ^ z_at) * rows, rows)
        for block in members:
            kv = rows_ref[block, pl.ds(start, rows), :]
            place = (meta_ref[2 + block] + group * 4) * rows
            scores = matmul(with_mask(kv, place, length), query)
            prob_grad = matmul(kv, grad)
            prob = jnp.exp(scores - log_sum)
            score_grad = (prob * (prob_grad - delta)).astype(BF16)
            value = matmul(prob.astype(BF16), gn_ref[...]) + matmul(score_grad, qn_ref[...])
            put(block, start, value.astype(BF16))
            acc_ref[...] += matmul(turned_ref[block, :, pl.ds(start, rows)], score_grad)

    def clear(group, members):
        start = pl.multiple_of((group ^ z_at) * rows, rows)
        for block in members:
            put(block, start, jnp.zeros((rows, 128), BF16))

    def loop(low, high, fn):
        def one(group, carry):
            fn(group)
            return carry

        lax.fori_loop(low, high, one, 0)

    for first in range(0, blocks, 4):
        members = tuple(range(first, first + 4))
        count = touched_groups(length, rows, meta_ref[2 + first] // 16)
        loop(0, count, lambda g: step(g, members))
        loop(count, ZS, lambda g: clear(g, members))
    dq = (acc_ref[...] * head_dim ** (-0.5)).astype(BF16)
    size = query_count // ZS
    for at in range(ZS):
        dq_refs[at][...] = dq[:, at * size : (at + 1) * size]


def attend_backward(meta, queries, grads, out, log_sum, kv_blocks, first, count, made=()):
    blocks = len(kv_blocks)
    half_rows, columns = kv_blocks[0][0].shape
    heads = columns // 128
    part, half_count = queries[0].shape
    head_dim, query_count = part // heads, 2 * half_count
    size = query_count // ZS
    piece = pl.BlockSpec((head_dim, size), lambda i, m: (i + first, 0))
    ins = [
        *queries,
        out,
        log_sum,
        *grads,
        *[item for pair in kv_blocks for item in pair],
        *made,
    ]
    return pl.pallas_call(
        partial(backward_kernel, blocks=blocks, rows=2 * half_rows // ZS, extra=len(made)),
        grid_spec=pltpu.PrefetchScalarGridSpec(
            num_scalar_prefetch=1,
            grid=(count,),
            in_specs=[pl.BlockSpec((head_dim, half_count), lambda i, m: (i + first, 0))] * 2
            + [
                pl.BlockSpec((head_dim, query_count), lambda i, m: (i + first, 0)),
                pl.BlockSpec((1, 1, query_count), lambda i, m: (i + first, 0, 0)),
            ]
            + [piece] * ZS
            + [pl.BlockSpec((half_rows, 128), lambda i, m: (0, i + first))] * (2 * blocks)
            + [pl.BlockSpec(memory_space=pl.ANY)] * len(made),
            out_specs=[piece] * ZS
            + [pl.BlockSpec((4 * half_rows, 128), lambda i, m: (0, i + first))] * (blocks // 2),
            scratch_shapes=[
                pltpu.VMEM((blocks, 2 * half_rows, 128), BF16),
                pltpu.VMEM((blocks, head_dim, 2 * half_rows), BF16),
                pltpu.VMEM((query_count, 128), BF16),
                pltpu.VMEM((query_count, 128), BF16),
                pltpu.VMEM((head_dim, query_count), F32),
            ],
        ),
        out_shape=[jax.ShapeDtypeStruct((part, size), BF16)] * ZS
        + [jax.ShapeDtypeStruct((4 * half_rows, columns), BF16)] * (blocks // 2),
        input_output_aliases={
            1 + len(ins) - len(made) + at: at for at in range(len(made))
        },
        compiler_params=pltpu.CompilerParams(vmem_limit_bytes=VMEM_LIMIT),
        cost_estimate=work(12 * count),
        name="attend_backward",
    )(meta, *ins)


IN_VMEM = pl.BlockSpec(memory_space=pltpu.VMEM)


def small_call(kernel, meta, values, shapes, scratch=(), limit=32, name=None):
    return pl.pallas_call(
        kernel,
        grid_spec=pltpu.PrefetchScalarGridSpec(
            num_scalar_prefetch=1,
            grid=(),
            in_specs=[IN_VMEM] * len(values),
            out_specs=[IN_VMEM] * len(shapes),
            scratch_shapes=list(scratch),
        ),
        out_shape=[jax.ShapeDtypeStruct(shape, kind) for shape, kind in shapes],
        compiler_params=pltpu.CompilerParams(vmem_limit_bytes=limit << 20),
        cost_estimate=work(1),
        name=name,
    )(meta, *values)


def fold_kernel(meta_ref, kept_ref, got_ref, keep_ref, sent_ref, sum_ref):
    sum_ref[...] = (kept_ref[...].astype(F32) + got_ref[...].astype(F32)).astype(BF16)
    rows = keep_ref.shape[0]
    for at, ref in enumerate((keep_ref, sent_ref)):
        start = pl.multiple_of((meta_ref[0] ^ at) * rows, 16)
        ref[...] = sum_ref[pl.ds(start, rows), :]


def fold(bit, kept, got):
    rows, columns = kept.shape
    half = ((rows // 2, columns), BF16)
    return small_call(
        fold_kernel,
        bit,
        (kept, got),
        [half, half],
        [pltpu.VMEM((rows, columns), BF16)],
        name="fold",
    )


def unite_kernel(meta_ref, own_ref, got_ref, out_ref):
    rows = own_ref.shape[0]
    for at, ref in enumerate((own_ref, got_ref)):
        start = pl.multiple_of((meta_ref[0] ^ at) * rows, 16)
        out_ref[pl.ds(start, rows), :] = ref[...]


def unite(bit, own, got):
    rows, columns = own.shape
    return small_call(
        unite_kernel, bit, (own, got), [((2 * rows, columns), BF16)], name="unite"
    )[0]


def plus_kernel(meta_ref, one_ref, two_ref, out_ref, *, low):
    cut = slice(low, low + out_ref.shape[0])
    out_ref[...] = (one_ref[cut, :].astype(F32) + two_ref[cut, :].astype(F32)).astype(BF16)


def plus(meta, one, two, low=0):
    rows, columns = one.shape
    return small_call(
        partial(plus_kernel, low=low),
        meta,
        (one, two),
        [((rows - low, columns), BF16)],
        name="plus",
    )[0]


def prepare_kernel(meta_ref, *refs):
    sources, refs = refs[:4], refs[4:]
    low_ref, pack_ref, low_refs, head_ref = refs[0], refs[1], refs[2:5], refs[5]
    places, sems = refs[6:10], refs[10]
    copies = []
    for at in range(4):
        copies.append(pltpu.make_async_copy(sources[at], places[at], sems.at[at]))
        copies[-1].start()
    z_at, c_at = meta_ref[0], meta_ref[1]
    width = places[0].shape[1]
    part = width // ZS
    head_dim = width // HEADS
    copies[0].wait()
    low_ref[...] = places[0][...].astype(BF16)
    parts = []
    for kind in range(3):
        ref = places[kind + 1]
        copies[kind + 1].wait()
        value = ref[...]
        low_refs[kind][...] = value.astype(BF16)
        half = ref.shape[0] // 2
        rows = ref[pl.ds(pl.multiple_of(c_at * half, half), half), :]
        head_ref[kind * half : (kind + 1) * half, :] = rows.astype(BF16)
        turn = lax.rem(width - z_at * part, width)
        parts.append(pltpu.roll(value, turn, 1)[:, :part])
    columns = []
    for head in range(part // head_dim):
        cut = slice(head * head_dim, (head + 1) * head_dim)
        columns += [parts[1][:, cut], parts[2][:, cut]]
    pack_ref[...] = jnp.concatenate(columns + [parts[0]], axis=1).astype(BF16)


def prepare(meta, tokens, weights):
    rows, width = tokens.shape
    count = weights[0].shape[0]
    shapes = [(rows, width), (count, 3 * width // ZS)] + [(count, width)] * 3
    shapes.append((3 * count // 2, width))
    return pl.pallas_call(
        prepare_kernel,
        grid_spec=pltpu.PrefetchScalarGridSpec(
            num_scalar_prefetch=1,
            grid=(),
            in_specs=[pl.BlockSpec(memory_space=pltpu.MemorySpace.HBM)] * 4,
            out_specs=[IN_VMEM] * len(shapes),
            scratch_shapes=[pltpu.VMEM((rows, width), F32)]
            + [pltpu.VMEM((count, width), F32)] * 3
            + [pltpu.SemaphoreType.DMA((4,))],
        ),
        out_shape=[jax.ShapeDtypeStruct(shape, BF16) for shape in shapes],
        compiler_params=pltpu.CompilerParams(vmem_limit_bytes=VMEM_LIMIT),
        cost_estimate=work(1),
        name="prepare",
    )(meta, tokens, *weights)


def round_kernel(meta_ref, out_w, up_w, down_w, low_out, low_up, low_down, pack_ref):
    core = meta_ref[1]
    for source, target in ((out_w, low_out), (up_w, low_up), (down_w, low_down)):
        target[...] = source[...].astype(BF16)
    width = pack_ref.shape[1]
    low = 0
    half = out_w.shape[0] // 2
    rows = pl.ds(pl.multiple_of(core * half, half), half)
    pack_ref[low : low + half, :] = out_w[rows, :].astype(BF16)
    low += half
    count = up_w.shape[1] // 2
    for block in range(count // width):
        lanes = pl.ds(pl.multiple_of(core * count + block * width, 128), width)
        pack_ref[low : low + up_w.shape[0], :] = up_w[:, lanes].astype(BF16)
        low += up_w.shape[0]
    half = down_w.shape[0] // 2
    rows = pl.ds(pl.multiple_of(core * half, half), half)
    pack_ref[low : low + half, :] = down_w[rows, :].astype(BF16)


def round_weights(meta, weights):
    out_w, up_w, down_w = weights
    width = out_w.shape[1]
    total = out_w.shape[0] // 2 + up_w.shape[0] * (up_w.shape[1] // 2 // width)
    total += down_w.shape[0] // 2
    return small_call(
        round_kernel,
        meta,
        weights,
        [(item.shape, BF16) for item in weights] + [((total, width), BF16)],
        limit=60,
        name="round_weights",
    )


def project_kernel(meta_ref, first_ref, second_ref, *refs, shared):
    query_ref, kv_ref, turned_ref, token_ref, bias_ref = refs[-5:]
    part = query_ref.shape[0]
    rows, width = first_ref.shape
    split = 2 * part
    token_ref[:rows, :] = first_ref[...]
    token_ref[rows:, :] = second_ref[...]
    if shared:
        w_at, z_at = meta_ref[0], meta_ref[1]
        both = None
        bias_ref[...] = jnp.zeros_like(bias_ref)
        for at in range(2):
            count = refs[at].shape[0]
            cut = pl.ds(pl.multiple_of((w_at ^ at) * count, 128), count)
            term = matmul(token_ref[:, cut], refs[at][...])
            both = term if both is None else both + term
            bias_ref[0:2, cut] = refs[2 + at][0:2, :].astype(F32)
        turn = lax.rem(width - z_at * part, width)
        bias = pltpu.roll(bias_ref[...], turn, 1)[:, :part]
        head_dim = width // HEADS
        pieces = []
        for head in range(part // head_dim):
            pieces.append(jnp.zeros((1, head_dim), F32))
            pieces.append(bias[1:2, head * head_dim : (head + 1) * head_dim])
        both = both + jnp.concatenate(pieces + [bias[0:1, :]], axis=1)
    else:
        both = matmul(token_ref[...], refs[0][...]) + refs[1][...]
    kv_ref[...] = both[:, :split].astype(BF16)
    scale = (part * ZS // HEADS) ** (-0.5)
    query_ref[...] = (both[:, split:].astype(BF16) * jnp.array(scale, BF16)).T
    turned_ref[...] = token_ref[...].T


def project(meta, first, second, sources):
    rows, width = first.shape
    part = sources[0].shape[1] // 3
    return small_call(
        partial(project_kernel, shared=len(sources) == 4),
        meta,
        (first, second, *sources),
        [((part, 2 * rows), BF16), ((2 * rows, 2 * part), BF16), ((width, 2 * rows), BF16)],
        [pltpu.VMEM((2 * rows, width), BF16), pltpu.VMEM((8, width), F32)],
        limit=40,
        name="project",
    )


def middle_kernel(meta_ref, tokens_ref, seed_ref, vec_ref, upoff_ref, *refs, groups, shared):
    mixed_refs = [refs[at * ZS : (at + 1) * ZS] for at in range(len(groups))]
    refs = refs[ZS * len(groups) :]
    weight_refs = refs[: 5 if shared else 3]
    refs = refs[len(weight_refs) :]
    outputs_ref, resid_ref = refs[:2]
    mgrad_refs = refs[2 : 2 + ZS]
    (
        send_ref,
        keep_ref,
        small_ref,
        out_w,
        up_w,
        down_w,
        slope_ref,
        wide_ref,
        tall_ref,
        sems,
    ) = refs[2 + ZS :]
    w_at, core, z_at = meta_ref[1], meta_ref[2], meta_ref[3]
    moves = [[], [], []]
    if shared:
        outs, ups, downs, got, pair = weight_refs
        count_o, count_u, count_d = outs.shape[0], ups.shape[0], downs.shape[0]
        for kind, (source, target) in enumerate(((outs, out_w), (ups, up_w), (downs, down_w))):
            start = pl.multiple_of(w_at * source.shape[0], source.shape[0])
            moves[kind].append((source, target.at[pl.ds(start, source.shape[0]), :]))
        lanes = got.shape[1]
        for source, which in ((got, core), (pair, 1 - core)):
            half = count_o // 2
            start = pl.multiple_of(((1 - w_at) * 2 + which) * half, half)
            moves[0].append((source.at[pl.ds(0, half), :], out_w.at[pl.ds(start, half), :]))
            low = half
            start = pl.multiple_of((1 - w_at) * count_u, count_u)
            for block in range(up_w.shape[1] // 2 // lanes):
                lane = pl.multiple_of(which * (up_w.shape[1] // 2) + block * lanes, 128)
                moves[1].append(
                    (
                        source.at[pl.ds(low, count_u), :],
                        up_w.at[pl.ds(start, count_u), pl.ds(lane, lanes)],
                    )
                )
                low += count_u
            half = count_d // 2
            start = pl.multiple_of(((1 - w_at) * 2 + which) * half, half)
            moves[2].append((source.at[pl.ds(low, half), :], down_w.at[pl.ds(start, half), :]))
    else:
        for kind, pair in enumerate(zip(weight_refs, (out_w, up_w, down_w))):
            moves[kind].append(pair)
    copies = []
    at = 0
    for kind in range(3):
        made = []
        for source, target in moves[kind]:
            made.append(pltpu.make_async_copy(source, target, sems.at[at]))
            made[-1].start()
            at += 1
        copies.append(made)
    rows, width = tokens_ref.shape
    hidden = upoff_ref.shape[1]
    part = width // ZS
    head_dim = width // HEADS
    quarter = hidden // 4

    def mean(value):
        return jnp.mean(value, axis=-1, keepdims=True)

    def norm(value):
        centered = value - mean(value)
        scale = lax.rsqrt(mean(centered * centered) + 1e-12)
        return centered * scale, scale

    def norm_back(grad, normal, scale):
        return scale * (grad - mean(grad) - normal * mean(grad * normal))

    def column(value):
        return jnp.sum(value, axis=0, keepdims=True)

    normed_at = 2 * quarter
    mixed_at = normed_at + width
    branch_at = mixed_at + width
    act_at = 5 * quarter
    for (first, count), pieces in zip(groups, mixed_refs):
        size = count * head_dim
        for at in range(ZS):
            low = mixed_at + (z_at ^ at) * part + first * head_dim
            send_ref[pl.ds(pl.multiple_of(low, head_dim), size), :] = pieces[at][...]
    mixed = send_ref[mixed_at:branch_at, :].T
    for copy in copies[0]:
        copy.wait()
    first_n, first_r = norm(tokens_ref[...] + (matmul(mixed, out_w[...]) + vec_ref[2:3, :]))
    normed = first_n * vec_ref[3:4, :] + vec_ref[4:5, :]
    low = normed.astype(BF16)
    send_ref[normed_at:mixed_at, :] = low.T
    for copy in copies[1] + copies[2]:
        copy.wait()
    quarters = []
    for half in range(2):
        for kept in (False, True):
            at = half * 2 * quarter + (core if kept else 1 - core) * quarter
            quarters.append((half, kept, pl.multiple_of(at, quarter)))
    acc = None
    for at, (half, kept, start) in enumerate(quarters):
        cut = pl.ds(start, quarter)
        pre_act = matmul(low, up_w[:, cut]) + upoff_ref[:, cut]
        phi = 0.5 + 0.5 * lax.erf(pre_act * (0.5**0.5))
        act = (pre_act * phi).astype(BF16)
        slope_ref[:, at * quarter : (at + 1) * quarter] = phi + pre_act * (
            jnp.exp(-0.5 * pre_act * pre_act) * 0.3989422804014327
        )
        target, base = (keep_ref, 0) if kept else (send_ref, act_at)
        target[base + half * quarter : base + (half + 1) * quarter, :] = act.T
        term = matmul(act, down_w[cut, :])
        acc = term if acc is None else acc + term
    second_n, second_r = norm(normed + (acc + vec_ref[5:6, :]))
    outputs_ref[...] = second_n * vec_ref[6:7, :] + vec_ref[7:8, :]
    place = lax.broadcasted_iota(jnp.int32, (rows, 1), 0)
    seed = jnp.where(place < meta_ref[0], seed_ref[...], 0.0)
    sum_grad = norm_back(seed * vec_ref[6:7, :], second_n, second_r)
    ffn = sum_grad.astype(BF16)
    for at in range(width // 256):
        low_row = act_at + 2 * quarter + at * rows
        send_ref[low_row : low_row + rows, :] = ffn[:, at * 256 : (at + 1) * 256]
    small_ref[3:4, :] = column(ffn.astype(F32))
    small_ref[4:5, :] = column(seed * second_n)
    small_ref[5:6, :] = column(seed)
    acc = sum_grad
    for at, (half, kept, start) in enumerate(quarters):
        cut = pl.ds(start, quarter)
        pre = right_trans(ffn, down_w[cut, :]) * slope_ref[:, at * quarter : (at + 1) * quarter]
        pre = pre.astype(BF16)
        target, base = (keep_ref, 2 * quarter) if kept else (send_ref, 0)
        for block in range(quarter // 256):
            row = base + (half * (quarter // 256) + block) * rows
            target[row : row + rows, :] = pre[:, block * 256 : (block + 1) * 256]
        sums = column(pre.astype(F32))
        line = 8 + half * (2 * quarter // width) + (core if kept else 1 - core)
        small_ref[pl.ds(line, 1), :] = sums
        acc = acc + right_trans(pre, up_w[:, cut])
    small_ref[1:2, :] = column(acc * first_n)
    small_ref[2:3, :] = column(acc)
    resid = norm_back(acc * vec_ref[3:4, :], first_n, first_r)
    resid_ref[...] = resid
    branch = resid.astype(BF16)
    wide_ref[...] = branch
    side = width // 2
    for target, base, which in (
        (send_ref, branch_at, 1 - core),
        (keep_ref, 4 * quarter, core),
    ):
        values = wide_ref[:, pl.ds(pl.multiple_of(which * side, 128), side)]
        target[base : base + rows, :] = values[:, :256]
        target[base + rows : base + 2 * rows, : side - 256] = values[:, 256:]
        target[base + rows : base + 2 * rows, side - 256 :] = jnp.zeros(
            (rows, 512 - side), BF16
        )
    small_ref[0:1, :] = column(branch.astype(F32))
    small_ref[6:8, :] = jnp.zeros((2, width), F32)
    small_ref[12:16, :] = jnp.zeros((4, width), F32)
    gap = branch_at + 2 * rows
    send_ref[gap:act_at, :] = jnp.zeros((act_at - gap, 256), BF16)
    tall_ref[...] = right_trans(out_w[...], branch).astype(BF16)
    for at in range(ZS):
        start = pl.multiple_of((z_at ^ at) * part, part)
        mgrad_refs[at][...] = tall_ref[pl.ds(start, part), :]


def middle(meta, mixed, groups, tokens, seed, vec, upoff, weights):
    rows, width = tokens.shape
    hidden = upoff.shape[1]
    in_vmem = pl.BlockSpec(memory_space=pltpu.VMEM)
    in_place = pl.BlockSpec(memory_space=pl.ANY)
    flat = [item for group in mixed for item in group]
    part = jax.ShapeDtypeStruct((width // ZS, rows), BF16)
    return pl.pallas_call(
        partial(middle_kernel, groups=groups, shared=len(weights) == 5),
        grid_spec=pltpu.PrefetchScalarGridSpec(
            num_scalar_prefetch=1,
            grid=(),
            in_specs=[in_vmem] * (4 + len(flat)) + [in_place] * len(weights),
            out_specs=[in_vmem] * (5 + ZS),
            scratch_shapes=[
                pltpu.VMEM((width, width), BF16),
                pltpu.VMEM((width, hidden), BF16),
                pltpu.VMEM((hidden, width), BF16),
                pltpu.VMEM((rows, hidden), F32),
                pltpu.VMEM((rows, width), BF16),
                pltpu.VMEM((width, rows), BF16),
                pltpu.SemaphoreType.DMA((11,)),
            ],
        ),
        out_shape=[jax.ShapeDtypeStruct((rows, width), F32)] * 2
        + [part] * ZS
        + [
            jax.ShapeDtypeStruct((2 * hidden, 256), BF16),
            jax.ShapeDtypeStruct((hidden + 2 * rows, 256), BF16),
            jax.ShapeDtypeStruct((16, width), F32),
        ],
        compiler_params=pltpu.CompilerParams(vmem_limit_bytes=VMEM_LIMIT),
        cost_estimate=work(15),
        name="middle",
    )(meta, tokens, seed, vec, upoff, *flat, *weights)


def down_kernel(meta_ref, keep_ref, got_ref, own_ffn_ref, got_ffn_ref, out_ref):
    keep, got = keep_ref[...], got_ref[...]
    rows = keep.shape[1]
    for at in range(out_ref.shape[1] // 256):
        cut = slice(at * rows, (at + 1) * rows)
        value = matmul(keep, own_ffn_ref[cut, :]) + matmul(got, got_ffn_ref[cut, :])
        out_ref[:, at * 256 : (at + 1) * 256] = value.astype(BF16)


def down_slab(meta, keep, send, got):
    block = send.shape[0] // 8
    kept = pl.BlockSpec((block, send.shape[1]), lambda i, m: (m[0], 0))
    act = pl.BlockSpec((block, send.shape[1]), lambda i, m: (5 + m[0], 0))
    ffn = pl.BlockSpec((block, send.shape[1]), lambda i, m: (7, 0))
    return pl.pallas_call(
        down_kernel,
        grid_spec=pltpu.PrefetchScalarGridSpec(
            num_scalar_prefetch=1,
            grid=(1,),
            in_specs=[kept, act, ffn, ffn],
            out_specs=pl.BlockSpec((block, block), lambda i, m: (0, 0)),
        ),
        out_shape=jax.ShapeDtypeStruct((block, block), BF16),
        compiler_params=pltpu.CompilerParams(vmem_limit_bytes=24 << 20),
        cost_estimate=work(2),
        name="down_slab",
    )(meta, keep, got, send, got)


def up_kernel(meta_ref, keep_ref, send_ref, got_ref, own_small_ref, got_small_ref, *refs):
    out_refs, table_ref = refs[:2], refs[2]
    rows = send_ref.shape[1]
    width = own_small_ref.shape[1]
    block = width // 4
    side = width // 2
    normed_at = 2 * width
    branch_at = normed_at + 2 * width
    x_at = meta_ref[0]
    pre_keep = 2 * width
    for w in range(2):
        small = own_small_ref[...] + got_small_ref[...]
        table_ref[...] = jnp.zeros_like(table_ref)
        for at in range(side // 128):
            low = w * side + at * 128
            table_ref[at * 8 : (at + 1) * 8, :] = small[:8, low : low + 128]
        base = side // 128 * 8
        for at in range(2 * width // 128):
            line = 8 + 2 * w + at // (width // 128)
            low = at % (width // 128) * 128
            table_ref[base + at : base + at + 1, :] = small[line : line + 1, low : low + 128]
        for out_ref, which in zip(out_refs, (1 - x_at, x_at)):
            start = pl.multiple_of(which * block, block)
            target = slice(w * block, (w + 1) * block)
            own = send_ref[pl.ds(normed_at + w * side + start, block), :]
            got = got_ref[pl.ds(normed_at + w * side + start, block), :]
            for at in range(normed_at // rows):
                cut = slice(at * rows, (at + 1) * rows)
                value = matmul(own, keep_ref[pre_keep + at * rows : pre_keep + (at + 1) * rows, :])
                value = value + matmul(got, got_ref[cut, :])
                out_ref[target, at * 256 : (at + 1) * 256] = value.astype(BF16)
            own = send_ref[pl.ds(normed_at + width + w * side + start, block), :]
            got = got_ref[pl.ds(normed_at + width + w * side + start, block), :]
            lane = normed_at // rows * 256
            for at in range(2):
                mine = 4 * width + at * rows
                theirs = branch_at + at * rows
                value = matmul(own, keep_ref[mine : mine + rows, :])
                value = value + matmul(got, got_ref[theirs : theirs + rows, :])
                value = value[:, : min(256, side - at * 256)].astype(BF16)
                out_ref[target, lane : lane + value.shape[1]] = value
                lane += value.shape[1]
            out_ref[target, lane : lane + 128] = table_ref[pl.ds(start, block), :].astype(BF16)


def up_slabs(meta, keep, send, got, own_small, got_small):
    width = own_small.shape[1]
    columns = 2 * width + width // 2 + 128
    first = pl.BlockSpec((5 * width, send.shape[1]), lambda i, m: (0, 0))

    def whole(value):
        return pl.BlockSpec(value.shape, lambda i, m: (0, 0))

    return pl.pallas_call(
        up_kernel,
        grid_spec=pltpu.PrefetchScalarGridSpec(
            num_scalar_prefetch=1,
            grid=(1,),
            in_specs=[whole(keep), first, first, whole(own_small), whole(own_small)],
            out_specs=[pl.BlockSpec((width // 2, columns), lambda i, m: (0, 0))] * 2,
            scratch_shapes=[pltpu.VMEM((width // 2, 128), F32)],
        ),
        out_shape=[jax.ShapeDtypeStruct((width // 2, columns), BF16)] * 2,
        compiler_params=pltpu.CompilerParams(vmem_limit_bytes=40 << 20),
        cost_estimate=work(4),
        name="up_slabs",
    )(meta, keep, send, got, own_small, got_small)


def key_sum_kernel(own_ref, core_ref, got_ref, *out_refs):
    size = out_refs[0].shape[1]
    for at, ref in enumerate(out_refs):
        cut = slice(at * size, (at + 1) * size)
        kept = (own_ref[cut, :].astype(F32) + core_ref[cut, :].astype(F32)).astype(BF16)
        ref[...] = (kept.astype(F32) + got_ref[cut, :].astype(F32)).astype(BF16).T


def key_sum(own, core, got):
    rows, columns = got.shape
    half = pl.BlockSpec((rows, columns), lambda i: (0, 0))
    return pl.pallas_call(
        key_sum_kernel,
        grid=(1,),
        in_specs=[half] * 3,
        out_specs=[pl.BlockSpec((columns, rows // ZS), lambda i: (0, 0))] * ZS,
        out_shape=[jax.ShapeDtypeStruct((columns, rows // ZS), BF16)] * ZS,
        compiler_params=pltpu.CompilerParams(vmem_limit_bytes=24 << 20),
        cost_estimate=work(2),
        name="key_sum",
    )(own, core, got)


def head_kernel(meta_ref, *refs):
    turned_refs, query_refs, kv_refs = refs[:2], refs[2 : 2 + ZS], refs[2 + ZS : 2 + 2 * ZS]
    refs = refs[2 + 2 * ZS :]
    out_ref = refs[-1]
    block = turned_refs[0].shape[0]

    def put(value, rows):
        if len(refs) == 2:
            value = value + refs[0][rows, :].astype(F32)
        out_ref[rows, :] = value.astype(BF16)

    grads = [jnp.concatenate([ref[...] for ref in items], axis=1) for items in (query_refs, kv_refs)]
    grads = jnp.concatenate(grads, axis=0)
    turned = jnp.concatenate([ref[...] for ref in turned_refs], axis=1)
    put(right_trans(turned, grads), slice(0, block))
    ones = jnp.ones((16, turned.shape[1]), BF16)
    put(right_trans(ones, grads), slice(block, block + 16))


def head_slab(meta, turned, query, kv, count, slabs, got=None, first=0):
    width, rows = turned[0].shape
    block = width // count
    columns = query[0].shape[0] + kv[0].shape[0]
    return pl.pallas_call(
        head_kernel,
        grid_spec=pltpu.PrefetchScalarGridSpec(
            num_scalar_prefetch=1,
            grid=(slabs,),
            in_specs=[pl.BlockSpec((block, rows), lambda i, m: (m[i] * 2 + m[slabs], 0))] * 2
            + [pl.BlockSpec(item.shape, lambda i, m: (0, 0)) for item in [*query, *kv]]
            + (
                []
                if got is None
                else [pl.BlockSpec((block + 16, columns), lambda i, m: (first + i, 0))]
            ),
            out_specs=pl.BlockSpec((block + 16, columns), lambda i, m: (i, 0)),
        ),
        out_shape=jax.ShapeDtypeStruct((slabs * (block + 16), columns), BF16),
        compiler_params=pltpu.CompilerParams(vmem_limit_bytes=24 << 20),
        cost_estimate=work(2),
        name="head_slab",
    )(meta, *turned, *query, *kv, *(() if got is None else (got,)))


def token_kernel(meta_ref, resid_ref, *refs, shared):
    query_refs, kv_refs, refs = refs[:ZS], refs[ZS : 2 * ZS], refs[2 * ZS :]
    weight_refs, refs = refs[: 5 if shared else 3], refs[5 if shared else 3 :]
    out_ref, full_ref, turned_ref, sems = refs
    w_at, c_at, z_at = meta_ref[1], meta_ref[2], meta_ref[3]
    width = full_ref.shape[1]
    moves = []
    if shared:
        count = weight_refs[0].shape[0]
        half = count // 2
        for kind in range(3):
            start = pl.multiple_of(w_at * count, count)
            moves.append((weight_refs[kind], full_ref.at[kind, pl.ds(start, count), :]))
            for ref, core in ((weight_refs[3], c_at), (weight_refs[4], 1 - c_at)):
                start = pl.multiple_of(((1 - w_at) * 2 + core) * half, half)
                moves.append(
                    (
                        ref.at[pl.ds(kind * half, half), :],
                        full_ref.at[kind, pl.ds(start, half), :],
                    )
                )
    else:
        for kind in range(3):
            moves.append((weight_refs[kind], full_ref.at[kind]))
    copies = []
    for at, (source, target) in enumerate(moves):
        copies.append(pltpu.make_async_copy(source, target, sems.at[at]))
        copies[-1].start()
    part = width // ZS
    head_dim = width // HEADS
    for at in range(ZS):
        low = (z_at ^ at) * part
        turned_ref[0, pl.ds(pl.multiple_of(low, part), part), :] = query_refs[at][...]
        for head in range(part // head_dim):
            start = pl.ds(pl.multiple_of(low + head * head_dim, head_dim), head_dim)
            for kind in (1, 2):
                row = (2 * head + kind - 1) * head_dim
                turned_ref[kind, start, :] = kv_refs[at][row : row + head_dim, :]
    parts = [turned_ref[kind].T for kind in range(3)]
    for copy in copies:
        copy.wait()
    out = resid_ref[...]
    for kind in range(3):
        out = out + right_trans(parts[kind], full_ref[kind])
    out_ref[...] = out


def token_gradient(meta, resid, query, kv, weights):
    rows, width = resid.shape
    in_vmem = pl.BlockSpec(memory_space=pltpu.VMEM)
    in_place = pl.BlockSpec(memory_space=pl.ANY)
    return pl.pallas_call(
        partial(token_kernel, shared=len(weights) == 5),
        grid_spec=pltpu.PrefetchScalarGridSpec(
            num_scalar_prefetch=1,
            grid=(),
            in_specs=[in_vmem] * (1 + 2 * ZS) + [in_place] * len(weights),
            out_specs=in_vmem,
            scratch_shapes=[
                pltpu.VMEM((3, width, width), BF16),
                pltpu.VMEM((3, width, rows), BF16),
                pltpu.SemaphoreType.DMA((9,)),
            ],
        ),
        out_shape=jax.ShapeDtypeStruct((rows, width), F32),
        compiler_params=pltpu.CompilerParams(vmem_limit_bytes=32 << 20),
        cost_estimate=work(4),
        name="token_gradient",
    )(meta, resid, *query, *kv, *weights)


def down_finish_kernel(meta_ref, *refs):
    block = refs[0].shape[0] // 4
    c_at, x_at = meta_ref[0], meta_ref[1]
    for at in range(4):
        for z in range(4):
            place = (c_at ^ (at >> 1)) * 8 + z * 2 + (x_at ^ (at & 1))
            start = pl.multiple_of(place * block, 8)
            refs[4][pl.ds(start, block), :] = refs[at][z * block : (z + 1) * block, :].astype(F32)


def down_finish(meta, pieces):
    block, width = pieces[0].shape
    in_vmem = pl.BlockSpec(memory_space=pltpu.VMEM)
    return pl.pallas_call(
        down_finish_kernel,
        grid_spec=pltpu.PrefetchScalarGridSpec(
            num_scalar_prefetch=1, grid=(), in_specs=[in_vmem] * 4, out_specs=in_vmem
        ),
        out_shape=jax.ShapeDtypeStruct((4 * block, width), F32),
        compiler_params=pltpu.CompilerParams(vmem_limit_bytes=32 << 20),
        cost_estimate=work(4),
        name="down_finish",
    )(meta, *pieces)


def up_finish_kernel(meta_ref, *refs):
    pieces = refs[:4]
    up_ref, out_ref, small_ref = refs[4:]
    block = pieces[0].shape[0]
    quarter = up_ref.shape[1] // 4
    side = out_ref.shape[1] // 2
    c_at, x_at = meta_ref[0], meta_ref[1]
    for at in range(4):
        start = pl.multiple_of((x_at ^ (at & 1)) * block, 8)
        rows = pl.ds(start, block)
        core = c_at ^ (at >> 1)
        for half in range(2):
            lanes = pl.ds(pl.multiple_of((2 * half + core) * quarter, 128), quarter)
            up_ref[rows, lanes] = pieces[at][:, half * quarter : (half + 1) * quarter].astype(F32)
        out_ref[rows, pl.ds(pl.multiple_of(core * side, 128), side)] = (
            pieces[at][:, 2 * quarter : 2 * quarter + side].astype(F32)
        )
        if at < 2:
            small_ref[rows, :] = pieces[at][:, 2 * quarter + side :].astype(F32)


def up_finish(meta, pieces, hidden, width):
    block = pieces[0].shape[0]
    in_vmem = pl.BlockSpec(memory_space=pltpu.VMEM)
    shapes = [(2 * block, hidden), (2 * block, width), (2 * block, 128)]
    return pl.pallas_call(
        up_finish_kernel,
        grid_spec=pltpu.PrefetchScalarGridSpec(
            num_scalar_prefetch=1,
            grid=(),
            in_specs=[in_vmem] * 4,
            out_specs=[in_vmem] * 3,
        ),
        out_shape=[jax.ShapeDtypeStruct(shape, F32) for shape in shapes],
        compiler_params=pltpu.CompilerParams(vmem_limit_bytes=40 << 20),
        cost_estimate=work(5),
        name="up_finish",
    )(meta, *pieces)


def head_finish_kernel(meta_ref, own_ref, got_ref, query_ref, key_ref, value_ref, bias_ref, *, part):
    size = own_ref.shape[0] // ZS
    block = size - 16
    head_dim = part // 3
    for at, source in enumerate((own_ref, got_ref)):
        start = pl.multiple_of((meta_ref[0] ^ at) * block, 8)
        rows = pl.ds(start, block)
        keys, values, queries = [], [], []
        for z in range(ZS):
            item = source[((z & 1) * 2 + (z >> 1)) * size :][:size].astype(F32)
            for head in range(3):
                low = part + head * 2 * head_dim
                keys.append(item[:, low : low + head_dim])
                values.append(item[:, low + head_dim : low + 2 * head_dim])
            queries.append(item[:, :part])
        key = jnp.concatenate(keys, axis=1)
        value = jnp.concatenate(values, axis=1)
        query = jnp.concatenate(queries, axis=1)
        query_ref[rows, :] = query[:block]
        key_ref[rows, :] = key[:block]
        value_ref[rows, :] = value[:block]
        if at == 0:
            bias_ref[0:8, :] = query[block : block + 8]
            bias_ref[8:16, :] = value[block : block + 8]


def head_finish(meta, own, got):
    rows, columns = own.shape
    rows = 2 * (rows // ZS - 16)
    width = ZS * columns // 3
    return small_call(
        partial(head_finish_kernel, part=columns // 3),
        meta,
        (own, got),
        [((rows, width), F32)] * 3 + [((16, width), F32)],
        limit=40,
        name="head_finish",
    )


def in_order(index, own, other, axis):
    return jnp.where(
        index == 0,
        jnp.concatenate([own, other], axis=axis),
        jnp.concatenate([other, own], axis=axis),
    )


def part_of(value, index, count, axis):
    size = value.shape[axis] // count
    return lax.dynamic_slice_in_dim(value, index * size, size, axis)


def body(
    inputs,
    lengths,
    cotangent,
    query_weight,
    query_bias,
    key_weight,
    value_weight,
    value_bias,
    output_weight,
    output_bias,
    first_gain,
    first_shift,
    up_weight,
    up_bias,
    down_weight,
    down_bias,
    second_gain,
    second_shift,
    *,
    sizes,
):
    count_o, count_w = sizes
    w_at = lax.axis_index("w")
    z_at = lax.axis_index("z")
    c_at = lax.axis_index("c")
    x_at = lax.axis_index("x")
    o_at = lax.axis_index("o")
    tokens = inputs[0]
    local_rows, width = tokens.shape
    head_dim = width // HEADS
    heads = HEADS // ZS
    part = heads * head_dim
    length = lengths[0]

    hold = lax.optimization_barrier

    near = ((0, 1), (1, 0), (2, 3), (3, 2))
    far = ((0, 2), (2, 0), (1, 3), (3, 1))
    cross = ((0, 3), (3, 0), (1, 2), (2, 1))

    def exchange(pieces):
        return [pieces[0]] + [
            lax.ppermute(item, "z", perm) for item, perm in zip(pieces[1:], (near, far, cross))
        ]

    own_rows = query_weight.shape[0]
    big_weights = (output_weight, up_weight, down_weight)
    sides = jnp.stack([z_at, c_at]).astype(jnp.int32)
    low_tokens, attn_own, *low_heads, head_pack = prepare(
        sides, tokens, (query_weight, key_weight, value_weight)
    )
    line_tokens = [low_tokens, lax.ppermute(low_tokens, "z", near)]
    line_tokens.append(lax.ppermute(low_tokens, "z", far))
    small = jnp.stack(
        [
            item.reshape(-1, own_rows)[row]
            for item in (
                query_bias,
                value_bias,
                output_bias,
                first_gain,
                first_shift,
                down_bias,
                second_gain,
                second_shift,
                up_bias,
            )
            for row in range(item.shape[0] // own_rows)
        ]
    ).astype(BF16)
    if count_w == 2:
        attn_got, small_got = swap(attn_own, "w"), swap(small, "w")
        *low_weights, weight_pack = round_weights(sides, big_weights)
        attn_got, small_got, weight_pack, *line_tokens[1:3] = hold(
            (attn_got, small_got, weight_pack, *line_tokens[1:3])
        )
        weight_got = swap(weight_pack, "w")
        sources = (attn_own, attn_got, small, small_got)
    else:
        attn_full = lax.all_gather(attn_own, "w", axis=0, tiled=True)
        small_all = lax.all_gather(small, "w", axis=0, tiled=False)
        low_weights = [item.astype(BF16) for item in big_weights]
        weight_got = [lax.all_gather(item, "w", axis=0, tiled=True) for item in low_weights]
        head_weights = [lax.all_gather(item, "w", axis=0, tiled=True) for item in low_heads]
        pair = jnp.transpose(small_all[:, :2], (1, 0, 2)).reshape(2, width).astype(F32)
        own_bias = lax.dynamic_slice_in_dim(pair, z_at * part, part, 1)
        value_bias_own = own_bias[1].reshape(heads, 1, head_dim)
        kv_bias = jnp.concatenate([jnp.zeros_like(value_bias_own), value_bias_own], axis=1)
        bias_row = jnp.concatenate([kv_bias.reshape(1, 2 * part), own_bias[:1]], axis=1)
        sources = (attn_full, bias_row)

    line_tokens.append(lax.ppermute(line_tokens[2], "z", near))
    corner = jnp.stack([w_at, z_at]).astype(jnp.int32)
    made = [project(corner, *line_tokens[:2], sources)]
    made[0], *line_tokens[2:] = hold((made[0], *line_tokens[2:]))
    made.append(project(corner, *line_tokens[2:], sources))
    queries = [item[0] for item in made]
    turned = [item[2] for item in made]
    kv_blocks = [[item[1] for item in made]]
    for axis in ("x", "c", "o")[: 3 if count_o == 2 else 2]:
        kv_blocks = kv_blocks + [[swap(item, axis) for item in pair] for pair in kv_blocks]
    places = []
    for at in range(4 * count_o):
        o_of = o_at ^ (at >> 2)
        places.append(o_of * 16 + (x_at ^ (at & 1)) * 2 + (c_at ^ ((at >> 1) & 1)))
    meta = jnp.stack([length, z_at] + places).astype(jnp.int32)
    kv_blocks = [
        [pltpu.with_memory_space_constraint(item, pltpu.MemorySpace.HBM) for item in pair]
        for pair in kv_blocks
    ]
    attended, *made = attend_forward(meta, queries, kv_blocks, heads)
    logs = made[ZS]
    if count_w == 2:
        attended, weight_got, head_pack, small_own, small_got = hold(
            (attended, weight_got, head_pack, small, small_got)
        )
        small_all = in_order(w_at, small_own[None], small_got[None], 0)
        weights = [*low_weights, weight_got, swap(weight_got, "c")]
        head_got = swap(head_pack, "w")
    else:
        weights = weight_got
    mixed = exchange(made[:ZS])
    small_all = small_all.astype(F32)
    vec = jnp.transpose(small_all[:, :8], (1, 0, 2)).reshape(8, width)
    up_offset = small_all[:, 8:].reshape(1, -1)

    split = count_w == 2 and count_o == 1
    my_index = o_at * 16 + z_at * 4 + x_at * 2 + c_at
    rest = jnp.clip(length - my_index * local_rows, 0, local_rows)
    core = c_at if split else jnp.zeros_like(c_at)
    spots = jnp.stack([rest, w_at, core, z_at]).astype(jnp.int32)
    outputs, resid_grad, *made = middle(
        spots, [mixed], ((0, heads),), tokens, cotangent[0], vec, up_offset, weights
    )
    head_grads = exchange(made[:ZS])
    send, keep, small_own = made[ZS:]
    hidden = up_offset.shape[1]

    near_bit, far_bit = z_at & 1, z_at >> 1

    def add_pair(kept, got):
        return (kept.astype(F32) + got.astype(F32)).astype(BF16)

    def join(value, got, bit):
        return in_order(bit, value, got, 0)

    spot = jnp.stack([c_at, x_at]).astype(jnp.int32)
    token = [spot]

    def arrive(*values):
        token[0], *values = hold((token[0], *values))
        return values[0] if len(values) == 1 else values

    def backward(first, count, made=()):
        return attend_backward(
            meta, queries, head_grads, attended, logs, kv_blocks, first, count, made
        )

    def to_near(value):
        return lax.ppermute(value, "z", near)

    def to_far(value):
        return lax.ppermute(value, "z", far)

    def head_part(ws, core, got=None, first=0):
        at = jnp.stack([jnp.asarray(item) for item in (*ws, core)]).astype(jnp.int32)
        return head_slab(at, turned, query_low, kv_low, 2 * count_w, len(ws), got, first)

    def pick(w, c):
        return jnp.stack([jnp.asarray(w), jnp.asarray(c)]).astype(jnp.int32)

    if split:
        got, small_got = swap(send, "c"), swap(small_own, "c")
        down_far = down_slab(pick(1 - w_at, 0), keep, send, got)
        up_sent, up_kept = up_slabs(
            jnp.stack([x_at]).astype(jnp.int32), keep, send, got, small_own, small_got
        )
        down_near = down_slab(pick(1 * w_at, 0), keep, send, got)
        down_far, up_sent, down_near, *head_grads = hold(
            (down_far, up_sent, down_near, *head_grads)
        )
        made = backward(0, heads - 1)
        down_got, *made = arrive(swap(down_far, "w"), *made)
        down_sum = add_pair(down_near, down_got)
        down_got = to_near(part_of(down_sum, 1 - near_bit, 2, 0))
        down_sum, *head_grads = arrive(down_sum, *head_grads)
        made = backward(heads - 1, 1, made)
        down_got, up_got, head_got, *made = arrive(
            down_got, swap(up_sent, "x"), head_got, *made
        )
        query_low, pairs = made[:ZS], made[ZS:]
        head_weights = [*low_heads, head_got, swap(head_got, "c")]
        pair_got = swap(pairs[1], "c")
        query_got = exchange(query_low)
        down_sum = add_pair(part_of(down_sum, near_bit, 2, 0), down_got)
        down_got = to_far(part_of(down_sum, 1 - far_bit, 2, 0))
        up_sum = add_pair(up_kept, up_got).reshape(2, own_rows // 2, -1)
        up_got = swap(lax.dynamic_index_in_dim(up_sum, 1 - w_at, 0, keepdims=False), "w")
        pair_got = arrive(pair_got)
        half_rows = pair_got.shape[0] // 2
        pair_sent = add_pair(pairs[0][half_rows:], pair_got[half_rows:])
        pair_sent = arrive(pair_sent)
        key_got = swap(pair_sent, "x")
        down_got = arrive(down_got)
        down_sum = add_pair(part_of(down_sum, far_bit, 2, 0), down_got)
        down_got = swap(part_of(down_sum, 1 - x_at, 2, 0), "x")
        up_got = arrive(up_got)
        up_sum = add_pair(lax.dynamic_index_in_dim(up_sum, w_at, 0, keepdims=False), up_got)
        up_got = to_near(part_of(up_sum, 1 - near_bit, 2, 0))
        key_got, *query_got = arrive(key_got, *query_got)
        kv_low = key_sum(pairs[0], pair_got, key_got)
        head_far = swap(head_part((1 - w_at,), 1 - c_at), "c")
        kv_got = exchange(kv_low)
        head_near = swap(head_part((1 * w_at,), 1 - c_at), "c")
        down_got = arrive(down_got)
        down_sum = add_pair(part_of(down_sum, x_at, 2, 0), down_got)
        down_got = to_far(down_sum)
        head_far = arrive(head_far)
        head_sent = swap(head_part((1 - w_at,), c_at, head_far), "w")
        head_near = arrive(head_near)
        head_sum = head_part((1 * w_at,), c_at, head_near)
        up_got = arrive(up_got)
        up_sum = add_pair(part_of(up_sum, near_bit, 2, 0), up_got)
        up_got = to_far(part_of(up_sum, 1 - far_bit, 2, 0))
        head_sent = arrive(head_sent)
        head_sum = add_pair(head_sum, head_sent)
        head_got = swap(head_sum, "x")
        kv_got = arrive(*kv_got)
        input_grad = token_gradient(
            spots, resid_grad, query_got, kv_got, head_weights
        )
        up_got = arrive(up_got)
        up_sum = add_pair(part_of(up_sum, far_bit, 2, 0), up_got)
        up_got = to_far(up_sum)
        down_got = arrive(down_got)
        down_sum = join(down_sum[None], down_got[None], far_bit)
        down_got = to_near(down_sum)
        head_got = arrive(head_got)
        head_sum = add_pair(head_sum, head_got)
        head_got = to_far(head_sum)
        up_got = arrive(up_got)
        up_sum = join(up_sum, up_got, far_bit)
        up_got = to_near(up_sum)
        down_got = arrive(down_got)
        down_sum = join(down_sum[None], down_got[None], near_bit)
        down_sum = down_sum.reshape(-1, width)
        down_x = swap(down_sum, "x")
        down_c = swap(down_sum, "c")
        head_got = arrive(head_got)
        head_two = join(head_sum, head_got, far_bit)
        head_got = to_near(head_two)
        up_got = arrive(up_got)
        up_sum = join(up_sum, up_got, near_bit)
        up_x = swap(up_sum, "x")
        up_c = swap(up_sum, "c")
        down_x, input_grad = arrive(down_x, input_grad)
        down_pieces = [down_sum, down_x, down_c, swap(down_x, "c")]
        head_got = arrive(head_got)
        head_four = join(head_two, head_got, near_bit)
        head_other = swap(head_four, "c")
        total_down = down_finish(spot, down_pieces)
        up_x, total_down = arrive(up_x, total_down)
        up_pieces = [up_sum, up_x, up_c, swap(up_x, "c")]
        total_query, total_key, total_value, head_bias = head_finish(
            spot, head_four, head_other
        )
        total_query, total_key, total_value = arrive(total_query, total_key, total_value)
        total_up, total_out, table = up_finish(token[0], up_pieces, hidden, width)
        groups = own_rows // 128
        small_total = table[: 8 * groups].reshape(groups, 8, 128)
        vectors = [small_total[:, at].reshape(own_rows) for at in range(6)]
        lines = hidden // count_w // 128
        total_up_bias = table[8 * groups : 8 * groups + lines].reshape(-1)
    else:
        made = backward(0, heads)
        query_low, pairs = made[:ZS], made[ZS:]
        if count_o == 2:
            pairs = [plus(spot, pairs[at], swap(pairs[at + 2], "o")) for at in range(2)]
        pair_got = swap(pairs[1], "c")
        half_rows = pair_got.shape[0] // 2
        key_got = swap(plus(spot, pairs[0], pair_got, half_rows), "x")
        kv_low = key_sum(pairs[0], pair_got, key_got)
        if count_w == 2:
            head_weights = [*low_heads, head_got, swap(head_got, "c")]
        input_grad = token_gradient(
            spots.at[2].set(c_at.astype(jnp.int32)),
            resid_grad,
            exchange(query_low),
            exchange(kv_low),
            head_weights,
        )
        every_w = tuple(range(count_w))
        slabs = head_part(every_w, c_at, swap(head_part(every_w, 1 - c_at), "c"))
        head_sum = lax.psum_scatter(slabs, "w", scatter_dimension=0, tiled=True)
        head_sum = plus(spot, head_sum, swap(head_sum, "x"))
        if count_o == 2:
            head_sum = plus(spot, head_sum, swap(head_sum, "o"))
        n_bit, f_bit = [
            jnp.stack([bit, bit]).astype(jnp.int32) for bit in (near_bit, far_bit)
        ]
        head_sum = unite(f_bit, head_sum, to_far(head_sum))
        head_sum = unite(n_bit, head_sum, to_near(head_sum))
        total_query, total_key, total_value, head_bias = head_finish(
            spot, head_sum, swap(head_sum, "c")
        )
        quarter = hidden // 4
        count = quarter // 256
        act_at = 5 * quarter
        act = [keep[:quarter], send[act_at : act_at + quarter], keep[quarter : 2 * quarter]]
        act += [send[act_at + quarter : act_at + 2 * quarter]]
        act = jnp.concatenate(act, axis=0)

        def rows_of(value, low, at):
            return value[low + at * local_rows : low + (at + 1) * local_rows]

        ffn_at = act_at + 2 * quarter
        ffn = jnp.concatenate([rows_of(send, ffn_at, at) for at in range(width // 256)], axis=1)
        pre = []
        for half in range(2):
            pre += [rows_of(keep, 2 * quarter, half * count + at) for at in range(count)]
            pre += [rows_of(send, 0, half * count + at) for at in range(count)]
        pre = jnp.concatenate(pre, axis=1)
        normed_turned = send[2 * quarter : 2 * quarter + width]
        mixed_turned = send[2 * quarter + width : 2 * quarter + 2 * width]
        side = width // 2
        branch = jnp.concatenate(
            [
                rows_of(keep, 4 * quarter, 0),
                rows_of(keep, 4 * quarter, 1)[:, : side - 256],
                rows_of(send, 2 * quarter + 2 * width, 0),
                rows_of(send, 2 * quarter + 2 * width, 1)[:, : side - 256],
            ],
            axis=1,
        )

        def sum_all(value):
            value = value.astype(BF16)
            value = lax.psum_scatter(value, "w", scatter_dimension=0, tiled=True)
            return lax.psum(value, ("o", "z", "x", "c")).astype(F32)

        total_down = sum_all(matmul(act, ffn))
        total_up = sum_all(matmul(normed_turned, pre))
        total_out = sum_all(matmul(mixed_turned, branch))
        small_own = lax.psum(small_own, ("o", "z", "x", "c", "w"))
        vectors = [part_of(small_own[at], w_at, count_w, 0) for at in range(6)]
        total_up_bias = part_of(small_own[8:12].reshape(-1), w_at, count_w, 0)

    totals = [part_of(head_bias[at], w_at, count_w, 0) for at in (0, 8)] + vectors
    return (
        outputs[None],
        input_grad[None],
        total_query,
        totals[0],
        total_key,
        total_value,
        totals[1],
        total_out,
        totals[2],
        totals[3],
        totals[4],
        total_up,
        total_up_bias,
        total_down,
        totals[5],
        totals[6],
        totals[7],
    )


def solution(mesh):
    count_s = mesh.shape["seq"]
    count_w = mesh.shape["wshard"]
    count_o = count_s // 16
    fine = Mesh(
        mesh.devices.reshape(count_o, ZS, 2, 2, count_w), ("o", "z", "x", "c", "w")
    )
    seq = ("o", "z", "x", "c")
    rows = P("w", seq, None)
    matrix = P("w", None)
    vector = P("w")
    placed = (
        rows,
        vector,
        rows,
        matrix,
        vector,
        matrix,
        matrix,
        vector,
        matrix,
        vector,
        vector,
        vector,
        matrix,
        vector,
        matrix,
        vector,
        vector,
        vector,
    )
    return jax.shard_map(
        partial(body, sizes=(count_o, count_w)),
        mesh=fine,
        in_specs=placed,
        out_specs=(
            rows,
            rows,
            matrix,
            vector,
            matrix,
            matrix,
            vector,
            matrix,
            vector,
            vector,
            vector,
            matrix,
            vector,
            matrix,
            vector,
            vector,
            vector,
        ),
        check_vma=False,
    )
```

```python
from functools import partial

import jax
import jax.numpy as jnp
from jax import lax
from jax.experimental import pallas as pl
from jax.experimental.pallas import tpu as pltpu
from jax.sharding import Mesh, PartitionSpec as P

HEADS = 12
ZS = 4
NEG_FILL = -1e30
VMEM_LIMIT = 60 << 20
SWAP = ((0, 1), (1, 0))
F32 = jnp.float32
BF16 = jnp.bfloat16


def matmul(left_side, right_side):
    return jnp.dot(left_side, right_side, preferred_element_type=F32)


def right_trans(left_side, right_side):
    return lax.dot_general(
        left_side, right_side, (((1,), (1,)), ((), ())), preferred_element_type=F32
    )


def work(units):
    return pl.CostEstimate(flops=int(units * 1e3), bytes_accessed=1, transcendentals=0)


def swap(value, axis):
    return lax.ppermute(value, axis, SWAP)


def touched_groups(length, rows, outer):
    group = 4 * rows
    left = length - outer * (ZS * group)
    return jnp.clip((left + group - 1) // group, 0, ZS)


def with_mask(kv, place, length):
    at = place + lax.broadcasted_iota(jnp.int32, kv.shape, 0)
    lane = lax.broadcasted_iota(jnp.int32, kv.shape, 1)
    fill = jnp.where(at < length, 0.0, jnp.where(lane == 0, NEG_FILL, 0.0))
    return jnp.concatenate([kv, fill.astype(BF16)], axis=1)


def load_head(kv_refs, rows_ref, turned_ref, low):
    head_dim = turned_ref.shape[1]
    for at, ref in enumerate(kv_refs):
        block, half = at // 2, at % 2
        size = ref.shape[0]
        for start in range(0, size, 256):
            value = ref[start : start + 256, :]
            place = slice(half * size + start, half * size + start + 256)
            rows_ref[block, place, :] = value
            turned_ref[block, :, place] = value.T[low : low + head_dim, :]


def forward_kernel(meta_ref, *refs, blocks, rows):
    query_refs, kv_refs = refs[:2], refs[2 : 2 + 2 * blocks]
    out_ref, *refs = refs[2 + 2 * blocks :]
    piece_refs, (log_ref, rows_ref, turned_ref) = refs[:ZS], refs[ZS:]
    head_dim, query_count = out_ref.shape
    length, z_at = meta_ref[0], meta_ref[1]
    load_head(kv_refs, rows_ref, turned_ref, head_dim)
    query = jnp.concatenate([ref[...] for ref in query_refs], axis=1)
    query = jnp.concatenate(
        [
            query,
            jnp.zeros((head_dim, query_count), BF16),
            jnp.ones((128, query_count), BF16),
        ],
        axis=0,
    )

    def step(group, carry, members):
        top, total, acc = carry
        start = pl.multiple_of((group ^ z_at) * rows, rows)
        found = []
        for block in members:
            place = (meta_ref[2 + block] + group * 4) * rows
            kv = with_mask(rows_ref[block, pl.ds(start, rows), :], place, length)
            found.append(matmul(kv, query))
        new_top = top
        for scores in found:
            new_top = jnp.maximum(new_top, jnp.max(scores, axis=0, keepdims=True))
        fade = jnp.exp(top - new_top)
        total = total * fade
        acc = acc * fade
        for block, scores in zip(members, found):
            weights = jnp.exp(scores - new_top)
            total = total + jnp.sum(weights, axis=0, keepdims=True)
            acc = acc + matmul(
                turned_ref[block, :, pl.ds(start, rows)], weights.astype(BF16)
            )
        return new_top, total, acc

    carry = (
        jnp.full((1, query_count), NEG_FILL, F32),
        jnp.zeros((1, query_count), F32),
        jnp.zeros((head_dim, query_count), F32),
    )
    for first in range(0, blocks, 4):
        members = tuple(range(first, first + 4))
        count = touched_groups(length, rows, meta_ref[2 + first] // 16)
        carry = lax.fori_loop(0, count, lambda g, c: step(g, c, members), carry)
    top, total, acc = carry
    out = acc * (1.0 / total)
    out_ref[...] = out
    size = query_count // ZS
    for at in range(ZS):
        piece_refs[at][...] = out[:, at * size : (at + 1) * size].astype(BF16)
    log_ref[0] = top + jnp.log(total)


def attend_forward(meta, queries, kv_blocks, heads):
    blocks = len(kv_blocks)
    half_rows = kv_blocks[0][0].shape[0]
    part, half_count = queries[0].shape
    head_dim, query_count = part // heads, 2 * half_count
    size = query_count // ZS
    return pl.pallas_call(
        partial(forward_kernel, blocks=blocks, rows=2 * half_rows // ZS),
        grid_spec=pltpu.PrefetchScalarGridSpec(
            num_scalar_prefetch=1,
            grid=(heads,),
            in_specs=[pl.BlockSpec((head_dim, half_count), lambda i, m: (i, 0))] * 2
            + [pl.BlockSpec((half_rows, 128), lambda i, m: (0, i))] * (2 * blocks),
            out_specs=[pl.BlockSpec((head_dim, query_count), lambda i, m: (i, 0))]
            + [pl.BlockSpec((head_dim, size), lambda i, m: (i, 0))] * ZS
            + [pl.BlockSpec((1, 1, query_count), lambda i, m: (i, 0, 0))],
            scratch_shapes=[
                pltpu.VMEM((blocks, 2 * half_rows, 128), BF16),
                pltpu.VMEM((blocks, head_dim, 2 * half_rows), BF16),
            ],
        ),
        out_shape=[jax.ShapeDtypeStruct((part, query_count), F32)]
        + [jax.ShapeDtypeStruct((part, size), BF16)] * ZS
        + [jax.ShapeDtypeStruct((heads, 1, query_count), F32)],
        compiler_params=pltpu.CompilerParams(vmem_limit_bytes=VMEM_LIMIT),
        cost_estimate=work(8 * heads),
        name="attend_forward",
    )(meta, *queries, *[item for pair in kv_blocks for item in pair])


def backward_kernel(meta_ref, *refs, blocks, rows, extra):
    query_refs, (out_ref, log_ref), refs = refs[:2], refs[2:4], refs[4:]
    grad_refs, kv_refs = refs[:ZS], refs[ZS : ZS + 2 * blocks]
    refs = refs[ZS + 2 * blocks + extra :]
    dq_refs, pairs = refs[:ZS], refs[ZS : ZS + blocks // 2]
    rows_ref, turned_ref, qn_ref, gn_ref, acc_ref = refs[ZS + blocks // 2 :]
    head_dim, query_count = out_ref.shape
    length, z_at = meta_ref[0], meta_ref[1]
    block_rows = ZS * rows
    load_head(kv_refs, rows_ref, turned_ref, 0)
    query = jnp.concatenate([ref[...] for ref in query_refs], axis=1)
    grads = jnp.concatenate([ref[...] for ref in grad_refs], axis=1)
    blank = jnp.zeros((head_dim, query_count), BF16)
    query = jnp.concatenate([query, blank], axis=0)
    grad = jnp.concatenate([blank, grads], axis=0)
    qn_ref[...] = query.T
    gn_ref[...] = grad.T
    query = jnp.concatenate([query, jnp.ones((128, query_count), BF16)], axis=0)
    delta = jnp.sum(grads.astype(F32) * out_ref[...], axis=0, keepdims=True)
    log_sum = log_ref[0]
    acc_ref[...] = jnp.zeros_like(acc_ref)

    def put(block, start, value):
        pairs[block // 2][pl.ds(start + (block & 1) * block_rows, rows), :] = value

    def step(group, members):
        start = pl.multiple_of((group ^ z_at) * rows, rows)
        for block in members:
            kv = rows_ref[block, pl.ds(start, rows), :]
            place = (meta_ref[2 + block] + group * 4) * rows
            scores = matmul(with_mask(kv, place, length), query)
            prob_grad = matmul(kv, grad)
            prob = jnp.exp(scores - log_sum)
            score_grad = (prob * (prob_grad - delta)).astype(BF16)
            value = matmul(prob.astype(BF16), gn_ref[...]) + matmul(score_grad, qn_ref[...])
            put(block, start, value.astype(BF16))
            acc_ref[...] += matmul(turned_ref[block, :, pl.ds(start, rows)], score_grad)

    def clear(group, members):
        start = pl.multiple_of((group ^ z_at) * rows, rows)
        for block in members:
            put(block, start, jnp.zeros((rows, 128), BF16))

    def loop(low, high, fn):
        def one(group, carry):
            fn(group)
            return carry

        lax.fori_loop(low, high, one, 0)

    for first in range(0, blocks, 4):
        members = tuple(range(first, first + 4))
        count = touched_groups(length, rows, meta_ref[2 + first] // 16)
        loop(0, count, lambda g: step(g, members))
        loop(count, ZS, lambda g: clear(g, members))
    dq = (acc_ref[...] * head_dim ** (-0.5)).astype(BF16)
    size = query_count // ZS
    for at in range(ZS):
        dq_refs[at][...] = dq[:, at * size : (at + 1) * size]


def attend_backward(meta, queries, grads, out, log_sum, kv_blocks, first, count, made=()):
    blocks = len(kv_blocks)
    half_rows, columns = kv_blocks[0][0].shape
    heads = columns // 128
    part, half_count = queries[0].shape
    head_dim, query_count = part // heads, 2 * half_count
    size = query_count // ZS
    piece = pl.BlockSpec((head_dim, size), lambda i, m: (i + first, 0))
    ins = [
        *queries,
        out,
        log_sum,
        *grads,
        *[item for pair in kv_blocks for item in pair],
        *made,
    ]
    return pl.pallas_call(
        partial(backward_kernel, blocks=blocks, rows=2 * half_rows // ZS, extra=len(made)),
        grid_spec=pltpu.PrefetchScalarGridSpec(
            num_scalar_prefetch=1,
            grid=(count,),
            in_specs=[pl.BlockSpec((head_dim, half_count), lambda i, m: (i + first, 0))] * 2
            + [
                pl.BlockSpec((head_dim, query_count), lambda i, m: (i + first, 0)),
                pl.BlockSpec((1, 1, query_count), lambda i, m: (i + first, 0, 0)),
            ]
            + [piece] * ZS
            + [pl.BlockSpec((half_rows, 128), lambda i, m: (0, i + first))] * (2 * blocks)
            + [pl.BlockSpec(memory_space=pl.ANY)] * len(made),
            out_specs=[piece] * ZS
            + [pl.BlockSpec((4 * half_rows, 128), lambda i, m: (0, i + first))] * (blocks // 2),
            scratch_shapes=[
                pltpu.VMEM((blocks, 2 * half_rows, 128), BF16),
                pltpu.VMEM((blocks, head_dim, 2 * half_rows), BF16),
                pltpu.VMEM((query_count, 128), BF16),
                pltpu.VMEM((query_count, 128), BF16),
                pltpu.VMEM((head_dim, query_count), F32),
            ],
        ),
        out_shape=[jax.ShapeDtypeStruct((part, size), BF16)] * ZS
        + [jax.ShapeDtypeStruct((4 * half_rows, columns), BF16)] * (blocks // 2),
        input_output_aliases={
            1 + len(ins) - len(made) + at: at for at in range(len(made))
        },
        compiler_params=pltpu.CompilerParams(vmem_limit_bytes=VMEM_LIMIT),
        cost_estimate=work(12 * count),
        name="attend_backward",
    )(meta, *ins)


IN_VMEM = pl.BlockSpec(memory_space=pltpu.VMEM)


def small_call(kernel, meta, values, shapes, scratch=(), limit=32, name=None):
    return pl.pallas_call(
        kernel,
        grid_spec=pltpu.PrefetchScalarGridSpec(
            num_scalar_prefetch=1,
            grid=(),
            in_specs=[IN_VMEM] * len(values),
            out_specs=[IN_VMEM] * len(shapes),
            scratch_shapes=list(scratch),
        ),
        out_shape=[jax.ShapeDtypeStruct(shape, kind) for shape, kind in shapes],
        compiler_params=pltpu.CompilerParams(vmem_limit_bytes=limit << 20),
        cost_estimate=work(1),
        name=name,
    )(meta, *values)


def fold_kernel(meta_ref, kept_ref, got_ref, keep_ref, sent_ref, sum_ref):
    sum_ref[...] = (kept_ref[...].astype(F32) + got_ref[...].astype(F32)).astype(BF16)
    rows = keep_ref.shape[0]
    for at, ref in enumerate((keep_ref, sent_ref)):
        start = pl.multiple_of((meta_ref[0] ^ at) * rows, 16)
        ref[...] = sum_ref[pl.ds(start, rows), :]


def fold(bit, kept, got):
    rows, columns = kept.shape
    half = ((rows // 2, columns), BF16)
    return small_call(
        fold_kernel,
        bit,
        (kept, got),
        [half, half],
        [pltpu.VMEM((rows, columns), BF16)],
        name="fold",
    )


def unite_kernel(meta_ref, own_ref, got_ref, out_ref):
    rows = own_ref.shape[0]
    for at, ref in enumerate((own_ref, got_ref)):
        start = pl.multiple_of((meta_ref[0] ^ at) * rows, 16)
        out_ref[pl.ds(start, rows), :] = ref[...]


def unite(bit, own, got):
    rows, columns = own.shape
    return small_call(
        unite_kernel, bit, (own, got), [((2 * rows, columns), BF16)], name="unite"
    )[0]


def plus_kernel(meta_ref, one_ref, two_ref, out_ref, *, low):
    cut = slice(low, low + out_ref.shape[0])
    out_ref[...] = (one_ref[cut, :].astype(F32) + two_ref[cut, :].astype(F32)).astype(BF16)


def plus(meta, one, two, low=0):
    rows, columns = one.shape
    return small_call(
        partial(plus_kernel, low=low),
        meta,
        (one, two),
        [((rows - low, columns), BF16)],
        name="plus",
    )[0]


def prepare_kernel(meta_ref, *refs):
    sources, refs = refs[:3], refs[3:]
    kv_ref, query_ref, low_refs, head_ref = refs[0], refs[1], refs[2:5], refs[5]
    places, sems = refs[6:9], refs[9]
    copies = []
    for at in range(3):
        copies.append(pltpu.make_async_copy(sources[at], places[at], sems.at[at]))
        copies[-1].start()
    z_at, c_at = meta_ref[0], meta_ref[1]
    width = places[0].shape[1]
    part = width // ZS
    head_dim = width // HEADS
    parts = []
    for kind in range(3):
        ref = places[kind]
        copies[kind].wait()
        value = ref[...]
        low_refs[kind][...] = value.astype(BF16)
        half = ref.shape[0] // 2
        rows = ref[pl.ds(pl.multiple_of(c_at * half, half), half), :]
        head_ref[kind * half : (kind + 1) * half, :] = rows.astype(BF16)
        turn = lax.rem(width - z_at * part, width)
        parts.append(pltpu.roll(value, turn, 1)[:, :part])
    columns = []
    for head in range(part // head_dim):
        cut = slice(head * head_dim, (head + 1) * head_dim)
        columns += [parts[1][:, cut], parts[2][:, cut]]
    kv_ref[...] = jnp.concatenate(columns, axis=1).astype(BF16)
    query_ref[...] = parts[0].astype(BF16)


def prepare(meta, weights):
    count, width = weights[0].shape
    shapes = [(count, 2 * width // ZS), (count, width // ZS)] + [(count, width)] * 3
    shapes.append((3 * count // 2, width))
    return pl.pallas_call(
        prepare_kernel,
        grid_spec=pltpu.PrefetchScalarGridSpec(
            num_scalar_prefetch=1,
            grid=(),
            in_specs=[pl.BlockSpec(memory_space=pltpu.MemorySpace.HBM)] * 3,
            out_specs=[IN_VMEM] * len(shapes),
            scratch_shapes=[pltpu.VMEM((count, width), F32)] * 3
            + [pltpu.SemaphoreType.DMA((3,))],
        ),
        out_shape=[jax.ShapeDtypeStruct(shape, BF16) for shape in shapes],
        compiler_params=pltpu.CompilerParams(vmem_limit_bytes=VMEM_LIMIT),
        cost_estimate=work(1),
        name="prepare",
    )(meta, *weights)


def round_kernel(meta_ref, out_w, up_w, down_w, low_out, low_up, low_down, pack_ref):
    core = meta_ref[1]
    for source, target in ((out_w, low_out), (up_w, low_up), (down_w, low_down)):
        target[...] = source[...].astype(BF16)
    width = pack_ref.shape[1]
    low = 0
    half = out_w.shape[0] // 2
    rows = pl.ds(pl.multiple_of(core * half, half), half)
    pack_ref[low : low + half, :] = out_w[rows, :].astype(BF16)
    low += half
    count = up_w.shape[1] // 2
    for block in range(count // width):
        lanes = pl.ds(pl.multiple_of(core * count + block * width, 128), width)
        pack_ref[low : low + up_w.shape[0], :] = up_w[:, lanes].astype(BF16)
        low += up_w.shape[0]
    half = down_w.shape[0] // 2
    rows = pl.ds(pl.multiple_of(core * half, half), half)
    pack_ref[low : low + half, :] = down_w[rows, :].astype(BF16)


def round_weights(meta, weights):
    out_w, up_w, down_w = weights
    width = out_w.shape[1]
    total = out_w.shape[0] // 2 + up_w.shape[0] * (up_w.shape[1] // 2 // width)
    total += down_w.shape[0] // 2
    return small_call(
        round_kernel,
        meta,
        weights,
        [(item.shape, BF16) for item in weights] + [((total, width), BF16)],
        limit=60,
        name="round_weights",
    )


def project_kernel(meta_ref, first_ref, second_ref, *refs, shared):
    query_ref, kv_ref, turned_ref, token_ref, bias_ref = refs[-5:]
    part = query_ref.shape[0]
    rows, width = first_ref.shape
    split = 2 * part
    token_ref[:rows, :] = first_ref[...]
    token_ref[rows:, :] = second_ref[...]
    if shared:
        w_at, z_at = meta_ref[0], meta_ref[1]
        both = None
        bias_ref[...] = jnp.zeros_like(bias_ref)
        for at in range(2):
            count = refs[at].shape[0]
            cut = pl.ds(pl.multiple_of((w_at ^ at) * count, 128), count)
            tokens = token_ref[:, cut]
            terms = [matmul(tokens, refs[2 * at + kind][...]) for kind in range(2)]
            term = jnp.concatenate(terms, axis=1)
            both = term if both is None else both + term
            bias_ref[0:2, cut] = refs[4 + at][0:2, :].astype(F32)
        turn = lax.rem(width - z_at * part, width)
        bias = pltpu.roll(bias_ref[...], turn, 1)[:, :part]
        head_dim = width // HEADS
        pieces = []
        for head in range(part // head_dim):
            pieces.append(jnp.zeros((1, head_dim), F32))
            pieces.append(bias[1:2, head * head_dim : (head + 1) * head_dim])
        both = both + jnp.concatenate(pieces + [bias[0:1, :]], axis=1)
    else:
        both = matmul(token_ref[...], refs[0][...]) + refs[1][...]
    kv_ref[...] = both[:, :split].astype(BF16)
    scale = (part * ZS // HEADS) ** (-0.5)
    query_ref[...] = (both[:, split:].astype(BF16) * jnp.array(scale, BF16)).T
    turned_ref[...] = token_ref[...].T


def project(meta, first, second, sources):
    rows, width = first.shape
    part = width // ZS
    return small_call(
        partial(project_kernel, shared=len(sources) == 6),
        meta,
        (first, second, *sources),
        [((part, 2 * rows), BF16), ((2 * rows, 2 * part), BF16), ((width, 2 * rows), BF16)],
        [pltpu.VMEM((2 * rows, width), BF16), pltpu.VMEM((8, width), F32)],
        limit=40,
        name="project",
    )


def middle_kernel(meta_ref, tokens_ref, seed_ref, vec_ref, upoff_ref, *refs, groups, shared):
    mixed_refs = [refs[at * ZS : (at + 1) * ZS] for at in range(len(groups))]
    refs = refs[ZS * len(groups) :]
    weight_refs = refs[: 5 if shared else 3]
    refs = refs[len(weight_refs) :]
    outputs_ref, resid_ref = refs[:2]
    mgrad_refs = refs[2 : 2 + ZS]
    (
        send_ref,
        keep_ref,
        small_ref,
        out_w,
        up_w,
        down_w,
        slope_ref,
        wide_ref,
        tall_ref,
        sems,
    ) = refs[2 + ZS :]
    w_at, core, z_at = meta_ref[1], meta_ref[2], meta_ref[3]
    moves = [[], [], []]
    if shared:
        outs, ups, downs, got, pair = weight_refs
        count_o, count_u, count_d = outs.shape[0], ups.shape[0], downs.shape[0]
        for kind, (source, target) in enumerate(((outs, out_w), (ups, up_w), (downs, down_w))):
            start = pl.multiple_of(w_at * source.shape[0], source.shape[0])
            moves[kind].append((source, target.at[pl.ds(start, source.shape[0]), :]))
        lanes = got.shape[1]
        for source, which in ((got, core), (pair, 1 - core)):
            half = count_o // 2
            start = pl.multiple_of(((1 - w_at) * 2 + which) * half, half)
            moves[0].append((source.at[pl.ds(0, half), :], out_w.at[pl.ds(start, half), :]))
            low = half
            start = pl.multiple_of((1 - w_at) * count_u, count_u)
            for block in range(up_w.shape[1] // 2 // lanes):
                lane = pl.multiple_of(which * (up_w.shape[1] // 2) + block * lanes, 128)
                moves[1].append(
                    (
                        source.at[pl.ds(low, count_u), :],
                        up_w.at[pl.ds(start, count_u), pl.ds(lane, lanes)],
                    )
                )
                low += count_u
            half = count_d // 2
            start = pl.multiple_of(((1 - w_at) * 2 + which) * half, half)
            moves[2].append((source.at[pl.ds(low, half), :], down_w.at[pl.ds(start, half), :]))
    else:
        for kind, pair in enumerate(zip(weight_refs, (out_w, up_w, down_w))):
            moves[kind].append(pair)
    copies = []
    at = 0
    for kind in range(3):
        made = []
        for source, target in moves[kind]:
            made.append(pltpu.make_async_copy(source, target, sems.at[at]))
            made[-1].start()
            at += 1
        copies.append(made)
    rows, width = tokens_ref.shape
    hidden = upoff_ref.shape[1]
    part = width // ZS
    head_dim = width // HEADS
    quarter = hidden // 4

    def mean(value):
        return jnp.mean(value, axis=-1, keepdims=True)

    def norm(value):
        centered = value - mean(value)
        scale = lax.rsqrt(mean(centered * centered) + 1e-12)
        return centered * scale, scale

    def norm_back(grad, normal, scale):
        return scale * (grad - mean(grad) - normal * mean(grad * normal))

    def column(value):
        return jnp.sum(value, axis=0, keepdims=True)

    normed_at = 2 * quarter
    mixed_at = normed_at + width
    branch_at = mixed_at + width
    act_at = 5 * quarter
    for (first, count), pieces in zip(groups, mixed_refs):
        size = count * head_dim
        for at in range(ZS):
            low = mixed_at + (z_at ^ at) * part + first * head_dim
            send_ref[pl.ds(pl.multiple_of(low, head_dim), size), :] = pieces[at][...]
    mixed = send_ref[mixed_at:branch_at, :].T
    for copy in copies[0]:
        copy.wait()
    first_n, first_r = norm(tokens_ref[...] + (matmul(mixed, out_w[...]) + vec_ref[2:3, :]))
    normed = first_n * vec_ref[3:4, :] + vec_ref[4:5, :]
    low = normed.astype(BF16)
    send_ref[normed_at:mixed_at, :] = low.T
    for copy in copies[1] + copies[2]:
        copy.wait()
    quarters = []
    for half in range(2):
        for kept in (False, True):
            at = half * 2 * quarter + (core if kept else 1 - core) * quarter
            quarters.append((half, kept, pl.multiple_of(at, quarter)))
    acc = None
    for at, (half, kept, start) in enumerate(quarters):
        cut = pl.ds(start, quarter)
        pre_act = matmul(low, up_w[:, cut]) + upoff_ref[:, cut]
        phi = 0.5 + 0.5 * lax.erf(pre_act * (0.5**0.5))
        act = (pre_act * phi).astype(BF16)
        slope_ref[:, at * quarter : (at + 1) * quarter] = phi + pre_act * (
            jnp.exp(-0.5 * pre_act * pre_act) * 0.3989422804014327
        )
        target, base = (keep_ref, 0) if kept else (send_ref, act_at)
        target[base + half * quarter : base + (half + 1) * quarter, :] = act.T
        term = matmul(act, down_w[cut, :])
        acc = term if acc is None else acc + term
    second_n, second_r = norm(normed + (acc + vec_ref[5:6, :]))
    outputs_ref[...] = second_n * vec_ref[6:7, :] + vec_ref[7:8, :]
    place = lax.broadcasted_iota(jnp.int32, (rows, 1), 0)
    seed = jnp.where(place < meta_ref[0], seed_ref[...], 0.0)
    sum_grad = norm_back(seed * vec_ref[6:7, :], second_n, second_r)
    ffn = sum_grad.astype(BF16)
    for at in range(width // 256):
        low_row = act_at + 2 * quarter + at * rows
        send_ref[low_row : low_row + rows, :] = ffn[:, at * 256 : (at + 1) * 256]
    small_ref[3:4, :] = column(ffn.astype(F32))
    small_ref[4:5, :] = column(seed * second_n)
    small_ref[5:6, :] = column(seed)
    acc = sum_grad
    for at, (half, kept, start) in enumerate(quarters):
        cut = pl.ds(start, quarter)
        pre = right_trans(ffn, down_w[cut, :]) * slope_ref[:, at * quarter : (at + 1) * quarter]
        pre = pre.astype(BF16)
        target, base = (keep_ref, 2 * quarter) if kept else (send_ref, 0)
        for block in range(quarter // 256):
            row = base + (half * (quarter // 256) + block) * rows
            target[row : row + rows, :] = pre[:, block * 256 : (block + 1) * 256]
        sums = column(pre.astype(F32))
        line = 8 + half * (2 * quarter // width) + (core if kept else 1 - core)
        small_ref[pl.ds(line, 1), :] = sums
        acc = acc + right_trans(pre, up_w[:, cut])
    small_ref[1:2, :] = column(acc * first_n)
    small_ref[2:3, :] = column(acc)
    resid = norm_back(acc * vec_ref[3:4, :], first_n, first_r)
    resid_ref[...] = resid
    branch = resid.astype(BF16)
    wide_ref[...] = branch
    side = width // 2
    for target, base, which in (
        (send_ref, branch_at, 1 - core),
        (keep_ref, 4 * quarter, core),
    ):
        values = wide_ref[:, pl.ds(pl.multiple_of(which * side, 128), side)]
        target[base : base + rows, :] = values[:, :256]
        target[base + rows : base + 2 * rows, : side - 256] = values[:, 256:]
        target[base + rows : base + 2 * rows, side - 256 :] = jnp.zeros(
            (rows, 512 - side), BF16
        )
    small_ref[0:1, :] = column(branch.astype(F32))
    small_ref[6:8, :] = jnp.zeros((2, width), F32)
    small_ref[12:16, :] = jnp.zeros((4, width), F32)
    gap = branch_at + 2 * rows
    send_ref[gap:act_at, :] = jnp.zeros((act_at - gap, 256), BF16)
    tall_ref[...] = right_trans(out_w[...], branch).astype(BF16)
    for at in range(ZS):
        start = pl.multiple_of((z_at ^ at) * part, part)
        mgrad_refs[at][...] = tall_ref[pl.ds(start, part), :]


def middle(meta, mixed, groups, tokens, seed, vec, upoff, weights):
    rows, width = tokens.shape
    hidden = upoff.shape[1]
    in_vmem = pl.BlockSpec(memory_space=pltpu.VMEM)
    in_place = pl.BlockSpec(memory_space=pl.ANY)
    flat = [item for group in mixed for item in group]
    part = jax.ShapeDtypeStruct((width // ZS, rows), BF16)
    return pl.pallas_call(
        partial(middle_kernel, groups=groups, shared=len(weights) == 5),
        grid_spec=pltpu.PrefetchScalarGridSpec(
            num_scalar_prefetch=1,
            grid=(),
            in_specs=[in_vmem] * (4 + len(flat)) + [in_place] * len(weights),
            out_specs=[in_vmem] * (5 + ZS),
            scratch_shapes=[
                pltpu.VMEM((width, width), BF16),
                pltpu.VMEM((width, hidden), BF16),
                pltpu.VMEM((hidden, width), BF16),
                pltpu.VMEM((rows, hidden), F32),
                pltpu.VMEM((rows, width), BF16),
                pltpu.VMEM((width, rows), BF16),
                pltpu.SemaphoreType.DMA((11,)),
            ],
        ),
        out_shape=[jax.ShapeDtypeStruct((rows, width), F32)] * 2
        + [part] * ZS
        + [
            jax.ShapeDtypeStruct((2 * hidden, 256), BF16),
            jax.ShapeDtypeStruct((hidden + 2 * rows, 256), BF16),
            jax.ShapeDtypeStruct((16, width), F32),
        ],
        compiler_params=pltpu.CompilerParams(vmem_limit_bytes=VMEM_LIMIT),
        cost_estimate=work(15),
        name="middle",
    )(meta, tokens, seed, vec, upoff, *flat, *weights)


def down_kernel(meta_ref, keep_ref, got_ref, own_ffn_ref, got_ffn_ref, out_ref):
    keep, got = keep_ref[...], got_ref[...]
    rows = keep.shape[1]
    for at in range(out_ref.shape[1] // 256):
        cut = slice(at * rows, (at + 1) * rows)
        value = matmul(keep, own_ffn_ref[cut, :]) + matmul(got, got_ffn_ref[cut, :])
        out_ref[:, at * 256 : (at + 1) * 256] = value.astype(BF16)


def down_slab(meta, keep, send, got):
    block = send.shape[0] // 8
    kept = pl.BlockSpec((block, send.shape[1]), lambda i, m: (m[0], 0))
    act = pl.BlockSpec((block, send.shape[1]), lambda i, m: (5 + m[0], 0))
    ffn = pl.BlockSpec((block, send.shape[1]), lambda i, m: (7, 0))
    return pl.pallas_call(
        down_kernel,
        grid_spec=pltpu.PrefetchScalarGridSpec(
            num_scalar_prefetch=1,
            grid=(1,),
            in_specs=[kept, act, ffn, ffn],
            out_specs=pl.BlockSpec((block, block), lambda i, m: (0, 0)),
        ),
        out_shape=jax.ShapeDtypeStruct((block, block), BF16),
        compiler_params=pltpu.CompilerParams(vmem_limit_bytes=24 << 20),
        cost_estimate=work(2),
        name="down_slab",
    )(meta, keep, got, send, got)


def up_kernel(meta_ref, keep_ref, send_ref, got_ref, own_small_ref, got_small_ref, *refs):
    out_refs, table_ref = refs[:2], refs[2]
    rows = send_ref.shape[1]
    width = own_small_ref.shape[1]
    block = width // 4
    side = width // 2
    normed_at = 2 * width
    branch_at = normed_at + 2 * width
    x_at = meta_ref[0]
    pre_keep = 2 * width
    for w in range(2):
        small = own_small_ref[...] + got_small_ref[...]
        table_ref[...] = jnp.zeros_like(table_ref)
        for at in range(side // 128):
            low = w * side + at * 128
            table_ref[at * 8 : (at + 1) * 8, :] = small[:8, low : low + 128]
        base = side // 128 * 8
        for at in range(2 * width // 128):
            line = 8 + 2 * w + at // (width // 128)
            low = at % (width // 128) * 128
            table_ref[base + at : base + at + 1, :] = small[line : line + 1, low : low + 128]
        for out_ref, which in zip(out_refs, (1 - x_at, x_at)):
            start = pl.multiple_of(which * block, block)
            target = slice(w * block, (w + 1) * block)
            own = send_ref[pl.ds(normed_at + w * side + start, block), :]
            got = got_ref[pl.ds(normed_at + w * side + start, block), :]
            for at in range(normed_at // rows):
                cut = slice(at * rows, (at + 1) * rows)
                value = matmul(own, keep_ref[pre_keep + at * rows : pre_keep + (at + 1) * rows, :])
                value = value + matmul(got, got_ref[cut, :])
                out_ref[target, at * 256 : (at + 1) * 256] = value.astype(BF16)
            own = send_ref[pl.ds(normed_at + width + w * side + start, block), :]
            got = got_ref[pl.ds(normed_at + width + w * side + start, block), :]
            lane = normed_at // rows * 256
            for at in range(2):
                mine = 4 * width + at * rows
                theirs = branch_at + at * rows
                value = matmul(own, keep_ref[mine : mine + rows, :])
                value = value + matmul(got, got_ref[theirs : theirs + rows, :])
                value = value[:, : min(256, side - at * 256)].astype(BF16)
                out_ref[target, lane : lane + value.shape[1]] = value
                lane += value.shape[1]
            out_ref[target, lane : lane + 128] = table_ref[pl.ds(start, block), :].astype(BF16)


def up_slabs(meta, keep, send, got, own_small, got_small):
    width = own_small.shape[1]
    columns = 2 * width + width // 2 + 128
    first = pl.BlockSpec((5 * width, send.shape[1]), lambda i, m: (0, 0))

    def whole(value):
        return pl.BlockSpec(value.shape, lambda i, m: (0, 0))

    return pl.pallas_call(
        up_kernel,
        grid_spec=pltpu.PrefetchScalarGridSpec(
            num_scalar_prefetch=1,
            grid=(1,),
            in_specs=[whole(keep), first, first, whole(own_small), whole(own_small)],
            out_specs=[pl.BlockSpec((width // 2, columns), lambda i, m: (0, 0))] * 2,
            scratch_shapes=[pltpu.VMEM((width // 2, 128), F32)],
        ),
        out_shape=[jax.ShapeDtypeStruct((width // 2, columns), BF16)] * 2,
        compiler_params=pltpu.CompilerParams(vmem_limit_bytes=40 << 20),
        cost_estimate=work(4),
        name="up_slabs",
    )(meta, keep, send, got, own_small, got_small)


def key_sum_kernel(own_ref, core_ref, got_ref, *out_refs):
    size = out_refs[0].shape[1]
    for at, ref in enumerate(out_refs):
        cut = slice(at * size, (at + 1) * size)
        kept = (own_ref[cut, :].astype(F32) + core_ref[cut, :].astype(F32)).astype(BF16)
        ref[...] = (kept.astype(F32) + got_ref[cut, :].astype(F32)).astype(BF16).T


def key_sum(own, core, got):
    rows, columns = got.shape
    half = pl.BlockSpec((rows, columns), lambda i: (0, 0))
    return pl.pallas_call(
        key_sum_kernel,
        grid=(1,),
        in_specs=[half] * 3,
        out_specs=[pl.BlockSpec((columns, rows // ZS), lambda i: (0, 0))] * ZS,
        out_shape=[jax.ShapeDtypeStruct((columns, rows // ZS), BF16)] * ZS,
        compiler_params=pltpu.CompilerParams(vmem_limit_bytes=24 << 20),
        cost_estimate=work(2),
        name="key_sum",
    )(own, core, got)


def head_kernel(meta_ref, *refs):
    turned_refs, query_refs, kv_refs = refs[:2], refs[2 : 2 + ZS], refs[2 + ZS : 2 + 2 * ZS]
    refs = refs[2 + 2 * ZS :]
    out_ref = refs[-1]
    block = turned_refs[0].shape[0]

    def put(value, rows):
        if len(refs) == 2:
            value = value + refs[0][rows, :].astype(F32)
        out_ref[rows, :] = value.astype(BF16)

    grads = [jnp.concatenate([ref[...] for ref in items], axis=1) for items in (query_refs, kv_refs)]
    grads = jnp.concatenate(grads, axis=0)
    turned = jnp.concatenate([ref[...] for ref in turned_refs], axis=1)
    put(right_trans(turned, grads), slice(0, block))
    ones = jnp.ones((16, turned.shape[1]), BF16)
    put(right_trans(ones, grads), slice(block, block + 16))


def head_slab(meta, turned, query, kv, count, slabs, got=None, first=0):
    width, rows = turned[0].shape
    block = width // count
    columns = query[0].shape[0] + kv[0].shape[0]
    return pl.pallas_call(
        head_kernel,
        grid_spec=pltpu.PrefetchScalarGridSpec(
            num_scalar_prefetch=1,
            grid=(slabs,),
            in_specs=[pl.BlockSpec((block, rows), lambda i, m: (m[i] * 2 + m[slabs], 0))] * 2
            + [pl.BlockSpec(item.shape, lambda i, m: (0, 0)) for item in [*query, *kv]]
            + (
                []
                if got is None
                else [pl.BlockSpec((block + 16, columns), lambda i, m: (first + i, 0))]
            ),
            out_specs=pl.BlockSpec((block + 16, columns), lambda i, m: (i, 0)),
        ),
        out_shape=jax.ShapeDtypeStruct((slabs * (block + 16), columns), BF16),
        compiler_params=pltpu.CompilerParams(vmem_limit_bytes=24 << 20),
        cost_estimate=work(2),
        name="head_slab",
    )(meta, *turned, *query, *kv, *(() if got is None else (got,)))


def token_kernel(meta_ref, resid_ref, *refs, shared):
    query_refs, kv_refs, refs = refs[:ZS], refs[ZS : 2 * ZS], refs[2 * ZS :]
    weight_refs, refs = refs[: 5 if shared else 3], refs[5 if shared else 3 :]
    out_ref, full_ref, turned_ref, sems = refs
    w_at, c_at, z_at = meta_ref[1], meta_ref[2], meta_ref[3]
    width = full_ref.shape[1]
    moves = []
    if shared:
        count = weight_refs[0].shape[0]
        half = count // 2
        for kind in range(3):
            start = pl.multiple_of(w_at * count, count)
            moves.append((weight_refs[kind], full_ref.at[kind, pl.ds(start, count), :]))
            for ref, core in ((weight_refs[3], c_at), (weight_refs[4], 1 - c_at)):
                start = pl.multiple_of(((1 - w_at) * 2 + core) * half, half)
                moves.append(
                    (
                        ref.at[pl.ds(kind * half, half), :],
                        full_ref.at[kind, pl.ds(start, half), :],
                    )
                )
    else:
        for kind in range(3):
            moves.append((weight_refs[kind], full_ref.at[kind]))
    copies = []
    for at, (source, target) in enumerate(moves):
        copies.append(pltpu.make_async_copy(source, target, sems.at[at]))
        copies[-1].start()
    part = width // ZS
    head_dim = width // HEADS
    for at in range(ZS):
        low = (z_at ^ at) * part
        turned_ref[0, pl.ds(pl.multiple_of(low, part), part), :] = query_refs[at][...]
        for head in range(part // head_dim):
            start = pl.ds(pl.multiple_of(low + head * head_dim, head_dim), head_dim)
            for kind in (1, 2):
                row = (2 * head + kind - 1) * head_dim
                turned_ref[kind, start, :] = kv_refs[at][row : row + head_dim, :]
    parts = [turned_ref[kind].T for kind in range(3)]
    for copy in copies:
        copy.wait()
    out = resid_ref[...]
    for kind in range(3):
        out = out + right_trans(parts[kind], full_ref[kind])
    out_ref[...] = out


def token_gradient(meta, resid, query, kv, weights):
    rows, width = resid.shape
    in_vmem = pl.BlockSpec(memory_space=pltpu.VMEM)
    in_place = pl.BlockSpec(memory_space=pl.ANY)
    return pl.pallas_call(
        partial(token_kernel, shared=len(weights) == 5),
        grid_spec=pltpu.PrefetchScalarGridSpec(
            num_scalar_prefetch=1,
            grid=(),
            in_specs=[in_vmem] * (1 + 2 * ZS) + [in_place] * len(weights),
            out_specs=in_vmem,
            scratch_shapes=[
                pltpu.VMEM((3, width, width), BF16),
                pltpu.VMEM((3, width, rows), BF16),
                pltpu.SemaphoreType.DMA((9,)),
            ],
        ),
        out_shape=jax.ShapeDtypeStruct((rows, width), F32),
        compiler_params=pltpu.CompilerParams(vmem_limit_bytes=32 << 20),
        cost_estimate=work(4),
        name="token_gradient",
    )(meta, resid, *query, *kv, *weights)


def down_finish_kernel(meta_ref, *refs):
    block = refs[0].shape[0] // 4
    c_at, x_at = meta_ref[0], meta_ref[1]
    for at in range(4):
        for z in range(4):
            place = (c_at ^ (at >> 1)) * 8 + z * 2 + (x_at ^ (at & 1))
            start = pl.multiple_of(place * block, 8)
            refs[4][pl.ds(start, block), :] = refs[at][z * block : (z + 1) * block, :].astype(F32)


def down_finish(meta, pieces):
    block, width = pieces[0].shape
    in_vmem = pl.BlockSpec(memory_space=pltpu.VMEM)
    return pl.pallas_call(
        down_finish_kernel,
        grid_spec=pltpu.PrefetchScalarGridSpec(
            num_scalar_prefetch=1, grid=(), in_specs=[in_vmem] * 4, out_specs=in_vmem
        ),
        out_shape=jax.ShapeDtypeStruct((4 * block, width), F32),
        compiler_params=pltpu.CompilerParams(vmem_limit_bytes=32 << 20),
        cost_estimate=work(4),
        name="down_finish",
    )(meta, *pieces)


def up_finish_kernel(meta_ref, *refs):
    pieces = refs[:4]
    up_ref, out_ref, small_ref = refs[4:]
    block = pieces[0].shape[0]
    quarter = up_ref.shape[1] // 4
    side = out_ref.shape[1] // 2
    c_at, x_at = meta_ref[0], meta_ref[1]
    for at in range(4):
        start = pl.multiple_of((x_at ^ (at & 1)) * block, 8)
        rows = pl.ds(start, block)
        core = c_at ^ (at >> 1)
        for half in range(2):
            lanes = pl.ds(pl.multiple_of((2 * half + core) * quarter, 128), quarter)
            up_ref[rows, lanes] = pieces[at][:, half * quarter : (half + 1) * quarter].astype(F32)
        out_ref[rows, pl.ds(pl.multiple_of(core * side, 128), side)] = (
            pieces[at][:, 2 * quarter : 2 * quarter + side].astype(F32)
        )
        if at < 2:
            small_ref[rows, :] = pieces[at][:, 2 * quarter + side :].astype(F32)


def up_finish(meta, pieces, hidden, width):
    block = pieces[0].shape[0]
    in_vmem = pl.BlockSpec(memory_space=pltpu.VMEM)
    shapes = [(2 * block, hidden), (2 * block, width), (2 * block, 128)]
    return pl.pallas_call(
        up_finish_kernel,
        grid_spec=pltpu.PrefetchScalarGridSpec(
            num_scalar_prefetch=1,
            grid=(),
            in_specs=[in_vmem] * 4,
            out_specs=[in_vmem] * 3,
        ),
        out_shape=[jax.ShapeDtypeStruct(shape, F32) for shape in shapes],
        compiler_params=pltpu.CompilerParams(vmem_limit_bytes=40 << 20),
        cost_estimate=work(5),
        name="up_finish",
    )(meta, *pieces)


def head_finish_kernel(meta_ref, own_ref, got_ref, query_ref, key_ref, value_ref, bias_ref, *, part):
    size = own_ref.shape[0] // ZS
    block = size - 16
    head_dim = part // 3
    for at, source in enumerate((own_ref, got_ref)):
        start = pl.multiple_of((meta_ref[0] ^ at) * block, 8)
        rows = pl.ds(start, block)
        keys, values, queries = [], [], []
        for z in range(ZS):
            item = source[((z & 1) * 2 + (z >> 1)) * size :][:size].astype(F32)
            for head in range(3):
                low = part + head * 2 * head_dim
                keys.append(item[:, low : low + head_dim])
                values.append(item[:, low + head_dim : low + 2 * head_dim])
            queries.append(item[:, :part])
        key = jnp.concatenate(keys, axis=1)
        value = jnp.concatenate(values, axis=1)
        query = jnp.concatenate(queries, axis=1)
        query_ref[rows, :] = query[:block]
        key_ref[rows, :] = key[:block]
        value_ref[rows, :] = value[:block]
        if at == 0:
            bias_ref[0:8, :] = query[block : block + 8]
            bias_ref[8:16, :] = value[block : block + 8]


def head_finish(meta, own, got):
    rows, columns = own.shape
    rows = 2 * (rows // ZS - 16)
    width = ZS * columns // 3
    return small_call(
        partial(head_finish_kernel, part=columns // 3),
        meta,
        (own, got),
        [((rows, width), F32)] * 3 + [((16, width), F32)],
        limit=40,
        name="head_finish",
    )


def in_order(index, own, other, axis):
    return jnp.where(
        index == 0,
        jnp.concatenate([own, other], axis=axis),
        jnp.concatenate([other, own], axis=axis),
    )


def part_of(value, index, count, axis):
    size = value.shape[axis] // count
    return lax.dynamic_slice_in_dim(value, index * size, size, axis)


def body(
    inputs,
    lengths,
    cotangent,
    query_weight,
    query_bias,
    key_weight,
    value_weight,
    value_bias,
    output_weight,
    output_bias,
    first_gain,
    first_shift,
    up_weight,
    up_bias,
    down_weight,
    down_bias,
    second_gain,
    second_shift,
    *,
    sizes,
):
    count_o, count_w = sizes
    w_at = lax.axis_index("w")
    z_at = lax.axis_index("z")
    c_at = lax.axis_index("c")
    x_at = lax.axis_index("x")
    o_at = lax.axis_index("o")
    tokens = inputs[0]
    local_rows, width = tokens.shape
    head_dim = width // HEADS
    heads = HEADS // ZS
    part = heads * head_dim
    length = lengths[0]

    hold = lax.optimization_barrier

    near = ((0, 1), (1, 0), (2, 3), (3, 2))
    far = ((0, 2), (2, 0), (1, 3), (3, 1))
    cross = ((0, 3), (3, 0), (1, 2), (2, 1))

    def exchange(pieces):
        return [pieces[0]] + [
            lax.ppermute(item, "z", perm) for item, perm in zip(pieces[1:], (near, far, cross))
        ]

    own_rows = query_weight.shape[0]
    big_weights = (output_weight, up_weight, down_weight)
    sides = jnp.stack([z_at, c_at]).astype(jnp.int32)
    low_tokens = tokens.astype(BF16)
    kv_own, query_own, *low_heads, head_pack = prepare(
        sides, (query_weight, key_weight, value_weight)
    )
    line_tokens = [low_tokens, lax.ppermute(low_tokens, "z", near)]
    line_tokens.append(lax.ppermute(low_tokens, "z", far))
    early = jnp.stack([query_bias, value_bias]).astype(BF16)
    late = jnp.stack(
        [
            item.reshape(-1, own_rows)[row]
            for item in (
                output_bias,
                first_gain,
                first_shift,
                down_bias,
                second_gain,
                second_shift,
                up_bias,
            )
            for row in range(item.shape[0] // own_rows)
        ]
    )
    if count_w == 2:
        kv_other, query_other, early_got = [
            swap(item, "w") for item in (kv_own, query_own, early)
        ]
        *low_weights, weight_pack = round_weights(sides, big_weights)
        kv_other, query_other, early_got, weight_pack, *line_tokens[1:3] = hold(
            (kv_other, query_other, early_got, weight_pack, *line_tokens[1:3])
        )
        weight_got = swap(weight_pack, "w")
        sources = (kv_own, query_own, kv_other, query_other, early, early_got)
    else:
        attn_own = jnp.concatenate([kv_own, query_own], axis=1)
        attn_full = lax.all_gather(attn_own, "w", axis=0, tiled=True)
        small = jnp.concatenate([early, late.astype(BF16)], axis=0)
        small_all = lax.all_gather(small, "w", axis=0, tiled=False)
        low_weights = [item.astype(BF16) for item in big_weights]
        weight_got = [lax.all_gather(item, "w", axis=0, tiled=True) for item in low_weights]
        head_weights = [lax.all_gather(item, "w", axis=0, tiled=True) for item in low_heads]
        pair = jnp.transpose(small_all[:, :2], (1, 0, 2)).reshape(2, width).astype(F32)
        own_bias = lax.dynamic_slice_in_dim(pair, z_at * part, part, 1)
        value_bias_own = own_bias[1].reshape(heads, 1, head_dim)
        kv_bias = jnp.concatenate([jnp.zeros_like(value_bias_own), value_bias_own], axis=1)
        bias_row = jnp.concatenate([kv_bias.reshape(1, 2 * part), own_bias[:1]], axis=1)
        sources = (attn_full, bias_row)

    line_tokens.append(lax.ppermute(line_tokens[2], "z", near))
    corner = jnp.stack([w_at, z_at]).astype(jnp.int32)
    made = [project(corner, *line_tokens[:2], sources)]
    made[0], *line_tokens[2:] = hold((made[0], *line_tokens[2:]))
    made.append(project(corner, *line_tokens[2:], sources))
    queries = [item[0] for item in made]
    turned = [item[2] for item in made]
    kv_blocks = [[item[1] for item in made]]
    for axis in ("x", "c", "o")[: 3 if count_o == 2 else 2]:
        kv_blocks = kv_blocks + [[swap(item, axis) for item in pair] for pair in kv_blocks]
    places = []
    for at in range(4 * count_o):
        o_of = o_at ^ (at >> 2)
        places.append(o_of * 16 + (x_at ^ (at & 1)) * 2 + (c_at ^ ((at >> 1) & 1)))
    meta = jnp.stack([length, z_at] + places).astype(jnp.int32)
    kv_blocks = [
        [pltpu.with_memory_space_constraint(item, pltpu.MemorySpace.HBM) for item in pair]
        for pair in kv_blocks
    ]
    attended, *made = attend_forward(meta, queries, kv_blocks, heads)
    logs = made[ZS]
    if count_w == 2:
        attended, weight_got, head_pack, late = hold((attended, weight_got, head_pack, late))
        late = late.astype(BF16)
        small_own = jnp.concatenate([early, late], axis=0)
        small_got = jnp.concatenate([early_got, swap(late, "w")], axis=0)
        small_all = in_order(w_at, small_own[None], small_got[None], 0)
        weights = [*low_weights, weight_got, swap(weight_got, "c")]
        head_got = swap(head_pack, "w")
    else:
        weights = weight_got
    mixed = exchange(made[:ZS])
    small_all = small_all.astype(F32)
    vec = jnp.transpose(small_all[:, :8], (1, 0, 2)).reshape(8, width)
    up_offset = small_all[:, 8:].reshape(1, -1)

    split = count_w == 2 and count_o == 1
    my_index = o_at * 16 + z_at * 4 + x_at * 2 + c_at
    rest = jnp.clip(length - my_index * local_rows, 0, local_rows)
    core = c_at if split else jnp.zeros_like(c_at)
    spots = jnp.stack([rest, w_at, core, z_at]).astype(jnp.int32)
    outputs, resid_grad, *made = middle(
        spots, [mixed], ((0, heads),), tokens, cotangent[0], vec, up_offset, weights
    )
    head_grads = exchange(made[:ZS])
    send, keep, small_own = made[ZS:]
    hidden = up_offset.shape[1]

    near_bit, far_bit = z_at & 1, z_at >> 1

    def add_pair(kept, got):
        return (kept.astype(F32) + got.astype(F32)).astype(BF16)

    def join(value, got, bit):
        return in_order(bit, value, got, 0)

    spot = jnp.stack([c_at, x_at]).astype(jnp.int32)
    token = [spot]

    def arrive(*values):
        token[0], *values = hold((token[0], *values))
        return values[0] if len(values) == 1 else values

    def backward(first, count, made=()):
        return attend_backward(
            meta, queries, head_grads, attended, logs, kv_blocks, first, count, made
        )

    def to_near(value):
        return lax.ppermute(value, "z", near)

    def to_far(value):
        return lax.ppermute(value, "z", far)

    def head_part(ws, core, got=None, first=0):
        at = jnp.stack([jnp.asarray(item) for item in (*ws, core)]).astype(jnp.int32)
        return head_slab(at, turned, query_low, kv_low, 2 * count_w, len(ws), got, first)

    def pick(w, c):
        return jnp.stack([jnp.asarray(w), jnp.asarray(c)]).astype(jnp.int32)

    if split:
        got, small_got = swap(send, "c"), swap(small_own, "c")
        down_far = down_slab(pick(1 - w_at, 0), keep, send, got)
        up_sent, up_kept = up_slabs(
            jnp.stack([x_at]).astype(jnp.int32), keep, send, got, small_own, small_got
        )
        down_near = down_slab(pick(1 * w_at, 0), keep, send, got)
        down_far, up_sent, down_near, *head_grads = hold(
            (down_far, up_sent, down_near, *head_grads)
        )
        made = backward(0, heads - 1)
        down_got, *made = arrive(swap(down_far, "w"), *made)
        down_sum = add_pair(down_near, down_got)
        down_got = to_near(part_of(down_sum, 1 - near_bit, 2, 0))
        down_sum, *head_grads = arrive(down_sum, *head_grads)
        made = backward(heads - 1, 1, made)
        down_got, up_got, head_got, *made = arrive(
            down_got, swap(up_sent, "x"), head_got, *made
        )
        query_low, pairs = made[:ZS], made[ZS:]
        head_weights = [*low_heads, head_got, swap(head_got, "c")]
        pair_got = swap(pairs[1], "c")
        query_got = exchange(query_low)
        down_sum = add_pair(part_of(down_sum, near_bit, 2, 0), down_got)
        down_got = to_far(part_of(down_sum, 1 - far_bit, 2, 0))
        up_sum = add_pair(up_kept, up_got).reshape(2, own_rows // 2, -1)
        up_got = swap(lax.dynamic_index_in_dim(up_sum, 1 - w_at, 0, keepdims=False), "w")
        pair_got = arrive(pair_got)
        half_rows = pair_got.shape[0] // 2
        pair_sent = add_pair(pairs[0][half_rows:], pair_got[half_rows:])
        pair_sent = arrive(pair_sent)
        key_got = swap(pair_sent, "x")
        key_got, down_got, up_got, *query_got = arrive(key_got, down_got, up_got, *query_got)
        kv_low = key_sum(pairs[0], pair_got, key_got)
        down_sum = add_pair(part_of(down_sum, far_bit, 2, 0), down_got)
        down_got = swap(part_of(down_sum, 1 - x_at, 2, 0), "x")
        up_sum = add_pair(lax.dynamic_index_in_dim(up_sum, w_at, 0, keepdims=False), up_got)
        up_got = to_near(part_of(up_sum, 1 - near_bit, 2, 0))
        head_core = swap(head_part((1 - w_at, 1 * w_at), 1 - c_at), "c")
        kv_got = exchange(kv_low)
        down_got = arrive(down_got)
        down_sum = add_pair(part_of(down_sum, x_at, 2, 0), down_got)
        down_got = to_far(down_sum)
        head_core = arrive(head_core)
        head_sent = swap(head_part((1 - w_at,), c_at, head_core), "w")
        head_sum = head_part((1 * w_at,), c_at, head_core, 1)
        up_got = arrive(up_got)
        up_sum = add_pair(part_of(up_sum, near_bit, 2, 0), up_got)
        up_got = to_far(part_of(up_sum, 1 - far_bit, 2, 0))
        head_sent = arrive(head_sent)
        head_sum = add_pair(head_sum, head_sent)
        head_got = swap(head_sum, "x")
        kv_got = arrive(*kv_got)
        input_grad = token_gradient(
            spots, resid_grad, query_got, kv_got, head_weights
        )
        up_got = arrive(up_got)
        up_sum = add_pair(part_of(up_sum, far_bit, 2, 0), up_got)
        up_got = to_far(up_sum)
        down_got = arrive(down_got)
        down_sum = join(down_sum[None], down_got[None], far_bit)
        down_got = to_near(down_sum)
        head_got = arrive(head_got)
        head_sum = add_pair(head_sum, head_got)
        head_got = to_far(head_sum)
        up_got = arrive(up_got)
        up_sum = join(up_sum, up_got, far_bit)
        up_got = to_near(up_sum)
        down_got = arrive(down_got)
        down_sum = join(down_sum[None], down_got[None], near_bit)
        down_sum = down_sum.reshape(-1, width)
        down_x = swap(down_sum, "x")
        down_c = swap(down_sum, "c")
        head_got = arrive(head_got)
        head_two = join(head_sum, head_got, far_bit)
        head_got = to_near(head_two)
        up_got = arrive(up_got)
        up_sum = join(up_sum, up_got, near_bit)
        up_x = swap(up_sum, "x")
        up_c = swap(up_sum, "c")
        down_x, input_grad = arrive(down_x, input_grad)
        down_pieces = [down_sum, down_x, down_c, swap(down_x, "c")]
        head_got = arrive(head_got)
        head_four = join(head_two, head_got, near_bit)
        head_other = swap(head_four, "c")
        total_down = down_finish(spot, down_pieces)
        up_x, total_down = arrive(up_x, total_down)
        up_pieces = [up_sum, up_x, up_c, swap(up_x, "c")]
        total_query, total_key, total_value, head_bias = head_finish(
            spot, head_four, head_other
        )
        total_query, total_key, total_value = arrive(total_query, total_key, total_value)
        total_up, total_out, table = up_finish(token[0], up_pieces, hidden, width)
        groups = own_rows // 128
        small_total = table[: 8 * groups].reshape(groups, 8, 128)
        vectors = [small_total[:, at].reshape(own_rows) for at in range(6)]
        lines = hidden // count_w // 128
        total_up_bias = table[8 * groups : 8 * groups + lines].reshape(-1)
    else:
        made = backward(0, heads)
        query_low, pairs = made[:ZS], made[ZS:]
        if count_o == 2:
            pairs = [plus(spot, pairs[at], swap(pairs[at + 2], "o")) for at in range(2)]
        pair_got = swap(pairs[1], "c")
        half_rows = pair_got.shape[0] // 2
        key_got = swap(plus(spot, pairs[0], pair_got, half_rows), "x")
        kv_low = key_sum(pairs[0], pair_got, key_got)
        if count_w == 2:
            head_weights = [*low_heads, head_got, swap(head_got, "c")]
        input_grad = token_gradient(
            spots.at[2].set(c_at.astype(jnp.int32)),
            resid_grad,
            exchange(query_low),
            exchange(kv_low),
            head_weights,
        )
        every_w = tuple(range(count_w))
        slabs = head_part(every_w, c_at, swap(head_part(every_w, 1 - c_at), "c"))
        head_sum = lax.psum_scatter(slabs, "w", scatter_dimension=0, tiled=True)
        head_sum = plus(spot, head_sum, swap(head_sum, "x"))
        if count_o == 2:
            head_sum = plus(spot, head_sum, swap(head_sum, "o"))
        n_bit, f_bit = [
            jnp.stack([bit, bit]).astype(jnp.int32) for bit in (near_bit, far_bit)
        ]
        head_sum = unite(f_bit, head_sum, to_far(head_sum))
        head_sum = unite(n_bit, head_sum, to_near(head_sum))
        total_query, total_key, total_value, head_bias = head_finish(
            spot, head_sum, swap(head_sum, "c")
        )
        quarter = hidden // 4
        count = quarter // 256
        act_at = 5 * quarter
        act = [keep[:quarter], send[act_at : act_at + quarter], keep[quarter : 2 * quarter]]
        act += [send[act_at + quarter : act_at + 2 * quarter]]
        act = jnp.concatenate(act, axis=0)

        def rows_of(value, low, at):
            return value[low + at * local_rows : low + (at + 1) * local_rows]

        ffn_at = act_at + 2 * quarter
        ffn = jnp.concatenate([rows_of(send, ffn_at, at) for at in range(width // 256)], axis=1)
        pre = []
        for half in range(2):
            pre += [rows_of(keep, 2 * quarter, half * count + at) for at in range(count)]
            pre += [rows_of(send, 0, half * count + at) for at in range(count)]
        pre = jnp.concatenate(pre, axis=1)
        normed_turned = send[2 * quarter : 2 * quarter + width]
        mixed_turned = send[2 * quarter + width : 2 * quarter + 2 * width]
        side = width // 2
        branch = jnp.concatenate(
            [
                rows_of(keep, 4 * quarter, 0),
                rows_of(keep, 4 * quarter, 1)[:, : side - 256],
                rows_of(send, 2 * quarter + 2 * width, 0),
                rows_of(send, 2 * quarter + 2 * width, 1)[:, : side - 256],
            ],
            axis=1,
        )

        def sum_all(value):
            value = value.astype(BF16)
            value = lax.psum_scatter(value, "w", scatter_dimension=0, tiled=True)
            return lax.psum(value, ("o", "z", "x", "c")).astype(F32)

        total_down = sum_all(matmul(act, ffn))
        total_up = sum_all(matmul(normed_turned, pre))
        total_out = sum_all(matmul(mixed_turned, branch))
        small_own = lax.psum(small_own, ("o", "z", "x", "c", "w"))
        vectors = [part_of(small_own[at], w_at, count_w, 0) for at in range(6)]
        total_up_bias = part_of(small_own[8:12].reshape(-1), w_at, count_w, 0)

    totals = [part_of(head_bias[at], w_at, count_w, 0) for at in (0, 8)] + vectors
    return (
        outputs[None],
        input_grad[None],
        total_query,
        totals[0],
        total_key,
        total_value,
        totals[1],
        total_out,
        totals[2],
        totals[3],
        totals[4],
        total_up,
        total_up_bias,
        total_down,
        totals[5],
        totals[6],
        totals[7],
    )


def solution(mesh):
    count_s = mesh.shape["seq"]
    count_w = mesh.shape["wshard"]
    count_o = count_s // 16
    fine = Mesh(
        mesh.devices.reshape(count_o, ZS, 2, 2, count_w), ("o", "z", "x", "c", "w")
    )
    seq = ("o", "z", "x", "c")
    rows = P("w", seq, None)
    matrix = P("w", None)
    vector = P("w")
    placed = (
        rows,
        vector,
        rows,
        matrix,
        vector,
        matrix,
        matrix,
        vector,
        matrix,
        vector,
        vector,
        vector,
        matrix,
        vector,
        matrix,
        vector,
        vector,
        vector,
    )
    return jax.shard_map(
        partial(body, sizes=(count_o, count_w)),
        mesh=fine,
        in_specs=placed,
        out_specs=(
            rows,
            rows,
            matrix,
            vector,
            matrix,
            matrix,
            vector,
            matrix,
            vector,
            vector,
            vector,
            matrix,
            vector,
            matrix,
            vector,
            vector,
            vector,
        ),
        check_vma=False,
    )
```

```python
from functools import partial

import jax
import jax.numpy as jnp
from jax import lax
from jax.experimental import pallas as pl
from jax.experimental.pallas import tpu as pltpu
from jax.sharding import Mesh, PartitionSpec as P

HEADS = 12
ZS = 4
NEG_FILL = -1e30
VMEM_LIMIT = 60 << 20
SWAP = ((0, 1), (1, 0))
F32 = jnp.float32
BF16 = jnp.bfloat16


def matmul(left_side, right_side):
    return jnp.dot(left_side, right_side, preferred_element_type=F32)


def right_trans(left_side, right_side):
    return lax.dot_general(
        left_side, right_side, (((1,), (1,)), ((), ())), preferred_element_type=F32
    )


def work(units):
    return pl.CostEstimate(flops=int(units * 1e3), bytes_accessed=1, transcendentals=0)


def swap(value, axis):
    return lax.ppermute(value, axis, SWAP)


def touched_groups(length, rows, outer):
    group = 4 * rows
    left = length - outer * (ZS * group)
    return jnp.clip((left + group - 1) // group, 0, ZS)


def with_mask(kv, place, length):
    at = place + lax.broadcasted_iota(jnp.int32, kv.shape, 0)
    lane = lax.broadcasted_iota(jnp.int32, kv.shape, 1)
    fill = jnp.where(at < length, 0.0, jnp.where(lane == 0, NEG_FILL, 0.0))
    return jnp.concatenate([kv, fill.astype(BF16)], axis=1)


def load_head(kv_refs, rows_ref, turned_ref, low):
    head_dim = turned_ref.shape[1]
    for at, ref in enumerate(kv_refs):
        block, half = at // 2, at % 2
        size = ref.shape[0]
        for start in range(0, size, 256):
            value = ref[start : start + 256, :]
            place = slice(half * size + start, half * size + start + 256)
            rows_ref[block, place, :] = value
            turned_ref[block, :, place] = value.T[low : low + head_dim, :]


def forward_kernel(meta_ref, *refs, blocks, rows):
    query_refs, kv_refs = refs[:2], refs[2 : 2 + 2 * blocks]
    out_ref, *refs = refs[2 + 2 * blocks :]
    piece_refs, (log_ref, rows_ref, turned_ref) = refs[:ZS], refs[ZS:]
    head_dim, query_count = out_ref.shape
    length, z_at = meta_ref[0], meta_ref[1]
    load_head(kv_refs, rows_ref, turned_ref, head_dim)
    query = jnp.concatenate([ref[...] for ref in query_refs], axis=1)
    query = jnp.concatenate(
        [
            query,
            jnp.zeros((head_dim, query_count), BF16),
            jnp.ones((128, query_count), BF16),
        ],
        axis=0,
    )

    def step(group, carry, members):
        top, total, acc = carry
        start = pl.multiple_of((group ^ z_at) * rows, rows)
        found = []
        for block in members:
            place = (meta_ref[2 + block] + group * 4) * rows
            kv = with_mask(rows_ref[block, pl.ds(start, rows), :], place, length)
            found.append(matmul(kv, query))
        new_top = top
        for scores in found:
            new_top = jnp.maximum(new_top, jnp.max(scores, axis=0, keepdims=True))
        fade = jnp.exp(top - new_top)
        total = total * fade
        acc = acc * fade
        for block, scores in zip(members, found):
            weights = jnp.exp(scores - new_top)
            total = total + jnp.sum(weights, axis=0, keepdims=True)
            acc = acc + matmul(
                turned_ref[block, :, pl.ds(start, rows)], weights.astype(BF16)
            )
        return new_top, total, acc

    carry = (
        jnp.full((1, query_count), NEG_FILL, F32),
        jnp.zeros((1, query_count), F32),
        jnp.zeros((head_dim, query_count), F32),
    )
    for first in range(0, blocks, 4):
        members = tuple(range(first, first + 4))
        count = touched_groups(length, rows, meta_ref[2 + first] // 16)
        carry = lax.fori_loop(0, count, lambda g, c: step(g, c, members), carry)
    top, total, acc = carry
    out = acc * (1.0 / total)
    out_ref[...] = out
    size = query_count // ZS
    for at in range(ZS):
        piece_refs[at][...] = out[:, at * size : (at + 1) * size].astype(BF16)
    log_ref[0] = top + jnp.log(total)


def attend_forward(meta, queries, kv_blocks, heads):
    blocks = len(kv_blocks)
    half_rows = kv_blocks[0][0].shape[0]
    part, half_count = queries[0].shape
    head_dim, query_count = part // heads, 2 * half_count
    size = query_count // ZS
    return pl.pallas_call(
        partial(forward_kernel, blocks=blocks, rows=2 * half_rows // ZS),
        grid_spec=pltpu.PrefetchScalarGridSpec(
            num_scalar_prefetch=1,
            grid=(heads,),
            in_specs=[pl.BlockSpec((head_dim, half_count), lambda i, m: (i, 0))] * 2
            + [pl.BlockSpec((half_rows, 128), lambda i, m: (0, i))] * (2 * blocks),
            out_specs=[pl.BlockSpec((head_dim, query_count), lambda i, m: (i, 0))]
            + [pl.BlockSpec((head_dim, size), lambda i, m: (i, 0))] * ZS
            + [pl.BlockSpec((1, 1, query_count), lambda i, m: (i, 0, 0))],
            scratch_shapes=[
                pltpu.VMEM((blocks, 2 * half_rows, 128), BF16),
                pltpu.VMEM((blocks, head_dim, 2 * half_rows), BF16),
            ],
        ),
        out_shape=[jax.ShapeDtypeStruct((part, query_count), F32)]
        + [jax.ShapeDtypeStruct((part, size), BF16)] * ZS
        + [jax.ShapeDtypeStruct((heads, 1, query_count), F32)],
        compiler_params=pltpu.CompilerParams(vmem_limit_bytes=VMEM_LIMIT),
        cost_estimate=work(8 * heads),
        name="attend_forward",
    )(meta, *queries, *[item for pair in kv_blocks for item in pair])


def backward_kernel(meta_ref, *refs, blocks, rows, extra):
    query_refs, (out_ref, log_ref), refs = refs[:2], refs[2:4], refs[4:]
    grad_refs, kv_refs = refs[:ZS], refs[ZS : ZS + 2 * blocks]
    refs = refs[ZS + 2 * blocks + extra :]
    dq_refs, pairs = refs[:ZS], refs[ZS : ZS + blocks // 2]
    rows_ref, turned_ref, qn_ref, gn_ref, acc_ref = refs[ZS + blocks // 2 :]
    head_dim, query_count = out_ref.shape
    length, z_at = meta_ref[0], meta_ref[1]
    block_rows = ZS * rows
    load_head(kv_refs, rows_ref, turned_ref, 0)
    query = jnp.concatenate([ref[...] for ref in query_refs], axis=1)
    grads = jnp.concatenate([ref[...] for ref in grad_refs], axis=1)
    blank = jnp.zeros((head_dim, query_count), BF16)
    query = jnp.concatenate([query, blank], axis=0)
    grad = jnp.concatenate([blank, grads], axis=0)
    qn_ref[...] = query.T
    gn_ref[...] = grad.T
    query = jnp.concatenate([query, jnp.ones((128, query_count), BF16)], axis=0)
    delta = jnp.sum(grads.astype(F32) * out_ref[...], axis=0, keepdims=True)
    log_sum = log_ref[0]
    acc_ref[...] = jnp.zeros_like(acc_ref)

    def put(block, start, value):
        pairs[block // 2][pl.ds(start + (block & 1) * block_rows, rows), :] = value

    def step(group, members):
        start = pl.multiple_of((group ^ z_at) * rows, rows)
        for block in members:
            kv = rows_ref[block, pl.ds(start, rows), :]
            place = (meta_ref[2 + block] + group * 4) * rows
            scores = matmul(with_mask(kv, place, length), query)
            prob_grad = matmul(kv, grad)
            prob = jnp.exp(scores - log_sum)
            score_grad = (prob * (prob_grad - delta)).astype(BF16)
            value = matmul(prob.astype(BF16), gn_ref[...]) + matmul(score_grad, qn_ref[...])
            put(block, start, value.astype(BF16))
            acc_ref[...] += matmul(turned_ref[block, :, pl.ds(start, rows)], score_grad)

    def clear(group, members):
        start = pl.multiple_of((group ^ z_at) * rows, rows)
        for block in members:
            put(block, start, jnp.zeros((rows, 128), BF16))

    def loop(low, high, fn):
        def one(group, carry):
            fn(group)
            return carry

        lax.fori_loop(low, high, one, 0)

    for first in range(0, blocks, 4):
        members = tuple(range(first, first + 4))
        count = touched_groups(length, rows, meta_ref[2 + first] // 16)
        loop(0, count, lambda g: step(g, members))
        loop(count, ZS, lambda g: clear(g, members))
    dq = (acc_ref[...] * head_dim ** (-0.5)).astype(BF16)
    size = query_count // ZS
    for at in range(ZS):
        dq_refs[at][...] = dq[:, at * size : (at + 1) * size]


def attend_backward(meta, queries, grads, out, log_sum, kv_blocks, first, count, made=()):
    blocks = len(kv_blocks)
    half_rows, columns = kv_blocks[0][0].shape
    heads = columns // 128
    part, half_count = queries[0].shape
    head_dim, query_count = part // heads, 2 * half_count
    size = query_count // ZS
    piece = pl.BlockSpec((head_dim, size), lambda i, m: (i + first, 0))
    ins = [
        *queries,
        out,
        log_sum,
        *grads,
        *[item for pair in kv_blocks for item in pair],
        *made,
    ]
    return pl.pallas_call(
        partial(backward_kernel, blocks=blocks, rows=2 * half_rows // ZS, extra=len(made)),
        grid_spec=pltpu.PrefetchScalarGridSpec(
            num_scalar_prefetch=1,
            grid=(count,),
            in_specs=[pl.BlockSpec((head_dim, half_count), lambda i, m: (i + first, 0))] * 2
            + [
                pl.BlockSpec((head_dim, query_count), lambda i, m: (i + first, 0)),
                pl.BlockSpec((1, 1, query_count), lambda i, m: (i + first, 0, 0)),
            ]
            + [piece] * ZS
            + [pl.BlockSpec((half_rows, 128), lambda i, m: (0, i + first))] * (2 * blocks)
            + [pl.BlockSpec(memory_space=pl.ANY)] * len(made),
            out_specs=[piece] * ZS
            + [pl.BlockSpec((4 * half_rows, 128), lambda i, m: (0, i + first))] * (blocks // 2),
            scratch_shapes=[
                pltpu.VMEM((blocks, 2 * half_rows, 128), BF16),
                pltpu.VMEM((blocks, head_dim, 2 * half_rows), BF16),
                pltpu.VMEM((query_count, 128), BF16),
                pltpu.VMEM((query_count, 128), BF16),
                pltpu.VMEM((head_dim, query_count), F32),
            ],
        ),
        out_shape=[jax.ShapeDtypeStruct((part, size), BF16)] * ZS
        + [jax.ShapeDtypeStruct((4 * half_rows, columns), BF16)] * (blocks // 2),
        input_output_aliases={
            1 + len(ins) - len(made) + at: at for at in range(len(made))
        },
        compiler_params=pltpu.CompilerParams(vmem_limit_bytes=VMEM_LIMIT),
        cost_estimate=work(12 * count),
        name="attend_backward",
    )(meta, *ins)


IN_VMEM = pl.BlockSpec(memory_space=pltpu.VMEM)


def small_call(kernel, meta, values, shapes, scratch=(), limit=32, name=None):
    return pl.pallas_call(
        kernel,
        grid_spec=pltpu.PrefetchScalarGridSpec(
            num_scalar_prefetch=1,
            grid=(),
            in_specs=[IN_VMEM] * len(values),
            out_specs=[IN_VMEM] * len(shapes),
            scratch_shapes=list(scratch),
        ),
        out_shape=[jax.ShapeDtypeStruct(shape, kind) for shape, kind in shapes],
        compiler_params=pltpu.CompilerParams(vmem_limit_bytes=limit << 20),
        cost_estimate=work(1),
        name=name,
    )(meta, *values)


def fold_kernel(meta_ref, kept_ref, got_ref, keep_ref, sent_ref, sum_ref):
    sum_ref[...] = (kept_ref[...].astype(F32) + got_ref[...].astype(F32)).astype(BF16)
    rows = keep_ref.shape[0]
    for at, ref in enumerate((keep_ref, sent_ref)):
        start = pl.multiple_of((meta_ref[0] ^ at) * rows, 16)
        ref[...] = sum_ref[pl.ds(start, rows), :]


def fold(bit, kept, got):
    rows, columns = kept.shape
    half = ((rows // 2, columns), BF16)
    return small_call(
        fold_kernel,
        bit,
        (kept, got),
        [half, half],
        [pltpu.VMEM((rows, columns), BF16)],
        name="fold",
    )


def unite_kernel(meta_ref, own_ref, got_ref, out_ref):
    rows = own_ref.shape[0]
    for at, ref in enumerate((own_ref, got_ref)):
        start = pl.multiple_of((meta_ref[0] ^ at) * rows, 16)
        out_ref[pl.ds(start, rows), :] = ref[...]


def unite(bit, own, got):
    rows, columns = own.shape
    return small_call(
        unite_kernel, bit, (own, got), [((2 * rows, columns), BF16)], name="unite"
    )[0]


def plus_kernel(meta_ref, one_ref, two_ref, out_ref, *, low):
    cut = slice(low, low + out_ref.shape[0])
    out_ref[...] = (one_ref[cut, :].astype(F32) + two_ref[cut, :].astype(F32)).astype(BF16)


def plus(meta, one, two, low=0):
    rows, columns = one.shape
    return small_call(
        partial(plus_kernel, low=low),
        meta,
        (one, two),
        [((rows - low, columns), BF16)],
        name="plus",
    )[0]


def prepare_kernel(meta_ref, *refs):
    sources, refs = refs[:3], refs[3:]
    kv_ref, query_ref, low_refs, head_ref = refs[0], refs[1], refs[2:5], refs[5]
    places, sems = refs[6:9], refs[9]
    copies = []
    for at in range(3):
        copies.append(pltpu.make_async_copy(sources[at], places[at], sems.at[at]))
        copies[-1].start()
    z_at, c_at = meta_ref[0], meta_ref[1]
    width = places[0].shape[1]
    part = width // ZS
    head_dim = width // HEADS
    parts = []
    for kind in range(3):
        ref = places[kind]
        copies[kind].wait()
        value = ref[...]
        low_refs[kind][...] = value.astype(BF16)
        half = ref.shape[0] // 2
        rows = ref[pl.ds(pl.multiple_of(c_at * half, half), half), :]
        head_ref[kind * half : (kind + 1) * half, :] = rows.astype(BF16)
        turn = lax.rem(width - z_at * part, width)
        parts.append(pltpu.roll(value, turn, 1)[:, :part])
    columns = []
    for head in range(part // head_dim):
        cut = slice(head * head_dim, (head + 1) * head_dim)
        columns += [parts[1][:, cut], parts[2][:, cut]]
    kv_ref[...] = jnp.concatenate(columns, axis=1).astype(BF16)
    query_ref[...] = parts[0].astype(BF16)


def prepare(meta, weights):
    count, width = weights[0].shape
    shapes = [(count, 2 * width // ZS), (count, width // ZS)] + [(count, width)] * 3
    shapes.append((3 * count // 2, width))
    return pl.pallas_call(
        prepare_kernel,
        grid_spec=pltpu.PrefetchScalarGridSpec(
            num_scalar_prefetch=1,
            grid=(),
            in_specs=[pl.BlockSpec(memory_space=pltpu.MemorySpace.HBM)] * 3,
            out_specs=[IN_VMEM] * len(shapes),
            scratch_shapes=[pltpu.VMEM((count, width), F32)] * 3
            + [pltpu.SemaphoreType.DMA((3,))],
        ),
        out_shape=[jax.ShapeDtypeStruct(shape, BF16) for shape in shapes],
        compiler_params=pltpu.CompilerParams(vmem_limit_bytes=VMEM_LIMIT),
        cost_estimate=work(1),
        name="prepare",
    )(meta, *weights)


def round_kernel(meta_ref, out_w, up_w, down_w, low_out, low_up, low_down, pack_ref):
    core = meta_ref[1]
    for source, target in ((out_w, low_out), (up_w, low_up), (down_w, low_down)):
        target[...] = source[...].astype(BF16)
    width = pack_ref.shape[1]
    low = 0
    half = out_w.shape[0] // 2
    rows = pl.ds(pl.multiple_of(core * half, half), half)
    pack_ref[low : low + half, :] = out_w[rows, :].astype(BF16)
    low += half
    count = up_w.shape[1] // 2
    for block in range(count // width):
        lanes = pl.ds(pl.multiple_of(core * count + block * width, 128), width)
        pack_ref[low : low + up_w.shape[0], :] = up_w[:, lanes].astype(BF16)
        low += up_w.shape[0]
    half = down_w.shape[0] // 2
    rows = pl.ds(pl.multiple_of(core * half, half), half)
    pack_ref[low : low + half, :] = down_w[rows, :].astype(BF16)


def round_weights(meta, weights):
    out_w, up_w, down_w = weights
    width = out_w.shape[1]
    total = out_w.shape[0] // 2 + up_w.shape[0] * (up_w.shape[1] // 2 // width)
    total += down_w.shape[0] // 2
    return small_call(
        round_kernel,
        meta,
        weights,
        [(item.shape, BF16) for item in weights] + [((total, width), BF16)],
        limit=60,
        name="round_weights",
    )


def project_kernel(meta_ref, first_ref, second_ref, *refs, shared):
    query_ref, kv_ref, turned_ref, token_ref, bias_ref = refs[-5:]
    part = query_ref.shape[0]
    rows, width = first_ref.shape
    split = 2 * part
    token_ref[:rows, :] = first_ref[...]
    token_ref[rows:, :] = second_ref[...]
    if shared:
        w_at, z_at = meta_ref[0], meta_ref[1]
        both = None
        bias_ref[...] = jnp.zeros_like(bias_ref)
        for at in range(2):
            count = refs[at].shape[0]
            cut = pl.ds(pl.multiple_of((w_at ^ at) * count, 128), count)
            tokens = token_ref[:, cut]
            terms = [matmul(tokens, refs[2 * at + kind][...]) for kind in range(2)]
            term = jnp.concatenate(terms, axis=1)
            both = term if both is None else both + term
            bias_ref[0:2, cut] = refs[4 + at][0:2, :].astype(F32)
        turn = lax.rem(width - z_at * part, width)
        bias = pltpu.roll(bias_ref[...], turn, 1)[:, :part]
        head_dim = width // HEADS
        pieces = []
        for head in range(part // head_dim):
            pieces.append(jnp.zeros((1, head_dim), F32))
            pieces.append(bias[1:2, head * head_dim : (head + 1) * head_dim])
        both = both + jnp.concatenate(pieces + [bias[0:1, :]], axis=1)
    else:
        both = matmul(token_ref[...], refs[0][...]) + refs[1][...]
    kv_ref[...] = both[:, :split].astype(BF16)
    scale = (part * ZS // HEADS) ** (-0.5)
    query_ref[...] = (both[:, split:].astype(BF16) * jnp.array(scale, BF16)).T
    turned_ref[...] = token_ref[...].T


def project(meta, first, second, sources):
    rows, width = first.shape
    part = width // ZS
    return small_call(
        partial(project_kernel, shared=len(sources) == 6),
        meta,
        (first, second, *sources),
        [((part, 2 * rows), BF16), ((2 * rows, 2 * part), BF16), ((width, 2 * rows), BF16)],
        [pltpu.VMEM((2 * rows, width), BF16), pltpu.VMEM((8, width), F32)],
        limit=40,
        name="project",
    )


def middle_kernel(meta_ref, tokens_ref, seed_ref, vec_ref, upoff_ref, *refs, groups, shared):
    mixed_refs = [refs[at * ZS : (at + 1) * ZS] for at in range(len(groups))]
    refs = refs[ZS * len(groups) :]
    weight_refs = refs[: 5 if shared else 3]
    refs = refs[len(weight_refs) :]
    outputs_ref, resid_ref = refs[:2]
    mgrad_refs = refs[2 : 2 + ZS]
    (
        send_ref,
        keep_ref,
        small_ref,
        out_w,
        up_w,
        down_w,
        slope_ref,
        wide_ref,
        tall_ref,
        sems,
    ) = refs[2 + ZS :]
    w_at, core, z_at = meta_ref[1], meta_ref[2], meta_ref[3]
    moves = [[], [], []]
    if shared:
        outs, ups, downs, got, pair = weight_refs
        count_o, count_u, count_d = outs.shape[0], ups.shape[0], downs.shape[0]
        for kind, (source, target) in enumerate(((outs, out_w), (ups, up_w), (downs, down_w))):
            start = pl.multiple_of(w_at * source.shape[0], source.shape[0])
            moves[kind].append((source, target.at[pl.ds(start, source.shape[0]), :]))
        lanes = got.shape[1]
        for source, which in ((got, core), (pair, 1 - core)):
            half = count_o // 2
            start = pl.multiple_of(((1 - w_at) * 2 + which) * half, half)
            moves[0].append((source.at[pl.ds(0, half), :], out_w.at[pl.ds(start, half), :]))
            low = half
            start = pl.multiple_of((1 - w_at) * count_u, count_u)
            for block in range(up_w.shape[1] // 2 // lanes):
                lane = pl.multiple_of(which * (up_w.shape[1] // 2) + block * lanes, 128)
                moves[1].append(
                    (
                        source.at[pl.ds(low, count_u), :],
                        up_w.at[pl.ds(start, count_u), pl.ds(lane, lanes)],
                    )
                )
                low += count_u
            half = count_d // 2
            start = pl.multiple_of(((1 - w_at) * 2 + which) * half, half)
            moves[2].append((source.at[pl.ds(low, half), :], down_w.at[pl.ds(start, half), :]))
    else:
        for kind, pair in enumerate(zip(weight_refs, (out_w, up_w, down_w))):
            moves[kind].append(pair)
    copies = []
    at = 0
    for kind in range(3):
        made = []
        for source, target in moves[kind]:
            made.append(pltpu.make_async_copy(source, target, sems.at[at]))
            made[-1].start()
            at += 1
        copies.append(made)
    rows, width = tokens_ref.shape
    hidden = upoff_ref.shape[1]
    part = width // ZS
    head_dim = width // HEADS
    quarter = hidden // 4

    def mean(value):
        return jnp.mean(value, axis=-1, keepdims=True)

    def norm(value):
        centered = value - mean(value)
        scale = lax.rsqrt(mean(centered * centered) + 1e-12)
        return centered * scale, scale

    def norm_back(grad, normal, scale):
        return scale * (grad - mean(grad) - normal * mean(grad * normal))

    def column(value):
        return jnp.sum(value, axis=0, keepdims=True)

    normed_at = 2 * quarter
    mixed_at = normed_at + width
    branch_at = mixed_at + width
    act_at = 5 * quarter
    for (first, count), pieces in zip(groups, mixed_refs):
        size = count * head_dim
        for at in range(ZS):
            low = mixed_at + (z_at ^ at) * part + first * head_dim
            send_ref[pl.ds(pl.multiple_of(low, head_dim), size), :] = pieces[at][...]
    mixed = send_ref[mixed_at:branch_at, :].T
    for copy in copies[0]:
        copy.wait()
    first_n, first_r = norm(tokens_ref[...] + (matmul(mixed, out_w[...]) + vec_ref[2:3, :]))
    normed = first_n * vec_ref[3:4, :] + vec_ref[4:5, :]
    low = normed.astype(BF16)
    send_ref[normed_at:mixed_at, :] = low.T
    for copy in copies[1] + copies[2]:
        copy.wait()
    quarters = []
    for half in range(2):
        for kept in (False, True):
            at = half * 2 * quarter + (core if kept else 1 - core) * quarter
            quarters.append((half, kept, pl.multiple_of(at, quarter)))
    acc = None
    for at, (half, kept, start) in enumerate(quarters):
        cut = pl.ds(start, quarter)
        pre_act = matmul(low, up_w[:, cut]) + upoff_ref[:, cut]
        phi = 0.5 + 0.5 * lax.erf(pre_act * (0.5**0.5))
        act = (pre_act * phi).astype(BF16)
        slope_ref[:, at * quarter : (at + 1) * quarter] = phi + pre_act * (
            jnp.exp(-0.5 * pre_act * pre_act) * 0.3989422804014327
        )
        target, base = (keep_ref, 0) if kept else (send_ref, act_at)
        target[base + half * quarter : base + (half + 1) * quarter, :] = act.T
        term = matmul(act, down_w[cut, :])
        acc = term if acc is None else acc + term
    second_n, second_r = norm(normed + (acc + vec_ref[5:6, :]))
    outputs_ref[...] = second_n * vec_ref[6:7, :] + vec_ref[7:8, :]
    place = lax.broadcasted_iota(jnp.int32, (rows, 1), 0)
    seed = jnp.where(place < meta_ref[0], seed_ref[...], 0.0)
    sum_grad = norm_back(seed * vec_ref[6:7, :], second_n, second_r)
    ffn = sum_grad.astype(BF16)
    for at in range(width // 256):
        low_row = act_at + 2 * quarter + at * rows
        send_ref[low_row : low_row + rows, :] = ffn[:, at * 256 : (at + 1) * 256]
    small_ref[3:4, :] = column(ffn.astype(F32))
    small_ref[4:5, :] = column(seed * second_n)
    small_ref[5:6, :] = column(seed)
    acc = sum_grad
    for at, (half, kept, start) in enumerate(quarters):
        cut = pl.ds(start, quarter)
        pre = right_trans(ffn, down_w[cut, :]) * slope_ref[:, at * quarter : (at + 1) * quarter]
        pre = pre.astype(BF16)
        target, base = (keep_ref, 2 * quarter) if kept else (send_ref, 0)
        for block in range(quarter // 256):
            row = base + (half * (quarter // 256) + block) * rows
            target[row : row + rows, :] = pre[:, block * 256 : (block + 1) * 256]
        sums = column(pre.astype(F32))
        line = 8 + half * (2 * quarter // width) + (core if kept else 1 - core)
        small_ref[pl.ds(line, 1), :] = sums
        acc = acc + right_trans(pre, up_w[:, cut])
    small_ref[1:2, :] = column(acc * first_n)
    small_ref[2:3, :] = column(acc)
    resid = norm_back(acc * vec_ref[3:4, :], first_n, first_r)
    resid_ref[...] = resid
    branch = resid.astype(BF16)
    wide_ref[...] = branch
    side = width // 2
    for target, base, which in (
        (send_ref, branch_at, 1 - core),
        (keep_ref, 4 * quarter, core),
    ):
        values = wide_ref[:, pl.ds(pl.multiple_of(which * side, 128), side)]
        target[base : base + rows, :] = values[:, :256]
        target[base + rows : base + 2 * rows, : side - 256] = values[:, 256:]
        target[base + rows : base + 2 * rows, side - 256 :] = jnp.zeros(
            (rows, 512 - side), BF16
        )
    small_ref[0:1, :] = column(branch.astype(F32))
    small_ref[6:8, :] = jnp.zeros((2, width), F32)
    small_ref[12:16, :] = jnp.zeros((4, width), F32)
    gap = branch_at + 2 * rows
    send_ref[gap:act_at, :] = jnp.zeros((act_at - gap, 256), BF16)
    tall_ref[...] = right_trans(out_w[...], branch).astype(BF16)
    for at in range(ZS):
        start = pl.multiple_of((z_at ^ at) * part, part)
        mgrad_refs[at][...] = tall_ref[pl.ds(start, part), :]


def middle(meta, mixed, groups, tokens, seed, vec, upoff, weights):
    rows, width = tokens.shape
    hidden = upoff.shape[1]
    in_vmem = pl.BlockSpec(memory_space=pltpu.VMEM)
    in_place = pl.BlockSpec(memory_space=pl.ANY)
    flat = [item for group in mixed for item in group]
    part = jax.ShapeDtypeStruct((width // ZS, rows), BF16)
    return pl.pallas_call(
        partial(middle_kernel, groups=groups, shared=len(weights) == 5),
        grid_spec=pltpu.PrefetchScalarGridSpec(
            num_scalar_prefetch=1,
            grid=(),
            in_specs=[in_vmem] * (4 + len(flat)) + [in_place] * len(weights),
            out_specs=[in_vmem] * (5 + ZS),
            scratch_shapes=[
                pltpu.VMEM((width, width), BF16),
                pltpu.VMEM((width, hidden), BF16),
                pltpu.VMEM((hidden, width), BF16),
                pltpu.VMEM((rows, hidden), F32),
                pltpu.VMEM((rows, width), BF16),
                pltpu.VMEM((width, rows), BF16),
                pltpu.SemaphoreType.DMA((11,)),
            ],
        ),
        out_shape=[jax.ShapeDtypeStruct((rows, width), F32)] * 2
        + [part] * ZS
        + [
            jax.ShapeDtypeStruct((2 * hidden, 256), BF16),
            jax.ShapeDtypeStruct((hidden + 2 * rows, 256), BF16),
            jax.ShapeDtypeStruct((16, width), F32),
        ],
        compiler_params=pltpu.CompilerParams(vmem_limit_bytes=VMEM_LIMIT),
        cost_estimate=work(15),
        name="middle",
    )(meta, tokens, seed, vec, upoff, *flat, *weights)


def down_kernel(meta_ref, keep_ref, got_ref, own_ffn_ref, got_ffn_ref, out_ref):
    keep, got = keep_ref[...], got_ref[...]
    rows = keep.shape[1]
    for at in range(out_ref.shape[1] // 256):
        cut = slice(at * rows, (at + 1) * rows)
        value = matmul(keep, own_ffn_ref[cut, :]) + matmul(got, got_ffn_ref[cut, :])
        out_ref[:, at * 256 : (at + 1) * 256] = value.astype(BF16)


def down_slab(meta, keep, send, got):
    block = send.shape[0] // 8
    kept = pl.BlockSpec((block, send.shape[1]), lambda i, m: (m[0], 0))
    act = pl.BlockSpec((block, send.shape[1]), lambda i, m: (5 + m[0], 0))
    ffn = pl.BlockSpec((block, send.shape[1]), lambda i, m: (7, 0))
    return pl.pallas_call(
        down_kernel,
        grid_spec=pltpu.PrefetchScalarGridSpec(
            num_scalar_prefetch=1,
            grid=(1,),
            in_specs=[kept, act, ffn, ffn],
            out_specs=pl.BlockSpec((block, block), lambda i, m: (0, 0)),
        ),
        out_shape=jax.ShapeDtypeStruct((block, block), BF16),
        compiler_params=pltpu.CompilerParams(vmem_limit_bytes=24 << 20),
        cost_estimate=work(2),
        name="down_slab",
    )(meta, keep, got, send, got)


def up_kernel(meta_ref, keep_ref, send_ref, got_ref, own_small_ref, got_small_ref, *refs):
    out_refs, table_ref = refs[:2], refs[2]
    rows = send_ref.shape[1]
    width = own_small_ref.shape[1]
    block = width // 4
    side = width // 2
    normed_at = 2 * width
    branch_at = normed_at + 2 * width
    x_at = meta_ref[0]
    pre_keep = 2 * width
    for w in range(2):
        small = own_small_ref[...] + got_small_ref[...]
        table_ref[...] = jnp.zeros_like(table_ref)
        for at in range(side // 128):
            low = w * side + at * 128
            table_ref[at * 8 : (at + 1) * 8, :] = small[:8, low : low + 128]
        base = side // 128 * 8
        for at in range(2 * width // 128):
            line = 8 + 2 * w + at // (width // 128)
            low = at % (width // 128) * 128
            table_ref[base + at : base + at + 1, :] = small[line : line + 1, low : low + 128]
        for out_ref, which in zip(out_refs, (1 - x_at, x_at)):
            start = pl.multiple_of(which * block, block)
            target = slice(w * block, (w + 1) * block)
            own = send_ref[pl.ds(normed_at + w * side + start, block), :]
            got = got_ref[pl.ds(normed_at + w * side + start, block), :]
            for at in range(normed_at // rows):
                cut = slice(at * rows, (at + 1) * rows)
                value = matmul(own, keep_ref[pre_keep + at * rows : pre_keep + (at + 1) * rows, :])
                value = value + matmul(got, got_ref[cut, :])
                out_ref[target, at * 256 : (at + 1) * 256] = value.astype(BF16)
            own = send_ref[pl.ds(normed_at + width + w * side + start, block), :]
            got = got_ref[pl.ds(normed_at + width + w * side + start, block), :]
            lane = normed_at // rows * 256
            for at in range(2):
                mine = 4 * width + at * rows
                theirs = branch_at + at * rows
                value = matmul(own, keep_ref[mine : mine + rows, :])
                value = value + matmul(got, got_ref[theirs : theirs + rows, :])
                value = value[:, : min(256, side - at * 256)].astype(BF16)
                out_ref[target, lane : lane + value.shape[1]] = value
                lane += value.shape[1]
            out_ref[target, lane : lane + 128] = table_ref[pl.ds(start, block), :].astype(BF16)


def up_slabs(meta, keep, send, got, own_small, got_small):
    width = own_small.shape[1]
    columns = 2 * width + width // 2 + 128
    first = pl.BlockSpec((5 * width, send.shape[1]), lambda i, m: (0, 0))

    def whole(value):
        return pl.BlockSpec(value.shape, lambda i, m: (0, 0))

    return pl.pallas_call(
        up_kernel,
        grid_spec=pltpu.PrefetchScalarGridSpec(
            num_scalar_prefetch=1,
            grid=(1,),
            in_specs=[whole(keep), first, first, whole(own_small), whole(own_small)],
            out_specs=[pl.BlockSpec((width // 2, columns), lambda i, m: (0, 0))] * 2,
            scratch_shapes=[pltpu.VMEM((width // 2, 128), F32)],
        ),
        out_shape=[jax.ShapeDtypeStruct((width // 2, columns), BF16)] * 2,
        compiler_params=pltpu.CompilerParams(vmem_limit_bytes=40 << 20),
        cost_estimate=work(4),
        name="up_slabs",
    )(meta, keep, send, got, own_small, got_small)


def key_sum_kernel(own_ref, core_ref, got_ref, *out_refs):
    size = out_refs[0].shape[1]
    for at, ref in enumerate(out_refs):
        cut = slice(at * size, (at + 1) * size)
        kept = (own_ref[cut, :].astype(F32) + core_ref[cut, :].astype(F32)).astype(BF16)
        ref[...] = (kept.astype(F32) + got_ref[cut, :].astype(F32)).astype(BF16).T


def key_sum(own, core, got):
    rows, columns = got.shape
    half = pl.BlockSpec((rows, columns), lambda i: (0, 0))
    return pl.pallas_call(
        key_sum_kernel,
        grid=(1,),
        in_specs=[half] * 3,
        out_specs=[pl.BlockSpec((columns, rows // ZS), lambda i: (0, 0))] * ZS,
        out_shape=[jax.ShapeDtypeStruct((columns, rows // ZS), BF16)] * ZS,
        compiler_params=pltpu.CompilerParams(vmem_limit_bytes=24 << 20),
        cost_estimate=work(2),
        name="key_sum",
    )(own, core, got)


def head_kernel(meta_ref, *refs):
    turned_refs, query_refs, kv_refs = refs[:2], refs[2 : 2 + ZS], refs[2 + ZS : 2 + 2 * ZS]
    refs = refs[2 + 2 * ZS :]
    out_ref = refs[-1]
    block = turned_refs[0].shape[0]

    def put(value, rows):
        columns = value.shape[1]
        if len(refs) == 2:
            value = value + refs[0][rows, :columns].astype(F32)
        out_ref[rows, :columns] = value.astype(BF16)
        out_ref[rows, columns:] = jnp.zeros((value.shape[0], out_ref.shape[1] - columns), BF16)

    grads = [jnp.concatenate([ref[...] for ref in items], axis=1) for items in (query_refs, kv_refs)]
    grads = jnp.concatenate(grads, axis=0)
    turned = jnp.concatenate([ref[...] for ref in turned_refs], axis=1)
    put(right_trans(turned, grads), slice(0, block))
    ones = jnp.ones((16, turned.shape[1]), BF16)
    put(right_trans(ones, grads), slice(block, block + 16))


def head_slab(meta, turned, query, kv, count, slabs, got=None, first=0):
    width, rows = turned[0].shape
    block = width // count
    columns = -(-(query[0].shape[0] + kv[0].shape[0]) // 128) * 128
    return pl.pallas_call(
        head_kernel,
        grid_spec=pltpu.PrefetchScalarGridSpec(
            num_scalar_prefetch=1,
            grid=(slabs,),
            in_specs=[pl.BlockSpec((block, rows), lambda i, m: (m[i] * 2 + m[slabs], 0))] * 2
            + [pl.BlockSpec(item.shape, lambda i, m: (0, 0)) for item in [*query, *kv]]
            + (
                []
                if got is None
                else [pl.BlockSpec((block + 16, columns), lambda i, m: (first + i, 0))]
            ),
            out_specs=pl.BlockSpec((block + 16, columns), lambda i, m: (i, 0)),
        ),
        out_shape=jax.ShapeDtypeStruct((slabs * (block + 16), columns), BF16),
        compiler_params=pltpu.CompilerParams(vmem_limit_bytes=24 << 20),
        cost_estimate=work(2),
        name="head_slab",
    )(meta, *turned, *query, *kv, *(() if got is None else (got,)))


def token_kernel(meta_ref, resid_ref, *refs, shared):
    query_refs, kv_refs, refs = refs[:ZS], refs[ZS : 2 * ZS], refs[2 * ZS :]
    weight_refs, refs = refs[: 5 if shared else 3], refs[5 if shared else 3 :]
    out_ref, full_ref, turned_ref, sems = refs
    w_at, c_at, z_at = meta_ref[1], meta_ref[2], meta_ref[3]
    width = full_ref.shape[1]
    moves = []
    if shared:
        count = weight_refs[0].shape[0]
        half = count // 2
        for kind in range(3):
            start = pl.multiple_of(w_at * count, count)
            moves.append((weight_refs[kind], full_ref.at[kind, pl.ds(start, count), :]))
            for ref, core in ((weight_refs[3], c_at), (weight_refs[4], 1 - c_at)):
                start = pl.multiple_of(((1 - w_at) * 2 + core) * half, half)
                moves.append(
                    (
                        ref.at[pl.ds(kind * half, half), :],
                        full_ref.at[kind, pl.ds(start, half), :],
                    )
                )
    else:
        for kind in range(3):
            moves.append((weight_refs[kind], full_ref.at[kind]))
    copies = []
    for at, (source, target) in enumerate(moves):
        copies.append(pltpu.make_async_copy(source, target, sems.at[at]))
        copies[-1].start()
    part = width // ZS
    head_dim = width // HEADS
    for at in range(ZS):
        low = (z_at ^ at) * part
        turned_ref[0, pl.ds(pl.multiple_of(low, part), part), :] = query_refs[at][...]
        for head in range(part // head_dim):
            start = pl.ds(pl.multiple_of(low + head * head_dim, head_dim), head_dim)
            for kind in (1, 2):
                row = (2 * head + kind - 1) * head_dim
                turned_ref[kind, start, :] = kv_refs[at][row : row + head_dim, :]
    parts = [turned_ref[kind].T for kind in range(3)]
    for copy in copies:
        copy.wait()
    out = resid_ref[...]
    for kind in range(3):
        out = out + right_trans(parts[kind], full_ref[kind])
    out_ref[...] = out


def token_gradient(meta, resid, query, kv, weights):
    rows, width = resid.shape
    in_vmem = pl.BlockSpec(memory_space=pltpu.VMEM)
    in_place = pl.BlockSpec(memory_space=pl.ANY)
    return pl.pallas_call(
        partial(token_kernel, shared=len(weights) == 5),
        grid_spec=pltpu.PrefetchScalarGridSpec(
            num_scalar_prefetch=1,
            grid=(),
            in_specs=[in_vmem] * (1 + 2 * ZS) + [in_place] * len(weights),
            out_specs=in_vmem,
            scratch_shapes=[
                pltpu.VMEM((3, width, width), BF16),
                pltpu.VMEM((3, width, rows), BF16),
                pltpu.SemaphoreType.DMA((9,)),
            ],
        ),
        out_shape=jax.ShapeDtypeStruct((rows, width), F32),
        compiler_params=pltpu.CompilerParams(vmem_limit_bytes=32 << 20),
        cost_estimate=work(4),
        name="token_gradient",
    )(meta, resid, *query, *kv, *weights)


def down_finish_kernel(meta_ref, *refs):
    block = refs[0].shape[0] // 4
    c_at, x_at = meta_ref[0], meta_ref[1]
    for at in range(4):
        for z in range(4):
            place = (c_at ^ (at >> 1)) * 8 + z * 2 + (x_at ^ (at & 1))
            start = pl.multiple_of(place * block, 8)
            refs[4][pl.ds(start, block), :] = refs[at][z * block : (z + 1) * block, :].astype(F32)


def down_finish(meta, pieces):
    block, width = pieces[0].shape
    in_vmem = pl.BlockSpec(memory_space=pltpu.VMEM)
    return pl.pallas_call(
        down_finish_kernel,
        grid_spec=pltpu.PrefetchScalarGridSpec(
            num_scalar_prefetch=1, grid=(), in_specs=[in_vmem] * 4, out_specs=in_vmem
        ),
        out_shape=jax.ShapeDtypeStruct((4 * block, width), F32),
        compiler_params=pltpu.CompilerParams(vmem_limit_bytes=32 << 20),
        cost_estimate=work(4),
        name="down_finish",
    )(meta, *pieces)


def up_finish_kernel(meta_ref, *refs):
    pieces = refs[:4]
    up_ref, out_ref, small_ref = refs[4:]
    block = pieces[0].shape[0]
    quarter = up_ref.shape[1] // 4
    side = out_ref.shape[1] // 2
    c_at, x_at = meta_ref[0], meta_ref[1]
    for at in range(4):
        start = pl.multiple_of((x_at ^ (at & 1)) * block, 8)
        rows = pl.ds(start, block)
        core = c_at ^ (at >> 1)
        for half in range(2):
            lanes = pl.ds(pl.multiple_of((2 * half + core) * quarter, 128), quarter)
            up_ref[rows, lanes] = pieces[at][:, half * quarter : (half + 1) * quarter].astype(F32)
        out_ref[rows, pl.ds(pl.multiple_of(core * side, 128), side)] = (
            pieces[at][:, 2 * quarter : 2 * quarter + side].astype(F32)
        )
        if at < 2:
            small_ref[rows, :] = pieces[at][:, 2 * quarter + side :].astype(F32)


def up_finish(meta, pieces, hidden, width):
    block = pieces[0].shape[0]
    in_vmem = pl.BlockSpec(memory_space=pltpu.VMEM)
    shapes = [(2 * block, hidden), (2 * block, width), (2 * block, 128)]
    return pl.pallas_call(
        up_finish_kernel,
        grid_spec=pltpu.PrefetchScalarGridSpec(
            num_scalar_prefetch=1,
            grid=(),
            in_specs=[in_vmem] * 4,
            out_specs=[in_vmem] * 3,
        ),
        out_shape=[jax.ShapeDtypeStruct(shape, F32) for shape in shapes],
        compiler_params=pltpu.CompilerParams(vmem_limit_bytes=40 << 20),
        cost_estimate=work(5),
        name="up_finish",
    )(meta, *pieces)


def head_finish_kernel(meta_ref, own_ref, got_ref, query_ref, key_ref, value_ref, bias_ref, *, part):
    size = own_ref.shape[0] // ZS
    block = size - 16
    head_dim = part // 3
    for at, source in enumerate((own_ref, got_ref)):
        start = pl.multiple_of((meta_ref[0] ^ at) * block, 8)
        rows = pl.ds(start, block)
        keys, values, queries = [], [], []
        for z in range(ZS):
            item = source[((z & 1) * 2 + (z >> 1)) * size :][:size].astype(F32)
            for head in range(3):
                low = part + head * 2 * head_dim
                keys.append(item[:, low : low + head_dim])
                values.append(item[:, low + head_dim : low + 2 * head_dim])
            queries.append(item[:, :part])
        key = jnp.concatenate(keys, axis=1)
        value = jnp.concatenate(values, axis=1)
        query = jnp.concatenate(queries, axis=1)
        query_ref[rows, :] = query[:block]
        key_ref[rows, :] = key[:block]
        value_ref[rows, :] = value[:block]
        if at == 0:
            bias_ref[0:8, :] = query[block : block + 8]
            bias_ref[8:16, :] = value[block : block + 8]


def head_finish(meta, own, got, width):
    rows = own.shape[0]
    rows = 2 * (rows // ZS - 16)
    return small_call(
        partial(head_finish_kernel, part=width // ZS),
        meta,
        (own, got),
        [((rows, width), F32)] * 3 + [((16, width), F32)],
        limit=40,
        name="head_finish",
    )


def in_order(index, own, other, axis):
    return jnp.where(
        index == 0,
        jnp.concatenate([own, other], axis=axis),
        jnp.concatenate([other, own], axis=axis),
    )


def part_of(value, index, count, axis):
    size = value.shape[axis] // count
    return lax.dynamic_slice_in_dim(value, index * size, size, axis)


def body(
    inputs,
    lengths,
    cotangent,
    query_weight,
    query_bias,
    key_weight,
    value_weight,
    value_bias,
    output_weight,
    output_bias,
    first_gain,
    first_shift,
    up_weight,
    up_bias,
    down_weight,
    down_bias,
    second_gain,
    second_shift,
    *,
    sizes,
):
    count_o, count_w = sizes
    w_at = lax.axis_index("w")
    z_at = lax.axis_index("z")
    c_at = lax.axis_index("c")
    x_at = lax.axis_index("x")
    o_at = lax.axis_index("o")
    tokens = inputs[0]
    local_rows, width = tokens.shape
    head_dim = width // HEADS
    heads = HEADS // ZS
    part = heads * head_dim
    length = lengths[0]

    hold = lax.optimization_barrier

    near = ((0, 1), (1, 0), (2, 3), (3, 2))
    far = ((0, 2), (2, 0), (1, 3), (3, 1))
    cross = ((0, 3), (3, 0), (1, 2), (2, 1))

    def exchange(pieces):
        return [pieces[0]] + [
            lax.ppermute(item, "z", perm) for item, perm in zip(pieces[1:], (near, far, cross))
        ]

    own_rows = query_weight.shape[0]
    big_weights = (output_weight, up_weight, down_weight)
    sides = jnp.stack([z_at, c_at]).astype(jnp.int32)
    low_tokens = tokens.astype(BF16)
    kv_own, query_own, *low_heads, head_pack = prepare(
        sides, (query_weight, key_weight, value_weight)
    )
    line_tokens = [low_tokens, lax.ppermute(low_tokens, "z", near)]
    line_tokens.append(lax.ppermute(low_tokens, "z", far))
    early = jnp.stack([query_bias, value_bias]).astype(BF16)
    late = jnp.stack(
        [
            item.reshape(-1, own_rows)[row]
            for item in (
                output_bias,
                first_gain,
                first_shift,
                down_bias,
                second_gain,
                second_shift,
                up_bias,
            )
            for row in range(item.shape[0] // own_rows)
        ]
    )
    if count_w == 2:
        kv_other, query_other, early_got = [
            swap(item, "w") for item in (kv_own, query_own, early)
        ]
        *low_weights, weight_pack = round_weights(sides, big_weights)
        kv_other, query_other, early_got, weight_pack, *line_tokens[1:3] = hold(
            (kv_other, query_other, early_got, weight_pack, *line_tokens[1:3])
        )
        weight_got = swap(weight_pack, "w")
        sources = (kv_own, query_own, kv_other, query_other, early, early_got)
    else:
        attn_own = jnp.concatenate([kv_own, query_own], axis=1)
        attn_full = lax.all_gather(attn_own, "w", axis=0, tiled=True)
        small = jnp.concatenate([early, late.astype(BF16)], axis=0)
        small_all = lax.all_gather(small, "w", axis=0, tiled=False)
        low_weights = [item.astype(BF16) for item in big_weights]
        weight_got = [lax.all_gather(item, "w", axis=0, tiled=True) for item in low_weights]
        head_weights = [lax.all_gather(item, "w", axis=0, tiled=True) for item in low_heads]
        pair = jnp.transpose(small_all[:, :2], (1, 0, 2)).reshape(2, width).astype(F32)
        own_bias = lax.dynamic_slice_in_dim(pair, z_at * part, part, 1)
        value_bias_own = own_bias[1].reshape(heads, 1, head_dim)
        kv_bias = jnp.concatenate([jnp.zeros_like(value_bias_own), value_bias_own], axis=1)
        bias_row = jnp.concatenate([kv_bias.reshape(1, 2 * part), own_bias[:1]], axis=1)
        sources = (attn_full, bias_row)

    line_tokens.append(lax.ppermute(line_tokens[2], "z", near))
    corner = jnp.stack([w_at, z_at]).astype(jnp.int32)
    made = [project(corner, *line_tokens[:2], sources)]
    made[0], *line_tokens[2:] = hold((made[0], *line_tokens[2:]))
    made.append(project(corner, *line_tokens[2:], sources))
    queries = [item[0] for item in made]
    turned = [item[2] for item in made]
    kv_blocks = [[item[1] for item in made]]
    for axis in ("x", "c", "o")[: 3 if count_o == 2 else 2]:
        kv_blocks = kv_blocks + [[swap(item, axis) for item in pair] for pair in kv_blocks]
    places = []
    for at in range(4 * count_o):
        o_of = o_at ^ (at >> 2)
        places.append(o_of * 16 + (x_at ^ (at & 1)) * 2 + (c_at ^ ((at >> 1) & 1)))
    meta = jnp.stack([length, z_at] + places).astype(jnp.int32)
    kv_blocks = [
        [pltpu.with_memory_space_constraint(item, pltpu.MemorySpace.HBM) for item in pair]
        for pair in kv_blocks
    ]
    attended, *made = attend_forward(meta, queries, kv_blocks, heads)
    logs = made[ZS]
    if count_w == 2:
        attended, weight_got, head_pack, late = hold((attended, weight_got, head_pack, late))
        late = late.astype(BF16)
        small_own = jnp.concatenate([early, late], axis=0)
        small_got = jnp.concatenate([early_got, swap(late, "w")], axis=0)
        small_all = in_order(w_at, small_own[None], small_got[None], 0)
        weights = [*low_weights, weight_got, swap(weight_got, "c")]
        head_got = swap(head_pack, "w")
    else:
        weights = weight_got
    mixed = exchange(made[:ZS])
    small_all = small_all.astype(F32)
    vec = jnp.transpose(small_all[:, :8], (1, 0, 2)).reshape(8, width)
    up_offset = small_all[:, 8:].reshape(1, -1)

    split = count_w == 2 and count_o == 1
    my_index = o_at * 16 + z_at * 4 + x_at * 2 + c_at
    rest = jnp.clip(length - my_index * local_rows, 0, local_rows)
    core = c_at if split else jnp.zeros_like(c_at)
    spots = jnp.stack([rest, w_at, core, z_at]).astype(jnp.int32)
    outputs, resid_grad, *made = middle(
        spots, [mixed], ((0, heads),), tokens, cotangent[0], vec, up_offset, weights
    )
    head_grads = exchange(made[:ZS])
    send, keep, small_own = made[ZS:]
    hidden = up_offset.shape[1]

    near_bit, far_bit = z_at & 1, z_at >> 1

    def add_pair(kept, got):
        return (kept.astype(F32) + got.astype(F32)).astype(BF16)

    def join(value, got, bit):
        return in_order(bit, value, got, 0)

    spot = jnp.stack([c_at, x_at]).astype(jnp.int32)
    token = [spot]

    def arrive(*values):
        token[0], *values = hold((token[0], *values))
        return values[0] if len(values) == 1 else values

    def backward(first, count, made=()):
        return attend_backward(
            meta, queries, head_grads, attended, logs, kv_blocks, first, count, made
        )

    def to_near(value):
        return lax.ppermute(value, "z", near)

    def to_far(value):
        return lax.ppermute(value, "z", far)

    def head_part(ws, core, got=None, first=0):
        at = jnp.stack([jnp.asarray(item) for item in (*ws, core)]).astype(jnp.int32)
        return head_slab(at, turned, query_low, kv_low, 2 * count_w, len(ws), got, first)

    def pick(w, c):
        return jnp.stack([jnp.asarray(w), jnp.asarray(c)]).astype(jnp.int32)

    if split:
        got, small_got = swap(send, "c"), swap(small_own, "c")
        down_far = down_slab(pick(1 - w_at, 0), keep, send, got)
        up_sent, up_kept = up_slabs(
            jnp.stack([x_at]).astype(jnp.int32), keep, send, got, small_own, small_got
        )
        down_near = down_slab(pick(1 * w_at, 0), keep, send, got)
        down_far, up_sent, down_near, *head_grads = hold(
            (down_far, up_sent, down_near, *head_grads)
        )
        made = backward(0, heads - 1)
        down_got, *made = arrive(swap(down_far, "w"), *made)
        down_sum = add_pair(down_near, down_got)
        down_got = to_near(part_of(down_sum, 1 - near_bit, 2, 0))
        down_sum, *head_grads = arrive(down_sum, *head_grads)
        made = backward(heads - 1, 1, made)
        down_got, up_got, head_got, *made = arrive(
            down_got, swap(up_sent, "x"), head_got, *made
        )
        query_low, pairs = made[:ZS], made[ZS:]
        head_weights = [*low_heads, head_got, swap(head_got, "c")]
        pair_got = swap(pairs[1], "c")
        query_got = exchange(query_low)
        down_sum = add_pair(part_of(down_sum, near_bit, 2, 0), down_got)
        down_got = to_far(part_of(down_sum, 1 - far_bit, 2, 0))
        up_sum = add_pair(up_kept, up_got).reshape(2, own_rows // 2, -1)
        up_got = swap(lax.dynamic_index_in_dim(up_sum, 1 - w_at, 0, keepdims=False), "w")
        pair_got = arrive(pair_got)
        half_rows = pair_got.shape[0] // 2
        pair_sent = add_pair(pairs[0][half_rows:], pair_got[half_rows:])
        pair_sent = arrive(pair_sent)
        key_got = swap(pair_sent, "x")
        key_got, down_got, up_got, *query_got = arrive(key_got, down_got, up_got, *query_got)
        up_sum = add_pair(lax.dynamic_index_in_dim(up_sum, w_at, 0, keepdims=False), up_got)
        up_sent, key_got = arrive(part_of(up_sum, 1 - near_bit, 2, 0), key_got)
        up_got = to_near(up_sent)
        kv_low = key_sum(pairs[0], pair_got, key_got)
        down_sum = add_pair(part_of(down_sum, far_bit, 2, 0), down_got)
        down_got = swap(part_of(down_sum, 1 - x_at, 2, 0), "x")
        head_core = swap(head_part((1 - w_at, 1 * w_at), 1 - c_at), "c")
        kv_got = exchange(kv_low)
        down_got = arrive(down_got)
        down_sum = add_pair(part_of(down_sum, x_at, 2, 0), down_got)
        down_got = to_far(down_sum)
        head_core = arrive(head_core)
        head_sent = swap(head_part((1 - w_at,), c_at, head_core), "w")
        head_sum = head_part((1 * w_at,), c_at, head_core, 1)
        up_got = arrive(up_got)
        up_sum = add_pair(part_of(up_sum, near_bit, 2, 0), up_got)
        up_got = to_far(part_of(up_sum, 1 - far_bit, 2, 0))
        head_sent = arrive(head_sent)
        head_sum = add_pair(head_sum, head_sent)
        head_got = swap(head_sum, "x")
        kv_got = arrive(*kv_got)
        input_grad = token_gradient(
            spots, resid_grad, query_got, kv_got, head_weights
        )
        up_got = arrive(up_got)
        up_sum = add_pair(part_of(up_sum, far_bit, 2, 0), up_got)
        up_got = to_far(up_sum)
        down_got = arrive(down_got)
        down_sum = join(down_sum[None], down_got[None], far_bit)
        down_got = to_near(down_sum)
        head_got = arrive(head_got)
        head_sum = add_pair(head_sum, head_got)
        head_got = to_far(head_sum)
        up_got = arrive(up_got)
        up_sum = join(up_sum, up_got, far_bit)
        up_got = to_near(up_sum)
        down_got = arrive(down_got)
        down_sum = join(down_sum[None], down_got[None], near_bit)
        down_sum = down_sum.reshape(-1, width)
        down_x = swap(down_sum, "x")
        down_c = swap(down_sum, "c")
        head_got = arrive(head_got)
        head_two = join(head_sum, head_got, far_bit)
        head_got = to_near(head_two)
        up_got = arrive(up_got)
        up_sum = join(up_sum, up_got, near_bit)
        up_x = swap(up_sum, "x")
        up_c = swap(up_sum, "c")
        down_x, input_grad = arrive(down_x, input_grad)
        down_pieces = [down_sum, down_x, down_c, swap(down_x, "c")]
        head_got = arrive(head_got)
        head_four = join(head_two, head_got, near_bit)
        head_other = swap(head_four, "c")
        total_down = down_finish(spot, down_pieces)
        up_x, total_down = arrive(up_x, total_down)
        up_pieces = [up_sum, up_x, up_c, swap(up_x, "c")]
        total_query, total_key, total_value, head_bias = head_finish(
            spot, head_four, head_other, width
        )
        total_query, total_key, total_value = arrive(total_query, total_key, total_value)
        total_up, total_out, table = up_finish(token[0], up_pieces, hidden, width)
        groups = own_rows // 128
        small_total = table[: 8 * groups].reshape(groups, 8, 128)
        vectors = [small_total[:, at].reshape(own_rows) for at in range(6)]
        lines = hidden // count_w // 128
        total_up_bias = table[8 * groups : 8 * groups + lines].reshape(-1)
    else:
        made = backward(0, heads)
        query_low, pairs = made[:ZS], made[ZS:]
        if count_o == 2:
            pairs = [plus(spot, pairs[at], swap(pairs[at + 2], "o")) for at in range(2)]
        pair_got = swap(pairs[1], "c")
        half_rows = pair_got.shape[0] // 2
        key_got = swap(plus(spot, pairs[0], pair_got, half_rows), "x")
        kv_low = key_sum(pairs[0], pair_got, key_got)
        if count_w == 2:
            head_weights = [*low_heads, head_got, swap(head_got, "c")]
        input_grad = token_gradient(
            spots.at[2].set(c_at.astype(jnp.int32)),
            resid_grad,
            exchange(query_low),
            exchange(kv_low),
            head_weights,
        )
        every_w = tuple(range(count_w))
        slabs = head_part(every_w, c_at, swap(head_part(every_w, 1 - c_at), "c"))
        head_sum = lax.psum_scatter(slabs, "w", scatter_dimension=0, tiled=True)
        head_sum = plus(spot, head_sum, swap(head_sum, "x"))
        if count_o == 2:
            head_sum = plus(spot, head_sum, swap(head_sum, "o"))
        n_bit, f_bit = [
            jnp.stack([bit, bit]).astype(jnp.int32) for bit in (near_bit, far_bit)
        ]
        head_sum = unite(f_bit, head_sum, to_far(head_sum))
        head_sum = unite(n_bit, head_sum, to_near(head_sum))
        total_query, total_key, total_value, head_bias = head_finish(
            spot, head_sum, swap(head_sum, "c"), width
        )
        quarter = hidden // 4
        count = quarter // 256
        act_at = 5 * quarter
        act = [keep[:quarter], send[act_at : act_at + quarter], keep[quarter : 2 * quarter]]
        act += [send[act_at + quarter : act_at + 2 * quarter]]
        act = jnp.concatenate(act, axis=0)

        def rows_of(value, low, at):
            return value[low + at * local_rows : low + (at + 1) * local_rows]

        ffn_at = act_at + 2 * quarter
        ffn = jnp.concatenate([rows_of(send, ffn_at, at) for at in range(width // 256)], axis=1)
        pre = []
        for half in range(2):
            pre += [rows_of(keep, 2 * quarter, half * count + at) for at in range(count)]
            pre += [rows_of(send, 0, half * count + at) for at in range(count)]
        pre = jnp.concatenate(pre, axis=1)
        normed_turned = send[2 * quarter : 2 * quarter + width]
        mixed_turned = send[2 * quarter + width : 2 * quarter + 2 * width]
        side = width // 2
        branch = jnp.concatenate(
            [
                rows_of(keep, 4 * quarter, 0),
                rows_of(keep, 4 * quarter, 1)[:, : side - 256],
                rows_of(send, 2 * quarter + 2 * width, 0),
                rows_of(send, 2 * quarter + 2 * width, 1)[:, : side - 256],
            ],
            axis=1,
        )

        def sum_all(value):
            value = value.astype(BF16)
            value = lax.psum_scatter(value, "w", scatter_dimension=0, tiled=True)
            return lax.psum(value, ("o", "z", "x", "c")).astype(F32)

        total_down = sum_all(matmul(act, ffn))
        total_up = sum_all(matmul(normed_turned, pre))
        total_out = sum_all(matmul(mixed_turned, branch))
        small_own = lax.psum(small_own, ("o", "z", "x", "c", "w"))
        vectors = [part_of(small_own[at], w_at, count_w, 0) for at in range(6)]
        total_up_bias = part_of(small_own[8:12].reshape(-1), w_at, count_w, 0)

    totals = [part_of(head_bias[at], w_at, count_w, 0) for at in (0, 8)] + vectors
    return (
        outputs[None],
        input_grad[None],
        total_query,
        totals[0],
        total_key,
        total_value,
        totals[1],
        total_out,
        totals[2],
        totals[3],
        totals[4],
        total_up,
        total_up_bias,
        total_down,
        totals[5],
        totals[6],
        totals[7],
    )


def solution(mesh):
    count_s = mesh.shape["seq"]
    count_w = mesh.shape["wshard"]
    count_o = count_s // 16
    fine = Mesh(
        mesh.devices.reshape(count_o, ZS, 2, 2, count_w), ("o", "z", "x", "c", "w")
    )
    seq = ("o", "z", "x", "c")
    rows = P("w", seq, None)
    matrix = P("w", None)
    vector = P("w")
    placed = (
        rows,
        vector,
        rows,
        matrix,
        vector,
        matrix,
        matrix,
        vector,
        matrix,
        vector,
        vector,
        vector,
        matrix,
        vector,
        matrix,
        vector,
        vector,
        vector,
    )
    return jax.shard_map(
        partial(body, sizes=(count_o, count_w)),
        mesh=fine,
        in_specs=placed,
        out_specs=(
            rows,
            rows,
            matrix,
            vector,
            matrix,
            matrix,
            vector,
            matrix,
            vector,
            vector,
            vector,
            matrix,
            vector,
            matrix,
            vector,
            vector,
            vector,
        ),
        check_vma=False,
    )
```

```python
from functools import partial

import jax
import jax.numpy as jnp
from jax import lax
from jax.experimental import pallas as pl
from jax.experimental.pallas import tpu as pltpu
from jax.sharding import Mesh, PartitionSpec as P

HEADS = 12
ZS = 4
NEG_FILL = -1e30
VMEM_LIMIT = 60 << 20
SWAP = ((0, 1), (1, 0))
F32 = jnp.float32
BF16 = jnp.bfloat16


def matmul(left_side, right_side):
    return jnp.dot(left_side, right_side, preferred_element_type=F32)


def right_trans(left_side, right_side):
    return lax.dot_general(
        left_side, right_side, (((1,), (1,)), ((), ())), preferred_element_type=F32
    )


def work(units):
    return pl.CostEstimate(flops=int(units * 1e3), bytes_accessed=1, transcendentals=0)


def swap(value, axis):
    return lax.ppermute(value, axis, SWAP)


def touched_groups(length, rows, outer):
    group = 4 * rows
    left = length - outer * (ZS * group)
    return jnp.clip((left + group - 1) // group, 0, ZS)


def with_mask(kv, place, length):
    at = place + lax.broadcasted_iota(jnp.int32, kv.shape, 0)
    lane = lax.broadcasted_iota(jnp.int32, kv.shape, 1)
    fill = jnp.where(at < length, 0.0, jnp.where(lane == 0, NEG_FILL, 0.0))
    return jnp.concatenate([kv, fill.astype(BF16)], axis=1)


def load_head(kv_refs, rows_ref, turned_ref, low):
    head_dim = turned_ref.shape[1]
    for at, ref in enumerate(kv_refs):
        block, half = at // 2, at % 2
        size = ref.shape[0]
        for start in range(0, size, 256):
            value = ref[start : start + 256, :]
            place = slice(half * size + start, half * size + start + 256)
            rows_ref[block, place, :] = value
            turned_ref[block, :, place] = value.T[low : low + head_dim, :]


def forward_kernel(meta_ref, *refs, blocks, rows):
    query_refs, kv_refs = refs[:2], refs[2 : 2 + 2 * blocks]
    out_ref, *refs = refs[2 + 2 * blocks :]
    piece_refs, (log_ref, rows_ref, turned_ref) = refs[:ZS], refs[ZS:]
    head_dim, query_count = out_ref.shape
    length, z_at = meta_ref[0], meta_ref[1]
    load_head(kv_refs, rows_ref, turned_ref, head_dim)
    query = jnp.concatenate([ref[...] for ref in query_refs], axis=1)
    query = jnp.concatenate(
        [
            query,
            jnp.zeros((head_dim, query_count), BF16),
            jnp.ones((128, query_count), BF16),
        ],
        axis=0,
    )

    def step(group, carry, members):
        top, total, acc = carry
        start = pl.multiple_of((group ^ z_at) * rows, rows)
        found = []
        for block in members:
            place = (meta_ref[2 + block] + group * 4) * rows
            kv = with_mask(rows_ref[block, pl.ds(start, rows), :], place, length)
            found.append(matmul(kv, query))
        new_top = top
        for scores in found:
            new_top = jnp.maximum(new_top, jnp.max(scores, axis=0, keepdims=True))
        fade = jnp.exp(top - new_top)
        total = total * fade
        acc = acc * fade
        for block, scores in zip(members, found):
            weights = jnp.exp(scores - new_top)
            total = total + jnp.sum(weights, axis=0, keepdims=True)
            acc = acc + matmul(
                turned_ref[block, :, pl.ds(start, rows)], weights.astype(BF16)
            )
        return new_top, total, acc

    carry = (
        jnp.full((1, query_count), NEG_FILL, F32),
        jnp.zeros((1, query_count), F32),
        jnp.zeros((head_dim, query_count), F32),
    )
    for first in range(0, blocks, 4):
        members = tuple(range(first, first + 4))
        count = touched_groups(length, rows, meta_ref[2 + first] // 16)
        carry = lax.fori_loop(0, count, lambda g, c: step(g, c, members), carry)
    top, total, acc = carry
    out = acc * (1.0 / total)
    out_ref[...] = out
    size = query_count // ZS
    for at in range(ZS):
        piece_refs[at][...] = out[:, at * size : (at + 1) * size].astype(BF16)
    log_ref[0] = top + jnp.log(total)


def attend_forward(meta, queries, kv_blocks, heads):
    blocks = len(kv_blocks)
    half_rows = kv_blocks[0][0].shape[0]
    part, half_count = queries[0].shape
    head_dim, query_count = part // heads, 2 * half_count
    size = query_count // ZS
    return pl.pallas_call(
        partial(forward_kernel, blocks=blocks, rows=2 * half_rows // ZS),
        grid_spec=pltpu.PrefetchScalarGridSpec(
            num_scalar_prefetch=1,
            grid=(heads,),
            in_specs=[pl.BlockSpec((head_dim, half_count), lambda i, m: (i, 0))] * 2
            + [pl.BlockSpec((half_rows, 128), lambda i, m: (0, i))] * (2 * blocks),
            out_specs=[pl.BlockSpec((head_dim, query_count), lambda i, m: (i, 0))]
            + [pl.BlockSpec((head_dim, size), lambda i, m: (i, 0))] * ZS
            + [pl.BlockSpec((1, 1, query_count), lambda i, m: (i, 0, 0))],
            scratch_shapes=[
                pltpu.VMEM((blocks, 2 * half_rows, 128), BF16),
                pltpu.VMEM((blocks, head_dim, 2 * half_rows), BF16),
            ],
        ),
        out_shape=[jax.ShapeDtypeStruct((part, query_count), F32)]
        + [jax.ShapeDtypeStruct((part, size), BF16)] * ZS
        + [jax.ShapeDtypeStruct((heads, 1, query_count), F32)],
        compiler_params=pltpu.CompilerParams(vmem_limit_bytes=VMEM_LIMIT),
        cost_estimate=work(8 * heads),
        name="attend_forward",
    )(meta, *queries, *[item for pair in kv_blocks for item in pair])


def backward_kernel(meta_ref, *refs, blocks, rows, extra):
    query_refs, (out_ref, log_ref), refs = refs[:2], refs[2:4], refs[4:]
    grad_refs, kv_refs = refs[:ZS], refs[ZS : ZS + 2 * blocks]
    refs = refs[ZS + 2 * blocks + extra :]
    dq_refs, pairs = refs[:ZS], refs[ZS : ZS + blocks // 2]
    rows_ref, turned_ref, qn_ref, gn_ref, acc_ref = refs[ZS + blocks // 2 :]
    head_dim, query_count = out_ref.shape
    length, z_at = meta_ref[0], meta_ref[1]
    block_rows = ZS * rows
    load_head(kv_refs, rows_ref, turned_ref, 0)
    query = jnp.concatenate([ref[...] for ref in query_refs], axis=1)
    grads = jnp.concatenate([ref[...] for ref in grad_refs], axis=1)
    blank = jnp.zeros((head_dim, query_count), BF16)
    query = jnp.concatenate([query, blank], axis=0)
    grad = jnp.concatenate([blank, grads], axis=0)
    qn_ref[...] = query.T
    gn_ref[...] = grad.T
    query = jnp.concatenate([query, jnp.ones((128, query_count), BF16)], axis=0)
    delta = jnp.sum(grads.astype(F32) * out_ref[...], axis=0, keepdims=True)
    log_sum = log_ref[0]
    acc_ref[...] = jnp.zeros_like(acc_ref)

    def put(block, start, value):
        pairs[block // 2][pl.ds(start + (block & 1) * block_rows, rows), :] = value

    def step(group, members):
        start = pl.multiple_of((group ^ z_at) * rows, rows)
        for block in members:
            kv = rows_ref[block, pl.ds(start, rows), :]
            place = (meta_ref[2 + block] + group * 4) * rows
            scores = matmul(with_mask(kv, place, length), query)
            prob_grad = matmul(kv, grad)
            prob = jnp.exp(scores - log_sum)
            score_grad = (prob * (prob_grad - delta)).astype(BF16)
            value = matmul(prob.astype(BF16), gn_ref[...]) + matmul(score_grad, qn_ref[...])
            put(block, start, value.astype(BF16))
            acc_ref[...] += matmul(turned_ref[block, :, pl.ds(start, rows)], score_grad)

    def clear(group, members):
        start = pl.multiple_of((group ^ z_at) * rows, rows)
        for block in members:
            put(block, start, jnp.zeros((rows, 128), BF16))

    def loop(low, high, fn):
        def one(group, carry):
            fn(group)
            return carry

        lax.fori_loop(low, high, one, 0)

    for first in range(0, blocks, 4):
        members = tuple(range(first, first + 4))
        count = touched_groups(length, rows, meta_ref[2 + first] // 16)
        loop(0, count, lambda g: step(g, members))
        loop(count, ZS, lambda g: clear(g, members))
    dq = (acc_ref[...] * head_dim ** (-0.5)).astype(BF16)
    size = query_count // ZS
    for at in range(ZS):
        dq_refs[at][...] = dq[:, at * size : (at + 1) * size]


def attend_backward(meta, queries, grads, out, log_sum, kv_blocks, first, count, made=()):
    blocks = len(kv_blocks)
    half_rows, columns = kv_blocks[0][0].shape
    heads = columns // 128
    part, half_count = queries[0].shape
    head_dim, query_count = part // heads, 2 * half_count
    size = query_count // ZS
    piece = pl.BlockSpec((head_dim, size), lambda i, m: (i + first, 0))
    ins = [
        *queries,
        out,
        log_sum,
        *grads,
        *[item for pair in kv_blocks for item in pair],
        *made,
    ]
    return pl.pallas_call(
        partial(backward_kernel, blocks=blocks, rows=2 * half_rows // ZS, extra=len(made)),
        grid_spec=pltpu.PrefetchScalarGridSpec(
            num_scalar_prefetch=1,
            grid=(count,),
            in_specs=[pl.BlockSpec((head_dim, half_count), lambda i, m: (i + first, 0))] * 2
            + [
                pl.BlockSpec((head_dim, query_count), lambda i, m: (i + first, 0)),
                pl.BlockSpec((1, 1, query_count), lambda i, m: (i + first, 0, 0)),
            ]
            + [piece] * ZS
            + [pl.BlockSpec((half_rows, 128), lambda i, m: (0, i + first))] * (2 * blocks)
            + [pl.BlockSpec(memory_space=pl.ANY)] * len(made),
            out_specs=[piece] * ZS
            + [pl.BlockSpec((4 * half_rows, 128), lambda i, m: (0, i + first))] * (blocks // 2),
            scratch_shapes=[
                pltpu.VMEM((blocks, 2 * half_rows, 128), BF16),
                pltpu.VMEM((blocks, head_dim, 2 * half_rows), BF16),
                pltpu.VMEM((query_count, 128), BF16),
                pltpu.VMEM((query_count, 128), BF16),
                pltpu.VMEM((head_dim, query_count), F32),
            ],
        ),
        out_shape=[jax.ShapeDtypeStruct((part, size), BF16)] * ZS
        + [jax.ShapeDtypeStruct((4 * half_rows, columns), BF16)] * (blocks // 2),
        input_output_aliases={
            1 + len(ins) - len(made) + at: at for at in range(len(made))
        },
        compiler_params=pltpu.CompilerParams(vmem_limit_bytes=VMEM_LIMIT),
        cost_estimate=work(12 * count),
        name="attend_backward",
    )(meta, *ins)


IN_VMEM = pl.BlockSpec(memory_space=pltpu.VMEM)


def small_call(kernel, meta, values, shapes, scratch=(), limit=32, name=None):
    return pl.pallas_call(
        kernel,
        grid_spec=pltpu.PrefetchScalarGridSpec(
            num_scalar_prefetch=1,
            grid=(),
            in_specs=[IN_VMEM] * len(values),
            out_specs=[IN_VMEM] * len(shapes),
            scratch_shapes=list(scratch),
        ),
        out_shape=[jax.ShapeDtypeStruct(shape, kind) for shape, kind in shapes],
        compiler_params=pltpu.CompilerParams(vmem_limit_bytes=limit << 20),
        cost_estimate=work(1),
        name=name,
    )(meta, *values)


def fold_kernel(meta_ref, kept_ref, got_ref, keep_ref, sent_ref, sum_ref):
    sum_ref[...] = (kept_ref[...].astype(F32) + got_ref[...].astype(F32)).astype(BF16)
    rows = keep_ref.shape[0]
    for at, ref in enumerate((keep_ref, sent_ref)):
        start = pl.multiple_of((meta_ref[0] ^ at) * rows, 16)
        ref[...] = sum_ref[pl.ds(start, rows), :]


def fold(bit, kept, got):
    rows, columns = kept.shape
    half = ((rows // 2, columns), BF16)
    return small_call(
        fold_kernel,
        bit,
        (kept, got),
        [half, half],
        [pltpu.VMEM((rows, columns), BF16)],
        name="fold",
    )


def unite_kernel(meta_ref, own_ref, got_ref, out_ref):
    rows = own_ref.shape[0]
    for at, ref in enumerate((own_ref, got_ref)):
        start = pl.multiple_of((meta_ref[0] ^ at) * rows, 16)
        out_ref[pl.ds(start, rows), :] = ref[...]


def unite(bit, own, got):
    rows, columns = own.shape
    return small_call(
        unite_kernel, bit, (own, got), [((2 * rows, columns), BF16)], name="unite"
    )[0]


def plus_kernel(meta_ref, one_ref, two_ref, out_ref, *, low):
    cut = slice(low, low + out_ref.shape[0])
    out_ref[...] = (one_ref[cut, :].astype(F32) + two_ref[cut, :].astype(F32)).astype(BF16)


def plus(meta, one, two, low=0):
    rows, columns = one.shape
    return small_call(
        partial(plus_kernel, low=low),
        meta,
        (one, two),
        [((rows - low, columns), BF16)],
        name="plus",
    )[0]


def prepare_kernel(meta_ref, *refs):
    sources, refs = refs[:3], refs[3:]
    kv_ref, query_ref, low_refs, head_ref = refs[0], refs[1], refs[2:5], refs[5]
    places, sems = refs[6:9], refs[9]
    copies = []
    for at in range(3):
        copies.append(pltpu.make_async_copy(sources[at], places[at], sems.at[at]))
        copies[-1].start()
    z_at, c_at = meta_ref[0], meta_ref[1]
    width = places[0].shape[1]
    part = width // ZS
    head_dim = width // HEADS
    parts = []
    for kind in range(3):
        ref = places[kind]
        copies[kind].wait()
        value = ref[...]
        low_refs[kind][...] = value.astype(BF16)
        half = ref.shape[0] // 2
        rows = ref[pl.ds(pl.multiple_of(c_at * half, half), half), :]
        head_ref[kind * half : (kind + 1) * half, :] = rows.astype(BF16)
        turn = lax.rem(width - z_at * part, width)
        parts.append(pltpu.roll(value, turn, 1)[:, :part])
    columns = []
    for head in range(part // head_dim):
        cut = slice(head * head_dim, (head + 1) * head_dim)
        columns += [parts[1][:, cut], parts[2][:, cut]]
    kv_ref[...] = jnp.concatenate(columns, axis=1).astype(BF16)
    query_ref[...] = parts[0].astype(BF16)


def prepare(meta, weights):
    count, width = weights[0].shape
    shapes = [(count, 2 * width // ZS), (count, width // ZS)] + [(count, width)] * 3
    shapes.append((3 * count // 2, width))
    return pl.pallas_call(
        prepare_kernel,
        grid_spec=pltpu.PrefetchScalarGridSpec(
            num_scalar_prefetch=1,
            grid=(),
            in_specs=[pl.BlockSpec(memory_space=pltpu.MemorySpace.HBM)] * 3,
            out_specs=[IN_VMEM] * len(shapes),
            scratch_shapes=[pltpu.VMEM((count, width), F32)] * 3
            + [pltpu.SemaphoreType.DMA((3,))],
        ),
        out_shape=[jax.ShapeDtypeStruct(shape, BF16) for shape in shapes],
        compiler_params=pltpu.CompilerParams(vmem_limit_bytes=VMEM_LIMIT),
        cost_estimate=work(1),
        name="prepare",
    )(meta, *weights)


def round_kernel(meta_ref, out_w, up_w, down_w, low_out, low_up, low_down, pack_ref):
    core = meta_ref[1]
    for source, target in ((out_w, low_out), (up_w, low_up), (down_w, low_down)):
        target[...] = source[...].astype(BF16)
    width = pack_ref.shape[1]
    low = 0
    half = out_w.shape[0] // 2
    rows = pl.ds(pl.multiple_of(core * half, half), half)
    pack_ref[low : low + half, :] = out_w[rows, :].astype(BF16)
    low += half
    count = up_w.shape[1] // 2
    for block in range(count // width):
        lanes = pl.ds(pl.multiple_of(core * count + block * width, 128), width)
        pack_ref[low : low + up_w.shape[0], :] = up_w[:, lanes].astype(BF16)
        low += up_w.shape[0]
    half = down_w.shape[0] // 2
    rows = pl.ds(pl.multiple_of(core * half, half), half)
    pack_ref[low : low + half, :] = down_w[rows, :].astype(BF16)


def round_weights(meta, weights):
    out_w, up_w, down_w = weights
    width = out_w.shape[1]
    total = out_w.shape[0] // 2 + up_w.shape[0] * (up_w.shape[1] // 2 // width)
    total += down_w.shape[0] // 2
    return small_call(
        round_kernel,
        meta,
        weights,
        [(item.shape, BF16) for item in weights] + [((total, width), BF16)],
        limit=60,
        name="round_weights",
    )


def project_kernel(meta_ref, first_ref, second_ref, *refs, shared):
    query_ref, kv_ref, turned_ref, token_ref, bias_ref = refs[-5:]
    part = query_ref.shape[0]
    rows, width = first_ref.shape
    split = 2 * part
    token_ref[:rows, :] = first_ref[...]
    token_ref[rows:, :] = second_ref[...]
    if shared:
        w_at, z_at = meta_ref[0], meta_ref[1]
        both = None
        bias_ref[...] = jnp.zeros_like(bias_ref)
        for at in range(2):
            count = refs[at].shape[0]
            cut = pl.ds(pl.multiple_of((w_at ^ at) * count, 128), count)
            tokens = token_ref[:, cut]
            terms = [matmul(tokens, refs[2 * at + kind][...]) for kind in range(2)]
            term = jnp.concatenate(terms, axis=1)
            both = term if both is None else both + term
            bias_ref[0:2, cut] = refs[4 + at][0:2, :].astype(F32)
        turn = lax.rem(width - z_at * part, width)
        bias = pltpu.roll(bias_ref[...], turn, 1)[:, :part]
        head_dim = width // HEADS
        pieces = []
        for head in range(part // head_dim):
            pieces.append(jnp.zeros((1, head_dim), F32))
            pieces.append(bias[1:2, head * head_dim : (head + 1) * head_dim])
        both = both + jnp.concatenate(pieces + [bias[0:1, :]], axis=1)
    else:
        both = matmul(token_ref[...], refs[0][...]) + refs[1][...]
    kv_ref[...] = both[:, :split].astype(BF16)
    scale = (part * ZS // HEADS) ** (-0.5)
    query_ref[...] = (both[:, split:].astype(BF16) * jnp.array(scale, BF16)).T
    turned_ref[...] = token_ref[...].T


def project(meta, first, second, sources):
    rows, width = first.shape
    part = width // ZS
    return small_call(
        partial(project_kernel, shared=len(sources) == 6),
        meta,
        (first, second, *sources),
        [((part, 2 * rows), BF16), ((2 * rows, 2 * part), BF16), ((width, 2 * rows), BF16)],
        [pltpu.VMEM((2 * rows, width), BF16), pltpu.VMEM((8, width), F32)],
        limit=40,
        name="project",
    )


def middle_kernel(meta_ref, tokens_ref, seed_ref, vec_ref, upoff_ref, *refs, groups, shared):
    mixed_refs = [refs[at * ZS : (at + 1) * ZS] for at in range(len(groups))]
    refs = refs[ZS * len(groups) :]
    weight_refs = refs[: 5 if shared else 3]
    refs = refs[len(weight_refs) :]
    outputs_ref, resid_ref = refs[:2]
    mgrad_refs = refs[2 : 2 + ZS]
    (
        send_ref,
        keep_ref,
        small_ref,
        out_w,
        up_w,
        down_w,
        slope_ref,
        wide_ref,
        tall_ref,
        sems,
    ) = refs[2 + ZS :]
    w_at, core, z_at = meta_ref[1], meta_ref[2], meta_ref[3]
    moves = [[], [], []]
    if shared:
        outs, ups, downs, got, pair = weight_refs
        count_o, count_u, count_d = outs.shape[0], ups.shape[0], downs.shape[0]
        for kind, (source, target) in enumerate(((outs, out_w), (ups, up_w), (downs, down_w))):
            start = pl.multiple_of(w_at * source.shape[0], source.shape[0])
            moves[kind].append((source, target.at[pl.ds(start, source.shape[0]), :]))
        lanes = got.shape[1]
        for source, which in ((got, core), (pair, 1 - core)):
            half = count_o // 2
            start = pl.multiple_of(((1 - w_at) * 2 + which) * half, half)
            moves[0].append((source.at[pl.ds(0, half), :], out_w.at[pl.ds(start, half), :]))
            low = half
            start = pl.multiple_of((1 - w_at) * count_u, count_u)
            for block in range(up_w.shape[1] // 2 // lanes):
                lane = pl.multiple_of(which * (up_w.shape[1] // 2) + block * lanes, 128)
                moves[1].append(
                    (
                        source.at[pl.ds(low, count_u), :],
                        up_w.at[pl.ds(start, count_u), pl.ds(lane, lanes)],
                    )
                )
                low += count_u
            half = count_d // 2
            start = pl.multiple_of(((1 - w_at) * 2 + which) * half, half)
            moves[2].append((source.at[pl.ds(low, half), :], down_w.at[pl.ds(start, half), :]))
    else:
        for kind, pair in enumerate(zip(weight_refs, (out_w, up_w, down_w))):
            moves[kind].append(pair)
    copies = []
    at = 0
    for kind in range(3):
        made = []
        for source, target in moves[kind]:
            made.append(pltpu.make_async_copy(source, target, sems.at[at]))
            made[-1].start()
            at += 1
        copies.append(made)
    rows, width = tokens_ref.shape
    hidden = upoff_ref.shape[1]
    part = width // ZS
    head_dim = width // HEADS
    quarter = hidden // 4

    def mean(value):
        return jnp.mean(value, axis=-1, keepdims=True)

    def norm(value):
        centered = value - mean(value)
        scale = lax.rsqrt(mean(centered * centered) + 1e-12)
        return centered * scale, scale

    def norm_back(grad, normal, scale):
        return scale * (grad - mean(grad) - normal * mean(grad * normal))

    def column(value):
        return jnp.sum(value, axis=0, keepdims=True)

    normed_at = 2 * quarter
    mixed_at = normed_at + width
    branch_at = mixed_at + width
    act_at = 5 * quarter
    for (first, count), pieces in zip(groups, mixed_refs):
        size = count * head_dim
        for at in range(ZS):
            low = mixed_at + (z_at ^ at) * part + first * head_dim
            send_ref[pl.ds(pl.multiple_of(low, head_dim), size), :] = pieces[at][...]
    mixed = send_ref[mixed_at:branch_at, :].T
    for copy in copies[0]:
        copy.wait()
    first_n, first_r = norm(tokens_ref[...] + (matmul(mixed, out_w[...]) + vec_ref[2:3, :]))
    normed = first_n * vec_ref[3:4, :] + vec_ref[4:5, :]
    low = normed.astype(BF16)
    send_ref[normed_at:mixed_at, :] = low.T
    for copy in copies[1] + copies[2]:
        copy.wait()
    quarters = []
    for half in range(2):
        for kept in (False, True):
            at = half * 2 * quarter + (core if kept else 1 - core) * quarter
            quarters.append((half, kept, pl.multiple_of(at, quarter)))
    acc = None
    for at, (half, kept, start) in enumerate(quarters):
        cut = pl.ds(start, quarter)
        pre_act = matmul(low, up_w[:, cut]) + upoff_ref[:, cut]
        phi = 0.5 + 0.5 * lax.erf(pre_act * (0.5**0.5))
        act = (pre_act * phi).astype(BF16)
        slope_ref[:, at * quarter : (at + 1) * quarter] = phi + pre_act * (
            jnp.exp(-0.5 * pre_act * pre_act) * 0.3989422804014327
        )
        target, base = (keep_ref, 0) if kept else (send_ref, act_at)
        target[base + half * quarter : base + (half + 1) * quarter, :] = act.T
        term = matmul(act, down_w[cut, :])
        acc = term if acc is None else acc + term
    second_n, second_r = norm(normed + (acc + vec_ref[5:6, :]))
    outputs_ref[...] = second_n * vec_ref[6:7, :] + vec_ref[7:8, :]
    place = lax.broadcasted_iota(jnp.int32, (rows, 1), 0)
    seed = jnp.where(place < meta_ref[0], seed_ref[...], 0.0)
    sum_grad = norm_back(seed * vec_ref[6:7, :], second_n, second_r)
    ffn = sum_grad.astype(BF16)
    for at in range(width // 256):
        low_row = act_at + 2 * quarter + at * rows
        send_ref[low_row : low_row + rows, :] = ffn[:, at * 256 : (at + 1) * 256]
    small_ref[3:4, :] = column(ffn.astype(F32))
    small_ref[4:5, :] = column(seed * second_n)
    small_ref[5:6, :] = column(seed)
    acc = sum_grad
    for at, (half, kept, start) in enumerate(quarters):
        cut = pl.ds(start, quarter)
        pre = right_trans(ffn, down_w[cut, :]) * slope_ref[:, at * quarter : (at + 1) * quarter]
        pre = pre.astype(BF16)
        target, base = (keep_ref, 2 * quarter) if kept else (send_ref, 0)
        for block in range(quarter // 256):
            row = base + (half * (quarter // 256) + block) * rows
            target[row : row + rows, :] = pre[:, block * 256 : (block + 1) * 256]
        sums = column(pre.astype(F32))
        line = 8 + half * (2 * quarter // width) + (core if kept else 1 - core)
        small_ref[pl.ds(line, 1), :] = sums
        acc = acc + right_trans(pre, up_w[:, cut])
    small_ref[1:2, :] = column(acc * first_n)
    small_ref[2:3, :] = column(acc)
    resid = norm_back(acc * vec_ref[3:4, :], first_n, first_r)
    resid_ref[...] = resid
    branch = resid.astype(BF16)
    wide_ref[...] = branch
    side = width // 2
    for target, base, which in (
        (send_ref, branch_at, 1 - core),
        (keep_ref, 4 * quarter, core),
    ):
        values = wide_ref[:, pl.ds(pl.multiple_of(which * side, 128), side)]
        target[base : base + rows, :] = values[:, :256]
        target[base + rows : base + 2 * rows, : side - 256] = values[:, 256:]
        target[base + rows : base + 2 * rows, side - 256 :] = jnp.zeros(
            (rows, 512 - side), BF16
        )
    small_ref[0:1, :] = column(branch.astype(F32))
    small_ref[6:8, :] = jnp.zeros((2, width), F32)
    small_ref[12:16, :] = jnp.zeros((4, width), F32)
    gap = branch_at + 2 * rows
    send_ref[gap:act_at, :] = jnp.zeros((act_at - gap, 256), BF16)
    tall_ref[...] = right_trans(out_w[...], branch).astype(BF16)
    for at in range(ZS):
        start = pl.multiple_of((z_at ^ at) * part, part)
        mgrad_refs[at][...] = tall_ref[pl.ds(start, part), :]


def middle(meta, mixed, groups, tokens, seed, vec, upoff, weights):
    rows, width = tokens.shape
    hidden = upoff.shape[1]
    in_vmem = pl.BlockSpec(memory_space=pltpu.VMEM)
    in_place = pl.BlockSpec(memory_space=pl.ANY)
    flat = [item for group in mixed for item in group]
    part = jax.ShapeDtypeStruct((width // ZS, rows), BF16)
    return pl.pallas_call(
        partial(middle_kernel, groups=groups, shared=len(weights) == 5),
        grid_spec=pltpu.PrefetchScalarGridSpec(
            num_scalar_prefetch=1,
            grid=(),
            in_specs=[in_vmem] * (4 + len(flat)) + [in_place] * len(weights),
            out_specs=[in_vmem] * (5 + ZS),
            scratch_shapes=[
                pltpu.VMEM((width, width), BF16),
                pltpu.VMEM((width, hidden), BF16),
                pltpu.VMEM((hidden, width), BF16),
                pltpu.VMEM((rows, hidden), F32),
                pltpu.VMEM((rows, width), BF16),
                pltpu.VMEM((width, rows), BF16),
                pltpu.SemaphoreType.DMA((11,)),
            ],
        ),
        out_shape=[jax.ShapeDtypeStruct((rows, width), F32)] * 2
        + [part] * ZS
        + [
            jax.ShapeDtypeStruct((2 * hidden, 256), BF16),
            jax.ShapeDtypeStruct((hidden + 2 * rows, 256), BF16),
            jax.ShapeDtypeStruct((16, width), F32),
        ],
        compiler_params=pltpu.CompilerParams(vmem_limit_bytes=VMEM_LIMIT),
        cost_estimate=work(15),
        name="middle",
    )(meta, tokens, seed, vec, upoff, *flat, *weights)


def down_kernel(meta_ref, keep_ref, got_ref, own_ffn_ref, got_ffn_ref, out_ref):
    keep, got = keep_ref[...], got_ref[...]
    rows = keep.shape[1]
    for at in range(out_ref.shape[1] // 256):
        cut = slice(at * rows, (at + 1) * rows)
        value = matmul(keep, own_ffn_ref[cut, :]) + matmul(got, got_ffn_ref[cut, :])
        out_ref[:, at * 256 : (at + 1) * 256] = value.astype(BF16)


def down_slab(meta, keep, send, got):
    block = send.shape[0] // 8
    kept = pl.BlockSpec((block, send.shape[1]), lambda i, m: (m[0], 0))
    act = pl.BlockSpec((block, send.shape[1]), lambda i, m: (5 + m[0], 0))
    ffn = pl.BlockSpec((block, send.shape[1]), lambda i, m: (7, 0))
    return pl.pallas_call(
        down_kernel,
        grid_spec=pltpu.PrefetchScalarGridSpec(
            num_scalar_prefetch=1,
            grid=(1,),
            in_specs=[kept, act, ffn, ffn],
            out_specs=pl.BlockSpec((block, block), lambda i, m: (0, 0)),
        ),
        out_shape=jax.ShapeDtypeStruct((block, block), BF16),
        compiler_params=pltpu.CompilerParams(vmem_limit_bytes=24 << 20),
        cost_estimate=work(2),
        name="down_slab",
    )(meta, keep, got, send, got)


def up_kernel(meta_ref, keep_ref, send_ref, got_ref, own_small_ref, got_small_ref, *refs):
    out_refs, table_ref = refs[:2], refs[2]
    rows = send_ref.shape[1]
    width = own_small_ref.shape[1]
    block = width // 4
    side = width // 2
    normed_at = 2 * width
    branch_at = normed_at + 2 * width
    x_at = meta_ref[0]
    pre_keep = 2 * width
    for w in range(2):
        small = own_small_ref[...] + got_small_ref[...]
        table_ref[...] = jnp.zeros_like(table_ref)
        for at in range(side // 128):
            low = w * side + at * 128
            table_ref[at * 8 : (at + 1) * 8, :] = small[:8, low : low + 128]
        base = side // 128 * 8
        for at in range(2 * width // 128):
            line = 8 + 2 * w + at // (width // 128)
            low = at % (width // 128) * 128
            table_ref[base + at : base + at + 1, :] = small[line : line + 1, low : low + 128]
        for out_ref, which in zip(out_refs, (1 - x_at, x_at)):
            start = pl.multiple_of(which * block, block)
            target = slice(w * block, (w + 1) * block)
            own = send_ref[pl.ds(normed_at + w * side + start, block), :]
            got = got_ref[pl.ds(normed_at + w * side + start, block), :]
            for at in range(normed_at // rows):
                cut = slice(at * rows, (at + 1) * rows)
                value = matmul(own, keep_ref[pre_keep + at * rows : pre_keep + (at + 1) * rows, :])
                value = value + matmul(got, got_ref[cut, :])
                out_ref[target, at * 256 : (at + 1) * 256] = value.astype(BF16)
            own = send_ref[pl.ds(normed_at + width + w * side + start, block), :]
            got = got_ref[pl.ds(normed_at + width + w * side + start, block), :]
            lane = normed_at // rows * 256
            for at in range(2):
                mine = 4 * width + at * rows
                theirs = branch_at + at * rows
                value = matmul(own, keep_ref[mine : mine + rows, :])
                value = value + matmul(got, got_ref[theirs : theirs + rows, :])
                value = value[:, : min(256, side - at * 256)].astype(BF16)
                out_ref[target, lane : lane + value.shape[1]] = value
                lane += value.shape[1]
            out_ref[target, lane : lane + 128] = table_ref[pl.ds(start, block), :].astype(BF16)


def up_slabs(meta, keep, send, got, own_small, got_small):
    width = own_small.shape[1]
    columns = 2 * width + width // 2 + 128
    first = pl.BlockSpec((5 * width, send.shape[1]), lambda i, m: (0, 0))

    def whole(value):
        return pl.BlockSpec(value.shape, lambda i, m: (0, 0))

    return pl.pallas_call(
        up_kernel,
        grid_spec=pltpu.PrefetchScalarGridSpec(
            num_scalar_prefetch=1,
            grid=(1,),
            in_specs=[whole(keep), first, first, whole(own_small), whole(own_small)],
            out_specs=[pl.BlockSpec((width // 2, columns), lambda i, m: (0, 0))] * 2,
            scratch_shapes=[pltpu.VMEM((width // 2, 128), F32)],
        ),
        out_shape=[jax.ShapeDtypeStruct((width // 2, columns), BF16)] * 2,
        compiler_params=pltpu.CompilerParams(vmem_limit_bytes=40 << 20),
        cost_estimate=work(4),
        name="up_slabs",
    )(meta, keep, send, got, own_small, got_small)


def key_sum_kernel(own_ref, core_ref, got_ref, *out_refs):
    size = out_refs[0].shape[1]
    for at, ref in enumerate(out_refs):
        cut = slice(at * size, (at + 1) * size)
        kept = (own_ref[cut, :].astype(F32) + core_ref[cut, :].astype(F32)).astype(BF16)
        ref[...] = (kept.astype(F32) + got_ref[cut, :].astype(F32)).astype(BF16).T


def key_sum(own, core, got):
    rows, columns = got.shape
    half = pl.BlockSpec((rows, columns), lambda i: (0, 0))
    return pl.pallas_call(
        key_sum_kernel,
        grid=(1,),
        in_specs=[half] * 3,
        out_specs=[pl.BlockSpec((columns, rows // ZS), lambda i: (0, 0))] * ZS,
        out_shape=[jax.ShapeDtypeStruct((columns, rows // ZS), BF16)] * ZS,
        compiler_params=pltpu.CompilerParams(vmem_limit_bytes=24 << 20),
        cost_estimate=work(2),
        name="key_sum",
    )(own, core, got)


def head_kernel(meta_ref, *refs):
    turned_refs, query_refs, kv_refs = refs[:2], refs[2 : 2 + ZS], refs[2 + ZS : 2 + 2 * ZS]
    refs = refs[2 + 2 * ZS :]
    out_ref = refs[-1]
    block = turned_refs[0].shape[0]

    def put(value, rows):
        columns = value.shape[1]
        if len(refs) == 2:
            value = value + refs[0][rows, :columns].astype(F32)
        out_ref[rows, :columns] = value.astype(BF16)
        out_ref[rows, columns:] = jnp.zeros((value.shape[0], out_ref.shape[1] - columns), BF16)

    grads = [jnp.concatenate([ref[...] for ref in items], axis=1) for items in (query_refs, kv_refs)]
    grads = jnp.concatenate(grads, axis=0)
    turned = jnp.concatenate([ref[...] for ref in turned_refs], axis=1)
    put(right_trans(turned, grads), slice(0, block))
    ones = jnp.ones((16, turned.shape[1]), BF16)
    put(right_trans(ones, grads), slice(block, block + 16))


def head_slab(meta, turned, query, kv, count, slabs, got=None, first=0):
    width, rows = turned[0].shape
    block = width // count
    columns = -(-(query[0].shape[0] + kv[0].shape[0]) // 128) * 128
    return pl.pallas_call(
        head_kernel,
        grid_spec=pltpu.PrefetchScalarGridSpec(
            num_scalar_prefetch=1,
            grid=(slabs,),
            in_specs=[pl.BlockSpec((block, rows), lambda i, m: (m[i] * 2 + m[slabs], 0))] * 2
            + [pl.BlockSpec(item.shape, lambda i, m: (0, 0)) for item in [*query, *kv]]
            + (
                []
                if got is None
                else [pl.BlockSpec((block + 16, columns), lambda i, m: (first + i, 0))]
            ),
            out_specs=pl.BlockSpec((block + 16, columns), lambda i, m: (i, 0)),
        ),
        out_shape=jax.ShapeDtypeStruct((slabs * (block + 16), columns), BF16),
        compiler_params=pltpu.CompilerParams(vmem_limit_bytes=24 << 20),
        cost_estimate=work(2),
        name="head_slab",
    )(meta, *turned, *query, *kv, *(() if got is None else (got,)))


def token_kernel(meta_ref, resid_ref, *refs, shared):
    query_refs, kv_refs, refs = refs[:ZS], refs[ZS : 2 * ZS], refs[2 * ZS :]
    weight_refs, refs = refs[: 5 if shared else 3], refs[5 if shared else 3 :]
    out_ref, full_ref, turned_ref, sems = refs
    w_at, c_at, z_at = meta_ref[1], meta_ref[2], meta_ref[3]
    width = full_ref.shape[1]
    moves = []
    if shared:
        count = weight_refs[0].shape[0]
        half = count // 2
        for kind in range(3):
            start = pl.multiple_of(w_at * count, count)
            moves.append((weight_refs[kind], full_ref.at[kind, pl.ds(start, count), :]))
            for ref, core in ((weight_refs[3], c_at), (weight_refs[4], 1 - c_at)):
                start = pl.multiple_of(((1 - w_at) * 2 + core) * half, half)
                moves.append(
                    (
                        ref.at[pl.ds(kind * half, half), :],
                        full_ref.at[kind, pl.ds(start, half), :],
                    )
                )
    else:
        for kind in range(3):
            moves.append((weight_refs[kind], full_ref.at[kind]))
    copies = []
    for at, (source, target) in enumerate(moves):
        copies.append(pltpu.make_async_copy(source, target, sems.at[at]))
        copies[-1].start()
    part = width // ZS
    head_dim = width // HEADS
    for at in range(ZS):
        low = (z_at ^ at) * part
        turned_ref[0, pl.ds(pl.multiple_of(low, part), part), :] = query_refs[at][...]
        for head in range(part // head_dim):
            start = pl.ds(pl.multiple_of(low + head * head_dim, head_dim), head_dim)
            for kind in (1, 2):
                row = (2 * head + kind - 1) * head_dim
                turned_ref[kind, start, :] = kv_refs[at][row : row + head_dim, :]
    parts = [turned_ref[kind].T for kind in range(3)]
    for copy in copies:
        copy.wait()
    out = resid_ref[...]
    for kind in range(3):
        out = out + right_trans(parts[kind], full_ref[kind])
    out_ref[...] = out


def token_gradient(meta, resid, query, kv, weights):
    rows, width = resid.shape
    in_vmem = pl.BlockSpec(memory_space=pltpu.VMEM)
    in_place = pl.BlockSpec(memory_space=pl.ANY)
    return pl.pallas_call(
        partial(token_kernel, shared=len(weights) == 5),
        grid_spec=pltpu.PrefetchScalarGridSpec(
            num_scalar_prefetch=1,
            grid=(),
            in_specs=[in_vmem] * (1 + 2 * ZS) + [in_place] * len(weights),
            out_specs=in_vmem,
            scratch_shapes=[
                pltpu.VMEM((3, width, width), BF16),
                pltpu.VMEM((3, width, rows), BF16),
                pltpu.SemaphoreType.DMA((9,)),
            ],
        ),
        out_shape=jax.ShapeDtypeStruct((rows, width), F32),
        compiler_params=pltpu.CompilerParams(vmem_limit_bytes=32 << 20),
        cost_estimate=work(4),
        name="token_gradient",
    )(meta, resid, *query, *kv, *weights)


def down_finish_kernel(meta_ref, *refs):
    block = refs[0].shape[0] // 4
    c_at, x_at = meta_ref[0], meta_ref[1]
    for at in range(4):
        for z in range(4):
            place = (c_at ^ (at >> 1)) * 8 + z * 2 + (x_at ^ (at & 1))
            start = pl.multiple_of(place * block, 8)
            refs[4][pl.ds(start, block), :] = refs[at][z * block : (z + 1) * block, :].astype(F32)


def down_finish(meta, pieces):
    block, width = pieces[0].shape
    in_vmem = pl.BlockSpec(memory_space=pltpu.VMEM)
    return pl.pallas_call(
        down_finish_kernel,
        grid_spec=pltpu.PrefetchScalarGridSpec(
            num_scalar_prefetch=1, grid=(), in_specs=[in_vmem] * 4, out_specs=in_vmem
        ),
        out_shape=jax.ShapeDtypeStruct((4 * block, width), F32),
        compiler_params=pltpu.CompilerParams(vmem_limit_bytes=32 << 20),
        cost_estimate=work(4),
        name="down_finish",
    )(meta, *pieces)


def up_finish_kernel(meta_ref, *refs):
    pieces = refs[:4]
    up_ref, out_ref, small_ref = refs[4:]
    block = pieces[0].shape[0]
    quarter = up_ref.shape[1] // 4
    side = out_ref.shape[1] // 2
    c_at, x_at = meta_ref[0], meta_ref[1]
    for at in range(4):
        start = pl.multiple_of((x_at ^ (at & 1)) * block, 8)
        rows = pl.ds(start, block)
        core = c_at ^ (at >> 1)
        for half in range(2):
            lanes = pl.ds(pl.multiple_of((2 * half + core) * quarter, 128), quarter)
            up_ref[rows, lanes] = pieces[at][:, half * quarter : (half + 1) * quarter].astype(F32)
        out_ref[rows, pl.ds(pl.multiple_of(core * side, 128), side)] = (
            pieces[at][:, 2 * quarter : 2 * quarter + side].astype(F32)
        )
        if at < 2:
            small_ref[rows, :] = pieces[at][:, 2 * quarter + side :].astype(F32)


def up_finish(meta, pieces, hidden, width):
    block = pieces[0].shape[0]
    in_vmem = pl.BlockSpec(memory_space=pltpu.VMEM)
    shapes = [(2 * block, hidden), (2 * block, width), (2 * block, 128)]
    return pl.pallas_call(
        up_finish_kernel,
        grid_spec=pltpu.PrefetchScalarGridSpec(
            num_scalar_prefetch=1,
            grid=(),
            in_specs=[in_vmem] * 4,
            out_specs=[in_vmem] * 3,
        ),
        out_shape=[jax.ShapeDtypeStruct(shape, F32) for shape in shapes],
        compiler_params=pltpu.CompilerParams(vmem_limit_bytes=40 << 20),
        cost_estimate=work(5),
        name="up_finish",
    )(meta, *pieces)


def head_finish_kernel(meta_ref, own_ref, got_ref, query_ref, key_ref, value_ref, bias_ref, *, part):
    size = own_ref.shape[0] // ZS
    block = size - 16
    head_dim = part // 3
    for at, source in enumerate((own_ref, got_ref)):
        start = pl.multiple_of((meta_ref[0] ^ at) * block, 8)
        rows = pl.ds(start, block)
        keys, values, queries = [], [], []
        for z in range(ZS):
            item = source[((z & 1) * 2 + (z >> 1)) * size :][:size].astype(F32)
            for head in range(3):
                low = part + head * 2 * head_dim
                keys.append(item[:, low : low + head_dim])
                values.append(item[:, low + head_dim : low + 2 * head_dim])
            queries.append(item[:, :part])
        key = jnp.concatenate(keys, axis=1)
        value = jnp.concatenate(values, axis=1)
        query = jnp.concatenate(queries, axis=1)
        query_ref[rows, :] = query[:block]
        key_ref[rows, :] = key[:block]
        value_ref[rows, :] = value[:block]
        if at == 0:
            bias_ref[0:8, :] = query[block : block + 8]
            bias_ref[8:16, :] = value[block : block + 8]


def head_finish(meta, own, got, width):
    rows = own.shape[0]
    rows = 2 * (rows // ZS - 16)
    return small_call(
        partial(head_finish_kernel, part=width // ZS),
        meta,
        (own, got),
        [((rows, width), F32)] * 3 + [((16, width), F32)],
        limit=40,
        name="head_finish",
    )


def in_order(index, own, other, axis):
    return jnp.where(
        index == 0,
        jnp.concatenate([own, other], axis=axis),
        jnp.concatenate([other, own], axis=axis),
    )


def part_of(value, index, count, axis):
    size = value.shape[axis] // count
    return lax.dynamic_slice_in_dim(value, index * size, size, axis)


def body(
    inputs,
    lengths,
    cotangent,
    query_weight,
    query_bias,
    key_weight,
    value_weight,
    value_bias,
    output_weight,
    output_bias,
    first_gain,
    first_shift,
    up_weight,
    up_bias,
    down_weight,
    down_bias,
    second_gain,
    second_shift,
    *,
    sizes,
):
    count_o, count_w = sizes
    w_at = lax.axis_index("w")
    z_at = lax.axis_index("z")
    c_at = lax.axis_index("c")
    x_at = lax.axis_index("x")
    o_at = lax.axis_index("o")
    tokens = inputs[0]
    local_rows, width = tokens.shape
    head_dim = width // HEADS
    heads = HEADS // ZS
    part = heads * head_dim
    length = lengths[0]

    hold = lax.optimization_barrier

    near = ((0, 1), (1, 0), (2, 3), (3, 2))
    far = ((0, 2), (2, 0), (1, 3), (3, 1))
    cross = ((0, 3), (3, 0), (1, 2), (2, 1))

    def exchange(pieces):
        return [pieces[0]] + [
            lax.ppermute(item, "z", perm) for item, perm in zip(pieces[1:], (near, far, cross))
        ]

    own_rows = query_weight.shape[0]
    big_weights = (output_weight, up_weight, down_weight)
    sides = jnp.stack([z_at, c_at]).astype(jnp.int32)
    low_tokens = tokens.astype(BF16)
    kv_own, query_own, *low_heads, head_pack = prepare(
        sides, (query_weight, key_weight, value_weight)
    )
    line_tokens = [low_tokens, lax.ppermute(low_tokens, "z", near)]
    line_tokens.append(lax.ppermute(low_tokens, "z", far))
    early = jnp.stack([query_bias, value_bias]).astype(BF16)
    late = jnp.stack(
        [
            item.reshape(-1, own_rows)[row]
            for item in (
                output_bias,
                first_gain,
                first_shift,
                down_bias,
                second_gain,
                second_shift,
                up_bias,
            )
            for row in range(item.shape[0] // own_rows)
        ]
    )
    if count_w == 2:
        kv_other, query_other, early_got = [
            swap(item, "w") for item in (kv_own, query_own, early)
        ]
        *low_weights, weight_pack = round_weights(sides, big_weights)
        kv_other, query_other, early_got, weight_pack, *line_tokens[1:3] = hold(
            (kv_other, query_other, early_got, weight_pack, *line_tokens[1:3])
        )
        weight_got = swap(weight_pack, "w")
        sources = (kv_own, query_own, kv_other, query_other, early, early_got)
    else:
        attn_own = jnp.concatenate([kv_own, query_own], axis=1)
        attn_full = lax.all_gather(attn_own, "w", axis=0, tiled=True)
        small = jnp.concatenate([early, late.astype(BF16)], axis=0)
        small_all = lax.all_gather(small, "w", axis=0, tiled=False)
        low_weights = [item.astype(BF16) for item in big_weights]
        weight_got = [lax.all_gather(item, "w", axis=0, tiled=True) for item in low_weights]
        head_weights = [lax.all_gather(item, "w", axis=0, tiled=True) for item in low_heads]
        pair = jnp.transpose(small_all[:, :2], (1, 0, 2)).reshape(2, width).astype(F32)
        own_bias = lax.dynamic_slice_in_dim(pair, z_at * part, part, 1)
        value_bias_own = own_bias[1].reshape(heads, 1, head_dim)
        kv_bias = jnp.concatenate([jnp.zeros_like(value_bias_own), value_bias_own], axis=1)
        bias_row = jnp.concatenate([kv_bias.reshape(1, 2 * part), own_bias[:1]], axis=1)
        sources = (attn_full, bias_row)

    line_tokens.append(lax.ppermute(line_tokens[2], "z", near))
    corner = jnp.stack([w_at, z_at]).astype(jnp.int32)
    made = [project(corner, *line_tokens[:2], sources)]
    made[0], *line_tokens[2:] = hold((made[0], *line_tokens[2:]))
    made.append(project(corner, *line_tokens[2:], sources))
    queries = [item[0] for item in made]
    turned = [item[2] for item in made]
    kv_blocks = [[item[1] for item in made]]
    for axis in ("x", "c", "o")[: 3 if count_o == 2 else 2]:
        kv_blocks = kv_blocks + [[swap(item, axis) for item in pair] for pair in kv_blocks]
    places = []
    for at in range(4 * count_o):
        o_of = o_at ^ (at >> 2)
        places.append(o_of * 16 + (x_at ^ (at & 1)) * 2 + (c_at ^ ((at >> 1) & 1)))
    meta = jnp.stack([length, z_at] + places).astype(jnp.int32)
    kv_blocks = [
        [pltpu.with_memory_space_constraint(item, pltpu.MemorySpace.HBM) for item in pair]
        for pair in kv_blocks
    ]
    attended, *made = attend_forward(meta, queries, kv_blocks, heads)
    logs = made[ZS]
    if count_w == 2:
        attended, weight_got, head_pack, late = hold((attended, weight_got, head_pack, late))
        late = late.astype(BF16)
        small_own = jnp.concatenate([early, late], axis=0)
        small_got = jnp.concatenate([early_got, swap(late, "w")], axis=0)
        small_all = in_order(w_at, small_own[None], small_got[None], 0)
        weights = [*low_weights, weight_got, swap(weight_got, "c")]
        head_got = swap(head_pack, "w")
    else:
        weights = weight_got
    mixed = exchange(made[:ZS])
    small_all = small_all.astype(F32)
    vec = jnp.transpose(small_all[:, :8], (1, 0, 2)).reshape(8, width)
    up_offset = small_all[:, 8:].reshape(1, -1)

    split = count_w == 2 and count_o == 1
    my_index = o_at * 16 + z_at * 4 + x_at * 2 + c_at
    rest = jnp.clip(length - my_index * local_rows, 0, local_rows)
    core = c_at if split else jnp.zeros_like(c_at)
    spots = jnp.stack([rest, w_at, core, z_at]).astype(jnp.int32)
    outputs, resid_grad, *made = middle(
        spots, [mixed], ((0, heads),), tokens, cotangent[0], vec, up_offset, weights
    )
    head_grads = exchange(made[:ZS])
    send, keep, small_own = made[ZS:]
    hidden = up_offset.shape[1]

    near_bit, far_bit = z_at & 1, z_at >> 1

    def add_pair(kept, got):
        return (kept.astype(F32) + got.astype(F32)).astype(BF16)

    def join(value, got, bit):
        return in_order(bit, value, got, 0)

    spot = jnp.stack([c_at, x_at]).astype(jnp.int32)
    token = [spot]

    def arrive(*values):
        token[0], *values = hold((token[0], *values))
        return values[0] if len(values) == 1 else values

    def backward(first, count, made=()):
        return attend_backward(
            meta, queries, head_grads, attended, logs, kv_blocks, first, count, made
        )

    def to_near(value):
        return lax.ppermute(value, "z", near)

    def to_far(value):
        return lax.ppermute(value, "z", far)

    def head_part(ws, core, got=None, first=0):
        at = jnp.stack([jnp.asarray(item) for item in (*ws, core)]).astype(jnp.int32)
        return head_slab(at, turned, query_low, kv_low, 2 * count_w, len(ws), got, first)

    def pick(w, c):
        return jnp.stack([jnp.asarray(w), jnp.asarray(c)]).astype(jnp.int32)

    if split:
        got, small_got = swap(send, "c"), swap(small_own, "c")
        down_far = down_slab(pick(1 - w_at, 0), keep, send, got)
        up_sent, up_kept = up_slabs(
            jnp.stack([x_at]).astype(jnp.int32), keep, send, got, small_own, small_got
        )
        down_near = down_slab(pick(1 * w_at, 0), keep, send, got)
        down_far, up_sent, down_near, *head_grads = hold(
            (down_far, up_sent, down_near, *head_grads)
        )
        made = backward(0, heads - 1)
        down_got, *made = arrive(swap(down_far, "w"), *made)
        down_sum = add_pair(down_near, down_got)
        down_got = to_near(part_of(down_sum, 1 - near_bit, 2, 0))
        down_sum, *head_grads = arrive(down_sum, *head_grads)
        made = backward(heads - 1, 1, made)
        down_got, up_got, head_got, *made = arrive(
            down_got, swap(up_sent, "x"), head_got, *made
        )
        query_low, pairs = made[:ZS], made[ZS:]
        head_weights = [*low_heads, head_got, swap(head_got, "c")]
        pair_got = swap(pairs[1], "c")
        query_got = exchange(query_low)
        down_sum = add_pair(part_of(down_sum, near_bit, 2, 0), down_got)
        down_got = to_far(part_of(down_sum, 1 - far_bit, 2, 0))
        up_sum = add_pair(up_kept, up_got).reshape(2, own_rows // 2, -1)
        up_got = swap(lax.dynamic_index_in_dim(up_sum, 1 - w_at, 0, keepdims=False), "w")
        pair_got = arrive(pair_got)
        half_rows = pair_got.shape[0] // 2
        pair_sent = add_pair(pairs[0][half_rows:], pair_got[half_rows:])
        pair_sent = arrive(pair_sent)
        key_got = swap(pair_sent, "x")
        key_got, down_got, up_got, *query_got = arrive(key_got, down_got, up_got, *query_got)
        up_sum = add_pair(lax.dynamic_index_in_dim(up_sum, w_at, 0, keepdims=False), up_got)
        up_sent, key_got = arrive(part_of(up_sum, 1 - near_bit, 2, 0), key_got)
        up_got = to_near(up_sent)
        kv_low = key_sum(pairs[0], pair_got, key_got)
        down_sum = add_pair(part_of(down_sum, far_bit, 2, 0), down_got)
        down_got = swap(part_of(down_sum, 1 - x_at, 2, 0), "x")
        head_core = swap(head_part((1 - w_at, 1 * w_at), 1 - c_at), "c")
        kv_got = exchange(kv_low)
        down_got = arrive(down_got)
        down_sum = add_pair(part_of(down_sum, x_at, 2, 0), down_got)
        down_got = to_far(down_sum)
        head_core = arrive(head_core)
        head_both = head_part((1 - w_at, 1 * w_at), c_at, head_core)
        head_rows = head_both.shape[0] // 2
        head_sent = swap(head_both[:head_rows], "w")
        head_sum = head_both[head_rows:]
        up_got = arrive(up_got)
        up_sum = add_pair(part_of(up_sum, near_bit, 2, 0), up_got)
        up_got = to_far(part_of(up_sum, 1 - far_bit, 2, 0))
        head_sent = arrive(head_sent)
        head_sum = add_pair(head_sum, head_sent)
        head_got = swap(head_sum, "x")
        kv_got = arrive(*kv_got)
        input_grad = token_gradient(
            spots, resid_grad, query_got, kv_got, head_weights
        )
        up_got = arrive(up_got)
        up_sum = add_pair(part_of(up_sum, far_bit, 2, 0), up_got)
        up_got = to_far(up_sum)
        down_got = arrive(down_got)
        down_sum = join(down_sum[None], down_got[None], far_bit)
        down_got = to_near(down_sum)
        head_got = arrive(head_got)
        head_sum = add_pair(head_sum, head_got)
        head_got = to_far(head_sum)
        up_got = arrive(up_got)
        up_sum = join(up_sum, up_got, far_bit)
        up_got = to_near(up_sum)
        down_got = arrive(down_got)
        down_sum = join(down_sum[None], down_got[None], near_bit)
        down_sum = down_sum.reshape(-1, width)
        down_x = swap(down_sum, "x")
        down_c = swap(down_sum, "c")
        head_got = arrive(head_got)
        head_two = join(head_sum, head_got, far_bit)
        head_got = to_near(head_two)
        up_got = arrive(up_got)
        up_sum = join(up_sum, up_got, near_bit)
        up_x = swap(up_sum, "x")
        up_c = swap(up_sum, "c")
        down_x, input_grad = arrive(down_x, input_grad)
        down_pieces = [down_sum, down_x, down_c, swap(down_x, "c")]
        head_got = arrive(head_got)
        head_four = join(head_two, head_got, near_bit)
        head_other = swap(head_four, "c")
        total_down = down_finish(spot, down_pieces)
        up_x, total_down = arrive(up_x, total_down)
        up_pieces = [up_sum, up_x, up_c, swap(up_x, "c")]
        total_query, total_key, total_value, head_bias = head_finish(
            spot, head_four, head_other, width
        )
        total_query, total_key, total_value = arrive(total_query, total_key, total_value)
        total_up, total_out, table = up_finish(token[0], up_pieces, hidden, width)
        groups = own_rows // 128
        small_total = table[: 8 * groups].reshape(groups, 8, 128)
        vectors = [small_total[:, at].reshape(own_rows) for at in range(6)]
        lines = hidden // count_w // 128
        total_up_bias = table[8 * groups : 8 * groups + lines].reshape(-1)
    else:
        made = backward(0, heads)
        query_low, pairs = made[:ZS], made[ZS:]
        if count_o == 2:
            pairs = [plus(spot, pairs[at], swap(pairs[at + 2], "o")) for at in range(2)]
        pair_got = swap(pairs[1], "c")
        half_rows = pair_got.shape[0] // 2
        key_got = swap(plus(spot, pairs[0], pair_got, half_rows), "x")
        kv_low = key_sum(pairs[0], pair_got, key_got)
        if count_w == 2:
            head_weights = [*low_heads, head_got, swap(head_got, "c")]
        input_grad = token_gradient(
            spots.at[2].set(c_at.astype(jnp.int32)),
            resid_grad,
            exchange(query_low),
            exchange(kv_low),
            head_weights,
        )
        every_w = tuple(range(count_w))
        slabs = head_part(every_w, c_at, swap(head_part(every_w, 1 - c_at), "c"))
        head_sum = lax.psum_scatter(slabs, "w", scatter_dimension=0, tiled=True)
        head_sum = plus(spot, head_sum, swap(head_sum, "x"))
        if count_o == 2:
            head_sum = plus(spot, head_sum, swap(head_sum, "o"))
        n_bit, f_bit = [
            jnp.stack([bit, bit]).astype(jnp.int32) for bit in (near_bit, far_bit)
        ]
        head_sum = unite(f_bit, head_sum, to_far(head_sum))
        head_sum = unite(n_bit, head_sum, to_near(head_sum))
        total_query, total_key, total_value, head_bias = head_finish(
            spot, head_sum, swap(head_sum, "c"), width
        )
        quarter = hidden // 4
        count = quarter // 256
        act_at = 5 * quarter
        act = [keep[:quarter], send[act_at : act_at + quarter], keep[quarter : 2 * quarter]]
        act += [send[act_at + quarter : act_at + 2 * quarter]]
        act = jnp.concatenate(act, axis=0)

        def rows_of(value, low, at):
            return value[low + at * local_rows : low + (at + 1) * local_rows]

        ffn_at = act_at + 2 * quarter
        ffn = jnp.concatenate([rows_of(send, ffn_at, at) for at in range(width // 256)], axis=1)
        pre = []
        for half in range(2):
            pre += [rows_of(keep, 2 * quarter, half * count + at) for at in range(count)]
            pre += [rows_of(send, 0, half * count + at) for at in range(count)]
        pre = jnp.concatenate(pre, axis=1)
        normed_turned = send[2 * quarter : 2 * quarter + width]
        mixed_turned = send[2 * quarter + width : 2 * quarter + 2 * width]
        side = width // 2
        branch = jnp.concatenate(
            [
                rows_of(keep, 4 * quarter, 0),
                rows_of(keep, 4 * quarter, 1)[:, : side - 256],
                rows_of(send, 2 * quarter + 2 * width, 0),
                rows_of(send, 2 * quarter + 2 * width, 1)[:, : side - 256],
            ],
            axis=1,
        )

        def sum_all(value):
            value = value.astype(BF16)
            value = lax.psum_scatter(value, "w", scatter_dimension=0, tiled=True)
            return lax.psum(value, ("o", "z", "x", "c")).astype(F32)

        total_down = sum_all(matmul(act, ffn))
        total_up = sum_all(matmul(normed_turned, pre))
        total_out = sum_all(matmul(mixed_turned, branch))
        small_own = lax.psum(small_own, ("o", "z", "x", "c", "w"))
        vectors = [part_of(small_own[at], w_at, count_w, 0) for at in range(6)]
        total_up_bias = part_of(small_own[8:12].reshape(-1), w_at, count_w, 0)

    totals = [part_of(head_bias[at], w_at, count_w, 0) for at in (0, 8)] + vectors
    return (
        outputs[None],
        input_grad[None],
        total_query,
        totals[0],
        total_key,
        total_value,
        totals[1],
        total_out,
        totals[2],
        totals[3],
        totals[4],
        total_up,
        total_up_bias,
        total_down,
        totals[5],
        totals[6],
        totals[7],
    )


def solution(mesh):
    count_s = mesh.shape["seq"]
    count_w = mesh.shape["wshard"]
    count_o = count_s // 16
    fine = Mesh(
        mesh.devices.reshape(count_o, ZS, 2, 2, count_w), ("o", "z", "x", "c", "w")
    )
    seq = ("o", "z", "x", "c")
    rows = P("w", seq, None)
    matrix = P("w", None)
    vector = P("w")
    placed = (
        rows,
        vector,
        rows,
        matrix,
        vector,
        matrix,
        matrix,
        vector,
        matrix,
        vector,
        vector,
        vector,
        matrix,
        vector,
        matrix,
        vector,
        vector,
        vector,
    )
    return jax.shard_map(
        partial(body, sizes=(count_o, count_w)),
        mesh=fine,
        in_specs=placed,
        out_specs=(
            rows,
            rows,
            matrix,
            vector,
            matrix,
            matrix,
            vector,
            matrix,
            vector,
            vector,
            vector,
            matrix,
            vector,
            matrix,
            vector,
            vector,
            vector,
        ),
        check_vma=False,
    )
```

```python
from functools import partial

import jax
import jax.numpy as jnp
from jax import lax
from jax.experimental import pallas as pl
from jax.experimental.pallas import tpu as pltpu
from jax.sharding import Mesh, PartitionSpec as P

HEADS = 12
ZS = 4
NEG_FILL = -1e30
VMEM_LIMIT = 60 << 20
SWAP = ((0, 1), (1, 0))
F32 = jnp.float32
BF16 = jnp.bfloat16


def matmul(left_side, right_side):
    return jnp.dot(left_side, right_side, preferred_element_type=F32)


def right_trans(left_side, right_side):
    return lax.dot_general(
        left_side, right_side, (((1,), (1,)), ((), ())), preferred_element_type=F32
    )


def work(units):
    return pl.CostEstimate(flops=int(units * 1e3), bytes_accessed=1, transcendentals=0)


def swap(value, axis):
    return lax.ppermute(value, axis, SWAP)


def touched_groups(length, rows, outer):
    group = 4 * rows
    left = length - outer * (ZS * group)
    return jnp.clip((left + group - 1) // group, 0, ZS)


def with_mask(kv, place, length):
    at = place + lax.broadcasted_iota(jnp.int32, kv.shape, 0)
    lane = lax.broadcasted_iota(jnp.int32, kv.shape, 1)
    fill = jnp.where(at < length, 0.0, jnp.where(lane == 0, NEG_FILL, 0.0))
    return jnp.concatenate([kv, fill.astype(BF16)], axis=1)


def load_head(kv_refs, rows_ref, turned_ref, low):
    head_dim = turned_ref.shape[1]
    for at, ref in enumerate(kv_refs):
        block, half = at // 2, at % 2
        size = ref.shape[0]
        for start in range(0, size, 256):
            value = ref[start : start + 256, :]
            place = slice(half * size + start, half * size + start + 256)
            rows_ref[block, place, :] = value
            turned_ref[block, :, place] = value.T[low : low + head_dim, :]


def forward_kernel(meta_ref, *refs, blocks, rows):
    query_refs, kv_refs = refs[:2], refs[2 : 2 + 2 * blocks]
    out_ref, *refs = refs[2 + 2 * blocks :]
    piece_refs, (log_ref, rows_ref, turned_ref) = refs[:ZS], refs[ZS:]
    head_dim, query_count = out_ref.shape
    length, z_at = meta_ref[0], meta_ref[1]
    load_head(kv_refs, rows_ref, turned_ref, head_dim)
    query = jnp.concatenate([ref[...] for ref in query_refs], axis=1)
    query = jnp.concatenate(
        [
            query,
            jnp.zeros((head_dim, query_count), BF16),
            jnp.ones((128, query_count), BF16),
        ],
        axis=0,
    )

    def step(group, carry, members):
        top, total, acc = carry
        start = pl.multiple_of((group ^ z_at) * rows, rows)
        found = []
        for block in members:
            place = (meta_ref[2 + block] + group * 4) * rows
            kv = with_mask(rows_ref[block, pl.ds(start, rows), :], place, length)
            found.append(matmul(kv, query))
        new_top = top
        for scores in found:
            new_top = jnp.maximum(new_top, jnp.max(scores, axis=0, keepdims=True))
        fade = jnp.exp(top - new_top)
        total = total * fade
        acc = acc * fade
        for block, scores in zip(members, found):
            weights = jnp.exp(scores - new_top)
            total = total + jnp.sum(weights, axis=0, keepdims=True)
            acc = acc + matmul(
                turned_ref[block, :, pl.ds(start, rows)], weights.astype(BF16)
            )
        return new_top, total, acc

    carry = (
        jnp.full((1, query_count), NEG_FILL, F32),
        jnp.zeros((1, query_count), F32),
        jnp.zeros((head_dim, query_count), F32),
    )
    for first in range(0, blocks, 4):
        members = tuple(range(first, first + 4))
        count = touched_groups(length, rows, meta_ref[2 + first] // 16)
        carry = lax.fori_loop(0, count, lambda g, c: step(g, c, members), carry)
    top, total, acc = carry
    out = acc * (1.0 / total)
    out_ref[...] = out
    size = query_count // ZS
    for at in range(ZS):
        piece_refs[at][...] = out[:, at * size : (at + 1) * size].astype(BF16)
    log_ref[0] = top + jnp.log(total)


def attend_forward(meta, queries, kv_blocks, heads):
    blocks = len(kv_blocks)
    half_rows = kv_blocks[0][0].shape[0]
    part, half_count = queries[0].shape
    head_dim, query_count = part // heads, 2 * half_count
    size = query_count // ZS
    return pl.pallas_call(
        partial(forward_kernel, blocks=blocks, rows=2 * half_rows // ZS),
        grid_spec=pltpu.PrefetchScalarGridSpec(
            num_scalar_prefetch=1,
            grid=(heads,),
            in_specs=[pl.BlockSpec((head_dim, half_count), lambda i, m: (i, 0))] * 2
            + [pl.BlockSpec((half_rows, 128), lambda i, m: (0, i))] * (2 * blocks),
            out_specs=[pl.BlockSpec((head_dim, query_count), lambda i, m: (i, 0))]
            + [pl.BlockSpec((head_dim, size), lambda i, m: (i, 0))] * ZS
            + [pl.BlockSpec((1, 1, query_count), lambda i, m: (i, 0, 0))],
            scratch_shapes=[
                pltpu.VMEM((blocks, 2 * half_rows, 128), BF16),
                pltpu.VMEM((blocks, head_dim, 2 * half_rows), BF16),
            ],
        ),
        out_shape=[jax.ShapeDtypeStruct((part, query_count), F32)]
        + [jax.ShapeDtypeStruct((part, size), BF16)] * ZS
        + [jax.ShapeDtypeStruct((heads, 1, query_count), F32)],
        compiler_params=pltpu.CompilerParams(vmem_limit_bytes=VMEM_LIMIT),
        cost_estimate=work(8 * heads),
        name="attend_forward",
    )(meta, *queries, *[item for pair in kv_blocks for item in pair])


def backward_kernel(meta_ref, *refs, blocks, rows, extra):
    query_refs, (out_ref, log_ref), refs = refs[:2], refs[2:4], refs[4:]
    grad_refs, kv_refs = refs[:ZS], refs[ZS : ZS + 2 * blocks]
    refs = refs[ZS + 2 * blocks + extra :]
    dq_refs, pairs = refs[:ZS], refs[ZS : ZS + blocks // 2]
    rows_ref, turned_ref, qn_ref, gn_ref, acc_ref = refs[ZS + blocks // 2 :]
    head_dim, query_count = out_ref.shape
    length, z_at = meta_ref[0], meta_ref[1]
    block_rows = ZS * rows
    load_head(kv_refs, rows_ref, turned_ref, 0)
    query = jnp.concatenate([ref[...] for ref in query_refs], axis=1)
    grads = jnp.concatenate([ref[...] for ref in grad_refs], axis=1)
    blank = jnp.zeros((head_dim, query_count), BF16)
    query = jnp.concatenate([query, blank], axis=0)
    grad = jnp.concatenate([blank, grads], axis=0)
    qn_ref[...] = query.T
    gn_ref[...] = grad.T
    query = jnp.concatenate([query, jnp.ones((128, query_count), BF16)], axis=0)
    delta = jnp.sum(grads.astype(F32) * out_ref[...], axis=0, keepdims=True)
    log_sum = log_ref[0]
    acc_ref[...] = jnp.zeros_like(acc_ref)

    def put(block, start, value):
        pairs[block // 2][pl.ds(start + (block & 1) * block_rows, rows), :] = value

    def step(group, members):
        start = pl.multiple_of((group ^ z_at) * rows, rows)
        for block in members:
            kv = rows_ref[block, pl.ds(start, rows), :]
            place = (meta_ref[2 + block] + group * 4) * rows
            scores = matmul(with_mask(kv, place, length), query)
            prob_grad = matmul(kv, grad)
            prob = jnp.exp(scores - log_sum)
            score_grad = (prob * (prob_grad - delta)).astype(BF16)
            value = matmul(prob.astype(BF16), gn_ref[...]) + matmul(score_grad, qn_ref[...])
            put(block, start, value.astype(BF16))
            acc_ref[...] += matmul(turned_ref[block, :, pl.ds(start, rows)], score_grad)

    def clear(group, members):
        start = pl.multiple_of((group ^ z_at) * rows, rows)
        for block in members:
            put(block, start, jnp.zeros((rows, 128), BF16))

    def loop(low, high, fn):
        def one(group, carry):
            fn(group)
            return carry

        lax.fori_loop(low, high, one, 0)

    for first in range(0, blocks, 4):
        members = tuple(range(first, first + 4))
        count = touched_groups(length, rows, meta_ref[2 + first] // 16)
        loop(0, count, lambda g: step(g, members))
        loop(count, ZS, lambda g: clear(g, members))
    dq = (acc_ref[...] * head_dim ** (-0.5)).astype(BF16)
    size = query_count // ZS
    for at in range(ZS):
        dq_refs[at][...] = dq[:, at * size : (at + 1) * size]


def attend_backward(meta, queries, grads, out, log_sum, kv_blocks, first, count, made=()):
    blocks = len(kv_blocks)
    half_rows, columns = kv_blocks[0][0].shape
    heads = columns // 128
    part, half_count = queries[0].shape
    head_dim, query_count = part // heads, 2 * half_count
    size = query_count // ZS
    piece = pl.BlockSpec((head_dim, size), lambda i, m: (i + first, 0))
    ins = [
        *queries,
        out,
        log_sum,
        *grads,
        *[item for pair in kv_blocks for item in pair],
        *made,
    ]
    return pl.pallas_call(
        partial(backward_kernel, blocks=blocks, rows=2 * half_rows // ZS, extra=len(made)),
        grid_spec=pltpu.PrefetchScalarGridSpec(
            num_scalar_prefetch=1,
            grid=(count,),
            in_specs=[pl.BlockSpec((head_dim, half_count), lambda i, m: (i + first, 0))] * 2
            + [
                pl.BlockSpec((head_dim, query_count), lambda i, m: (i + first, 0)),
                pl.BlockSpec((1, 1, query_count), lambda i, m: (i + first, 0, 0)),
            ]
            + [piece] * ZS
            + [pl.BlockSpec((half_rows, 128), lambda i, m: (0, i + first))] * (2 * blocks)
            + [pl.BlockSpec(memory_space=pl.ANY)] * len(made),
            out_specs=[piece] * ZS
            + [pl.BlockSpec((4 * half_rows, 128), lambda i, m: (0, i + first))] * (blocks // 2),
            scratch_shapes=[
                pltpu.VMEM((blocks, 2 * half_rows, 128), BF16),
                pltpu.VMEM((blocks, head_dim, 2 * half_rows), BF16),
                pltpu.VMEM((query_count, 128), BF16),
                pltpu.VMEM((query_count, 128), BF16),
                pltpu.VMEM((head_dim, query_count), F32),
            ],
        ),
        out_shape=[jax.ShapeDtypeStruct((part, size), BF16)] * ZS
        + [jax.ShapeDtypeStruct((4 * half_rows, columns), BF16)] * (blocks // 2),
        input_output_aliases={
            1 + len(ins) - len(made) + at: at for at in range(len(made))
        },
        compiler_params=pltpu.CompilerParams(vmem_limit_bytes=VMEM_LIMIT),
        cost_estimate=work(12 * count),
        name="attend_backward",
    )(meta, *ins)


IN_VMEM = pl.BlockSpec(memory_space=pltpu.VMEM)


def small_call(kernel, meta, values, shapes, scratch=(), limit=32, name=None):
    return pl.pallas_call(
        kernel,
        grid_spec=pltpu.PrefetchScalarGridSpec(
            num_scalar_prefetch=1,
            grid=(),
            in_specs=[IN_VMEM] * len(values),
            out_specs=[IN_VMEM] * len(shapes),
            scratch_shapes=list(scratch),
        ),
        out_shape=[jax.ShapeDtypeStruct(shape, kind) for shape, kind in shapes],
        compiler_params=pltpu.CompilerParams(vmem_limit_bytes=limit << 20),
        cost_estimate=work(1),
        name=name,
    )(meta, *values)


def fold_kernel(meta_ref, kept_ref, got_ref, keep_ref, sent_ref, sum_ref):
    sum_ref[...] = (kept_ref[...].astype(F32) + got_ref[...].astype(F32)).astype(BF16)
    rows = keep_ref.shape[0]
    for at, ref in enumerate((keep_ref, sent_ref)):
        start = pl.multiple_of((meta_ref[0] ^ at) * rows, 16)
        ref[...] = sum_ref[pl.ds(start, rows), :]


def fold(bit, kept, got):
    rows, columns = kept.shape
    half = ((rows // 2, columns), BF16)
    return small_call(
        fold_kernel,
        bit,
        (kept, got),
        [half, half],
        [pltpu.VMEM((rows, columns), BF16)],
        name="fold",
    )


def unite_kernel(meta_ref, own_ref, got_ref, out_ref):
    rows = own_ref.shape[0]
    for at, ref in enumerate((own_ref, got_ref)):
        start = pl.multiple_of((meta_ref[0] ^ at) * rows, 16)
        out_ref[pl.ds(start, rows), :] = ref[...]


def unite(bit, own, got):
    rows, columns = own.shape
    return small_call(
        unite_kernel, bit, (own, got), [((2 * rows, columns), BF16)], name="unite"
    )[0]


def plus_kernel(meta_ref, one_ref, two_ref, out_ref, *, low):
    cut = slice(low, low + out_ref.shape[0])
    out_ref[...] = (one_ref[cut, :].astype(F32) + two_ref[cut, :].astype(F32)).astype(BF16)


def plus(meta, one, two, low=0):
    rows, columns = one.shape
    return small_call(
        partial(plus_kernel, low=low),
        meta,
        (one, two),
        [((rows - low, columns), BF16)],
        name="plus",
    )[0]


def prepare_kernel(meta_ref, *refs):
    sources, refs = refs[:3], refs[3:]
    kv_ref, query_ref, low_refs, head_ref = refs[0], refs[1], refs[2:5], refs[5]
    places, sems = refs[6:9], refs[9]
    copies = []
    for at in range(3):
        copies.append(pltpu.make_async_copy(sources[at], places[at], sems.at[at]))
        copies[-1].start()
    z_at, c_at = meta_ref[0], meta_ref[1]
    width = places[0].shape[1]
    part = width // ZS
    head_dim = width // HEADS
    parts = []
    for kind in range(3):
        ref = places[kind]
        copies[kind].wait()
        value = ref[...]
        low_refs[kind][...] = value.astype(BF16)
        half = ref.shape[0] // 2
        rows = ref[pl.ds(pl.multiple_of(c_at * half, half), half), :]
        head_ref[kind * half : (kind + 1) * half, :] = rows.astype(BF16)
        turn = lax.rem(width - z_at * part, width)
        parts.append(pltpu.roll(value, turn, 1)[:, :part])
    columns = []
    for head in range(part // head_dim):
        cut = slice(head * head_dim, (head + 1) * head_dim)
        columns += [parts[1][:, cut], parts[2][:, cut]]
    kv_ref[...] = jnp.concatenate(columns, axis=1).astype(BF16)
    query_ref[...] = parts[0].astype(BF16)


def prepare(meta, weights):
    count, width = weights[0].shape
    shapes = [(count, 2 * width // ZS), (count, width // ZS)] + [(count, width)] * 3
    shapes.append((3 * count // 2, width))
    return pl.pallas_call(
        prepare_kernel,
        grid_spec=pltpu.PrefetchScalarGridSpec(
            num_scalar_prefetch=1,
            grid=(),
            in_specs=[pl.BlockSpec(memory_space=pltpu.MemorySpace.HBM)] * 3,
            out_specs=[IN_VMEM] * len(shapes),
            scratch_shapes=[pltpu.VMEM((count, width), F32)] * 3
            + [pltpu.SemaphoreType.DMA((3,))],
        ),
        out_shape=[jax.ShapeDtypeStruct(shape, BF16) for shape in shapes],
        compiler_params=pltpu.CompilerParams(vmem_limit_bytes=VMEM_LIMIT),
        cost_estimate=work(1),
        name="prepare",
    )(meta, *weights)


def round_kernel(meta_ref, out_w, up_w, down_w, low_out, low_up, low_down, pack_ref):
    core = meta_ref[1]
    for source, target in ((out_w, low_out), (up_w, low_up), (down_w, low_down)):
        target[...] = source[...].astype(BF16)
    width = pack_ref.shape[1]
    low = 0
    half = out_w.shape[0] // 2
    rows = pl.ds(pl.multiple_of(core * half, half), half)
    pack_ref[low : low + half, :] = out_w[rows, :].astype(BF16)
    low += half
    count = up_w.shape[1] // 2
    for block in range(count // width):
        lanes = pl.ds(pl.multiple_of(core * count + block * width, 128), width)
        pack_ref[low : low + up_w.shape[0], :] = up_w[:, lanes].astype(BF16)
        low += up_w.shape[0]
    half = down_w.shape[0] // 2
    rows = pl.ds(pl.multiple_of(core * half, half), half)
    pack_ref[low : low + half, :] = down_w[rows, :].astype(BF16)


def round_weights(meta, weights):
    out_w, up_w, down_w = weights
    width = out_w.shape[1]
    total = out_w.shape[0] // 2 + up_w.shape[0] * (up_w.shape[1] // 2 // width)
    total += down_w.shape[0] // 2
    return small_call(
        round_kernel,
        meta,
        weights,
        [(item.shape, BF16) for item in weights] + [((total, width), BF16)],
        limit=60,
        name="round_weights",
    )


def project_kernel(meta_ref, first_ref, second_ref, *refs, shared):
    query_ref, kv_ref, turned_ref, token_ref, bias_ref = refs[-5:]
    part = query_ref.shape[0]
    rows, width = first_ref.shape
    split = 2 * part
    token_ref[:rows, :] = first_ref[...]
    token_ref[rows:, :] = second_ref[...]
    if shared:
        w_at, z_at = meta_ref[0], meta_ref[1]
        both = None
        bias_ref[...] = jnp.zeros_like(bias_ref)
        for at in range(2):
            count = refs[at].shape[0]
            cut = pl.ds(pl.multiple_of((w_at ^ at) * count, 128), count)
            tokens = token_ref[:, cut]
            terms = [matmul(tokens, refs[2 * at + kind][...]) for kind in range(2)]
            term = jnp.concatenate(terms, axis=1)
            both = term if both is None else both + term
            bias_ref[0:2, cut] = refs[4 + at][0:2, :].astype(F32)
        turn = lax.rem(width - z_at * part, width)
        bias = pltpu.roll(bias_ref[...], turn, 1)[:, :part]
        head_dim = width // HEADS
        pieces = []
        for head in range(part // head_dim):
            pieces.append(jnp.zeros((1, head_dim), F32))
            pieces.append(bias[1:2, head * head_dim : (head + 1) * head_dim])
        both = both + jnp.concatenate(pieces + [bias[0:1, :]], axis=1)
    else:
        both = matmul(token_ref[...], refs[0][...]) + refs[1][...]
    kv_ref[...] = both[:, :split].astype(BF16)
    scale = (part * ZS // HEADS) ** (-0.5)
    query_ref[...] = (both[:, split:].astype(BF16) * jnp.array(scale, BF16)).T
    turned_ref[...] = token_ref[...].T


def project(meta, first, second, sources):
    rows, width = first.shape
    part = width // ZS
    return small_call(
        partial(project_kernel, shared=len(sources) == 6),
        meta,
        (first, second, *sources),
        [((part, 2 * rows), BF16), ((2 * rows, 2 * part), BF16), ((width, 2 * rows), BF16)],
        [pltpu.VMEM((2 * rows, width), BF16), pltpu.VMEM((8, width), F32)],
        limit=40,
        name="project",
    )


def middle_kernel(meta_ref, tokens_ref, seed_ref, vec_ref, upoff_ref, *refs, groups, shared):
    mixed_refs = [refs[at * ZS : (at + 1) * ZS] for at in range(len(groups))]
    refs = refs[ZS * len(groups) :]
    weight_refs = refs[: 5 if shared else 3]
    refs = refs[len(weight_refs) :]
    outputs_ref, resid_ref = refs[:2]
    mgrad_refs = refs[2 : 2 + ZS]
    (
        send_ref,
        keep_ref,
        small_ref,
        out_w,
        up_w,
        down_w,
        slope_ref,
        wide_ref,
        tall_ref,
        sems,
    ) = refs[2 + ZS :]
    w_at, core, z_at = meta_ref[1], meta_ref[2], meta_ref[3]
    moves = [[], [], []]
    if shared:
        outs, ups, downs, got, pair = weight_refs
        count_o, count_u, count_d = outs.shape[0], ups.shape[0], downs.shape[0]
        for kind, (source, target) in enumerate(((outs, out_w), (ups, up_w), (downs, down_w))):
            start = pl.multiple_of(w_at * source.shape[0], source.shape[0])
            moves[kind].append((source, target.at[pl.ds(start, source.shape[0]), :]))
        lanes = got.shape[1]
        for source, which in ((got, core), (pair, 1 - core)):
            half = count_o // 2
            start = pl.multiple_of(((1 - w_at) * 2 + which) * half, half)
            moves[0].append((source.at[pl.ds(0, half), :], out_w.at[pl.ds(start, half), :]))
            low = half
            start = pl.multiple_of((1 - w_at) * count_u, count_u)
            for block in range(up_w.shape[1] // 2 // lanes):
                lane = pl.multiple_of(which * (up_w.shape[1] // 2) + block * lanes, 128)
                moves[1].append(
                    (
                        source.at[pl.ds(low, count_u), :],
                        up_w.at[pl.ds(start, count_u), pl.ds(lane, lanes)],
                    )
                )
                low += count_u
            half = count_d // 2
            start = pl.multiple_of(((1 - w_at) * 2 + which) * half, half)
            moves[2].append((source.at[pl.ds(low, half), :], down_w.at[pl.ds(start, half), :]))
    else:
        for kind, pair in enumerate(zip(weight_refs, (out_w, up_w, down_w))):
            moves[kind].append(pair)
    copies = []
    at = 0
    for kind in range(3):
        made = []
        for source, target in moves[kind]:
            made.append(pltpu.make_async_copy(source, target, sems.at[at]))
            made[-1].start()
            at += 1
        copies.append(made)
    rows, width = tokens_ref.shape
    hidden = upoff_ref.shape[1]
    part = width // ZS
    head_dim = width // HEADS
    quarter = hidden // 4

    def mean(value):
        return jnp.mean(value, axis=-1, keepdims=True)

    def norm(value):
        centered = value - mean(value)
        scale = lax.rsqrt(mean(centered * centered) + 1e-12)
        return centered * scale, scale

    def norm_back(grad, normal, scale):
        return scale * (grad - mean(grad) - normal * mean(grad * normal))

    def column(value):
        return jnp.sum(value, axis=0, keepdims=True)

    normed_at = 2 * quarter
    mixed_at = normed_at + width
    branch_at = mixed_at + width
    act_at = 5 * quarter
    for (first, count), pieces in zip(groups, mixed_refs):
        size = count * head_dim
        for at in range(ZS):
            low = mixed_at + (z_at ^ at) * part + first * head_dim
            send_ref[pl.ds(pl.multiple_of(low, head_dim), size), :] = pieces[at][...]
    mixed = send_ref[mixed_at:branch_at, :].T
    for copy in copies[0]:
        copy.wait()
    first_n, first_r = norm(tokens_ref[...] + (matmul(mixed, out_w[...]) + vec_ref[2:3, :]))
    normed = first_n * vec_ref[3:4, :] + vec_ref[4:5, :]
    low = normed.astype(BF16)
    send_ref[normed_at:mixed_at, :] = low.T
    for copy in copies[1] + copies[2]:
        copy.wait()
    quarters = []
    for half in range(2):
        for kept in (False, True):
            at = half * 2 * quarter + (core if kept else 1 - core) * quarter
            quarters.append((half, kept, pl.multiple_of(at, quarter)))
    acc = None
    for at, (half, kept, start) in enumerate(quarters):
        cut = pl.ds(start, quarter)
        pre_act = matmul(low, up_w[:, cut]) + upoff_ref[:, cut]
        phi = 0.5 + 0.5 * lax.erf(pre_act * (0.5**0.5))
        act = (pre_act * phi).astype(BF16)
        slope_ref[:, at * quarter : (at + 1) * quarter] = phi + pre_act * (
            jnp.exp(-0.5 * pre_act * pre_act) * 0.3989422804014327
        )
        target, base = (keep_ref, 0) if kept else (send_ref, act_at)
        target[base + half * quarter : base + (half + 1) * quarter, :] = act.T
        term = matmul(act, down_w[cut, :])
        acc = term if acc is None else acc + term
    second_n, second_r = norm(normed + (acc + vec_ref[5:6, :]))
    outputs_ref[...] = second_n * vec_ref[6:7, :] + vec_ref[7:8, :]
    place = lax.broadcasted_iota(jnp.int32, (rows, 1), 0)
    seed = jnp.where(place < meta_ref[0], seed_ref[...], 0.0)
    sum_grad = norm_back(seed * vec_ref[6:7, :], second_n, second_r)
    ffn = sum_grad.astype(BF16)
    for at in range(width // 256):
        low_row = act_at + 2 * quarter + at * rows
        send_ref[low_row : low_row + rows, :] = ffn[:, at * 256 : (at + 1) * 256]
    small_ref[3:4, :] = column(ffn.astype(F32))
    small_ref[4:5, :] = column(seed * second_n)
    small_ref[5:6, :] = column(seed)
    acc = sum_grad
    for at, (half, kept, start) in enumerate(quarters):
        cut = pl.ds(start, quarter)
        pre = right_trans(ffn, down_w[cut, :]) * slope_ref[:, at * quarter : (at + 1) * quarter]
        pre = pre.astype(BF16)
        target, base = (keep_ref, 2 * quarter) if kept else (send_ref, 0)
        for block in range(quarter // 256):
            row = base + (half * (quarter // 256) + block) * rows
            target[row : row + rows, :] = pre[:, block * 256 : (block + 1) * 256]
        sums = column(pre.astype(F32))
        line = 8 + half * (2 * quarter // width) + (core if kept else 1 - core)
        small_ref[pl.ds(line, 1), :] = sums
        acc = acc + right_trans(pre, up_w[:, cut])
    small_ref[1:2, :] = column(acc * first_n)
    small_ref[2:3, :] = column(acc)
    resid = norm_back(acc * vec_ref[3:4, :], first_n, first_r)
    resid_ref[...] = resid
    branch = resid.astype(BF16)
    wide_ref[...] = branch
    side = width // 2
    for target, base, which in (
        (send_ref, branch_at, 1 - core),
        (keep_ref, 4 * quarter, core),
    ):
        values = wide_ref[:, pl.ds(pl.multiple_of(which * side, 128), side)]
        target[base : base + rows, :] = values[:, :256]
        target[base + rows : base + 2 * rows, : side - 256] = values[:, 256:]
        target[base + rows : base + 2 * rows, side - 256 :] = jnp.zeros(
            (rows, 512 - side), BF16
        )
    small_ref[0:1, :] = column(branch.astype(F32))
    small_ref[6:8, :] = jnp.zeros((2, width), F32)
    small_ref[12:16, :] = jnp.zeros((4, width), F32)
    gap = branch_at + 2 * rows
    send_ref[gap:act_at, :] = jnp.zeros((act_at - gap, 256), BF16)
    tall_ref[...] = right_trans(out_w[...], branch).astype(BF16)
    for at in range(ZS):
        start = pl.multiple_of((z_at ^ at) * part, part)
        mgrad_refs[at][...] = tall_ref[pl.ds(start, part), :]


def middle(meta, mixed, groups, tokens, seed, vec, upoff, weights):
    rows, width = tokens.shape
    hidden = upoff.shape[1]
    in_vmem = pl.BlockSpec(memory_space=pltpu.VMEM)
    in_place = pl.BlockSpec(memory_space=pl.ANY)
    flat = [item for group in mixed for item in group]
    part = jax.ShapeDtypeStruct((width // ZS, rows), BF16)
    return pl.pallas_call(
        partial(middle_kernel, groups=groups, shared=len(weights) == 5),
        grid_spec=pltpu.PrefetchScalarGridSpec(
            num_scalar_prefetch=1,
            grid=(),
            in_specs=[in_vmem] * (4 + len(flat)) + [in_place] * len(weights),
            out_specs=[in_vmem] * (5 + ZS),
            scratch_shapes=[
                pltpu.VMEM((width, width), BF16),
                pltpu.VMEM((width, hidden), BF16),
                pltpu.VMEM((hidden, width), BF16),
                pltpu.VMEM((rows, hidden), F32),
                pltpu.VMEM((rows, width), BF16),
                pltpu.VMEM((width, rows), BF16),
                pltpu.SemaphoreType.DMA((11,)),
            ],
        ),
        out_shape=[jax.ShapeDtypeStruct((rows, width), F32)] * 2
        + [part] * ZS
        + [
            jax.ShapeDtypeStruct((2 * hidden, 256), BF16),
            jax.ShapeDtypeStruct((hidden + 2 * rows, 256), BF16),
            jax.ShapeDtypeStruct((16, width), F32),
        ],
        compiler_params=pltpu.CompilerParams(vmem_limit_bytes=VMEM_LIMIT),
        cost_estimate=work(15),
        name="middle",
    )(meta, tokens, seed, vec, upoff, *flat, *weights)


def down_kernel(meta_ref, keep_ref, got_ref, own_ffn_ref, got_ffn_ref, out_ref):
    keep, got = keep_ref[...], got_ref[...]
    rows = keep.shape[1]
    for at in range(out_ref.shape[1] // 256):
        cut = slice(at * rows, (at + 1) * rows)
        value = matmul(keep, own_ffn_ref[cut, :]) + matmul(got, got_ffn_ref[cut, :])
        out_ref[:, at * 256 : (at + 1) * 256] = value.astype(BF16)


def down_slab(meta, keep, send, got):
    block = send.shape[0] // 8
    kept = pl.BlockSpec((block, send.shape[1]), lambda i, m: (m[0], 0))
    act = pl.BlockSpec((block, send.shape[1]), lambda i, m: (5 + m[0], 0))
    ffn = pl.BlockSpec((block, send.shape[1]), lambda i, m: (7, 0))
    return pl.pallas_call(
        down_kernel,
        grid_spec=pltpu.PrefetchScalarGridSpec(
            num_scalar_prefetch=1,
            grid=(1,),
            in_specs=[kept, act, ffn, ffn],
            out_specs=pl.BlockSpec((block, block), lambda i, m: (0, 0)),
        ),
        out_shape=jax.ShapeDtypeStruct((block, block), BF16),
        compiler_params=pltpu.CompilerParams(vmem_limit_bytes=24 << 20),
        cost_estimate=work(2),
        name="down_slab",
    )(meta, keep, got, send, got)


def up_kernel(meta_ref, keep_ref, send_ref, got_ref, own_small_ref, got_small_ref, *refs):
    out_refs, table_ref = refs[:2], refs[2]
    rows = send_ref.shape[1]
    width = own_small_ref.shape[1]
    block = width // 4
    side = width // 2
    normed_at = 2 * width
    branch_at = normed_at + 2 * width
    x_at = meta_ref[0]
    pre_keep = 2 * width
    for w in range(2):
        small = own_small_ref[...] + got_small_ref[...]
        table_ref[...] = jnp.zeros_like(table_ref)
        for at in range(side // 128):
            low = w * side + at * 128
            table_ref[at * 8 : (at + 1) * 8, :] = small[:8, low : low + 128]
        base = side // 128 * 8
        for at in range(2 * width // 128):
            line = 8 + 2 * w + at // (width // 128)
            low = at % (width // 128) * 128
            table_ref[base + at : base + at + 1, :] = small[line : line + 1, low : low + 128]
        for out_ref, which in zip(out_refs, (1 - x_at, x_at)):
            start = pl.multiple_of(which * block, block)
            target = slice(w * block, (w + 1) * block)
            own = send_ref[pl.ds(normed_at + w * side + start, block), :]
            got = got_ref[pl.ds(normed_at + w * side + start, block), :]
            for at in range(normed_at // rows):
                cut = slice(at * rows, (at + 1) * rows)
                value = matmul(own, keep_ref[pre_keep + at * rows : pre_keep + (at + 1) * rows, :])
                value = value + matmul(got, got_ref[cut, :])
                out_ref[target, at * 256 : (at + 1) * 256] = value.astype(BF16)
            own = send_ref[pl.ds(normed_at + width + w * side + start, block), :]
            got = got_ref[pl.ds(normed_at + width + w * side + start, block), :]
            lane = normed_at // rows * 256
            for at in range(2):
                mine = 4 * width + at * rows
                theirs = branch_at + at * rows
                value = matmul(own, keep_ref[mine : mine + rows, :])
                value = value + matmul(got, got_ref[theirs : theirs + rows, :])
                value = value[:, : min(256, side - at * 256)].astype(BF16)
                out_ref[target, lane : lane + value.shape[1]] = value
                lane += value.shape[1]
            out_ref[target, lane : lane + 128] = table_ref[pl.ds(start, block), :].astype(BF16)


def up_slabs(meta, keep, send, got, own_small, got_small):
    width = own_small.shape[1]
    columns = 2 * width + width // 2 + 128
    first = pl.BlockSpec((5 * width, send.shape[1]), lambda i, m: (0, 0))

    def whole(value):
        return pl.BlockSpec(value.shape, lambda i, m: (0, 0))

    return pl.pallas_call(
        up_kernel,
        grid_spec=pltpu.PrefetchScalarGridSpec(
            num_scalar_prefetch=1,
            grid=(1,),
            in_specs=[whole(keep), first, first, whole(own_small), whole(own_small)],
            out_specs=[pl.BlockSpec((width // 2, columns), lambda i, m: (0, 0))] * 2,
            scratch_shapes=[pltpu.VMEM((width // 2, 128), F32)],
        ),
        out_shape=[jax.ShapeDtypeStruct((width // 2, columns), BF16)] * 2,
        compiler_params=pltpu.CompilerParams(vmem_limit_bytes=40 << 20),
        cost_estimate=work(4),
        name="up_slabs",
    )(meta, keep, send, got, own_small, got_small)


def key_sum_kernel(own_ref, core_ref, got_ref, *out_refs):
    size = out_refs[0].shape[1]
    for at, ref in enumerate(out_refs):
        cut = slice(at * size, (at + 1) * size)
        kept = (own_ref[cut, :].astype(F32) + core_ref[cut, :].astype(F32)).astype(BF16)
        ref[...] = (kept.astype(F32) + got_ref[cut, :].astype(F32)).astype(BF16).T


def key_sum(own, core, got):
    rows, columns = got.shape
    half = pl.BlockSpec((rows, columns), lambda i: (0, 0))
    return pl.pallas_call(
        key_sum_kernel,
        grid=(1,),
        in_specs=[half] * 3,
        out_specs=[pl.BlockSpec((columns, rows // ZS), lambda i: (0, 0))] * ZS,
        out_shape=[jax.ShapeDtypeStruct((columns, rows // ZS), BF16)] * ZS,
        compiler_params=pltpu.CompilerParams(vmem_limit_bytes=24 << 20),
        cost_estimate=work(2),
        name="key_sum",
    )(own, core, got)


def head_kernel(meta_ref, *refs):
    turned_refs, query_refs, kv_refs = refs[:2], refs[2 : 2 + ZS], refs[2 + ZS : 2 + 2 * ZS]
    refs = refs[2 + 2 * ZS :]
    out_ref = refs[-1]
    block = turned_refs[0].shape[0]

    def put(value, rows):
        columns = value.shape[1]
        if len(refs) == 2:
            value = value + refs[0][rows, :columns].astype(F32)
        out_ref[rows, :columns] = value.astype(BF16)
        out_ref[rows, columns:] = jnp.zeros((value.shape[0], out_ref.shape[1] - columns), BF16)

    grads = [jnp.concatenate([ref[...] for ref in items], axis=1) for items in (query_refs, kv_refs)]
    grads = jnp.concatenate(grads, axis=0)
    turned = jnp.concatenate([ref[...] for ref in turned_refs], axis=1)
    put(right_trans(turned, grads), slice(0, block))
    ones = jnp.ones((16, turned.shape[1]), BF16)
    put(right_trans(ones, grads), slice(block, block + 16))


def head_slab(meta, turned, query, kv, count, slabs, got=None, first=0):
    width, rows = turned[0].shape
    block = width // count
    columns = -(-(query[0].shape[0] + kv[0].shape[0]) // 128) * 128
    return pl.pallas_call(
        head_kernel,
        grid_spec=pltpu.PrefetchScalarGridSpec(
            num_scalar_prefetch=1,
            grid=(slabs,),
            in_specs=[pl.BlockSpec((block, rows), lambda i, m: (m[i] * 2 + m[slabs], 0))] * 2
            + [pl.BlockSpec(item.shape, lambda i, m: (0, 0)) for item in [*query, *kv]]
            + (
                []
                if got is None
                else [pl.BlockSpec((block + 16, columns), lambda i, m: (first + i, 0))]
            ),
            out_specs=pl.BlockSpec((block + 16, columns), lambda i, m: (i, 0)),
        ),
        out_shape=jax.ShapeDtypeStruct((slabs * (block + 16), columns), BF16),
        compiler_params=pltpu.CompilerParams(vmem_limit_bytes=24 << 20),
        cost_estimate=work(2),
        name="head_slab",
    )(meta, *turned, *query, *kv, *(() if got is None else (got,)))


def token_kernel(meta_ref, resid_ref, *refs, shared):
    query_refs, kv_refs, refs = refs[:ZS], refs[ZS : 2 * ZS], refs[2 * ZS :]
    weight_refs, refs = refs[: 5 if shared else 3], refs[5 if shared else 3 :]
    out_ref, full_ref, turned_ref, sems = refs
    w_at, c_at, z_at = meta_ref[1], meta_ref[2], meta_ref[3]
    width = full_ref.shape[1]
    moves = []
    if shared:
        count = weight_refs[0].shape[0]
        half = count // 2
        for kind in range(3):
            start = pl.multiple_of(w_at * count, count)
            moves.append((weight_refs[kind], full_ref.at[kind, pl.ds(start, count), :]))
            for ref, core in ((weight_refs[3], c_at), (weight_refs[4], 1 - c_at)):
                start = pl.multiple_of(((1 - w_at) * 2 + core) * half, half)
                moves.append(
                    (
                        ref.at[pl.ds(kind * half, half), :],
                        full_ref.at[kind, pl.ds(start, half), :],
                    )
                )
    else:
        for kind in range(3):
            moves.append((weight_refs[kind], full_ref.at[kind]))
    copies = []
    for at, (source, target) in enumerate(moves):
        copies.append(pltpu.make_async_copy(source, target, sems.at[at]))
        copies[-1].start()
    part = width // ZS
    head_dim = width // HEADS
    for at in range(ZS):
        low = (z_at ^ at) * part
        turned_ref[0, pl.ds(pl.multiple_of(low, part), part), :] = query_refs[at][...]
        for head in range(part // head_dim):
            start = pl.ds(pl.multiple_of(low + head * head_dim, head_dim), head_dim)
            for kind in (1, 2):
                row = (2 * head + kind - 1) * head_dim
                turned_ref[kind, start, :] = kv_refs[at][row : row + head_dim, :]
    parts = [turned_ref[kind].T for kind in range(3)]
    for copy in copies:
        copy.wait()
    out = resid_ref[...]
    for kind in range(3):
        out = out + right_trans(parts[kind], full_ref[kind])
    out_ref[...] = out


def token_gradient(meta, resid, query, kv, weights):
    rows, width = resid.shape
    in_vmem = pl.BlockSpec(memory_space=pltpu.VMEM)
    in_place = pl.BlockSpec(memory_space=pl.ANY)
    return pl.pallas_call(
        partial(token_kernel, shared=len(weights) == 5),
        grid_spec=pltpu.PrefetchScalarGridSpec(
            num_scalar_prefetch=1,
            grid=(),
            in_specs=[in_vmem] * (1 + 2 * ZS) + [in_place] * len(weights),
            out_specs=in_vmem,
            scratch_shapes=[
                pltpu.VMEM((3, width, width), BF16),
                pltpu.VMEM((3, width, rows), BF16),
                pltpu.SemaphoreType.DMA((9,)),
            ],
        ),
        out_shape=jax.ShapeDtypeStruct((rows, width), F32),
        compiler_params=pltpu.CompilerParams(vmem_limit_bytes=32 << 20),
        cost_estimate=work(4),
        name="token_gradient",
    )(meta, resid, *query, *kv, *weights)


def down_finish_kernel(meta_ref, *refs):
    block = refs[0].shape[0] // 4
    c_at, x_at = meta_ref[0], meta_ref[1]
    for at in range(4):
        for z in range(4):
            place = (c_at ^ (at >> 1)) * 8 + z * 2 + (x_at ^ (at & 1))
            start = pl.multiple_of(place * block, 8)
            refs[4][pl.ds(start, block), :] = refs[at][z * block : (z + 1) * block, :].astype(F32)


def down_finish(meta, pieces):
    block, width = pieces[0].shape
    in_vmem = pl.BlockSpec(memory_space=pltpu.VMEM)
    return pl.pallas_call(
        down_finish_kernel,
        grid_spec=pltpu.PrefetchScalarGridSpec(
            num_scalar_prefetch=1, grid=(), in_specs=[in_vmem] * 4, out_specs=in_vmem
        ),
        out_shape=jax.ShapeDtypeStruct((4 * block, width), F32),
        compiler_params=pltpu.CompilerParams(vmem_limit_bytes=32 << 20),
        cost_estimate=work(4),
        name="down_finish",
    )(meta, *pieces)


def up_finish_kernel(meta_ref, *refs):
    pieces = refs[:4]
    up_ref, out_ref, small_ref = refs[4:]
    block = pieces[0].shape[0]
    quarter = up_ref.shape[1] // 4
    side = out_ref.shape[1] // 2
    c_at, x_at = meta_ref[0], meta_ref[1]
    for at in range(4):
        start = pl.multiple_of((x_at ^ (at & 1)) * block, 8)
        rows = pl.ds(start, block)
        core = c_at ^ (at >> 1)
        for half in range(2):
            lanes = pl.ds(pl.multiple_of((2 * half + core) * quarter, 128), quarter)
            up_ref[rows, lanes] = pieces[at][:, half * quarter : (half + 1) * quarter].astype(F32)
        out_ref[rows, pl.ds(pl.multiple_of(core * side, 128), side)] = (
            pieces[at][:, 2 * quarter : 2 * quarter + side].astype(F32)
        )
        if at < 2:
            small_ref[rows, :] = pieces[at][:, 2 * quarter + side :].astype(F32)


def up_finish(meta, pieces, hidden, width):
    block = pieces[0].shape[0]
    in_vmem = pl.BlockSpec(memory_space=pltpu.VMEM)
    shapes = [(2 * block, hidden), (2 * block, width), (2 * block, 128)]
    return pl.pallas_call(
        up_finish_kernel,
        grid_spec=pltpu.PrefetchScalarGridSpec(
            num_scalar_prefetch=1,
            grid=(),
            in_specs=[in_vmem] * 4,
            out_specs=[in_vmem] * 3,
        ),
        out_shape=[jax.ShapeDtypeStruct(shape, F32) for shape in shapes],
        compiler_params=pltpu.CompilerParams(vmem_limit_bytes=40 << 20),
        cost_estimate=work(5),
        name="up_finish",
    )(meta, *pieces)


def head_finish_kernel(meta_ref, own_ref, got_ref, query_ref, key_ref, value_ref, bias_ref, *, part):
    size = own_ref.shape[0] // ZS
    block = size - 16
    head_dim = part // 3
    for at, source in enumerate((own_ref, got_ref)):
        start = pl.multiple_of((meta_ref[0] ^ at) * block, 8)
        rows = pl.ds(start, block)
        keys, values, queries = [], [], []
        for z in range(ZS):
            item = source[((z & 1) * 2 + (z >> 1)) * size :][:size].astype(F32)
            for head in range(3):
                low = part + head * 2 * head_dim
                keys.append(item[:, low : low + head_dim])
                values.append(item[:, low + head_dim : low + 2 * head_dim])
            queries.append(item[:, :part])
        key = jnp.concatenate(keys, axis=1)
        value = jnp.concatenate(values, axis=1)
        query = jnp.concatenate(queries, axis=1)
        query_ref[rows, :] = query[:block]
        key_ref[rows, :] = key[:block]
        value_ref[rows, :] = value[:block]
        if at == 0:
            bias_ref[0:8, :] = query[block : block + 8]
            bias_ref[8:16, :] = value[block : block + 8]


def head_finish(meta, own, got, width):
    rows = own.shape[0]
    rows = 2 * (rows // ZS - 16)
    return small_call(
        partial(head_finish_kernel, part=width // ZS),
        meta,
        (own, got),
        [((rows, width), F32)] * 3 + [((16, width), F32)],
        limit=40,
        name="head_finish",
    )


def in_order(index, own, other, axis):
    return jnp.where(
        index == 0,
        jnp.concatenate([own, other], axis=axis),
        jnp.concatenate([other, own], axis=axis),
    )


def part_of(value, index, count, axis):
    size = value.shape[axis] // count
    return lax.dynamic_slice_in_dim(value, index * size, size, axis)


def body(
    inputs,
    lengths,
    cotangent,
    query_weight,
    query_bias,
    key_weight,
    value_weight,
    value_bias,
    output_weight,
    output_bias,
    first_gain,
    first_shift,
    up_weight,
    up_bias,
    down_weight,
    down_bias,
    second_gain,
    second_shift,
    *,
    sizes,
):
    count_o, count_w = sizes
    w_at = lax.axis_index("w")
    z_at = lax.axis_index("z")
    c_at = lax.axis_index("c")
    x_at = lax.axis_index("x")
    o_at = lax.axis_index("o")
    tokens = inputs[0]
    local_rows, width = tokens.shape
    head_dim = width // HEADS
    heads = HEADS // ZS
    part = heads * head_dim
    length = lengths[0]

    hold = lax.optimization_barrier

    near = ((0, 1), (1, 0), (2, 3), (3, 2))
    far = ((0, 2), (2, 0), (1, 3), (3, 1))
    cross = ((0, 3), (3, 0), (1, 2), (2, 1))

    def exchange(pieces):
        return [pieces[0]] + [
            lax.ppermute(item, "z", perm) for item, perm in zip(pieces[1:], (near, far, cross))
        ]

    own_rows = query_weight.shape[0]
    big_weights = (output_weight, up_weight, down_weight)
    sides = jnp.stack([z_at, c_at]).astype(jnp.int32)
    low_tokens = tokens.astype(BF16)
    kv_own, query_own, *low_heads, head_pack = prepare(
        sides, (query_weight, key_weight, value_weight)
    )
    line_tokens = [low_tokens, lax.ppermute(low_tokens, "z", near)]
    line_tokens.append(lax.ppermute(low_tokens, "z", far))
    early = jnp.stack([query_bias, value_bias]).astype(BF16)
    late = jnp.stack(
        [
            item.reshape(-1, own_rows)[row]
            for item in (
                output_bias,
                first_gain,
                first_shift,
                down_bias,
                second_gain,
                second_shift,
                up_bias,
            )
            for row in range(item.shape[0] // own_rows)
        ]
    )
    if count_w == 2:
        kv_other, query_other, early_got = [
            swap(item, "w") for item in (kv_own, query_own, early)
        ]
        *low_weights, weight_pack = round_weights(sides, big_weights)
        kv_other, query_other, early_got, weight_pack, *line_tokens[1:3] = hold(
            (kv_other, query_other, early_got, weight_pack, *line_tokens[1:3])
        )
        weight_got = swap(weight_pack, "w")
        sources = (kv_own, query_own, kv_other, query_other, early, early_got)
    else:
        attn_own = jnp.concatenate([kv_own, query_own], axis=1)
        attn_full = lax.all_gather(attn_own, "w", axis=0, tiled=True)
        small = jnp.concatenate([early, late.astype(BF16)], axis=0)
        small_all = lax.all_gather(small, "w", axis=0, tiled=False)
        low_weights = [item.astype(BF16) for item in big_weights]
        weight_got = [lax.all_gather(item, "w", axis=0, tiled=True) for item in low_weights]
        head_weights = [lax.all_gather(item, "w", axis=0, tiled=True) for item in low_heads]
        pair = jnp.transpose(small_all[:, :2], (1, 0, 2)).reshape(2, width).astype(F32)
        own_bias = lax.dynamic_slice_in_dim(pair, z_at * part, part, 1)
        value_bias_own = own_bias[1].reshape(heads, 1, head_dim)
        kv_bias = jnp.concatenate([jnp.zeros_like(value_bias_own), value_bias_own], axis=1)
        bias_row = jnp.concatenate([kv_bias.reshape(1, 2 * part), own_bias[:1]], axis=1)
        sources = (attn_full, bias_row)

    line_tokens.append(lax.ppermute(line_tokens[2], "z", near))
    corner = jnp.stack([w_at, z_at]).astype(jnp.int32)
    made = [project(corner, *line_tokens[:2], sources)]
    made[0], *line_tokens[2:] = hold((made[0], *line_tokens[2:]))
    made.append(project(corner, *line_tokens[2:], sources))
    queries = [item[0] for item in made]
    turned = [item[2] for item in made]
    kv_blocks = [[item[1] for item in made]]
    for axis in ("x", "c", "o")[: 3 if count_o == 2 else 2]:
        kv_blocks = kv_blocks + [[swap(item, axis) for item in pair] for pair in kv_blocks]
    places = []
    for at in range(4 * count_o):
        o_of = o_at ^ (at >> 2)
        places.append(o_of * 16 + (x_at ^ (at & 1)) * 2 + (c_at ^ ((at >> 1) & 1)))
    meta = jnp.stack([length, z_at] + places).astype(jnp.int32)
    kv_blocks = [
        [pltpu.with_memory_space_constraint(item, pltpu.MemorySpace.HBM) for item in pair]
        for pair in kv_blocks
    ]
    attended, *made = attend_forward(meta, queries, kv_blocks, heads)
    logs = made[ZS]
    if count_w == 2:
        attended, weight_got, head_pack, late = hold((attended, weight_got, head_pack, late))
        late = late.astype(BF16)
        small_own = jnp.concatenate([early, late], axis=0)
        small_got = jnp.concatenate([early_got, swap(late, "w")], axis=0)
        small_all = in_order(w_at, small_own[None], small_got[None], 0)
        weights = [*low_weights, weight_got, swap(weight_got, "c")]
        head_got = swap(head_pack, "w")
    else:
        weights = weight_got
    mixed = exchange(made[:ZS])
    small_all = small_all.astype(F32)
    vec = jnp.transpose(small_all[:, :8], (1, 0, 2)).reshape(8, width)
    up_offset = small_all[:, 8:].reshape(1, -1)

    split = count_w == 2 and count_o == 1
    my_index = o_at * 16 + z_at * 4 + x_at * 2 + c_at
    rest = jnp.clip(length - my_index * local_rows, 0, local_rows)
    core = c_at if split else jnp.zeros_like(c_at)
    spots = jnp.stack([rest, w_at, core, z_at]).astype(jnp.int32)
    outputs, resid_grad, *made = middle(
        spots, [mixed], ((0, heads),), tokens, cotangent[0], vec, up_offset, weights
    )
    head_grads = exchange(made[:ZS])
    send, keep, small_own = made[ZS:]
    hidden = up_offset.shape[1]

    near_bit, far_bit = z_at & 1, z_at >> 1

    def add_pair(kept, got):
        return (kept.astype(F32) + got.astype(F32)).astype(BF16)

    def join(value, got, bit):
        return in_order(bit, value, got, 0)

    spot = jnp.stack([c_at, x_at]).astype(jnp.int32)
    token = [spot]

    def arrive(*values):
        token[0], *values = hold((token[0], *values))
        return values[0] if len(values) == 1 else values

    def backward(first, count, made=()):
        return attend_backward(
            meta, queries, head_grads, attended, logs, kv_blocks, first, count, made
        )

    def to_near(value):
        return lax.ppermute(value, "z", near)

    def to_far(value):
        return lax.ppermute(value, "z", far)

    def head_part(ws, core, got=None, first=0):
        at = jnp.stack([jnp.asarray(item) for item in (*ws, core)]).astype(jnp.int32)
        return head_slab(at, turned, query_low, kv_low, 2 * count_w, len(ws), got, first)

    def pick(w, c):
        return jnp.stack([jnp.asarray(w), jnp.asarray(c)]).astype(jnp.int32)

    if split:
        got, small_got = swap(send, "c"), swap(small_own, "c")
        down_far = down_slab(pick(1 - w_at, 0), keep, send, got)
        up_sent, up_kept = up_slabs(
            jnp.stack([x_at]).astype(jnp.int32), keep, send, got, small_own, small_got
        )
        down_near = down_slab(pick(1 * w_at, 0), keep, send, got)
        down_far, up_sent, down_near, *head_grads = hold(
            (down_far, up_sent, down_near, *head_grads)
        )
        made = backward(0, heads - 1)
        down_got, *made = arrive(swap(down_far, "w"), *made)
        down_sum = add_pair(down_near, down_got)
        down_got = to_near(part_of(down_sum, 1 - near_bit, 2, 0))
        down_sum, *head_grads = arrive(down_sum, *head_grads)
        made = backward(heads - 1, 1, made)
        down_got, up_got, head_got, *made = arrive(
            down_got, swap(up_sent, "x"), head_got, *made
        )
        query_low, pairs = made[:ZS], made[ZS:]
        head_weights = [*low_heads, head_got, swap(head_got, "c")]
        pair_got = swap(pairs[1], "c")
        query_got = exchange(query_low)
        up_sum = add_pair(up_kept, up_got).reshape(2, own_rows // 2, -1)
        up_got = swap(lax.dynamic_index_in_dim(up_sum, 1 - w_at, 0, keepdims=False), "w")
        pair_got = arrive(pair_got)
        half_rows = pair_got.shape[0] // 2
        pair_sent = add_pair(pairs[0][half_rows:], pair_got[half_rows:])
        pair_sent, down_got = arrive(pair_sent, down_got)
        key_got = swap(pair_sent, "x")
        down_sum = add_pair(part_of(down_sum, near_bit, 2, 0), down_got)
        down_got = to_far(part_of(down_sum, 1 - far_bit, 2, 0))
        key_got, down_got, up_got, *query_got = arrive(key_got, down_got, up_got, *query_got)
        up_sum = add_pair(lax.dynamic_index_in_dim(up_sum, w_at, 0, keepdims=False), up_got)
        up_sent, key_got = arrive(part_of(up_sum, 1 - near_bit, 2, 0), key_got)
        up_got = to_near(up_sent)
        kv_low = key_sum(pairs[0], pair_got, key_got)
        down_sum = add_pair(part_of(down_sum, far_bit, 2, 0), down_got)
        down_got = swap(part_of(down_sum, 1 - x_at, 2, 0), "x")
        head_core = swap(head_part((1 - w_at, 1 * w_at), 1 - c_at), "c")
        kv_got = exchange(kv_low)
        down_got = arrive(down_got)
        down_sum = add_pair(part_of(down_sum, x_at, 2, 0), down_got)
        down_got = to_far(down_sum)
        head_core = arrive(head_core)
        head_both = head_part((1 - w_at, 1 * w_at), c_at, head_core)
        head_rows = head_both.shape[0] // 2
        head_sent = swap(head_both[:head_rows], "w")
        head_sum = head_both[head_rows:]
        up_got = arrive(up_got)
        up_sum = add_pair(part_of(up_sum, near_bit, 2, 0), up_got)
        up_got = to_far(part_of(up_sum, 1 - far_bit, 2, 0))
        head_sent = arrive(head_sent)
        head_sum = add_pair(head_sum, head_sent)
        head_got = swap(head_sum, "x")
        kv_got = arrive(*kv_got)
        input_grad = token_gradient(
            spots, resid_grad, query_got, kv_got, head_weights
        )
        up_got = arrive(up_got)
        up_sum = add_pair(part_of(up_sum, far_bit, 2, 0), up_got)
        up_got = to_far(up_sum)
        down_got = arrive(down_got)
        down_sum = join(down_sum[None], down_got[None], far_bit)
        down_got = to_near(down_sum)
        head_got = arrive(head_got)
        head_sum = add_pair(head_sum, head_got)
        head_got = to_far(head_sum)
        up_got = arrive(up_got)
        up_sum = join(up_sum, up_got, far_bit)
        up_got = to_near(up_sum)
        down_got = arrive(down_got)
        down_sum = join(down_sum[None], down_got[None], near_bit)
        down_sum = down_sum.reshape(-1, width)
        down_x = swap(down_sum, "x")
        down_c = swap(down_sum, "c")
        head_got = arrive(head_got)
        head_two = join(head_sum, head_got, far_bit)
        head_got = to_near(head_two)
        up_got = arrive(up_got)
        up_sum = join(up_sum, up_got, near_bit)
        up_x = swap(up_sum, "x")
        up_c = swap(up_sum, "c")
        down_x, input_grad = arrive(down_x, input_grad)
        down_pieces = [down_sum, down_x, down_c, swap(down_x, "c")]
        head_got = arrive(head_got)
        head_four = join(head_two, head_got, near_bit)
        head_other = swap(head_four, "c")
        total_down = down_finish(spot, down_pieces)
        up_x, total_down = arrive(up_x, total_down)
        up_pieces = [up_sum, up_x, up_c, swap(up_x, "c")]
        total_query, total_key, total_value, head_bias = head_finish(
            spot, head_four, head_other, width
        )
        total_query, total_key, total_value = arrive(total_query, total_key, total_value)
        total_up, total_out, table = up_finish(token[0], up_pieces, hidden, width)
        groups = own_rows // 128
        small_total = table[: 8 * groups].reshape(groups, 8, 128)
        vectors = [small_total[:, at].reshape(own_rows) for at in range(6)]
        lines = hidden // count_w // 128
        total_up_bias = table[8 * groups : 8 * groups + lines].reshape(-1)
    else:
        made = backward(0, heads)
        query_low, pairs = made[:ZS], made[ZS:]
        if count_o == 2:
            pairs = [plus(spot, pairs[at], swap(pairs[at + 2], "o")) for at in range(2)]
        pair_got = swap(pairs[1], "c")
        half_rows = pair_got.shape[0] // 2
        key_got = swap(plus(spot, pairs[0], pair_got, half_rows), "x")
        kv_low = key_sum(pairs[0], pair_got, key_got)
        if count_w == 2:
            head_weights = [*low_heads, head_got, swap(head_got, "c")]
        input_grad = token_gradient(
            spots.at[2].set(c_at.astype(jnp.int32)),
            resid_grad,
            exchange(query_low),
            exchange(kv_low),
            head_weights,
        )
        every_w = tuple(range(count_w))
        slabs = head_part(every_w, c_at, swap(head_part(every_w, 1 - c_at), "c"))
        head_sum = lax.psum_scatter(slabs, "w", scatter_dimension=0, tiled=True)
        head_sum = plus(spot, head_sum, swap(head_sum, "x"))
        if count_o == 2:
            head_sum = plus(spot, head_sum, swap(head_sum, "o"))
        n_bit, f_bit = [
            jnp.stack([bit, bit]).astype(jnp.int32) for bit in (near_bit, far_bit)
        ]
        head_sum = unite(f_bit, head_sum, to_far(head_sum))
        head_sum = unite(n_bit, head_sum, to_near(head_sum))
        total_query, total_key, total_value, head_bias = head_finish(
            spot, head_sum, swap(head_sum, "c"), width
        )
        quarter = hidden // 4
        count = quarter // 256
        act_at = 5 * quarter
        act = [keep[:quarter], send[act_at : act_at + quarter], keep[quarter : 2 * quarter]]
        act += [send[act_at + quarter : act_at + 2 * quarter]]
        act = jnp.concatenate(act, axis=0)

        def rows_of(value, low, at):
            return value[low + at * local_rows : low + (at + 1) * local_rows]

        ffn_at = act_at + 2 * quarter
        ffn = jnp.concatenate([rows_of(send, ffn_at, at) for at in range(width // 256)], axis=1)
        pre = []
        for half in range(2):
            pre += [rows_of(keep, 2 * quarter, half * count + at) for at in range(count)]
            pre += [rows_of(send, 0, half * count + at) for at in range(count)]
        pre = jnp.concatenate(pre, axis=1)
        normed_turned = send[2 * quarter : 2 * quarter + width]
        mixed_turned = send[2 * quarter + width : 2 * quarter + 2 * width]
        side = width // 2
        branch = jnp.concatenate(
            [
                rows_of(keep, 4 * quarter, 0),
                rows_of(keep, 4 * quarter, 1)[:, : side - 256],
                rows_of(send, 2 * quarter + 2 * width, 0),
                rows_of(send, 2 * quarter + 2 * width, 1)[:, : side - 256],
            ],
            axis=1,
        )

        def sum_all(value):
            value = value.astype(BF16)
            value = lax.psum_scatter(value, "w", scatter_dimension=0, tiled=True)
            return lax.psum(value, ("o", "z", "x", "c")).astype(F32)

        total_down = sum_all(matmul(act, ffn))
        total_up = sum_all(matmul(normed_turned, pre))
        total_out = sum_all(matmul(mixed_turned, branch))
        small_own = lax.psum(small_own, ("o", "z", "x", "c", "w"))
        vectors = [part_of(small_own[at], w_at, count_w, 0) for at in range(6)]
        total_up_bias = part_of(small_own[8:12].reshape(-1), w_at, count_w, 0)

    totals = [part_of(head_bias[at], w_at, count_w, 0) for at in (0, 8)] + vectors
    return (
        outputs[None],
        input_grad[None],
        total_query,
        totals[0],
        total_key,
        total_value,
        totals[1],
        total_out,
        totals[2],
        totals[3],
        totals[4],
        total_up,
        total_up_bias,
        total_down,
        totals[5],
        totals[6],
        totals[7],
    )


def solution(mesh):
    count_s = mesh.shape["seq"]
    count_w = mesh.shape["wshard"]
    count_o = count_s // 16
    fine = Mesh(
        mesh.devices.reshape(count_o, ZS, 2, 2, count_w), ("o", "z", "x", "c", "w")
    )
    seq = ("o", "z", "x", "c")
    rows = P("w", seq, None)
    matrix = P("w", None)
    vector = P("w")
    placed = (
        rows,
        vector,
        rows,
        matrix,
        vector,
        matrix,
        matrix,
        vector,
        matrix,
        vector,
        vector,
        vector,
        matrix,
        vector,
        matrix,
        vector,
        vector,
        vector,
    )
    return jax.shard_map(
        partial(body, sizes=(count_o, count_w)),
        mesh=fine,
        in_specs=placed,
        out_specs=(
            rows,
            rows,
            matrix,
            vector,
            matrix,
            matrix,
            vector,
            matrix,
            vector,
            vector,
            vector,
            matrix,
            vector,
            matrix,
            vector,
            vector,
            vector,
        ),
        check_vma=False,
    )
```
